32 devices in a mesh: clip: 4 (over y, core), tok: 8 (over z, x).
Axes of the slice: x: 2, y: 2, z: 4, core: 2. Of those that a mesh axis runs over, the one named last changes fastest.
Arguments:
- tokens: float32 [32, 2, 2, 196, 768], P(('clip', 'tok')), may hold values from -48 to 48
- adapter_index: int32 [8], P('clip'), may hold values from 0 to 7
- norm_gain: float32 [3, 768], replicated, may hold values from 0.25 to 1.75
- norm_shift: float32 [3, 768], replicated, may hold values from -1.5 to 1.5
- spatial_weights: bfloat16 [3, 768, 768], P(None, ('clip', 'tok')), may hold values from -0.21875 to 0.21875
- spatial_output: bfloat16 [768, 768], P(('clip', 'tok')), may hold values from -1.75 to 1.75
- temporal_weights: bfloat16 [3, 768, 768], P(None, ('clip', 'tok')), may hold values from -0.21875 to 0.21875
- temporal_output: bfloat16 [768, 768], P(('clip', 'tok')), may hold values from -0.625 to 0.625
- expand_weight: bfloat16 [768, 3072], P(('clip', 'tok')), may hold values from -0.21875 to 0.21875
- reduce_weight: bfloat16 [3072, 768], P(('clip', 'tok')), may hold values from -0.109375 to 0.109375
- attention_down: bfloat16 [8, 768, 128], P(None, ('clip', 'tok')), may hold values from -0.21875 to 0.21875
- attention_up: bfloat16 [8, 128, 768], P(None, None, ('clip', 'tok')), may hold values from -1 to 1
- expand_down: bfloat16 [768, 128], P(('clip', 'tok')), may hold values from -0.21875 to 0.21875
- expand_up: bfloat16 [128, 3072], P(None, ('clip', 'tok')), may hold values from -1 to 1
- reduce_down: bfloat16 [3072, 128], P(('clip', 'tok')), may hold values from -0.109375 to 0.109375
- reduce_up: bfloat16 [128, 768], P(None, ('clip', 'tok')), may hold values from -1 to 1
- cotangent: float32 [32, 2, 2, 196, 768], P(('clip', 'tok')), may hold values from -6 to 6
Outputs:
- layer_output: float32 [32, 2, 2, 196, 768], P(('clip', 'tok'))
- input_gradient: float32 [32, 2, 2, 196, 768], P(('clip', 'tok'))
- attention_down_gradient: float32 [8, 768, 128], P(None, ('clip', 'tok'))
- attention_up_gradient: float32 [8, 128, 768], P(None, None, ('clip', 'tok'))
- expand_down_gradient: float32 [768, 128], P(('clip', 'tok'))
- expand_up_gradient: float32 [128, 3072], P(None, ('clip', 'tok'))
- reduce_down_gradient: float32 [3072, 128], P(('clip', 'tok'))
- reduce_up_gradient: float32 [128, 768], P(None, ('clip', 'tok'))
The draws below stay inside these ranges and needn't reach their ends.
Inputs may be any that keep to these rules, and one draw needn't show every extreme that they name: `adapter_index`: which of the 8 adapter sets each clip uses.
All inputs are finite; a program needn't handle non-finite values.
Results may differ from the reference program's by a relative error of at most 0.02.
Values may be sent and summed in bfloat16 or wider, within the bound.
A program may use at most 256 MiB of HBM per device.

```python
from functools import partial
import jax
import jax.numpy as jnp
from jax import lax

D = 768
HEADS = 12
HEAD_DIM = 64
FF = 3072
FRAMES = 16
PLACES = 196
ADAPTERS = 8
RANK = 16
FRAMES_DEV = 2
CLIPS_DEV = 2
CLIPS = 8
BLOCKS = 32
ADAPT_COLS = 128


def draw_tokens(key, part):
    base_key, row_key, column_key = jax.random.split(jax.random.fold_in(key, 11), 3)
    full_shape = (BLOCKS, FRAMES_DEV, CLIPS_DEV, PLACES, D)
    base_draw = jax.random.truncated_normal(base_key, -4.0, 4.0, full_shape, jnp.float32)
    row_scale = jnp.exp(jax.random.uniform(row_key, full_shape[:-1] + (1,), jnp.float32, -1.2, 1.2))
    column_scale = jnp.exp(jax.random.uniform(column_key, (D,), jnp.float32, -1.2, 1.2))
    return base_draw * row_scale * column_scale


def set_ends(entries, own_key, low, high):
    spot = [jax.random.randint(jax.random.fold_in(own_key, axis), (), 0, length) for axis, length in enumerate(entries.shape)]
    main_axis = entries.shape.index(max(entries.shape))
    beside = spot[:main_axis] + [(spot[main_axis] + 1) % entries.shape[main_axis]] + spot[main_axis + 1:]
    return entries.at[tuple(spot)].set(low).at[tuple(beside)].set(high)


def shard_levels(key, shape, cuts, least, top_value):
    gain, own = 1.0, jax.random.fold_in(key, 6)
    for position, shards_of in cuts:
        heights = jnp.exp(jax.random.uniform(jax.random.fold_in(own, position), (shards_of,), jnp.float32, least / len(cuts), top_value / len(cuts)))
        gain = gain * jnp.repeat(heights, shape[position] // shards_of).reshape([-1 if axis == position else 1 for axis in range(len(shape))])
    return gain


def noise(own_key, dims, scale, bound, pieces=(), kind=jnp.bfloat16):
    level = shard_levels(own_key, dims, pieces, -0.22, 0.18) if pieces else 1.0
    drawn = jax.random.normal(own_key, dims, jnp.float32) * scale * level
    return jnp.minimum(jnp.maximum(drawn, -bound), bound).astype(kind)


def setup_inputs(seed: int = 0) -> dict:
    keys = jax.random.split(jax.random.key(seed), 18)
    return {
        "tokens": draw_tokens(jax.random.fold_in(keys[17], 71), 0),
        "adapter_index": set_ends(jax.random.randint(keys[1], (CLIPS,), 0, ADAPTERS), jax.random.fold_in(keys[1], 1), 0, ADAPTERS - 1).astype(jnp.int32),
        "norm_gain": jnp.clip(1.0 + 0.15 * jax.random.normal(keys[2], (3, D), jnp.float32), 0.25, 1.75),
        "norm_shift": noise(keys[3], (3, D), 0.3, 1.5, (), jnp.float32),
        "spatial_weights": noise(keys[4], (3, D, D), D ** -0.5, 0.21875, ((1, 32),)),
        "spatial_output": noise(keys[5], (D, D), (D // 64) ** -0.5, 1.75, ((0, 32),)),
        "temporal_weights": noise(keys[6], (3, D, D), D ** -0.5, 0.21875, ((1, 32),)),
        "temporal_output": noise(keys[7], (D, D), (D // 8) ** -0.5, 0.625, ((0, 32),)),
        "expand_weight": noise(keys[8], (D, FF), D ** -0.5, 0.21875, ((0, 32),)),
        "reduce_weight": noise(keys[9], (FF, D), FF ** -0.5, 0.109375, ((0, 32),)),
        "attention_down": noise(keys[10], (8, D, ADAPT_COLS), D ** -0.5, 0.21875, ((1, 32),)),
        "attention_up": noise(keys[11], (8, ADAPT_COLS, D), (2 * RANK) ** -0.5, 1.0, ((2, 32),)),
        "expand_down": noise(keys[12], (D, ADAPT_COLS), D ** -0.5, 0.21875, ((0, 32),)),
        "expand_up": noise(keys[13], (ADAPT_COLS, FF), (2 * RANK) ** -0.5, 1.0, ((1, 32),)),
        "reduce_down": noise(keys[14], (FF, ADAPT_COLS), FF ** -0.5, 0.109375, ((0, 32),)),
        "reduce_up": noise(keys[15], (ADAPT_COLS, D), (2 * RANK) ** -0.5, 1.0, ((1, 32),)),
        "cotangent": noise(keys[16], (BLOCKS, FRAMES_DEV, CLIPS_DEV, PLACES, D), 1.0, 6.0, ((0, 32),), jnp.float32),
    }


@jax.custom_vjp
def low(v):
    return lax.optimization_barrier(v.astype(jnp.bfloat16)).astype(jnp.float32)

@jax.custom_vjp
def low_back(v):
    return v

def low_keep(v):
    return (low(v), None)

def low_pass(kept, grad):
    return (grad,)

def back_keep(v):
    return (v, None)

def back_low(kept, grad):
    return (low(grad),)
low.defvjp(low_keep, low_pass)
low_back.defvjp(back_keep, back_low)
EPSILON = 1e-06
HIGHEST = lax.Precision.HIGHEST

def rounded_both(value):
    return low_back(low(value))

def layer_norm(stream, gain_row, shift_row):
    average = lax.optimization_barrier(jnp.mean(stream, axis=-1, keepdims=True))
    centred = stream - average
    variance = lax.optimization_barrier(jnp.mean(centred * centred, axis=-1, keepdims=True))
    return centred * lax.rsqrt(variance + EPSILON) * gain_row + shift_row

def project(inputs, weight, down_rows, up_rows, mask):
    result = jnp.einsum('...d,de->...e', inputs, weight, precision=HIGHEST)
    hidden = rounded_both(jnp.einsum('...d,dc->...c', inputs, down_rows, precision=HIGHEST) * mask)
    return result + jnp.einsum('...c,ce->...e', hidden, up_rows, precision=HIGHEST)

def attention_block(stream, gain_row, shift_row, inner_weights, outer_weight, down_rows, up_rows, mask, score_eq, mix_eq):
    normed = low(layer_norm(stream, gain_row, shift_row))
    split_shape = stream.shape[:-1] + (HEADS, HEAD_DIM)
    queries = rounded_both(project(normed, inner_weights[0], down_rows[0], up_rows[0], mask)).reshape(split_shape)
    key_rows = rounded_both(project(normed, inner_weights[1], down_rows[1], up_rows[1], mask)).reshape(split_shape)
    values = rounded_both(project(normed, inner_weights[2], down_rows[2], up_rows[2], mask)).reshape(split_shape)
    scores = low_back(jnp.einsum(score_eq, queries, key_rows, precision=HIGHEST) * HEAD_DIM ** (-0.5))
    weights_soft = low(jax.nn.softmax(scores, axis=-1))
    mixed_rows = rounded_both(jnp.einsum(mix_eq, weights_soft, values, precision=HIGHEST).reshape(stream.shape))
    return stream + low_back(project(mixed_rows, outer_weight, down_rows[3], up_rows[3], mask))

def expand_block(stream, gain_row, shift_row, up_weight, down_weight, in_down, in_up, out_down, out_up, mask):
    normed = low(layer_norm(stream, gain_row, shift_row))
    inner_rows = low_back(project(normed, up_weight, in_down, in_up, mask))
    active = low(jax.nn.gelu(inner_rows, approximate=True))
    return stream + low_back(project(active, down_weight, out_down, out_up, mask))

def per_clip(frozen, adapter_set, clip_item):
    clip_rows, choice_row = clip_item
    gain_rows, shift_rows, spatial_weights, spatial_output, temporal_weights, temporal_output, expand_weight, reduce_weight = frozen
    attention_down, attention_up, expand_down, expand_up, reduce_down, reduce_up = adapter_set
    columns = jnp.arange(ADAPTERS * RANK, dtype=jnp.int32) // RANK
    mask = (columns == choice_row).astype(jnp.float32)
    stream = attention_block(clip_rows, gain_rows[0], shift_rows[0], spatial_weights, spatial_output, attention_down[0:4], attention_up[0:4], mask, 'fqhd,fkhd->fhqk', 'fhqk,fkhd->fqhd')
    stream = attention_block(stream, gain_rows[1], shift_rows[1], temporal_weights, temporal_output, attention_down[4:8], attention_up[4:8], mask, 'qphd,kphd->phqk', 'phqk,kphd->qphd')
    return expand_block(stream, gain_rows[2], shift_rows[2], expand_weight, reduce_weight, expand_down, expand_up, reduce_down, reduce_up, mask)

def to_clips(stream_all):
    shaped = stream_all.reshape(CLIPS // CLIPS_DEV, FRAMES // FRAMES_DEV, FRAMES_DEV, CLIPS_DEV, PLACES, D)
    return shaped.transpose(0, 3, 1, 2, 4, 5).reshape(CLIPS, FRAMES, PLACES, D)

def from_clips(clip_stack):
    shaped = clip_stack.reshape(CLIPS // CLIPS_DEV, CLIPS_DEV, FRAMES // FRAMES_DEV, FRAMES_DEV, PLACES, D)
    return shaped.transpose(0, 2, 3, 1, 4, 5).reshape(BLOCKS, FRAMES_DEV, CLIPS_DEV, PLACES, D)

def reference(tokens, adapter_index, norm_gain, norm_shift, spatial_weights, spatial_output, temporal_weights, temporal_output, expand_weight, reduce_weight, attention_down, attention_up, expand_down, expand_up, reduce_down, reduce_up, cotangent):
    frozen = (norm_gain, norm_shift) + tuple((weight.astype(jnp.float32) for weight in (spatial_weights, spatial_output, temporal_weights, temporal_output, expand_weight, reduce_weight)))
    adapters = tuple((weight.astype(jnp.float32) for weight in (attention_down, attention_up, expand_down, expand_up, reduce_down, reduce_up)))

    def forward(stream_all, adapter_set):
        clip_stack = to_clips(stream_all)
        result = lax.map(jax.checkpoint(partial(per_clip, frozen, adapter_set)), (clip_stack, adapter_index))
        return from_clips(result)
    layer_output, pull_back = jax.vjp(forward, tokens, adapters)
    input_gradient, adapter_grads = pull_back(cotangent)
    return (layer_output, input_gradient, adapter_grads[0], adapter_grads[1], adapter_grads[2], adapter_grads[3], adapter_grads[4], adapter_grads[5])
```

```python
import functools

import jax
import jax.numpy as jnp
from jax import lax
from jax.experimental import pallas as pl
from jax.experimental.pallas import tpu as pltpu
from jax.sharding import PartitionSpec as P

HEADS = 12
HEAD_DIM = 64
FRAMES = 16
ADAPTERS = 8
RANK = 16


EPSILON = 1e-06


def layer_norm(stream, gain_row, shift_row):
    average = jnp.mean(stream, axis=-1, keepdims=True)
    centred = stream - average
    variance = jnp.mean(centred * centred, axis=-1, keepdims=True)
    return centred * lax.rsqrt(variance + EPSILON) * gain_row + shift_row


def adapter_mask(choice_rows):
    columns = jnp.arange(ADAPTERS * RANK, dtype=jnp.int32) // RANK
    return (columns[None, :] == choice_rows[:, None]).astype(jnp.float32)


def project_many(inputs, weight, down_rows, up_rows, mask):
    hidden = jnp.einsum("rd,ndc->nrc", inputs, down_rows, preferred_element_type=jnp.float32)
    hidden = (hidden * mask).astype(jnp.bfloat16)
    result = jnp.einsum("rd,nde->nre", inputs, weight, preferred_element_type=jnp.float32)
    result = result + jnp.einsum(
        "nrc,nce->nre", hidden, up_rows, preferred_element_type=jnp.float32
    )
    return (result, hidden)


def project_back(inputs, hidden, grad_rows, weight, down_rows, up_rows, mask):
    hidden_grad = jnp.einsum("nre,nce->nrc", grad_rows, up_rows, preferred_element_type=jnp.float32)
    hidden_grad = (hidden_grad * mask).astype(jnp.bfloat16)
    input_grad = jnp.einsum("nre,nde->rd", grad_rows, weight, preferred_element_type=jnp.float32)
    input_grad = input_grad + jnp.einsum(
        "nrc,ndc->rd", hidden_grad, down_rows, preferred_element_type=jnp.float32
    )
    down_grad = jnp.einsum("rd,nrc->ndc", inputs, hidden_grad, preferred_element_type=jnp.float32)
    up_grad = jnp.einsum("nrc,nre->nce", hidden, grad_rows, preferred_element_type=jnp.float32)
    return (input_grad, down_grad, up_grad)


def attend_forward(packed, layout):
    view_shape, score_eq, mix_eq, back_eq = layout
    queries = packed[0].reshape(view_shape)
    key_rows = packed[1].reshape(view_shape)
    values = packed[2].reshape(view_shape)
    scores = jnp.einsum(
        score_eq, queries, key_rows, preferred_element_type=jnp.float32
    ) * HEAD_DIM ** (-0.5)
    ceiling = jnp.max(scores, axis=-1, keepdims=True)
    expo_rows = jnp.exp(scores - ceiling)
    totals = jnp.sum(expo_rows, axis=-1, keepdims=True)
    weights_soft = (expo_rows / totals).astype(jnp.bfloat16)
    mixed_rows = jnp.einsum(mix_eq, weights_soft, values, preferred_element_type=jnp.float32)
    return (mixed_rows.reshape(packed.shape[1:]), ceiling + jnp.log(totals))


def attend_backward(packed, log_total, mixed_grad, layout):
    view_shape, score_eq, mix_eq, back_eq = layout
    scaling = HEAD_DIM ** (-0.5)
    queries = packed[0].reshape(view_shape)
    key_rows = packed[1].reshape(view_shape)
    values = packed[2].reshape(view_shape)
    scores = jnp.einsum(score_eq, queries, key_rows, preferred_element_type=jnp.float32) * scaling
    weights_soft = jnp.exp(scores - log_total)
    output_grad = mixed_grad.reshape(view_shape)
    soft_grad = jnp.einsum(score_eq, output_grad, values, preferred_element_type=jnp.float32)
    row_inner = jnp.sum(weights_soft * soft_grad, axis=-1, keepdims=True)
    score_grad = (weights_soft * (soft_grad - row_inner)).astype(jnp.bfloat16)
    query_grad = (
        jnp.einsum(mix_eq, score_grad, key_rows, preferred_element_type=jnp.float32) * scaling
    )
    key_grad = (
        jnp.einsum(back_eq, score_grad, queries, preferred_element_type=jnp.float32) * scaling
    )
    value_grad = jnp.einsum(
        back_eq, weights_soft.astype(jnp.bfloat16), output_grad, preferred_element_type=jnp.float32
    )
    stacked = jnp.stack([query_grad, key_grad, value_grad])
    return stacked.reshape(packed.shape).astype(jnp.bfloat16)


def attention_forward(stream, gain_row, shift_row, weight_set, mask, layout):
    inner_weights, outer_weight, down_rows, up_rows = weight_set
    normed = layer_norm(stream, gain_row, shift_row).astype(jnp.bfloat16)
    packed, packed_hidden = project_many(normed, inner_weights, down_rows[0:3], up_rows[0:3], mask)
    packed = packed.astype(jnp.bfloat16)
    mixed_rows, log_total = attend_forward(packed, layout)
    mixed_rows = mixed_rows.astype(jnp.bfloat16)
    branch, outer_hidden = project_many(
        mixed_rows, outer_weight[None], down_rows[3:4], up_rows[3:4], mask
    )
    return (
        stream + branch[0],
        (normed, packed, packed_hidden, mixed_rows, outer_hidden, log_total),
    )


def attention_backward(
    stream, stream_grad, gain_row, shift_row, weight_set, mask, layout, kept_values
):
    inner_weights, outer_weight, down_rows, up_rows = weight_set
    normed, packed, packed_hidden, mixed_rows, outer_hidden, log_total = kept_values
    branch_grad = stream_grad.astype(jnp.bfloat16)[None]
    mixed_grad, outer_down, outer_up = project_back(
        mixed_rows,
        outer_hidden,
        branch_grad,
        outer_weight[None],
        down_rows[3:4],
        up_rows[3:4],
        mask,
    )
    packed_grad = attend_backward(packed, log_total, mixed_grad.astype(jnp.bfloat16), layout)
    normed_grad, inner_down, inner_up = project_back(
        normed, packed_hidden, packed_grad, inner_weights, down_rows[0:3], up_rows[0:3], mask
    )
    unused, norm_pull = jax.vjp(lambda rows_in: layer_norm(rows_in, gain_row, shift_row), stream)
    before_grad = stream_grad + norm_pull(normed_grad)[0]
    return (
        before_grad,
        jnp.concatenate([inner_down, outer_down], axis=0),
        jnp.concatenate([inner_up, outer_up], axis=0),
    )


def expand_forward(stream, gain_row, shift_row, weight_set, mask):
    up_weight, down_weight, in_down, in_up, out_down, out_up = weight_set
    normed = layer_norm(stream, gain_row, shift_row).astype(jnp.bfloat16)
    inner_rows, inner_hidden = project_many(
        normed, up_weight[None], in_down[None], in_up[None], mask
    )
    inner_rows = inner_rows[0]
    active = jax.nn.gelu(inner_rows, approximate=True).astype(jnp.bfloat16)
    branch, outer_hidden = project_many(
        active, down_weight[None], out_down[None], out_up[None], mask
    )
    return (stream + branch[0], (normed, inner_rows, inner_hidden, active, outer_hidden))


def expand_backward(stream, stream_grad, gain_row, shift_row, weight_set, mask, kept_values):
    up_weight, down_weight, in_down, in_up, out_down, out_up = weight_set
    normed, inner_rows, inner_hidden, active, outer_hidden = kept_values
    branch_grad = stream_grad.astype(jnp.bfloat16)[None]
    active_grad, out_down_grad, out_up_grad = project_back(
        active, outer_hidden, branch_grad, down_weight[None], out_down[None], out_up[None], mask
    )
    unused, gelu_pull = jax.vjp(
        lambda values_in: jax.nn.gelu(values_in, approximate=True), inner_rows
    )
    inner_grad = gelu_pull(active_grad)[0].astype(jnp.bfloat16)[None]
    normed_grad, in_down_grad, in_up_grad = project_back(
        normed, inner_hidden, inner_grad, up_weight[None], in_down[None], in_up[None], mask
    )
    unused_norm, norm_pull = jax.vjp(
        lambda rows_in: layer_norm(rows_in, gain_row, shift_row), stream
    )
    before_grad = stream_grad + norm_pull(normed_grad)[0]
    return (before_grad, (in_down_grad[0], in_up_grad[0], out_down_grad[0], out_up_grad[0]))


def regroup_places(stream, layout_sizes, backward):
    frames_dev, clips_dev, places, model_width, clip_rows, place_blocks, place_part = layout_sizes
    padded = jnp.pad(
        stream.reshape(frames_dev, clips_dev, places, model_width),
        ((0, 0), (0, 0), (0, place_part * place_blocks - places), (0, 0)),
    )
    padded = padded.reshape(frames_dev, clips_dev * place_blocks, place_part, model_width)
    if backward:
        arrived = lax.all_to_all(
            padded.astype(jnp.bfloat16), "tok", split_axis=1, concat_axis=0, tiled=True
        ).astype(padded.dtype)
    else:
        arrived = lax.all_to_all(
            padded.astype(jnp.bfloat16), "tok", split_axis=1, concat_axis=0, tiled=True
        ).astype(padded.dtype)
    return arrived.reshape(clip_rows * FRAMES * place_part, model_width)


def regroup_frames(stream, layout_sizes, backward):
    frames_dev, clips_dev, places, model_width, clip_rows, place_blocks, place_part = layout_sizes
    shaped = stream.reshape(clip_rows * FRAMES, 1, place_part, model_width)
    if backward:
        arrived = lax.all_to_all(
            shaped.astype(jnp.bfloat16), "tok", split_axis=0, concat_axis=1, tiled=True
        ).astype(shaped.dtype)
    else:
        arrived = lax.all_to_all(
            shaped.astype(jnp.bfloat16), "tok", split_axis=0, concat_axis=1, tiled=True
        ).astype(shaped.dtype)
    arrived = arrived.reshape(frames_dev, clips_dev, place_part * place_blocks, model_width)
    return arrived[:, :, :places].reshape(frames_dev * clips_dev * places, model_width)


def general_device(
    tokens,
    adapter_index,
    norm_gain,
    norm_shift,
    spatial_weights,
    spatial_output,
    temporal_weights,
    temporal_output,
    expand_weight,
    reduce_weight,
    attention_down,
    attention_up,
    expand_down,
    expand_up,
    reduce_down,
    reduce_up,
    cotangent,
):
    frames_dev, clips_dev, places, model_width = tokens.shape[1:]
    tok_count = lax.axis_size("tok")
    frame_blocks = FRAMES // frames_dev
    clip_rows = tok_count // frame_blocks
    place_blocks = tok_count // clips_dev
    place_part = -(-places // place_blocks)
    layout_sizes = (frames_dev, clips_dev, places, model_width, clip_rows, place_blocks, place_part)
    adapt_cols = ADAPTERS * RANK
    position = lax.axis_index("tok")
    spatial_choice = lax.dynamic_slice_in_dim(
        adapter_index, position // frame_blocks * clips_dev, clips_dev
    )
    spatial_mask = jnp.broadcast_to(
        adapter_mask(spatial_choice)[None, :, None, :], (frames_dev, clips_dev, places, adapt_cols)
    ).reshape(-1, adapt_cols)
    temporal_choice = lax.dynamic_slice_in_dim(
        adapter_index.reshape(clip_rows, clips_dev), position // place_blocks, 1, 1
    )[:, 0]
    temporal_mask = jnp.broadcast_to(
        adapter_mask(temporal_choice)[:, None, None, :], (clip_rows, FRAMES, place_part, adapt_cols)
    ).reshape(-1, adapt_cols)
    spatial_layout = (
        (frames_dev * clips_dev, places, HEADS, HEAD_DIM),
        "gqhd,gkhd->ghqk",
        "ghqk,gkhd->gqhd",
        "ghqk,gqhd->gkhd",
    )
    temporal_layout = (
        (clip_rows, FRAMES, place_part, HEADS, HEAD_DIM),
        "aqphd,akphd->aphqk",
        "aphqk,akphd->aqphd",
        "aphqk,aqphd->akphd",
    )
    spatial_set = (
        lax.all_gather(spatial_weights, ("clip", "tok"), axis=1, tiled=True),
        lax.all_gather(spatial_output, ("clip", "tok"), axis=0, tiled=True),
        lax.all_gather(attention_down[0:4], ("clip", "tok"), axis=1, tiled=True),
        lax.all_gather(attention_up[0:4], ("clip", "tok"), axis=2, tiled=True),
    )
    stream0 = tokens.reshape(-1, model_width)
    stream1, spatial_kept = attention_forward(
        stream0, norm_gain[0], norm_shift[0], spatial_set, spatial_mask, spatial_layout
    )
    placed1 = regroup_places(stream1, layout_sizes, False)
    temporal_set = (
        lax.all_gather(temporal_weights, ("clip", "tok"), axis=1, tiled=True),
        lax.all_gather(temporal_output, ("clip", "tok"), axis=0, tiled=True),
        lax.all_gather(attention_down[4:8], ("clip", "tok"), axis=1, tiled=True),
        lax.all_gather(attention_up[4:8], ("clip", "tok"), axis=2, tiled=True),
    )
    placed2, temporal_kept = attention_forward(
        placed1, norm_gain[1], norm_shift[1], temporal_set, temporal_mask, temporal_layout
    )
    stream2 = regroup_frames(placed2, layout_sizes, False)
    expand_set = (
        lax.all_gather(expand_weight, ("clip", "tok"), axis=0, tiled=True),
        lax.all_gather(reduce_weight, ("clip", "tok"), axis=0, tiled=True),
        lax.all_gather(expand_down, ("clip", "tok"), axis=0, tiled=True),
        lax.all_gather(expand_up, ("clip", "tok"), axis=1, tiled=True),
        lax.all_gather(reduce_down, ("clip", "tok"), axis=0, tiled=True),
        lax.all_gather(reduce_up, ("clip", "tok"), axis=1, tiled=True),
    )
    stream3, expand_kept = expand_forward(
        stream2, norm_gain[2], norm_shift[2], expand_set, spatial_mask
    )
    expand_set = (
        lax.all_gather(expand_weight, ("clip", "tok"), axis=0, tiled=True),
        lax.all_gather(reduce_weight, ("clip", "tok"), axis=0, tiled=True),
        lax.all_gather(expand_down, ("clip", "tok"), axis=0, tiled=True),
        lax.all_gather(expand_up, ("clip", "tok"), axis=1, tiled=True),
        lax.all_gather(reduce_down, ("clip", "tok"), axis=0, tiled=True),
        lax.all_gather(reduce_up, ("clip", "tok"), axis=1, tiled=True),
    )
    grad2, expand_grads = expand_backward(
        stream2,
        cotangent.reshape(-1, model_width),
        norm_gain[2],
        norm_shift[2],
        expand_set,
        spatial_mask,
        expand_kept,
    )
    placed_grad2 = regroup_places(grad2, layout_sizes, True)
    temporal_set = (
        lax.all_gather(temporal_weights, ("clip", "tok"), axis=1, tiled=True),
        lax.all_gather(temporal_output, ("clip", "tok"), axis=0, tiled=True),
        lax.all_gather(attention_down[4:8], ("clip", "tok"), axis=1, tiled=True),
        lax.all_gather(attention_up[4:8], ("clip", "tok"), axis=2, tiled=True),
    )
    placed_grad1, temporal_down, temporal_up = attention_backward(
        placed1,
        placed_grad2,
        norm_gain[1],
        norm_shift[1],
        temporal_set,
        temporal_mask,
        temporal_layout,
        temporal_kept,
    )
    grad1 = regroup_frames(placed_grad1, layout_sizes, True)
    spatial_set = (
        lax.all_gather(spatial_weights, ("clip", "tok"), axis=1, tiled=True),
        lax.all_gather(spatial_output, ("clip", "tok"), axis=0, tiled=True),
        lax.all_gather(attention_down[0:4], ("clip", "tok"), axis=1, tiled=True),
        lax.all_gather(attention_up[0:4], ("clip", "tok"), axis=2, tiled=True),
    )
    grad0, spatial_down, spatial_up = attention_backward(
        stream0,
        grad1,
        norm_gain[0],
        norm_shift[0],
        spatial_set,
        spatial_mask,
        spatial_layout,
        spatial_kept,
    )
    owned = (
        lax.psum_scatter(
            jnp.concatenate([spatial_down, temporal_down], axis=0),
            ("clip", "tok"),
            scatter_dimension=1,
            tiled=True,
        ),
        lax.psum_scatter(
            jnp.concatenate([spatial_up, temporal_up], axis=0),
            ("clip", "tok"),
            scatter_dimension=2,
            tiled=True,
        ),
        lax.psum_scatter(expand_grads[0], ("clip", "tok"), scatter_dimension=0, tiled=True),
        lax.psum_scatter(expand_grads[1], ("clip", "tok"), scatter_dimension=1, tiled=True),
        lax.psum_scatter(expand_grads[2], ("clip", "tok"), scatter_dimension=0, tiled=True),
        lax.psum_scatter(expand_grads[3], ("clip", "tok"), scatter_dimension=1, tiled=True),
    )
    return (
        stream3.reshape(tokens.shape),
        grad0.reshape(tokens.shape),
        owned[0],
        owned[1],
        owned[2],
        owned[3],
        owned[4],
        owned[5],
    )


F32 = jnp.float32
BF16 = jnp.bfloat16
ADAPT = ADAPTERS * RANK


def nn(left, right):
    return lax.dot_general(left, right, (((1,), (0,)), ((), ())), preferred_element_type=F32)


def nt(left, right):
    return lax.dot_general(left, right, (((1,), (1,)), ((), ())), preferred_element_type=F32)


def tn(left, right):
    return lax.dot_general(left, right, (((0,), (0,)), ((), ())), preferred_element_type=F32)


def one_hot(target_row, rows):
    row_ids = lax.broadcasted_iota(jnp.int32, (rows, target_row.shape[1]), 0)
    return (row_ids == target_row).astype(F32).astype(BF16)


def column_mask(choice):
    return (lax.broadcasted_iota(jnp.int32, (1, ADAPT), 1) // RANK == choice).astype(F32)


def norm_rows(rows, gain_row, shift_row):
    average = jnp.mean(rows, axis=-1, keepdims=True)
    centred = rows - average
    variance = jnp.mean(centred * centred, axis=-1, keepdims=True)
    return centred * lax.rsqrt(variance + EPSILON) * gain_row + shift_row


def norm_back(rows, pulled, gain_row):
    average = jnp.mean(rows, axis=-1, keepdims=True)
    centred = rows - average
    variance = jnp.mean(centred * centred, axis=-1, keepdims=True)
    scale = lax.rsqrt(variance + EPSILON)
    unit = centred * scale
    scaled = pulled * gain_row
    return scale * (
        scaled
        - jnp.mean(scaled, axis=-1, keepdims=True)
        - unit * jnp.mean(scaled * unit, axis=-1, keepdims=True)
    )


def soften(scores, keep):
    scores = jnp.where(keep, scores, -1e30)
    ceiling = jnp.max(scores, axis=-1, keepdims=True)
    expo = jnp.exp(scores - ceiling)
    return expo * (1.0 / jnp.sum(expo, axis=-1, keepdims=True))


def spatial_forward(
    sizes, idx, to_send, x, gain, shift, w, wo, ad, sent, qkv, soft, mixed, hid, zs, stream
):
    frames, clips, places, width, padded = sizes
    half = frames * padded
    for b in range(clips):
        for i in range(frames):
            base = b * half + i * padded
            zs[base + padded - 16 : base + padded] = jnp.zeros((16, width), BF16)
            stream[base + padded - 16 : base + padded] = jnp.zeros((16, width), BF16)
            zs[base : base + places] = norm_rows(x[i, b], gain[0:1], shift[0:1]).astype(BF16)
    for b in range(clips):
        rows = slice(b * half, (b + 1) * half)
        mask = column_mask(idx[b])

        @pl.loop(0, 3)
        def _(n):
            hidden = (nn(zs[rows], ad[n]) * mask).astype(BF16)
            hid[n, rows] = hidden
            result = nn(zs[rows], w[n]) + nt(hidden, ad[4 + n])
            result = result * jnp.where(n == 0, HEAD_DIM**-0.5, 1.0)
            qkv[n, rows] = result.astype(BF16)

    keep = lax.broadcasted_iota(jnp.int32, (padded, padded), 1) < places
    pairs = width // 128
    low = lax.broadcasted_iota(jnp.int32, (padded, 128), 1) < HEAD_DIM

    @pl.loop(0, frames * clips * pairs)
    def _(step):
        group = step // pairs
        pair = step - group * pairs
        rows = pl.ds(pl.multiple_of(group * padded, 16), padded)
        lanes = pl.ds(pl.multiple_of(pair * 128, 128), 128)
        query, key, value = qkv[0, rows, lanes], qkv[1, rows, lanes], qkv[2, rows, lanes]
        total = jnp.zeros((padded, 128), F32)
        for h in range(2):
            own = low if h == 0 else ~low
            zero = jnp.zeros_like(query)
            weights = soften(nt(jnp.where(own, query, zero), key), keep).astype(BF16)
            soft[step * 2 + h] = weights
            total += nn(weights, jnp.where(own, value, zero))
        mixed[rows, lanes] = total.astype(BF16)

    for b in range(clips):
        rows = slice(b * half, (b + 1) * half)
        hidden = (nn(mixed[rows], ad[3]) * column_mask(idx[b])).astype(BF16)
        hid[3, rows] = hidden
        branch = nn(mixed[rows], wo[...]) + nt(hidden, ad[7])
        for i in range(frames):
            base = b * half + i * padded
            stream[base : base + places] = (
                x[i, b] + branch[i * padded : i * padded + places]
            ).astype(BF16)
        sent[rows] = nn(one_hot(to_send[...], half), stream[rows]).astype(BF16)


def attention_back(query, key, value, weights, grads, low):
    zero = jnp.zeros_like(query)
    totals = [jnp.zeros(query.shape, F32) for _ in range(3)]
    for h in range(2):
        own = low if h == 0 else ~low
        soft = weights[h]
        grad = jnp.where(own, grads, zero)
        pulled = nt(grad, value)
        wide = soft.astype(F32)
        inner = jnp.sum(wide * pulled, axis=-1, keepdims=True)
        score = (wide * (pulled - inner)).astype(BF16)
        totals[0] += nn(score, jnp.where(own, key, zero))
        totals[1] += tn(score, jnp.where(own, query, zero))
        totals[2] += tn(soft, grad)
    return totals[0] * HEAD_DIM**-0.5, totals[1], totals[2]


def spatial_backward(
    sizes, idx, from_sent, x, gain, w, wo, ad, qkv, soft, mixed, hid, zs, got, made,
    dx, out, pay, grad, gmix, gqkv, gpull, gdown, gup
):
    frames, clips, places, width, padded = sizes
    half = frames * padded
    for b in range(clips):
        rows = slice(b * half, (b + 1) * half)
        mask = column_mask(idx[b])
        back = one_hot(from_sent[...], half)
        final = nn(back, made[rows])
        for i in range(frames):
            out[i, b] = final[i * padded : i * padded + places]
        grad[rows] = nn(back, got[rows]).astype(BF16)
        hidden_grad = (nn(grad[rows], ad[7]) * mask).astype(BF16)
        gmix[rows] = (nt(grad[rows], wo[...]) + nt(hidden_grad, ad[3])).astype(BF16)
        down, up = tn(hidden_grad, mixed[rows]), tn(hid[3, rows], grad[rows])
        if b == 0:
            gdown[3], gup[3] = down, up
        else:
            gdown[3] += down
            gup[3] += up

    pairs = width // 128
    low = lax.broadcasted_iota(jnp.int32, (padded, 128), 1) < HEAD_DIM

    @pl.loop(0, frames * clips * pairs)
    def _(step):
        group = step // pairs
        pair = step - group * pairs
        rows = pl.ds(pl.multiple_of(group * padded, 16), padded)
        lanes = pl.ds(pl.multiple_of(pair * 128, 128), 128)
        weights = [soft[step * 2 + h] for h in range(2)]
        gq, gk, gv = attention_back(
            qkv[0, rows, lanes], qkv[1, rows, lanes], qkv[2, rows, lanes], weights, gmix[rows, lanes], low
        )
        gqkv[0, rows, lanes] = gq.astype(BF16)
        gqkv[1, rows, lanes] = gk.astype(BF16)
        gqkv[2, rows, lanes] = gv.astype(BF16)

    for b in range(clips):
        rows = slice(b * half, (b + 1) * half)
        mask = column_mask(idx[b])
        gpull[...] = jnp.zeros(gpull.shape, F32)

        @pl.loop(0, 3)
        def _(n):
            own = gqkv[n, rows]
            hidden_grad = (nn(own, ad[4 + n]) * mask).astype(BF16)
            gpull[...] += nt(own, w[n]) + nt(hidden_grad, ad[n])
            down, up = tn(hidden_grad, zs[rows]), tn(hid[n, rows], own)
            if b == 0:
                gdown[n], gup[n] = down, up
            else:
                gdown[n] += down
                gup[n] += up

        for i in range(frames):
            base = i * padded
            dx[i, b] = grad[b * half + base : b * half + base + places].astype(F32) + norm_back(
                x[i, b], gpull[base : base + places], gain[0:1]
            )
    repeat = jnp.where(idx[0] == idx[1], 0.0, 1.0)
    pieces = []
    for n in range(4):
        for source in (gdown, gup):
            pieces.append(source[n, pl.ds(pl.multiple_of(idx[0] * RANK, RANK), RANK)])
            pieces.append(source[n, pl.ds(pl.multiple_of(idx[1] * RANK, RANK), RANK)] * repeat)
    pay[...] = jnp.transpose(jnp.concatenate(pieces, axis=0)).astype(BF16)


def middle(
    sizes, idx, to_place, to_frame, got, cot, gain, shift, w, wo, ad, we, wr, ea, eb, ra, rb,
    out_sent, grad_sent, pay,
    x1, x2, zt, ze, qkv, soft, mixed, hid, hide, gy, acc, pull, ghe, gmix, gqkv, gdown, gup, wide
):
    rows_all, width, group, chunk, owners = sizes
    choice = idx[0]
    mask = column_mask(choice)
    groups = rows_all // group

    @pl.loop(0, groups)
    def _(j):
        rows = pl.ds(pl.multiple_of(j * group, 16), group)
        pick = one_hot_rows(to_place[...], group, j * group)
        own = nn(pick, got[...])
        x1[rows] = own.astype(BF16)
        zt[rows] = norm_rows(own, gain[1:2], shift[1:2]).astype(BF16)
        gy[rows] = nn(pick, cot[...]).astype(BF16)

    @pl.loop(0, 3)
    def _(n):
        hidden = (nn(zt[...], ad[n]) * mask).astype(BF16)
        hid[n] = hidden
        result = nn(zt[...], w[n]) + nt(hidden, ad[4 + n])
        result = result * jnp.where(n == 0, HEAD_DIM**-0.5, 1.0)
        qkv[n] = result.astype(BF16)

    pairs = width // 128
    keep = (
        lax.broadcasted_iota(jnp.int32, (group, group), 0) // FRAMES
        == lax.broadcasted_iota(jnp.int32, (group, group), 1) // FRAMES
    )
    low = lax.broadcasted_iota(jnp.int32, (group, 128), 1) < HEAD_DIM

    @pl.loop(0, groups * pairs)
    def _(step):
        block = step // pairs
        pair = step - block * pairs
        rows = pl.ds(pl.multiple_of(block * group, 16), group)
        lanes = pl.ds(pl.multiple_of(pair * 128, 128), 128)
        query, key, value = qkv[0, rows, lanes], qkv[1, rows, lanes], qkv[2, rows, lanes]
        total = jnp.zeros((group, 128), F32)
        for h in range(2):
            own = low if h == 0 else ~low
            zero = jnp.zeros_like(query)
            weights = soften(nt(jnp.where(own, query, zero), key), keep).astype(BF16)
            soft[step * 2 + h] = weights
            total += nn(weights, jnp.where(own, value, zero))
        mixed[rows, lanes] = total.astype(BF16)

    hidden = (nn(mixed[...], ad[3]) * mask).astype(BF16)
    hid[3] = hidden
    acc[...] = nn(mixed[...], wo[...]) + nt(hidden, ad[7])

    @pl.loop(0, groups)
    def _(j):
        rows = pl.ds(pl.multiple_of(j * group, 16), group)
        own = x1[rows].astype(F32) + acc[rows]
        x2[rows] = own
        acc[rows] = own
        pull[rows] = jnp.zeros((group, width), F32)
        ze[rows] = norm_rows(own, gain[2:3], shift[2:3]).astype(BF16)

    hide[...] = (nn(ze[...], ea[...]) * mask).astype(BF16)
    ghr = (nn(gy[...], rb[...]) * mask).astype(BF16)
    hid[0 + 4] = ghr
    ghe[...] = jnp.zeros(ghe.shape, F32)

    @pl.loop(0, we.shape[1] // chunk)
    def _(c):
        part = pl.ds(pl.multiple_of(c * chunk, chunk), chunk)
        inner = nn(ze[...], we[:, part]) + nt(hide[...], eb[part])
        cube = 0.7978845608028654 * (inner + 0.044715 * inner * inner * inner)
        bend = jnp.tanh(cube)
        act = (0.5 * inner * (1.0 + bend)).astype(BF16)
        slope = 0.5 * (1.0 + bend) + 0.5 * inner * (1.0 - bend * bend) * (
            0.7978845608028654 * (1.0 + 3.0 * 0.044715 * inner * inner)
        )
        acc[...] += nn(act, wr[part])
        ghe[0] += nn(act, ra[part])
        wide[0, :, part] = tn(hid[4], act)
        gact = nt(gy[...], wr[part]) + nt(hid[4], ra[part])
        ginner = (gact * slope).astype(BF16)
        pull[...] += nt(ginner, we[:, part])
        ghe[1] += nn(ginner, eb[part])
        wide[1, :, part] = tn(hide[...], ginner)

    hidr = (ghe[0] * mask).astype(BF16)
    acc[...] += nt(hidr, rb[...])
    out_sent[...] = nn(one_hot(to_frame[...], got.shape[0]), acc[...].astype(BF16)).astype(BF16)
    gdown[4] = tn(hidr, gy[...])
    gheb = (ghe[1] * mask).astype(BF16)
    gup[4] = tn(gheb, ze[...])
    pull[...] += nt(gheb, ea[...])

    @pl.loop(0, groups)
    def _(j):
        rows = pl.ds(pl.multiple_of(j * group, 16), group)
        own = gy[rows].astype(F32) + norm_back(x2[rows], pull[rows], gain[2:3])
        acc[rows] = own
        ze[rows] = own.astype(BF16)

    grad = ze
    hidden_grad = (nn(grad[...], ad[7]) * mask).astype(BF16)
    gmix[...] = (nt(grad[...], wo[...]) + nt(hidden_grad, ad[3])).astype(BF16)
    gdown[3] = tn(hidden_grad, mixed[...])
    gup[3] = tn(hid[3], grad[...])

    @pl.loop(0, groups * pairs)
    def _(step):
        block = step // pairs
        pair = step - block * pairs
        rows = pl.ds(pl.multiple_of(block * group, 16), group)
        lanes = pl.ds(pl.multiple_of(pair * 128, 128), 128)
        weights = [soft[step * 2 + h] for h in range(2)]
        gq, gk, gv = attention_back(
            qkv[0, rows, lanes], qkv[1, rows, lanes], qkv[2, rows, lanes], weights, gmix[rows, lanes], low
        )
        gqkv[0, rows, lanes] = gq.astype(BF16)
        gqkv[1, rows, lanes] = gk.astype(BF16)
        gqkv[2, rows, lanes] = gv.astype(BF16)

    pull[...] = jnp.zeros(pull.shape, F32)

    @pl.loop(0, 3)
    def _(n):
        own = gqkv[n]
        hidden_grad = (nn(own, ad[4 + n]) * mask).astype(BF16)
        pull[...] += nt(own, w[n]) + nt(hidden_grad, ad[n])
        gdown[n] = tn(hidden_grad, zt[...])
        gup[n] = tn(hid[n], own)

    @pl.loop(0, groups)
    def _(j):
        rows = pl.ds(pl.multiple_of(j * group, 16), group)
        own = acc[rows] + norm_back(x1[rows].astype(F32), pull[rows], gain[1:2])
        ze[rows] = own.astype(BF16)

    grad_sent[...] = nn(one_hot(to_frame[...], got.shape[0]), ze[...]).astype(BF16)

    chosen = pl.ds(pl.multiple_of(choice * RANK, RANK), RANK)
    pieces = []
    for n in range(4):
        pieces += [gdown[n, chosen], gup[n, chosen]]
    pay[:, 0:128] = jnp.transpose(jnp.concatenate(pieces, axis=0)).astype(BF16)
    line = lax.broadcasted_iota(jnp.int32, (128 - 2 * RANK, width), 0)
    blank = jnp.zeros((128 - 2 * RANK, width), F32)
    for k in range(3):
        blank = jnp.where(line == k, idx[k].astype(F32), blank)
    pay[:, 128:256] = jnp.transpose(
        jnp.concatenate([gup[4, chosen], gdown[4, chosen], blank], axis=0)
    ).astype(BF16)
    tall = jnp.concatenate(
        [wide[1, chosen], wide[0, chosen], jnp.zeros((128 - 2 * RANK, we.shape[1]), F32)], axis=0
    )
    tall = jnp.transpose(tall)
    step = width // owners
    fold = we.shape[1] // width
    tall = tall.reshape(owners, fold, step, 128)
    total = tall[:, 0].reshape(width, 128)
    for f in range(1, fold):
        total += pltpu.roll(tall[:, f].reshape(width, 128), 2 * RANK * f, 1)
    pay[:, 256:384] = total.astype(BF16)


def one_hot_rows(target_row, rows, first):
    row_ids = lax.broadcasted_iota(jnp.int32, (rows, target_row.shape[1]), 0) + first
    return (row_ids == target_row).astype(F32).astype(BF16)


def spread_sum(stack, columns, first, choice, count):
    lanes = lax.broadcasted_iota(jnp.int32, (columns, ADAPT), 1)
    lines = lax.broadcasted_iota(jnp.int32, (columns, ADAPT), 0)
    spread = (lines == first + lanes % RANK).astype(F32)
    wide = lax.dot_general(
        stack, spread, (((1,), (0,)), ((), ())),
        preferred_element_type=F32, precision=lax.Precision.HIGHEST,
    )
    sets = lax.broadcasted_iota(jnp.int32, (1, ADAPT), 1) // RANK
    kept = jnp.where(sets.astype(F32) == choice, wide, 0.0)
    step = stack.shape[0] // count
    total = kept[0:step]
    for k in range(1, count):
        total += kept[k * step : (k + 1) * step]
    return total


def combine(sizes, got, down, up, ea, eb, ra, rb):
    groups, members, step, fold = sizes
    clips = 2
    share = members // clips
    mids, sps = [], []
    for g in range(groups):
        total = jnp.zeros((step, 256), F32)
        for b in range(clips):
            part = jnp.zeros((step, 384), F32)
            for t in range(share):
                own = got[g * members + b * share + t].astype(F32)
                part += own[:, 0:384]
                total += own[:, 384:640]
            mids.append(part)
        sps.append(total)
    mid = jnp.concatenate(mids, axis=0)
    sp = jnp.concatenate(sps, axis=0)
    mid_choice = mid[:, 160:161] * (1.0 / share)
    for n in range(4):
        for s, target in enumerate((down, up)):
            total = spread_sum(mid[:, 0:128], 128, (2 * n + s) * RANK, mid_choice, groups * clips)
            target[4 + n] = total
            total = jnp.zeros((step, ADAPT), F32)
            for b in range(clips):
                choice = jnp.concatenate(
                    [mids[g * clips][:, 161 + b : 162 + b] * (1.0 / share) for g in range(groups)], axis=0
                )
                total += spread_sum(sp, 256, ((2 * n + s) * clips + b) * RANK, choice, groups)
            target[n] = total
    ea[...] = spread_sum(mid[:, 128:256], 128, 0, mid_choice, groups * clips)
    rb[...] = spread_sum(mid[:, 128:256], 128, RANK, mid_choice, groups * clips)
    for f in range(fold):
        rows = slice(f * step, (f + 1) * step)
        eb[rows] = spread_sum(mid[:, 256:384], 128, 2 * RANK * f, mid_choice, groups * clips)
        ra[rows] = spread_sum(mid[:, 256:384], 128, 2 * RANK * f + RANK, mid_choice, groups * clips)


def pack(sizes, to_send, x, sent, stream):
    frames, clips, places, width, padded = sizes
    half = frames * padded
    for b in range(clips):
        for i in range(frames):
            base = b * half + i * padded
            stream[base + padded - 16 : base + padded] = jnp.zeros((16, width), BF16)
            stream[base : base + places] = x[i, b].astype(BF16)
        rows = slice(b * half, (b + 1) * half)
        sent[rows] = nn(one_hot(to_send[...], half), stream[rows]).astype(BF16)


def shape_of(*dims, kind=BF16):
    return jax.ShapeDtypeStruct(dims, kind)


def run(kernel, name, operands, outs, scratch, scalars=1, flops=0, spare=0):
    memory = [pl.BlockSpec(memory_space=pltpu.SMEM)] * scalars
    memory += [pl.BlockSpec(memory_space=pltpu.VMEM)] * (len(operands) - scalars)
    moved = sum(o.size * o.dtype.itemsize for o in operands)
    moved += sum(o.size * o.dtype.itemsize for o in outs)
    return pl.pallas_call(
        kernel,
        out_shape=outs,
        in_specs=memory,
        out_specs=[pl.BlockSpec(memory_space=pltpu.VMEM)] * len(outs),
        scratch_shapes=[pltpu.VMEM(s.shape, s.dtype) for s in scratch],
        compiler_params=pltpu.CompilerParams(vmem_limit_bytes=63 << 20),
        cost_estimate=pl.CostEstimate(flops=flops, bytes_accessed=moved, transcendentals=0),
        name=name,
    )(*operands)


def order_tables(frames, places, padded, blocks, part, chunk):
    half_rows, sent_rows = frames * padded, blocks * chunk
    assert half_rows == sent_rows
    to_send = [-1] * half_rows
    from_sent = [-1] * sent_rows
    for i in range(frames):
        for p in range(places):
            source, target = i * padded + p, (p // part) * chunk + i * part + p % part
            to_send[source] = target
            from_sent[target] = source
    senders = FRAMES // frames
    to_place = [-1] * (senders * chunk)
    to_frame = [-1] * (part * FRAMES)
    for p in range(part):
        for f in range(FRAMES):
            source, target = (f // frames) * chunk + (f % frames) * part + p, p * FRAMES + f
            to_place[source] = target
            to_frame[target] = source
    return [jnp.array([table], jnp.int32) for table in (to_send, from_sent, to_place, to_frame)]


def fits(mesh):
    return mesh.shape["tok"] == 8 and mesh.shape["clip"] == 4


def exchange(rows, senders):
    shaped = rows.reshape(senders, rows.shape[0] // senders, rows.shape[1])
    return lax.all_to_all(shaped, "tok", split_axis=0, concat_axis=0, tiled=True).reshape(rows.shape)


def gather(shard, dim):
    return lax.all_gather(shard, ("clip", "tok"), axis=dim, tiled=True)


def fast_device(
    tokens,
    adapter_index,
    norm_gain,
    norm_shift,
    spatial_weights,
    spatial_output,
    temporal_weights,
    temporal_output,
    expand_weight,
    reduce_weight,
    attention_down,
    attention_up,
    expand_down,
    expand_up,
    reduce_down,
    reduce_up,
    cotangent,
):
    frames, clips, places, width = tokens.shape[1:]
    members, groups = lax.axis_size("tok"), lax.axis_size("clip")
    blocks = members // clips
    part = places // blocks
    chunk = -(-frames * part // 8) * 8
    padded = -(-places // 16) * 16
    half, total = frames * padded, clips * frames * padded
    rows_all = FRAMES * part
    ff = expand_weight.shape[1]
    sizes = (frames, clips, places, width, padded)
    to_send, from_sent, to_place, to_frame = order_tables(frames, places, padded, blocks, part, chunk)
    position = lax.axis_index("tok")
    own_choice = lax.dynamic_slice_in_dim(adapter_index, position // blocks, 1)
    choices = jnp.concatenate([own_choice, adapter_index])

    adapt = jnp.concatenate([attention_down, jnp.swapaxes(attention_up, 1, 2)], axis=0)
    sp_adapt = gather(jnp.concatenate([adapt[0:4], adapt[8:12]]), 1)
    tp_adapt = gather(jnp.concatenate([adapt[4:8], adapt[12:16]]), 1)
    sp_w, sp_o = gather(spatial_weights, 1), gather(spatial_output, 0)
    tp_w, tp_o = gather(temporal_weights, 1), gather(temporal_output, 0)
    we, wr = gather(expand_weight, 0), gather(reduce_weight, 0)
    ea, eb = gather(expand_down, 0), gather(expand_up.T, 0)
    ra, rb = gather(reduce_down, 0), gather(reduce_up.T, 0)

    (cot_sent,) = run(
        functools.partial(pack, sizes), "cot_pack", (to_send, cotangent[0]),
        [shape_of(total, width)], [shape_of(total, width)], scalars=0,
    )
    cot = exchange(cot_sent, members)
    sent, qkv, soft, mixed, hid, zs = run(
        functools.partial(spatial_forward, sizes),
        "spatial_forward",
        (adapter_index, to_send, tokens[0], norm_gain, norm_shift, sp_w, sp_o, sp_adapt),
        [
            shape_of(total, width),
            shape_of(3, total, width),
            shape_of(frames * clips * HEADS, padded, padded),
            shape_of(total, width),
            shape_of(4, total, ADAPT),
            shape_of(total, width),
        ],
        [shape_of(total, width)],
    )
    got = exchange(sent, members)
    group = rows_all // 7
    out_sent, grad_sent, mid_pay = run(
        functools.partial(middle, (rows_all, width, group, 512, members * groups)),
        "middle",
        (choices, to_place, to_frame, got, cot, norm_gain, norm_shift, tp_w, tp_o, tp_adapt, we, wr, ea, eb, ra, rb),
        [shape_of(total, width), shape_of(total, width), shape_of(width, 384)],
        [
            shape_of(rows_all, width),
            shape_of(rows_all, width, kind=F32),
            shape_of(rows_all, width),
            shape_of(rows_all, width),
            shape_of(3, rows_all, width),
            shape_of(rows_all // group * HEADS, group, group),
            shape_of(rows_all, width),
            shape_of(5, rows_all, ADAPT),
            shape_of(rows_all, ADAPT),
            shape_of(rows_all, width),
            shape_of(rows_all, width, kind=F32),
            shape_of(rows_all, width, kind=F32),
            shape_of(2, rows_all, ADAPT, kind=F32),
            shape_of(rows_all, width),
            shape_of(3, rows_all, width),
            shape_of(5, ADAPT, width, kind=F32),
            shape_of(5, ADAPT, width, kind=F32),
            shape_of(2, ADAPT, ff, kind=F32),
        ],
    )
    made = exchange(out_sent, members)
    back = exchange(grad_sent, members)
    dx, out, sp_pay = run(
        functools.partial(spatial_backward, sizes),
        "spatial_backward",
        (adapter_index, from_sent, tokens[0], norm_gain, sp_w, sp_o, sp_adapt, qkv, soft, mixed, hid, zs, back, made),
        [
            shape_of(frames, clips, places, width, kind=F32),
            shape_of(frames, clips, places, width, kind=F32),
            shape_of(width, 256),
        ],
        [
            shape_of(total, width),
            shape_of(total, width),
            shape_of(3, total, width),
            shape_of(half, width, kind=F32),
            shape_of(4, ADAPT, width, kind=F32),
            shape_of(4, ADAPT, width, kind=F32),
        ],
    )
    pay = jnp.concatenate([mid_pay, sp_pay], axis=1).reshape(members * groups, -1, 640)
    terms = lax.all_to_all(pay, ("clip", "tok"), split_axis=0, concat_axis=0, tiled=True)
    step = width // (members * groups)
    fold = ff // width
    down, up, gea, geb, gra, grb = run(
        functools.partial(combine, (groups, members, step, fold)),
        "combine",
        (terms,),
        [
            shape_of(8, step, ADAPT, kind=F32),
            shape_of(8, step, ADAPT, kind=F32),
            shape_of(step, ADAPT, kind=F32),
            shape_of(fold * step, ADAPT, kind=F32),
            shape_of(fold * step, ADAPT, kind=F32),
            shape_of(step, ADAPT, kind=F32),
        ],
        [],
        scalars=0,
    )
    return (out[None], dx[None], down, jnp.swapaxes(up, 1, 2), gea, geb.T, gra, grb.T)


def solution(mesh):
    pick = fast_device if fits(mesh) else general_device

    placed = (
        P(("clip", "tok"), None, None, None, None),
        P("clip"),
        P(),
        P(),
        P(None, ("clip", "tok"), None),
        P(("clip", "tok"), None),
        P(None, ("clip", "tok"), None),
        P(("clip", "tok"), None),
        P(("clip", "tok"), None),
        P(("clip", "tok"), None),
        P(None, ("clip", "tok"), None),
        P(None, None, ("clip", "tok")),
        P(("clip", "tok"), None),
        P(None, ("clip", "tok")),
        P(("clip", "tok"), None),
        P(None, ("clip", "tok")),
        P(("clip", "tok"), None, None, None, None),
    )
    return jax.shard_map(
        pick,
        mesh=mesh,
        in_specs=placed,
        out_specs=(
            P(("clip", "tok"), None, None, None, None),
            P(("clip", "tok"), None, None, None, None),
            P(None, ("clip", "tok"), None),
            P(None, None, ("clip", "tok")),
            P(("clip", "tok"), None),
            P(None, ("clip", "tok")),
            P(("clip", "tok"), None),
            P(None, ("clip", "tok")),
        ),
        check_vma=False,
    )
```

```python
import functools

import jax
import jax.numpy as jnp
from jax import lax
from jax.experimental import pallas as pl
from jax.experimental.pallas import tpu as pltpu
from jax.sharding import PartitionSpec as P

HEADS = 12
HEAD_DIM = 64
FRAMES = 16
ADAPTERS = 8
RANK = 16


EPSILON = 1e-06


def layer_norm(stream, gain_row, shift_row):
    average = jnp.mean(stream, axis=-1, keepdims=True)
    centred = stream - average
    variance = jnp.mean(centred * centred, axis=-1, keepdims=True)
    return centred * lax.rsqrt(variance + EPSILON) * gain_row + shift_row


def adapter_mask(choice_rows):
    columns = jnp.arange(ADAPTERS * RANK, dtype=jnp.int32) // RANK
    return (columns[None, :] == choice_rows[:, None]).astype(jnp.float32)


def project_many(inputs, weight, down_rows, up_rows, mask):
    hidden = jnp.einsum("rd,ndc->nrc", inputs, down_rows, preferred_element_type=jnp.float32)
    hidden = (hidden * mask).astype(jnp.bfloat16)
    result = jnp.einsum("rd,nde->nre", inputs, weight, preferred_element_type=jnp.float32)
    result = result + jnp.einsum(
        "nrc,nce->nre", hidden, up_rows, preferred_element_type=jnp.float32
    )
    return (result, hidden)


def project_back(inputs, hidden, grad_rows, weight, down_rows, up_rows, mask):
    hidden_grad = jnp.einsum("nre,nce->nrc", grad_rows, up_rows, preferred_element_type=jnp.float32)
    hidden_grad = (hidden_grad * mask).astype(jnp.bfloat16)
    input_grad = jnp.einsum("nre,nde->rd", grad_rows, weight, preferred_element_type=jnp.float32)
    input_grad = input_grad + jnp.einsum(
        "nrc,ndc->rd", hidden_grad, down_rows, preferred_element_type=jnp.float32
    )
    down_grad = jnp.einsum("rd,nrc->ndc", inputs, hidden_grad, preferred_element_type=jnp.float32)
    up_grad = jnp.einsum("nrc,nre->nce", hidden, grad_rows, preferred_element_type=jnp.float32)
    return (input_grad, down_grad, up_grad)


def attend_forward(packed, layout):
    view_shape, score_eq, mix_eq, back_eq = layout
    queries = packed[0].reshape(view_shape)
    key_rows = packed[1].reshape(view_shape)
    values = packed[2].reshape(view_shape)
    scores = jnp.einsum(
        score_eq, queries, key_rows, preferred_element_type=jnp.float32
    ) * HEAD_DIM ** (-0.5)
    ceiling = jnp.max(scores, axis=-1, keepdims=True)
    expo_rows = jnp.exp(scores - ceiling)
    totals = jnp.sum(expo_rows, axis=-1, keepdims=True)
    weights_soft = (expo_rows / totals).astype(jnp.bfloat16)
    mixed_rows = jnp.einsum(mix_eq, weights_soft, values, preferred_element_type=jnp.float32)
    return (mixed_rows.reshape(packed.shape[1:]), ceiling + jnp.log(totals))


def attend_backward(packed, log_total, mixed_grad, layout):
    view_shape, score_eq, mix_eq, back_eq = layout
    scaling = HEAD_DIM ** (-0.5)
    queries = packed[0].reshape(view_shape)
    key_rows = packed[1].reshape(view_shape)
    values = packed[2].reshape(view_shape)
    scores = jnp.einsum(score_eq, queries, key_rows, preferred_element_type=jnp.float32) * scaling
    weights_soft = jnp.exp(scores - log_total)
    output_grad = mixed_grad.reshape(view_shape)
    soft_grad = jnp.einsum(score_eq, output_grad, values, preferred_element_type=jnp.float32)
    row_inner = jnp.sum(weights_soft * soft_grad, axis=-1, keepdims=True)
    score_grad = (weights_soft * (soft_grad - row_inner)).astype(jnp.bfloat16)
    query_grad = (
        jnp.einsum(mix_eq, score_grad, key_rows, preferred_element_type=jnp.float32) * scaling
    )
    key_grad = (
        jnp.einsum(back_eq, score_grad, queries, preferred_element_type=jnp.float32) * scaling
    )
    value_grad = jnp.einsum(
        back_eq, weights_soft.astype(jnp.bfloat16), output_grad, preferred_element_type=jnp.float32
    )
    stacked = jnp.stack([query_grad, key_grad, value_grad])
    return stacked.reshape(packed.shape).astype(jnp.bfloat16)


def attention_forward(stream, gain_row, shift_row, weight_set, mask, layout):
    inner_weights, outer_weight, down_rows, up_rows = weight_set
    normed = layer_norm(stream, gain_row, shift_row).astype(jnp.bfloat16)
    packed, packed_hidden = project_many(normed, inner_weights, down_rows[0:3], up_rows[0:3], mask)
    packed = packed.astype(jnp.bfloat16)
    mixed_rows, log_total = attend_forward(packed, layout)
    mixed_rows = mixed_rows.astype(jnp.bfloat16)
    branch, outer_hidden = project_many(
        mixed_rows, outer_weight[None], down_rows[3:4], up_rows[3:4], mask
    )
    return (
        stream + branch[0],
        (normed, packed, packed_hidden, mixed_rows, outer_hidden, log_total),
    )


def attention_backward(
    stream, stream_grad, gain_row, shift_row, weight_set, mask, layout, kept_values
):
    inner_weights, outer_weight, down_rows, up_rows = weight_set
    normed, packed, packed_hidden, mixed_rows, outer_hidden, log_total = kept_values
    branch_grad = stream_grad.astype(jnp.bfloat16)[None]
    mixed_grad, outer_down, outer_up = project_back(
        mixed_rows,
        outer_hidden,
        branch_grad,
        outer_weight[None],
        down_rows[3:4],
        up_rows[3:4],
        mask,
    )
    packed_grad = attend_backward(packed, log_total, mixed_grad.astype(jnp.bfloat16), layout)
    normed_grad, inner_down, inner_up = project_back(
        normed, packed_hidden, packed_grad, inner_weights, down_rows[0:3], up_rows[0:3], mask
    )
    unused, norm_pull = jax.vjp(lambda rows_in: layer_norm(rows_in, gain_row, shift_row), stream)
    before_grad = stream_grad + norm_pull(normed_grad)[0]
    return (
        before_grad,
        jnp.concatenate([inner_down, outer_down], axis=0),
        jnp.concatenate([inner_up, outer_up], axis=0),
    )


def expand_forward(stream, gain_row, shift_row, weight_set, mask):
    up_weight, down_weight, in_down, in_up, out_down, out_up = weight_set
    normed = layer_norm(stream, gain_row, shift_row).astype(jnp.bfloat16)
    inner_rows, inner_hidden = project_many(
        normed, up_weight[None], in_down[None], in_up[None], mask
    )
    inner_rows = inner_rows[0]
    active = jax.nn.gelu(inner_rows, approximate=True).astype(jnp.bfloat16)
    branch, outer_hidden = project_many(
        active, down_weight[None], out_down[None], out_up[None], mask
    )
    return (stream + branch[0], (normed, inner_rows, inner_hidden, active, outer_hidden))


def expand_backward(stream, stream_grad, gain_row, shift_row, weight_set, mask, kept_values):
    up_weight, down_weight, in_down, in_up, out_down, out_up = weight_set
    normed, inner_rows, inner_hidden, active, outer_hidden = kept_values
    branch_grad = stream_grad.astype(jnp.bfloat16)[None]
    active_grad, out_down_grad, out_up_grad = project_back(
        active, outer_hidden, branch_grad, down_weight[None], out_down[None], out_up[None], mask
    )
    unused, gelu_pull = jax.vjp(
        lambda values_in: jax.nn.gelu(values_in, approximate=True), inner_rows
    )
    inner_grad = gelu_pull(active_grad)[0].astype(jnp.bfloat16)[None]
    normed_grad, in_down_grad, in_up_grad = project_back(
        normed, inner_hidden, inner_grad, up_weight[None], in_down[None], in_up[None], mask
    )
    unused_norm, norm_pull = jax.vjp(
        lambda rows_in: layer_norm(rows_in, gain_row, shift_row), stream
    )
    before_grad = stream_grad + norm_pull(normed_grad)[0]
    return (before_grad, (in_down_grad[0], in_up_grad[0], out_down_grad[0], out_up_grad[0]))


def regroup_places(stream, layout_sizes, backward):
    frames_dev, clips_dev, places, model_width, clip_rows, place_blocks, place_part = layout_sizes
    padded = jnp.pad(
        stream.reshape(frames_dev, clips_dev, places, model_width),
        ((0, 0), (0, 0), (0, place_part * place_blocks - places), (0, 0)),
    )
    padded = padded.reshape(frames_dev, clips_dev * place_blocks, place_part, model_width)
    if backward:
        arrived = lax.all_to_all(
            padded.astype(jnp.bfloat16), "tok", split_axis=1, concat_axis=0, tiled=True
        ).astype(padded.dtype)
    else:
        arrived = lax.all_to_all(
            padded.astype(jnp.bfloat16), "tok", split_axis=1, concat_axis=0, tiled=True
        ).astype(padded.dtype)
    return arrived.reshape(clip_rows * FRAMES * place_part, model_width)


def regroup_frames(stream, layout_sizes, backward):
    frames_dev, clips_dev, places, model_width, clip_rows, place_blocks, place_part = layout_sizes
    shaped = stream.reshape(clip_rows * FRAMES, 1, place_part, model_width)
    if backward:
        arrived = lax.all_to_all(
            shaped.astype(jnp.bfloat16), "tok", split_axis=0, concat_axis=1, tiled=True
        ).astype(shaped.dtype)
    else:
        arrived = lax.all_to_all(
            shaped.astype(jnp.bfloat16), "tok", split_axis=0, concat_axis=1, tiled=True
        ).astype(shaped.dtype)
    arrived = arrived.reshape(frames_dev, clips_dev, place_part * place_blocks, model_width)
    return arrived[:, :, :places].reshape(frames_dev * clips_dev * places, model_width)


def general_device(
    tokens,
    adapter_index,
    norm_gain,
    norm_shift,
    spatial_weights,
    spatial_output,
    temporal_weights,
    temporal_output,
    expand_weight,
    reduce_weight,
    attention_down,
    attention_up,
    expand_down,
    expand_up,
    reduce_down,
    reduce_up,
    cotangent,
):
    frames_dev, clips_dev, places, model_width = tokens.shape[1:]
    tok_count = lax.axis_size("tok")
    frame_blocks = FRAMES // frames_dev
    clip_rows = tok_count // frame_blocks
    place_blocks = tok_count // clips_dev
    place_part = -(-places // place_blocks)
    layout_sizes = (frames_dev, clips_dev, places, model_width, clip_rows, place_blocks, place_part)
    adapt_cols = ADAPTERS * RANK
    position = lax.axis_index("tok")
    spatial_choice = lax.dynamic_slice_in_dim(
        adapter_index, position // frame_blocks * clips_dev, clips_dev
    )
    spatial_mask = jnp.broadcast_to(
        adapter_mask(spatial_choice)[None, :, None, :], (frames_dev, clips_dev, places, adapt_cols)
    ).reshape(-1, adapt_cols)
    temporal_choice = lax.dynamic_slice_in_dim(
        adapter_index.reshape(clip_rows, clips_dev), position // place_blocks, 1, 1
    )[:, 0]
    temporal_mask = jnp.broadcast_to(
        adapter_mask(temporal_choice)[:, None, None, :], (clip_rows, FRAMES, place_part, adapt_cols)
    ).reshape(-1, adapt_cols)
    spatial_layout = (
        (frames_dev * clips_dev, places, HEADS, HEAD_DIM),
        "gqhd,gkhd->ghqk",
        "ghqk,gkhd->gqhd",
        "ghqk,gqhd->gkhd",
    )
    temporal_layout = (
        (clip_rows, FRAMES, place_part, HEADS, HEAD_DIM),
        "aqphd,akphd->aphqk",
        "aphqk,akphd->aqphd",
        "aphqk,aqphd->akphd",
    )
    spatial_set = (
        lax.all_gather(spatial_weights, ("clip", "tok"), axis=1, tiled=True),
        lax.all_gather(spatial_output, ("clip", "tok"), axis=0, tiled=True),
        lax.all_gather(attention_down[0:4], ("clip", "tok"), axis=1, tiled=True),
        lax.all_gather(attention_up[0:4], ("clip", "tok"), axis=2, tiled=True),
    )
    stream0 = tokens.reshape(-1, model_width)
    stream1, spatial_kept = attention_forward(
        stream0, norm_gain[0], norm_shift[0], spatial_set, spatial_mask, spatial_layout
    )
    placed1 = regroup_places(stream1, layout_sizes, False)
    temporal_set = (
        lax.all_gather(temporal_weights, ("clip", "tok"), axis=1, tiled=True),
        lax.all_gather(temporal_output, ("clip", "tok"), axis=0, tiled=True),
        lax.all_gather(attention_down[4:8], ("clip", "tok"), axis=1, tiled=True),
        lax.all_gather(attention_up[4:8], ("clip", "tok"), axis=2, tiled=True),
    )
    placed2, temporal_kept = attention_forward(
        placed1, norm_gain[1], norm_shift[1], temporal_set, temporal_mask, temporal_layout
    )
    stream2 = regroup_frames(placed2, layout_sizes, False)
    expand_set = (
        lax.all_gather(expand_weight, ("clip", "tok"), axis=0, tiled=True),
        lax.all_gather(reduce_weight, ("clip", "tok"), axis=0, tiled=True),
        lax.all_gather(expand_down, ("clip", "tok"), axis=0, tiled=True),
        lax.all_gather(expand_up, ("clip", "tok"), axis=1, tiled=True),
        lax.all_gather(reduce_down, ("clip", "tok"), axis=0, tiled=True),
        lax.all_gather(reduce_up, ("clip", "tok"), axis=1, tiled=True),
    )
    stream3, expand_kept = expand_forward(
        stream2, norm_gain[2], norm_shift[2], expand_set, spatial_mask
    )
    expand_set = (
        lax.all_gather(expand_weight, ("clip", "tok"), axis=0, tiled=True),
        lax.all_gather(reduce_weight, ("clip", "tok"), axis=0, tiled=True),
        lax.all_gather(expand_down, ("clip", "tok"), axis=0, tiled=True),
        lax.all_gather(expand_up, ("clip", "tok"), axis=1, tiled=True),
        lax.all_gather(reduce_down, ("clip", "tok"), axis=0, tiled=True),
        lax.all_gather(reduce_up, ("clip", "tok"), axis=1, tiled=True),
    )
    grad2, expand_grads = expand_backward(
        stream2,
        cotangent.reshape(-1, model_width),
        norm_gain[2],
        norm_shift[2],
        expand_set,
        spatial_mask,
        expand_kept,
    )
    placed_grad2 = regroup_places(grad2, layout_sizes, True)
    temporal_set = (
        lax.all_gather(temporal_weights, ("clip", "tok"), axis=1, tiled=True),
        lax.all_gather(temporal_output, ("clip", "tok"), axis=0, tiled=True),
        lax.all_gather(attention_down[4:8], ("clip", "tok"), axis=1, tiled=True),
        lax.all_gather(attention_up[4:8], ("clip", "tok"), axis=2, tiled=True),
    )
    placed_grad1, temporal_down, temporal_up = attention_backward(
        placed1,
        placed_grad2,
        norm_gain[1],
        norm_shift[1],
        temporal_set,
        temporal_mask,
        temporal_layout,
        temporal_kept,
    )
    grad1 = regroup_frames(placed_grad1, layout_sizes, True)
    spatial_set = (
        lax.all_gather(spatial_weights, ("clip", "tok"), axis=1, tiled=True),
        lax.all_gather(spatial_output, ("clip", "tok"), axis=0, tiled=True),
        lax.all_gather(attention_down[0:4], ("clip", "tok"), axis=1, tiled=True),
        lax.all_gather(attention_up[0:4], ("clip", "tok"), axis=2, tiled=True),
    )
    grad0, spatial_down, spatial_up = attention_backward(
        stream0,
        grad1,
        norm_gain[0],
        norm_shift[0],
        spatial_set,
        spatial_mask,
        spatial_layout,
        spatial_kept,
    )
    owned = (
        lax.psum_scatter(
            jnp.concatenate([spatial_down, temporal_down], axis=0),
            ("clip", "tok"),
            scatter_dimension=1,
            tiled=True,
        ),
        lax.psum_scatter(
            jnp.concatenate([spatial_up, temporal_up], axis=0),
            ("clip", "tok"),
            scatter_dimension=2,
            tiled=True,
        ),
        lax.psum_scatter(expand_grads[0], ("clip", "tok"), scatter_dimension=0, tiled=True),
        lax.psum_scatter(expand_grads[1], ("clip", "tok"), scatter_dimension=1, tiled=True),
        lax.psum_scatter(expand_grads[2], ("clip", "tok"), scatter_dimension=0, tiled=True),
        lax.psum_scatter(expand_grads[3], ("clip", "tok"), scatter_dimension=1, tiled=True),
    )
    return (
        stream3.reshape(tokens.shape),
        grad0.reshape(tokens.shape),
        owned[0],
        owned[1],
        owned[2],
        owned[3],
        owned[4],
        owned[5],
    )


F32 = jnp.float32
BF16 = jnp.bfloat16
ADAPT = ADAPTERS * RANK


def nn(left, right):
    return lax.dot_general(left, right, (((1,), (0,)), ((), ())), preferred_element_type=F32)


def nt(left, right):
    return lax.dot_general(left, right, (((1,), (1,)), ((), ())), preferred_element_type=F32)


def tn(left, right):
    return lax.dot_general(left, right, (((0,), (0,)), ((), ())), preferred_element_type=F32)


def one_hot(target_row, rows):
    row_ids = lax.broadcasted_iota(jnp.int32, (rows, target_row.shape[1]), 0)
    return (row_ids == target_row).astype(F32).astype(BF16)


def column_mask(choice):
    return (lax.broadcasted_iota(jnp.int32, (1, ADAPT), 1) // RANK == choice).astype(F32)


def norm_rows(rows, gain_row, shift_row):
    average = jnp.mean(rows, axis=-1, keepdims=True)
    centred = rows - average
    variance = jnp.mean(centred * centred, axis=-1, keepdims=True)
    return centred * lax.rsqrt(variance + EPSILON) * gain_row + shift_row


def norm_back(rows, pulled, gain_row):
    average = jnp.mean(rows, axis=-1, keepdims=True)
    centred = rows - average
    variance = jnp.mean(centred * centred, axis=-1, keepdims=True)
    scale = lax.rsqrt(variance + EPSILON)
    unit = centred * scale
    scaled = pulled * gain_row
    return scale * (
        scaled
        - jnp.mean(scaled, axis=-1, keepdims=True)
        - unit * jnp.mean(scaled * unit, axis=-1, keepdims=True)
    )


def soften(scores, keep):
    scores = jnp.where(keep, scores, -1e30)
    ceiling = jnp.max(scores, axis=-1, keepdims=True)
    expo = jnp.exp(scores - ceiling)
    return expo * (1.0 / jnp.sum(expo, axis=-1, keepdims=True))


def spatial_forward(
    sizes, idx, to_send, x, gain, shift, w, ad, sent, qkv, soft, mixed, hid, zs, stream
):
    frames, clips, places, width, padded = sizes
    half = frames * padded
    for b in range(clips):
        for i in range(frames):
            base = b * half + i * padded
            zs[base + padded - 16 : base + padded] = jnp.zeros((16, width), BF16)
            stream[base + padded - 16 : base + padded] = jnp.zeros((16, width), BF16)
            zs[base : base + places] = norm_rows(x[i, b], gain[0:1], shift[0:1]).astype(BF16)
    for b in range(clips):
        rows = slice(b * half, (b + 1) * half)
        mask = column_mask(idx[b])

        @pl.loop(0, 3)
        def _(n):
            hidden = (nn(zs[rows], ad[n]) * mask).astype(BF16)
            hid[n, rows] = hidden
            result = nn(zs[rows], w[n]) + nt(hidden, ad[4 + n])
            result = result * jnp.where(n == 0, HEAD_DIM**-0.5, 1.0)
            qkv[n, rows] = result.astype(BF16)

    keep = lax.broadcasted_iota(jnp.int32, (padded, padded), 1) < places
    pairs = width // 128
    low = lax.broadcasted_iota(jnp.int32, (padded, 128), 1) < HEAD_DIM

    @pl.loop(0, frames * clips * pairs)
    def _(step):
        group = step // pairs
        pair = step - group * pairs
        rows = pl.ds(pl.multiple_of(group * padded, 16), padded)
        lanes = pl.ds(pl.multiple_of(pair * 128, 128), 128)
        query, key, value = qkv[0, rows, lanes], qkv[1, rows, lanes], qkv[2, rows, lanes]
        total = jnp.zeros((padded, 128), F32)
        for h in range(2):
            own = low if h == 0 else ~low
            zero = jnp.zeros_like(query)
            weights = soften(nt(jnp.where(own, query, zero), key), keep).astype(BF16)
            soft[step * 2 + h] = weights
            total += nn(weights, jnp.where(own, value, zero))
        mixed[rows, lanes] = total.astype(BF16)

    for b in range(clips):
        rows = slice(b * half, (b + 1) * half)
        hidden = (nn(mixed[rows], ad[3]) * column_mask(idx[b])).astype(BF16)
        hid[3, rows] = hidden
        branch = nn(mixed[rows], w[3]) + nt(hidden, ad[7])
        for i in range(frames):
            base = b * half + i * padded
            stream[base : base + places] = (
                x[i, b] + branch[i * padded : i * padded + places]
            ).astype(BF16)
        sent[rows] = nn(one_hot(to_send[...], half), stream[rows]).astype(BF16)


def attention_back(query, key, value, weights, grads, low):
    zero = jnp.zeros_like(query)
    totals = [jnp.zeros(query.shape, F32) for _ in range(3)]
    for h in range(2):
        own = low if h == 0 else ~low
        soft = weights[h]
        grad = jnp.where(own, grads, zero)
        pulled = nt(grad, value)
        wide = soft.astype(F32)
        inner = jnp.sum(wide * pulled, axis=-1, keepdims=True)
        score = (wide * (pulled - inner)).astype(BF16)
        totals[0] += nn(score, jnp.where(own, key, zero))
        totals[1] += tn(score, jnp.where(own, query, zero))
        totals[2] += tn(soft, grad)
    return totals[0] * HEAD_DIM**-0.5, totals[1], totals[2]


def spatial_backward(
    sizes, idx, from_sent, x, gain, w, ad, qkv, soft, mixed, hid, zs, got, made,
    dx, out, pay, grad, gmix, gqkv, gpull, gdown, gup
):
    frames, clips, places, width, padded = sizes
    half = frames * padded
    for b in range(clips):
        rows = slice(b * half, (b + 1) * half)
        mask = column_mask(idx[b])
        back = one_hot(from_sent[...], half)
        final = nn(back, made[rows])
        for i in range(frames):
            out[i, b] = final[i * padded : i * padded + places]
        grad[rows] = nn(back, got[rows]).astype(BF16)
        hidden_grad = (nn(grad[rows], ad[7]) * mask).astype(BF16)
        gmix[rows] = (nt(grad[rows], w[3]) + nt(hidden_grad, ad[3])).astype(BF16)
        down, up = tn(hidden_grad, mixed[rows]), tn(hid[3, rows], grad[rows])
        if b == 0:
            gdown[3], gup[3] = down, up
        else:
            gdown[3] += down
            gup[3] += up

    pairs = width // 128
    low = lax.broadcasted_iota(jnp.int32, (padded, 128), 1) < HEAD_DIM

    @pl.loop(0, frames * clips * pairs)
    def _(step):
        group = step // pairs
        pair = step - group * pairs
        rows = pl.ds(pl.multiple_of(group * padded, 16), padded)
        lanes = pl.ds(pl.multiple_of(pair * 128, 128), 128)
        weights = [soft[step * 2 + h] for h in range(2)]
        gq, gk, gv = attention_back(
            qkv[0, rows, lanes], qkv[1, rows, lanes], qkv[2, rows, lanes], weights, gmix[rows, lanes], low
        )
        gqkv[0, rows, lanes] = gq.astype(BF16)
        gqkv[1, rows, lanes] = gk.astype(BF16)
        gqkv[2, rows, lanes] = gv.astype(BF16)

    for b in range(clips):
        rows = slice(b * half, (b + 1) * half)
        mask = column_mask(idx[b])
        gpull[...] = jnp.zeros(gpull.shape, F32)

        @pl.loop(0, 3)
        def _(n):
            own = gqkv[n, rows]
            hidden_grad = (nn(own, ad[4 + n]) * mask).astype(BF16)
            gpull[...] += nt(own, w[n]) + nt(hidden_grad, ad[n])
            down, up = tn(hidden_grad, zs[rows]), tn(hid[n, rows], own)
            if b == 0:
                gdown[n], gup[n] = down, up
            else:
                gdown[n] += down
                gup[n] += up

        for i in range(frames):
            base = i * padded
            dx[i, b] = grad[b * half + base : b * half + base + places].astype(F32) + norm_back(
                x[i, b], gpull[base : base + places], gain[0:1]
            )
    repeat = jnp.where(idx[0] == idx[1], 0.0, 1.0)
    pieces = []
    for n in range(4):
        for source in (gdown, gup):
            pieces.append(source[n, pl.ds(pl.multiple_of(idx[0] * RANK, RANK), RANK)])
            pieces.append(source[n, pl.ds(pl.multiple_of(idx[1] * RANK, RANK), RANK)] * repeat)
    pay[...] = jnp.transpose(jnp.concatenate(pieces, axis=0)).astype(BF16)


def middle(
    sizes, idx, to_place, to_frame, got, cot, gain, shift, w, ad, we, wr, tall, flat,
    out_sent, grad_sent, pay,
    x1, x2, zt, ze, qkv, soft, mixed, hid, hide, gy, acc, pull, ghe, gmix, gqkv, gdown, gup, wide
):
    rows_all, width, group, chunk, owners = sizes
    choice = idx[0]
    mask = column_mask(choice)
    groups = rows_all // group

    @pl.loop(0, groups)
    def _(j):
        rows = pl.ds(pl.multiple_of(j * group, 16), group)
        pick = one_hot_rows(to_place[...], group, j * group)
        own = nn(pick, got[...])
        x1[rows] = own.astype(BF16)
        zt[rows] = norm_rows(own, gain[1:2], shift[1:2]).astype(BF16)
        gy[rows] = nn(pick, cot[...]).astype(BF16)

    @pl.loop(0, 3)
    def _(n):
        hidden = (nn(zt[...], ad[n]) * mask).astype(BF16)
        hid[n] = hidden
        result = nn(zt[...], w[n]) + nt(hidden, ad[4 + n])
        result = result * jnp.where(n == 0, HEAD_DIM**-0.5, 1.0)
        qkv[n] = result.astype(BF16)

    pairs = width // 128
    keep = (
        lax.broadcasted_iota(jnp.int32, (group, group), 0) // FRAMES
        == lax.broadcasted_iota(jnp.int32, (group, group), 1) // FRAMES
    )
    low = lax.broadcasted_iota(jnp.int32, (group, 128), 1) < HEAD_DIM

    @pl.loop(0, groups * pairs)
    def _(step):
        block = step // pairs
        pair = step - block * pairs
        rows = pl.ds(pl.multiple_of(block * group, 16), group)
        lanes = pl.ds(pl.multiple_of(pair * 128, 128), 128)
        query, key, value = qkv[0, rows, lanes], qkv[1, rows, lanes], qkv[2, rows, lanes]
        total = jnp.zeros((group, 128), F32)
        for h in range(2):
            own = low if h == 0 else ~low
            zero = jnp.zeros_like(query)
            weights = soften(nt(jnp.where(own, query, zero), key), keep).astype(BF16)
            soft[step * 2 + h] = weights
            total += nn(weights, jnp.where(own, value, zero))
        mixed[rows, lanes] = total.astype(BF16)

    hidden = (nn(mixed[...], ad[3]) * mask).astype(BF16)
    hid[3] = hidden
    acc[...] = nn(mixed[...], w[3]) + nt(hidden, ad[7])

    @pl.loop(0, groups)
    def _(j):
        rows = pl.ds(pl.multiple_of(j * group, 16), group)
        own = x1[rows].astype(F32) + acc[rows]
        x2[rows] = own
        acc[rows] = own
        pull[rows] = jnp.zeros((group, width), F32)
        ze[rows] = norm_rows(own, gain[2:3], shift[2:3]).astype(BF16)

    hide[...] = (nn(ze[...], flat[0]) * mask).astype(BF16)
    ghr = (nn(gy[...], flat[1]) * mask).astype(BF16)
    hid[0 + 4] = ghr
    ghe[...] = jnp.zeros(ghe.shape, F32)

    @pl.loop(0, we.shape[1] // chunk)
    def _(c):
        part = pl.ds(pl.multiple_of(c * chunk, chunk), chunk)
        inner = nn(ze[...], we[:, part]) + nt(hide[...], tall[0, part])
        cube = 0.7978845608028654 * (inner + 0.044715 * inner * inner * inner)
        bend = jnp.tanh(cube)
        act = (0.5 * inner * (1.0 + bend)).astype(BF16)
        slope = 0.5 * (1.0 + bend) + 0.5 * inner * (1.0 - bend * bend) * (
            0.7978845608028654 * (1.0 + 3.0 * 0.044715 * inner * inner)
        )
        acc[...] += nn(act, wr[part])
        ghe[0] += nn(act, tall[1, part])
        wide[0, :, part] = tn(hid[4], act)
        gact = nt(gy[...], wr[part]) + nt(hid[4], tall[1, part])
        ginner = (gact * slope).astype(BF16)
        pull[...] += nt(ginner, we[:, part])
        ghe[1] += nn(ginner, tall[0, part])
        wide[1, :, part] = tn(hide[...], ginner)

    hidr = (ghe[0] * mask).astype(BF16)
    acc[...] += nt(hidr, flat[1])
    out_sent[...] = nn(one_hot(to_frame[...], got.shape[0]), acc[...].astype(BF16)).astype(BF16)
    gdown[4] = tn(hidr, gy[...])
    gheb = (ghe[1] * mask).astype(BF16)
    gup[4] = tn(gheb, ze[...])
    pull[...] += nt(gheb, flat[0])

    @pl.loop(0, groups)
    def _(j):
        rows = pl.ds(pl.multiple_of(j * group, 16), group)
        own = gy[rows].astype(F32) + norm_back(x2[rows], pull[rows], gain[2:3])
        acc[rows] = own
        ze[rows] = own.astype(BF16)

    grad = ze
    hidden_grad = (nn(grad[...], ad[7]) * mask).astype(BF16)
    gmix[...] = (nt(grad[...], w[3]) + nt(hidden_grad, ad[3])).astype(BF16)
    gdown[3] = tn(hidden_grad, mixed[...])
    gup[3] = tn(hid[3], grad[...])

    @pl.loop(0, groups * pairs)
    def _(step):
        block = step // pairs
        pair = step - block * pairs
        rows = pl.ds(pl.multiple_of(block * group, 16), group)
        lanes = pl.ds(pl.multiple_of(pair * 128, 128), 128)
        weights = [soft[step * 2 + h] for h in range(2)]
        gq, gk, gv = attention_back(
            qkv[0, rows, lanes], qkv[1, rows, lanes], qkv[2, rows, lanes], weights, gmix[rows, lanes], low
        )
        gqkv[0, rows, lanes] = gq.astype(BF16)
        gqkv[1, rows, lanes] = gk.astype(BF16)
        gqkv[2, rows, lanes] = gv.astype(BF16)

    pull[...] = jnp.zeros(pull.shape, F32)

    @pl.loop(0, 3)
    def _(n):
        own = gqkv[n]
        hidden_grad = (nn(own, ad[4 + n]) * mask).astype(BF16)
        pull[...] += nt(own, w[n]) + nt(hidden_grad, ad[n])
        gdown[n] = tn(hidden_grad, zt[...])
        gup[n] = tn(hid[n], own)

    @pl.loop(0, groups)
    def _(j):
        rows = pl.ds(pl.multiple_of(j * group, 16), group)
        own = acc[rows] + norm_back(x1[rows].astype(F32), pull[rows], gain[1:2])
        ze[rows] = own.astype(BF16)

    grad_sent[...] = nn(one_hot(to_frame[...], got.shape[0]), ze[...]).astype(BF16)

    chosen = pl.ds(pl.multiple_of(choice * RANK, RANK), RANK)
    pieces = []
    for n in range(4):
        pieces += [gdown[n, chosen], gup[n, chosen]]
    pay[:, 0:128] = jnp.transpose(jnp.concatenate(pieces, axis=0)).astype(BF16)
    line = lax.broadcasted_iota(jnp.int32, (128 - 2 * RANK, width), 0)
    blank = jnp.zeros((128 - 2 * RANK, width), F32)
    for k in range(3):
        blank = jnp.where(line == k, idx[k].astype(F32), blank)
    pay[:, 128:256] = jnp.transpose(
        jnp.concatenate([gup[4, chosen], gdown[4, chosen], blank], axis=0)
    ).astype(BF16)
    high = jnp.concatenate(
        [wide[1, chosen], wide[0, chosen], jnp.zeros((128 - 2 * RANK, we.shape[1]), F32)], axis=0
    )
    high = jnp.transpose(high)
    step = width // owners
    fold = we.shape[1] // width
    high = high.reshape(owners, fold, step, 128)
    total = high[:, 0].reshape(width, 128)
    for f in range(1, fold):
        total += pltpu.roll(high[:, f].reshape(width, 128), 2 * RANK * f, 1)
    pay[:, 256:384] = total.astype(BF16)


def one_hot_rows(target_row, rows, first):
    row_ids = lax.broadcasted_iota(jnp.int32, (rows, target_row.shape[1]), 0) + first
    return (row_ids == target_row).astype(F32).astype(BF16)


def spread_sum(stack, columns, first, choice, count):
    lanes = lax.broadcasted_iota(jnp.int32, (columns, ADAPT), 1)
    lines = lax.broadcasted_iota(jnp.int32, (columns, ADAPT), 0)
    spread = (lines == first + lanes % RANK).astype(F32)
    wide = lax.dot_general(
        stack, spread, (((1,), (0,)), ((), ())),
        preferred_element_type=F32, precision=lax.Precision.HIGHEST,
    )
    sets = lax.broadcasted_iota(jnp.int32, (1, ADAPT), 1) // RANK
    kept = jnp.where(sets.astype(F32) == choice, wide, 0.0)
    step = stack.shape[0] // count
    total = kept[0:step]
    for k in range(1, count):
        total += kept[k * step : (k + 1) * step]
    return total


def combine(sizes, got, down, up, ea, eb, ra, rb):
    groups, members, step, fold = sizes
    clips = 2
    share = members // clips
    mids, sps = [], []
    for g in range(groups):
        total = jnp.zeros((step, 256), F32)
        for b in range(clips):
            part = jnp.zeros((step, 384), F32)
            for t in range(share):
                own = got[g * members + b * share + t].astype(F32)
                part += own[:, 0:384]
                total += own[:, 384:640]
            mids.append(part)
        sps.append(total)
    mid = jnp.concatenate(mids, axis=0)
    sp = jnp.concatenate(sps, axis=0)
    mid_choice = mid[:, 160:161] * (1.0 / share)
    for n in range(4):
        for s, target in enumerate((down, up)):
            total = spread_sum(mid[:, 0:128], 128, (2 * n + s) * RANK, mid_choice, groups * clips)
            target[4 + n] = total
            total = jnp.zeros((step, ADAPT), F32)
            for b in range(clips):
                choice = jnp.concatenate(
                    [mids[g * clips][:, 161 + b : 162 + b] * (1.0 / share) for g in range(groups)], axis=0
                )
                total += spread_sum(sp, 256, ((2 * n + s) * clips + b) * RANK, choice, groups)
            target[n] = total
    ea[...] = spread_sum(mid[:, 128:256], 128, 0, mid_choice, groups * clips)
    rb[...] = spread_sum(mid[:, 128:256], 128, RANK, mid_choice, groups * clips)
    for f in range(fold):
        rows = slice(f * step, (f + 1) * step)
        eb[rows] = spread_sum(mid[:, 256:384], 128, 2 * RANK * f, mid_choice, groups * clips)
        ra[rows] = spread_sum(mid[:, 256:384], 128, 2 * RANK * f + RANK, mid_choice, groups * clips)


def pack(sizes, to_send, x, sent, stream):
    frames, clips, places, width, padded = sizes
    half = frames * padded
    for b in range(clips):
        for i in range(frames):
            base = b * half + i * padded
            stream[base + padded - 16 : base + padded] = jnp.zeros((16, width), BF16)
            stream[base : base + places] = x[i, b].astype(BF16)
        rows = slice(b * half, (b + 1) * half)
        sent[rows] = nn(one_hot(to_send[...], half), stream[rows]).astype(BF16)


def shape_of(*dims, kind=BF16):
    return jax.ShapeDtypeStruct(dims, kind)


def run(kernel, name, operands, outs, scratch, scalars=1, flops=0, spare=0):
    memory = [pl.BlockSpec(memory_space=pltpu.SMEM)] * scalars
    memory += [pl.BlockSpec(memory_space=pltpu.VMEM)] * (len(operands) - scalars)
    moved = sum(o.size * o.dtype.itemsize for o in operands)
    moved += sum(o.size * o.dtype.itemsize for o in outs)
    return pl.pallas_call(
        kernel,
        out_shape=outs,
        in_specs=memory,
        out_specs=[pl.BlockSpec(memory_space=pltpu.VMEM)] * len(outs),
        scratch_shapes=[pltpu.VMEM(s.shape, s.dtype) for s in scratch],
        compiler_params=pltpu.CompilerParams(vmem_limit_bytes=63 << 20),
        cost_estimate=pl.CostEstimate(flops=flops, bytes_accessed=moved, transcendentals=0),
        name=name,
    )(*operands)


def order_tables(frames, places, padded, blocks, part, chunk):
    half_rows, sent_rows = frames * padded, blocks * chunk
    assert half_rows == sent_rows
    to_send = [-1] * half_rows
    from_sent = [-1] * sent_rows
    for i in range(frames):
        for p in range(places):
            source, target = i * padded + p, (p // part) * chunk + i * part + p % part
            to_send[source] = target
            from_sent[target] = source
    senders = FRAMES // frames
    to_place = [-1] * (senders * chunk)
    to_frame = [-1] * (part * FRAMES)
    for p in range(part):
        for f in range(FRAMES):
            source, target = (f // frames) * chunk + (f % frames) * part + p, p * FRAMES + f
            to_place[source] = target
            to_frame[target] = source
    return [jnp.array([table], jnp.int32) for table in (to_send, from_sent, to_place, to_frame)]


def fits(mesh):
    return mesh.shape["tok"] == 8 and mesh.shape["clip"] == 4


MESH = pl.DeviceIdType.MESH


def place_of():
    clip, tok = lax.axis_index("clip"), lax.axis_index("tok")
    return clip // 2, lax.rem(clip, 2), tok // 2, lax.rem(tok, 2)


def device_at(y, core, z, x):
    return (y * 2 + core, z * 2 + x)


def greet(peers):
    barrier = pltpu.get_barrier_semaphore()
    for peer in peers:
        pl.semaphore_signal(barrier, inc=1, device_id=peer, device_id_type=MESH)
    pl.semaphore_wait(barrier, len(peers))


def remote(source, target, send_sem, recv_sem, peer):
    return pltpu.make_async_remote_copy(
        src_ref=source, dst_ref=target, send_sem=send_sem, recv_sem=recv_sem, device_id=peer, device_id_type=MESH
    )


class Part:
    def __init__(self, shard, whole, dim, sems):
        self.shard, self.whole, self.dim, self.sems = shard, whole, dim, sems
        self.rows = shard.shape[dim]
        self.me = place_of()

    def span(self, first, count, half=None):
        rows = pl.ds(pl.multiple_of(first * self.rows, 8), count * self.rows)
        if self.dim == 1:
            lead = self.whole.shape[0] // 2
            front = slice(None) if half is None else slice(half * lead, (half + 1) * lead)
            return self.whole.at[front, rows]
        lanes = self.whole.shape[1] // 2
        if half is None or lanes % 128:
            return self.whole.at[rows]
        return self.whole.at[rows, half * lanes : (half + 1) * lanes]

    def slot(self, y, core, z, x, half=None):
        clip, tok = device_at(y, core, z, x)
        return self.span(clip * 8 + tok, 1, half)

    def send(self, source, target, sem, peer):
        remote(source, target, self.sems.at[0], self.sems.at[sem], device_at(*peer)).start()

    def arrive(self, target, sem):
        pltpu.make_async_copy(target, target, self.sems.at[sem]).wait()

    def local(self):
        return pltpu.make_async_copy(self.shard, self.slot(*self.me), self.sems.at[1])

    def pass_on(self, owner, source, y_too, x_too, step):
        y, core, z, x = self.me
        target = self.slot(*owner)
        source = target if source is None else source
        if x_too:
            self.send(source, target, 8 + step, (y, core, z, 1 - x))
        if y_too:
            self.send(source, target, 12 + step, (1 - y, core, z, x))

    def to_core(self, owner, source=None):
        y, core, z, x = self.me
        target = self.slot(*owner)
        self.send(target if source is None else source, target, 2 + owner[0], (y, 1 - core, z, x))

    def stage(self, number):
        y, core, z, x = self.me
        if number == 0:
            self.local().start()
            for d in range(1, 4):
                self.send(self.shard, self.slot(*self.me), 4 + d, (y, core, lax.rem(z + d, 4), x))
            self.pass_on(self.me, self.shard, True, True, 0)
            self.to_core(self.me, self.shard)
        elif number == 1:
            for d in range(1, 4):
                owner = (y, core, lax.rem(z + 4 - d, 4), x)
                self.arrive(self.slot(*owner), 4 + d)
                self.pass_on(owner, None, True, True, d)
                self.to_core(owner)
        elif number == 2:
            for d in range(4):
                far = lax.rem(z + 4 - d, 4)
                owner = (y, core, far, 1 - x)
                self.arrive(self.slot(*owner), 8 + d)
                self.send(self.slot(*owner, 0), self.slot(*owner, 0), 16 + d, (1 - y, core, z, x))
                self.to_core(owner)
                owner = (1 - y, core, far, x)
                self.arrive(self.slot(*owner), 12 + d)
                self.send(self.slot(*owner, 1), self.slot(*owner, 1), 20 + d, (y, core, z, 1 - x))
                self.to_core(owner)
        elif number == 3:
            for d in range(4):
                owner = (1 - y, core, lax.rem(z + 4 - d, 4), 1 - x)
                self.arrive(self.slot(*owner, 0), 16 + d)
                self.arrive(self.slot(*owner, 1), 20 + d)
                self.to_core(owner)
        else:
            self.local().wait()
            for far in range(2):
                self.arrive(self.span((far * 2 + 1 - core) * 8, 8), 2 + far)
            self.arrive(self.span(0, 31), 0)


PART_SEMS = 24


def gather_peers():
    y, core, z, x = place_of()
    peers = [device_at(y, core, lax.rem(z + d, 4), x) for d in range(1, 4)]
    return peers + [
        device_at(y, core, z, 1 - x), device_at(1 - y, core, z, x), device_at(y, 1 - core, z, x)
    ]


def gather_kernel(dims, *refs):
    count = len(dims)
    shards, wholes, sems = refs[:count], refs[count : 2 * count], refs[2 * count]
    parts = [Part(s, w, d, sems.at[i]) for i, (s, w, d) in enumerate(zip(shards, wholes, dims))]
    greet(gather_peers())
    for tick in range(count + 4):
        for number in range(5):
            if 0 <= tick - number < count:
                parts[tick - number].stage(number)


def gather(shards, dims, devices, ident):
    wholes = []
    for shard, dim in zip(shards, dims):
        dims_out = list(shard.shape)
        dims_out[dim] *= devices
        wholes.append(jax.ShapeDtypeStruct(tuple(dims_out), shard.dtype))
    return pl.pallas_call(
        functools.partial(gather_kernel, dims),
        out_shape=wholes,
        in_specs=[pl.BlockSpec(memory_space=pl.ANY)] * len(shards),
        out_specs=[pl.BlockSpec(memory_space=pl.ANY)] * len(shards),
        scratch_shapes=[pltpu.SemaphoreType.DMA((len(shards), PART_SEMS))],
        compiler_params=pltpu.CompilerParams(collective_id=ident, has_side_effects=True),
        name="gather",
    )(*shards)


def tok_peers(count):
    clip, tok = lax.axis_index("clip"), lax.axis_index("tok")
    return [(clip, lax.rem(tok + d, count)) for d in range(1, count)]


def all_peers(groups, members):
    clip, tok = lax.axis_index("clip"), lax.axis_index("tok")
    return [
        (lax.rem(clip + c, groups), lax.rem(tok + t, members))
        for c in range(groups) for t in range(members) if c or t
    ]


def exchange_kernel(groups, members, sent, got, send_sem, recv_sem, local_sem):
    clip, tok = lax.axis_index("clip"), lax.axis_index("tok")
    if groups == 1:
        peers, me = tok_peers(members), tok
        places = [peer[1] for peer in peers]
    else:
        peers, me = all_peers(groups, members), clip * members + tok
        places = [peer[0] * members + peer[1] for peer in peers]
    greet(peers)
    local = pltpu.make_async_copy(sent.at[me], got.at[me], local_sem)
    local.start()
    copies = [
        remote(sent.at[place], got.at[me], send_sem.at[n], recv_sem.at[n], peer)
        for n, (peer, place) in enumerate(zip(peers, places))
    ]
    for copy in copies:
        copy.start()
    local.wait()
    for copy in copies:
        copy.wait()


def exchange(blocks, groups, members, ident):
    count = groups * members - 1
    return pl.pallas_call(
        functools.partial(exchange_kernel, groups, members),
        out_shape=jax.ShapeDtypeStruct(blocks.shape, blocks.dtype),
        in_specs=[pl.BlockSpec(memory_space=pl.ANY)],
        out_specs=pl.BlockSpec(memory_space=pl.ANY),
        scratch_shapes=[
            pltpu.SemaphoreType.DMA((count,)), pltpu.SemaphoreType.DMA((count,)), pltpu.SemaphoreType.DMA
        ],
        compiler_params=pltpu.CompilerParams(collective_id=ident, has_side_effects=True),
        name="exchange",
    )(blocks)


def tok_exchange(rows, members, ident):
    shaped = rows.reshape(members, rows.shape[0] // members, rows.shape[1])
    return exchange(shaped, 1, members, ident).reshape(rows.shape)


def fast_device(
    tokens,
    adapter_index,
    norm_gain,
    norm_shift,
    spatial_weights,
    spatial_output,
    temporal_weights,
    temporal_output,
    expand_weight,
    reduce_weight,
    attention_down,
    attention_up,
    expand_down,
    expand_up,
    reduce_down,
    reduce_up,
    cotangent,
):
    frames, clips, places, width = tokens.shape[1:]
    members, groups = lax.axis_size("tok"), lax.axis_size("clip")
    blocks = members // clips
    part = places // blocks
    chunk = -(-frames * part // 8) * 8
    padded = -(-places // 16) * 16
    half, total = frames * padded, clips * frames * padded
    rows_all = FRAMES * part
    ff = expand_weight.shape[1]
    sizes = (frames, clips, places, width, padded)
    to_send, from_sent, to_place, to_frame = order_tables(frames, places, padded, blocks, part, chunk)
    position = lax.axis_index("tok")
    own_choice = lax.dynamic_slice_in_dim(adapter_index, position // blocks, 1)
    choices = jnp.concatenate([own_choice, adapter_index])

    adapt = jnp.concatenate([attention_down, jnp.swapaxes(attention_up, 1, 2)], axis=0)
    shards = [
        jnp.concatenate([spatial_weights, spatial_output[None]]),
        jnp.concatenate([adapt[0:4], adapt[8:12]]),
        jnp.concatenate([temporal_weights, temporal_output[None]]),
        jnp.concatenate([adapt[4:8], adapt[12:16]]),
        expand_weight,
        reduce_weight,
        jnp.stack([expand_up.T, reduce_down]),
        jnp.stack([expand_down, reduce_up.T]),
    ]
    dims = (1, 1, 1, 1, 0, 0, 1, 1)
    sp_w, sp_adapt, tp_w, tp_adapt, we, wr, wide, narrow = gather(shards, dims, members * groups, 0)

    (cot_sent,) = run(
        functools.partial(pack, sizes), "cot_pack", (to_send, cotangent[0]),
        [shape_of(total, width)], [shape_of(total, width)], scalars=0,
    )
    cot = lax.all_to_all(
        cot_sent.reshape(members, chunk, width), "tok", split_axis=0, concat_axis=0, tiled=True
    ).reshape(total, width)
    sent, qkv, soft, mixed, hid, zs = run(
        functools.partial(spatial_forward, sizes),
        "spatial_forward",
        (adapter_index, to_send, tokens[0], norm_gain, norm_shift, sp_w, sp_adapt),
        [
            shape_of(total, width),
            shape_of(3, total, width),
            shape_of(frames * clips * HEADS, padded, padded),
            shape_of(total, width),
            shape_of(4, total, ADAPT),
            shape_of(total, width),
        ],
        [shape_of(total, width)],
    )
    got = tok_exchange(sent, members, 1)
    group = rows_all // 7
    out_sent, grad_sent, mid_pay = run(
        functools.partial(middle, (rows_all, width, group, 512, members * groups)),
        "middle",
        (choices, to_place, to_frame, got, cot, norm_gain, norm_shift, tp_w, tp_adapt, we, wr, wide, narrow),
        [shape_of(total, width), shape_of(total, width), shape_of(width, 384)],
        [
            shape_of(rows_all, width),
            shape_of(rows_all, width, kind=F32),
            shape_of(rows_all, width),
            shape_of(rows_all, width),
            shape_of(3, rows_all, width),
            shape_of(rows_all // group * HEADS, group, group),
            shape_of(rows_all, width),
            shape_of(5, rows_all, ADAPT),
            shape_of(rows_all, ADAPT),
            shape_of(rows_all, width),
            shape_of(rows_all, width, kind=F32),
            shape_of(rows_all, width, kind=F32),
            shape_of(2, rows_all, ADAPT, kind=F32),
            shape_of(rows_all, width),
            shape_of(3, rows_all, width),
            shape_of(5, ADAPT, width, kind=F32),
            shape_of(5, ADAPT, width, kind=F32),
            shape_of(2, ADAPT, ff, kind=F32),
        ],
    )
    made = tok_exchange(out_sent, members, 2)
    back = tok_exchange(grad_sent, members, 3)
    dx, out, sp_pay = run(
        functools.partial(spatial_backward, sizes),
        "spatial_backward",
        (adapter_index, from_sent, tokens[0], norm_gain, sp_w, sp_adapt, qkv, soft, mixed, hid, zs, back, made),
        [
            shape_of(frames, clips, places, width, kind=F32),
            shape_of(frames, clips, places, width, kind=F32),
            shape_of(width, 256),
        ],
        [
            shape_of(total, width),
            shape_of(total, width),
            shape_of(3, total, width),
            shape_of(half, width, kind=F32),
            shape_of(4, ADAPT, width, kind=F32),
            shape_of(4, ADAPT, width, kind=F32),
        ],
    )
    pay = jnp.concatenate([mid_pay, sp_pay], axis=1).reshape(members * groups, -1, 640)
    terms = exchange(pay, groups, members, 4)
    step = width // (members * groups)
    fold = ff // width
    down, up, gea, geb, gra, grb = run(
        functools.partial(combine, (groups, members, step, fold)),
        "combine",
        (terms,),
        [
            shape_of(8, step, ADAPT, kind=F32),
            shape_of(8, step, ADAPT, kind=F32),
            shape_of(step, ADAPT, kind=F32),
            shape_of(fold * step, ADAPT, kind=F32),
            shape_of(fold * step, ADAPT, kind=F32),
            shape_of(step, ADAPT, kind=F32),
        ],
        [],
        scalars=0,
    )
    return (out[None], dx[None], down, jnp.swapaxes(up, 1, 2), gea, geb.T, gra, grb.T)


def solution(mesh):
    pick = fast_device if fits(mesh) else general_device

    placed = (
        P(("clip", "tok"), None, None, None, None),
        P("clip"),
        P(),
        P(),
        P(None, ("clip", "tok"), None),
        P(("clip", "tok"), None),
        P(None, ("clip", "tok"), None),
        P(("clip", "tok"), None),
        P(("clip", "tok"), None),
        P(("clip", "tok"), None),
        P(None, ("clip", "tok"), None),
        P(None, None, ("clip", "tok")),
        P(("clip", "tok"), None),
        P(None, ("clip", "tok")),
        P(("clip", "tok"), None),
        P(None, ("clip", "tok")),
        P(("clip", "tok"), None, None, None, None),
    )
    return jax.shard_map(
        pick,
        mesh=mesh,
        in_specs=placed,
        out_specs=(
            P(("clip", "tok"), None, None, None, None),
            P(("clip", "tok"), None, None, None, None),
            P(None, ("clip", "tok"), None),
            P(None, None, ("clip", "tok")),
            P(("clip", "tok"), None),
            P(None, ("clip", "tok")),
            P(("clip", "tok"), None),
            P(None, ("clip", "tok")),
        ),
        check_vma=False,
    )
```

```python
import functools

import jax
import jax.numpy as jnp
from jax import lax
from jax.experimental import pallas as pl
from jax.experimental.pallas import tpu as pltpu
from jax.sharding import PartitionSpec as P

HEADS = 12
HEAD_DIM = 64
FRAMES = 16
ADAPTERS = 8
RANK = 16


EPSILON = 1e-06


def layer_norm(stream, gain_row, shift_row):
    average = jnp.mean(stream, axis=-1, keepdims=True)
    centred = stream - average
    variance = jnp.mean(centred * centred, axis=-1, keepdims=True)
    return centred * lax.rsqrt(variance + EPSILON) * gain_row + shift_row


def adapter_mask(choice_rows):
    columns = jnp.arange(ADAPTERS * RANK, dtype=jnp.int32) // RANK
    return (columns[None, :] == choice_rows[:, None]).astype(jnp.float32)


def project_many(inputs, weight, down_rows, up_rows, mask):
    hidden = jnp.einsum("rd,ndc->nrc", inputs, down_rows, preferred_element_type=jnp.float32)
    hidden = (hidden * mask).astype(jnp.bfloat16)
    result = jnp.einsum("rd,nde->nre", inputs, weight, preferred_element_type=jnp.float32)
    result = result + jnp.einsum(
        "nrc,nce->nre", hidden, up_rows, preferred_element_type=jnp.float32
    )
    return (result, hidden)


def project_back(inputs, hidden, grad_rows, weight, down_rows, up_rows, mask):
    hidden_grad = jnp.einsum("nre,nce->nrc", grad_rows, up_rows, preferred_element_type=jnp.float32)
    hidden_grad = (hidden_grad * mask).astype(jnp.bfloat16)
    input_grad = jnp.einsum("nre,nde->rd", grad_rows, weight, preferred_element_type=jnp.float32)
    input_grad = input_grad + jnp.einsum(
        "nrc,ndc->rd", hidden_grad, down_rows, preferred_element_type=jnp.float32
    )
    down_grad = jnp.einsum("rd,nrc->ndc", inputs, hidden_grad, preferred_element_type=jnp.float32)
    up_grad = jnp.einsum("nrc,nre->nce", hidden, grad_rows, preferred_element_type=jnp.float32)
    return (input_grad, down_grad, up_grad)


def attend_forward(packed, layout):
    view_shape, score_eq, mix_eq, back_eq = layout
    queries = packed[0].reshape(view_shape)
    key_rows = packed[1].reshape(view_shape)
    values = packed[2].reshape(view_shape)
    scores = jnp.einsum(
        score_eq, queries, key_rows, preferred_element_type=jnp.float32
    ) * HEAD_DIM ** (-0.5)
    ceiling = jnp.max(scores, axis=-1, keepdims=True)
    expo_rows = jnp.exp(scores - ceiling)
    totals = jnp.sum(expo_rows, axis=-1, keepdims=True)
    weights_soft = (expo_rows / totals).astype(jnp.bfloat16)
    mixed_rows = jnp.einsum(mix_eq, weights_soft, values, preferred_element_type=jnp.float32)
    return (mixed_rows.reshape(packed.shape[1:]), ceiling + jnp.log(totals))


def attend_backward(packed, log_total, mixed_grad, layout):
    view_shape, score_eq, mix_eq, back_eq = layout
    scaling = HEAD_DIM ** (-0.5)
    queries = packed[0].reshape(view_shape)
    key_rows = packed[1].reshape(view_shape)
    values = packed[2].reshape(view_shape)
    scores = jnp.einsum(score_eq, queries, key_rows, preferred_element_type=jnp.float32) * scaling
    weights_soft = jnp.exp(scores - log_total)
    output_grad = mixed_grad.reshape(view_shape)
    soft_grad = jnp.einsum(score_eq, output_grad, values, preferred_element_type=jnp.float32)
    row_inner = jnp.sum(weights_soft * soft_grad, axis=-1, keepdims=True)
    score_grad = (weights_soft * (soft_grad - row_inner)).astype(jnp.bfloat16)
    query_grad = (
        jnp.einsum(mix_eq, score_grad, key_rows, preferred_element_type=jnp.float32) * scaling
    )
    key_grad = (
        jnp.einsum(back_eq, score_grad, queries, preferred_element_type=jnp.float32) * scaling
    )
    value_grad = jnp.einsum(
        back_eq, weights_soft.astype(jnp.bfloat16), output_grad, preferred_element_type=jnp.float32
    )
    stacked = jnp.stack([query_grad, key_grad, value_grad])
    return stacked.reshape(packed.shape).astype(jnp.bfloat16)


def attention_forward(stream, gain_row, shift_row, weight_set, mask, layout):
    inner_weights, outer_weight, down_rows, up_rows = weight_set
    normed = layer_norm(stream, gain_row, shift_row).astype(jnp.bfloat16)
    packed, packed_hidden = project_many(normed, inner_weights, down_rows[0:3], up_rows[0:3], mask)
    packed = packed.astype(jnp.bfloat16)
    mixed_rows, log_total = attend_forward(packed, layout)
    mixed_rows = mixed_rows.astype(jnp.bfloat16)
    branch, outer_hidden = project_many(
        mixed_rows, outer_weight[None], down_rows[3:4], up_rows[3:4], mask
    )
    return (
        stream + branch[0],
        (normed, packed, packed_hidden, mixed_rows, outer_hidden, log_total),
    )


def attention_backward(
    stream, stream_grad, gain_row, shift_row, weight_set, mask, layout, kept_values
):
    inner_weights, outer_weight, down_rows, up_rows = weight_set
    normed, packed, packed_hidden, mixed_rows, outer_hidden, log_total = kept_values
    branch_grad = stream_grad.astype(jnp.bfloat16)[None]
    mixed_grad, outer_down, outer_up = project_back(
        mixed_rows,
        outer_hidden,
        branch_grad,
        outer_weight[None],
        down_rows[3:4],
        up_rows[3:4],
        mask,
    )
    packed_grad = attend_backward(packed, log_total, mixed_grad.astype(jnp.bfloat16), layout)
    normed_grad, inner_down, inner_up = project_back(
        normed, packed_hidden, packed_grad, inner_weights, down_rows[0:3], up_rows[0:3], mask
    )
    unused, norm_pull = jax.vjp(lambda rows_in: layer_norm(rows_in, gain_row, shift_row), stream)
    before_grad = stream_grad + norm_pull(normed_grad)[0]
    return (
        before_grad,
        jnp.concatenate([inner_down, outer_down], axis=0),
        jnp.concatenate([inner_up, outer_up], axis=0),
    )


def expand_forward(stream, gain_row, shift_row, weight_set, mask):
    up_weight, down_weight, in_down, in_up, out_down, out_up = weight_set
    normed = layer_norm(stream, gain_row, shift_row).astype(jnp.bfloat16)
    inner_rows, inner_hidden = project_many(
        normed, up_weight[None], in_down[None], in_up[None], mask
    )
    inner_rows = inner_rows[0]
    active = jax.nn.gelu(inner_rows, approximate=True).astype(jnp.bfloat16)
    branch, outer_hidden = project_many(
        active, down_weight[None], out_down[None], out_up[None], mask
    )
    return (stream + branch[0], (normed, inner_rows, inner_hidden, active, outer_hidden))


def expand_backward(stream, stream_grad, gain_row, shift_row, weight_set, mask, kept_values):
    up_weight, down_weight, in_down, in_up, out_down, out_up = weight_set
    normed, inner_rows, inner_hidden, active, outer_hidden = kept_values
    branch_grad = stream_grad.astype(jnp.bfloat16)[None]
    active_grad, out_down_grad, out_up_grad = project_back(
        active, outer_hidden, branch_grad, down_weight[None], out_down[None], out_up[None], mask
    )
    unused, gelu_pull = jax.vjp(
        lambda values_in: jax.nn.gelu(values_in, approximate=True), inner_rows
    )
    inner_grad = gelu_pull(active_grad)[0].astype(jnp.bfloat16)[None]
    normed_grad, in_down_grad, in_up_grad = project_back(
        normed, inner_hidden, inner_grad, up_weight[None], in_down[None], in_up[None], mask
    )
    unused_norm, norm_pull = jax.vjp(
        lambda rows_in: layer_norm(rows_in, gain_row, shift_row), stream
    )
    before_grad = stream_grad + norm_pull(normed_grad)[0]
    return (before_grad, (in_down_grad[0], in_up_grad[0], out_down_grad[0], out_up_grad[0]))


def regroup_places(stream, layout_sizes, backward):
    frames_dev, clips_dev, places, model_width, clip_rows, place_blocks, place_part = layout_sizes
    padded = jnp.pad(
        stream.reshape(frames_dev, clips_dev, places, model_width),
        ((0, 0), (0, 0), (0, place_part * place_blocks - places), (0, 0)),
    )
    padded = padded.reshape(frames_dev, clips_dev * place_blocks, place_part, model_width)
    if backward:
        arrived = lax.all_to_all(
            padded.astype(jnp.bfloat16), "tok", split_axis=1, concat_axis=0, tiled=True
        ).astype(padded.dtype)
    else:
        arrived = lax.all_to_all(
            padded.astype(jnp.bfloat16), "tok", split_axis=1, concat_axis=0, tiled=True
        ).astype(padded.dtype)
    return arrived.reshape(clip_rows * FRAMES * place_part, model_width)


def regroup_frames(stream, layout_sizes, backward):
    frames_dev, clips_dev, places, model_width, clip_rows, place_blocks, place_part = layout_sizes
    shaped = stream.reshape(clip_rows * FRAMES, 1, place_part, model_width)
    if backward:
        arrived = lax.all_to_all(
            shaped.astype(jnp.bfloat16), "tok", split_axis=0, concat_axis=1, tiled=True
        ).astype(shaped.dtype)
    else:
        arrived = lax.all_to_all(
            shaped.astype(jnp.bfloat16), "tok", split_axis=0, concat_axis=1, tiled=True
        ).astype(shaped.dtype)
    arrived = arrived.reshape(frames_dev, clips_dev, place_part * place_blocks, model_width)
    return arrived[:, :, :places].reshape(frames_dev * clips_dev * places, model_width)


def general_device(
    tokens,
    adapter_index,
    norm_gain,
    norm_shift,
    spatial_weights,
    spatial_output,
    temporal_weights,
    temporal_output,
    expand_weight,
    reduce_weight,
    attention_down,
    attention_up,
    expand_down,
    expand_up,
    reduce_down,
    reduce_up,
    cotangent,
):
    frames_dev, clips_dev, places, model_width = tokens.shape[1:]
    tok_count = lax.axis_size("tok")
    frame_blocks = FRAMES // frames_dev
    clip_rows = tok_count // frame_blocks
    place_blocks = tok_count // clips_dev
    place_part = -(-places // place_blocks)
    layout_sizes = (frames_dev, clips_dev, places, model_width, clip_rows, place_blocks, place_part)
    adapt_cols = ADAPTERS * RANK
    position = lax.axis_index("tok")
    spatial_choice = lax.dynamic_slice_in_dim(
        adapter_index, position // frame_blocks * clips_dev, clips_dev
    )
    spatial_mask = jnp.broadcast_to(
        adapter_mask(spatial_choice)[None, :, None, :], (frames_dev, clips_dev, places, adapt_cols)
    ).reshape(-1, adapt_cols)
    temporal_choice = lax.dynamic_slice_in_dim(
        adapter_index.reshape(clip_rows, clips_dev), position // place_blocks, 1, 1
    )[:, 0]
    temporal_mask = jnp.broadcast_to(
        adapter_mask(temporal_choice)[:, None, None, :], (clip_rows, FRAMES, place_part, adapt_cols)
    ).reshape(-1, adapt_cols)
    spatial_layout = (
        (frames_dev * clips_dev, places, HEADS, HEAD_DIM),
        "gqhd,gkhd->ghqk",
        "ghqk,gkhd->gqhd",
        "ghqk,gqhd->gkhd",
    )
    temporal_layout = (
        (clip_rows, FRAMES, place_part, HEADS, HEAD_DIM),
        "aqphd,akphd->aphqk",
        "aphqk,akphd->aqphd",
        "aphqk,aqphd->akphd",
    )
    spatial_set = (
        lax.all_gather(spatial_weights, ("clip", "tok"), axis=1, tiled=True),
        lax.all_gather(spatial_output, ("clip", "tok"), axis=0, tiled=True),
        lax.all_gather(attention_down[0:4], ("clip", "tok"), axis=1, tiled=True),
        lax.all_gather(attention_up[0:4], ("clip", "tok"), axis=2, tiled=True),
    )
    stream0 = tokens.reshape(-1, model_width)
    stream1, spatial_kept = attention_forward(
        stream0, norm_gain[0], norm_shift[0], spatial_set, spatial_mask, spatial_layout
    )
    placed1 = regroup_places(stream1, layout_sizes, False)
    temporal_set = (
        lax.all_gather(temporal_weights, ("clip", "tok"), axis=1, tiled=True),
        lax.all_gather(temporal_output, ("clip", "tok"), axis=0, tiled=True),
        lax.all_gather(attention_down[4:8], ("clip", "tok"), axis=1, tiled=True),
        lax.all_gather(attention_up[4:8], ("clip", "tok"), axis=2, tiled=True),
    )
    placed2, temporal_kept = attention_forward(
        placed1, norm_gain[1], norm_shift[1], temporal_set, temporal_mask, temporal_layout
    )
    stream2 = regroup_frames(placed2, layout_sizes, False)
    expand_set = (
        lax.all_gather(expand_weight, ("clip", "tok"), axis=0, tiled=True),
        lax.all_gather(reduce_weight, ("clip", "tok"), axis=0, tiled=True),
        lax.all_gather(expand_down, ("clip", "tok"), axis=0, tiled=True),
        lax.all_gather(expand_up, ("clip", "tok"), axis=1, tiled=True),
        lax.all_gather(reduce_down, ("clip", "tok"), axis=0, tiled=True),
        lax.all_gather(reduce_up, ("clip", "tok"), axis=1, tiled=True),
    )
    stream3, expand_kept = expand_forward(
        stream2, norm_gain[2], norm_shift[2], expand_set, spatial_mask
    )
    expand_set = (
        lax.all_gather(expand_weight, ("clip", "tok"), axis=0, tiled=True),
        lax.all_gather(reduce_weight, ("clip", "tok"), axis=0, tiled=True),
        lax.all_gather(expand_down, ("clip", "tok"), axis=0, tiled=True),
        lax.all_gather(expand_up, ("clip", "tok"), axis=1, tiled=True),
        lax.all_gather(reduce_down, ("clip", "tok"), axis=0, tiled=True),
        lax.all_gather(reduce_up, ("clip", "tok"), axis=1, tiled=True),
    )
    grad2, expand_grads = expand_backward(
        stream2,
        cotangent.reshape(-1, model_width),
        norm_gain[2],
        norm_shift[2],
        expand_set,
        spatial_mask,
        expand_kept,
    )
    placed_grad2 = regroup_places(grad2, layout_sizes, True)
    temporal_set = (
        lax.all_gather(temporal_weights, ("clip", "tok"), axis=1, tiled=True),
        lax.all_gather(temporal_output, ("clip", "tok"), axis=0, tiled=True),
        lax.all_gather(attention_down[4:8], ("clip", "tok"), axis=1, tiled=True),
        lax.all_gather(attention_up[4:8], ("clip", "tok"), axis=2, tiled=True),
    )
    placed_grad1, temporal_down, temporal_up = attention_backward(
        placed1,
        placed_grad2,
        norm_gain[1],
        norm_shift[1],
        temporal_set,
        temporal_mask,
        temporal_layout,
        temporal_kept,
    )
    grad1 = regroup_frames(placed_grad1, layout_sizes, True)
    spatial_set = (
        lax.all_gather(spatial_weights, ("clip", "tok"), axis=1, tiled=True),
        lax.all_gather(spatial_output, ("clip", "tok"), axis=0, tiled=True),
        lax.all_gather(attention_down[0:4], ("clip", "tok"), axis=1, tiled=True),
        lax.all_gather(attention_up[0:4], ("clip", "tok"), axis=2, tiled=True),
    )
    grad0, spatial_down, spatial_up = attention_backward(
        stream0,
        grad1,
        norm_gain[0],
        norm_shift[0],
        spatial_set,
        spatial_mask,
        spatial_layout,
        spatial_kept,
    )
    owned = (
        lax.psum_scatter(
            jnp.concatenate([spatial_down, temporal_down], axis=0),
            ("clip", "tok"),
            scatter_dimension=1,
            tiled=True,
        ),
        lax.psum_scatter(
            jnp.concatenate([spatial_up, temporal_up], axis=0),
            ("clip", "tok"),
            scatter_dimension=2,
            tiled=True,
        ),
        lax.psum_scatter(expand_grads[0], ("clip", "tok"), scatter_dimension=0, tiled=True),
        lax.psum_scatter(expand_grads[1], ("clip", "tok"), scatter_dimension=1, tiled=True),
        lax.psum_scatter(expand_grads[2], ("clip", "tok"), scatter_dimension=0, tiled=True),
        lax.psum_scatter(expand_grads[3], ("clip", "tok"), scatter_dimension=1, tiled=True),
    )
    return (
        stream3.reshape(tokens.shape),
        grad0.reshape(tokens.shape),
        owned[0],
        owned[1],
        owned[2],
        owned[3],
        owned[4],
        owned[5],
    )


F32 = jnp.float32
BF16 = jnp.bfloat16
ADAPT = ADAPTERS * RANK
SPATIAL_UNROLL = 6
SPATIAL_BACK_UNROLL = 6
MIDDLE_UNROLL = 6
MIDDLE_BACK_UNROLL = 6


def nn(left, right):
    return lax.dot_general(left, right, (((1,), (0,)), ((), ())), preferred_element_type=F32)


def nt(left, right):
    return lax.dot_general(left, right, (((1,), (1,)), ((), ())), preferred_element_type=F32)


def tn(left, right):
    return lax.dot_general(left, right, (((0,), (0,)), ((), ())), preferred_element_type=F32)


def one_hot(target_row, rows):
    row_ids = lax.broadcasted_iota(jnp.int32, (rows, target_row.shape[1]), 0)
    return (row_ids == target_row).astype(F32).astype(BF16)


def column_mask(choice):
    return (lax.broadcasted_iota(jnp.int32, (1, ADAPT), 1) // RANK == choice).astype(F32)


def set_rows(rows, choice):
    total = jnp.zeros((RANK, rows.shape[1]), F32)
    for k in range(ADAPTERS):
        total = jnp.where(choice == k, rows[k * RANK : (k + 1) * RANK], total)
    return total


def norm_rows(rows, gain_row, shift_row):
    average = jnp.mean(rows, axis=-1, keepdims=True)
    centred = rows - average
    variance = jnp.mean(centred * centred, axis=-1, keepdims=True)
    return centred * lax.rsqrt(variance + EPSILON) * gain_row + shift_row


def norm_back(rows, pulled, gain_row):
    average = jnp.mean(rows, axis=-1, keepdims=True)
    centred = rows - average
    variance = jnp.mean(centred * centred, axis=-1, keepdims=True)
    scale = lax.rsqrt(variance + EPSILON)
    unit = centred * scale
    scaled = pulled * gain_row
    return scale * (
        scaled
        - jnp.mean(scaled, axis=-1, keepdims=True)
        - unit * jnp.mean(scaled * unit, axis=-1, keepdims=True)
    )


def soften(scores, keep):
    scores = jnp.where(keep, scores, -1e30)
    ceiling = jnp.max(scores, axis=-1, keepdims=True)
    expo = jnp.exp(scores - ceiling)
    return expo * (1.0 / jnp.sum(expo, axis=-1, keepdims=True))


def two_heads(rows, low):
    zero = jnp.zeros_like(rows)
    return jnp.concatenate([jnp.where(low, rows, zero), jnp.where(low, zero, rows)], axis=0)


def one_pair(both, low):
    count = both.shape[0] // 2
    return jnp.where(low, both[:count], both[count:])


def attention_pair(query, key, value, keep, low):
    weights = soften(nt(two_heads(query, low), key), keep).astype(BF16)
    return weights, one_pair(nn(weights, value), low).astype(BF16)


def attention_all(sizes, first, qkv, soft, mixed, keep, low, unroll):
    start, blocks, rows_each, pairs = sizes

    @pl.loop(0, blocks * pairs // unroll)
    def _(turn):
        block = turn // (pairs // unroll)
        lead = (turn - block * (pairs // unroll)) * unroll
        rows = pl.ds(pl.multiple_of(start + block * rows_each, 16), rows_each)
        for u in range(unroll):
            lanes = pl.ds(pl.multiple_of((lead + u) * 128, 128), 128)
            weights, made = attention_pair(
                qkv[0, rows, lanes], qkv[1, rows, lanes], qkv[2, rows, lanes], keep, low
            )
            soft[(first + block) * pairs + lead + u] = weights
            mixed[rows, lanes] = made


def attention_all_back(sizes, qkv, soft, gmix, gqkv, low, unroll):
    blocks, rows_each, pairs = sizes

    @pl.loop(0, blocks * pairs // unroll)
    def _(turn):
        block = turn // (pairs // unroll)
        lead = (turn - block * (pairs // unroll)) * unroll
        rows = pl.ds(pl.multiple_of(block * rows_each, 16), rows_each)
        for u in range(unroll):
            lanes = pl.ds(pl.multiple_of((lead + u) * 128, 128), 128)
            made = attention_back(
                qkv[0, rows, lanes], qkv[1, rows, lanes], qkv[2, rows, lanes],
                soft[block * pairs + lead + u], gmix[rows, lanes], low,
            )
            for n in range(3):
                gqkv[n, rows, lanes] = made[n].astype(BF16)


def block_rows(ref, slots, number):
    chunk = slots.shape[1]
    return ref.at[pl.ds(pl.multiple_of(number * chunk, 8), chunk)]


def send_blocks(slots, got, count, first, send_sems, recv_sems, local_sem):
    clip, tok = lax.axis_index("clip"), lax.axis_index("tok")
    target = block_rows(got, slots, tok)
    for n in range(count):
        place = first + lax.rem(tok + n, count)

        @pl.when(place != tok)
        def _():
            remote(slots.at[place], target, send_sems.at[place], recv_sems.at[tok], (clip, place)).start()

        @pl.when(place == tok)
        def _():
            pltpu.make_async_copy(slots.at[place], target, local_sem).start()


def wait_blocks(slots, got, members, send_sems, recv_sems, local_sem):
    tok = lax.axis_index("tok")
    for d in range(1, members):
        place = lax.rem(tok + d, members)
        target = block_rows(got, slots, place)
        pltpu.make_async_copy(slots.at[place], slots.at[place], send_sems.at[place]).wait()
        pltpu.make_async_copy(target, target, recv_sems.at[place]).wait()
    pltpu.make_async_copy(slots.at[tok], block_rows(got, slots, tok), local_sem).wait()


def spatial_kernel(
    sizes, members, idx, to_send, x_hbm, cot_hbm, gain, shift, sh_w, sh_o, sh_tw, sh_to, sh_down, sh_up, sh_we,
    all_w, all_ad, all_tw, all_tad, all_we, got, cots_hbm, qkv_hbm, soft_hbm, mixed_hbm, hid_hbm, zs_hbm,
    x, cot, w, ad, slots, cots, stream, qkv, soft, mixed, hid, zs, sems, copy_sems, send_sems, recv_sems
):
    frames, clips, places, width, padded = sizes
    half = frames * padded
    share = members // clips
    chunk = slots.shape[1]
    clip, tok = lax.axis_index("clip"), lax.axis_index("tok")

    def row_loads(source, target, first):
        return [
            pltpu.make_async_copy(source.at[i, :, b, :], target.at[i, b], copy_sems.at[first + i * clips + b])
            for i in range(frames) for b in range(clips)
        ]

    parts = [
        Part([(sh_w.at[0:2], None)], all_w.at[0:2], 1, sems.at[0]),
        Part([(sh_w.at[2], 0), (sh_o, 1)], all_w.at[2:4], 1, sems.at[1]),
        Part([(sh_down.at[0:4], slice(0, 4)), (sh_up.at[0:4], slice(4, 8))], all_ad, 1, sems.at[2]),
        Part([(sh_tw, slice(0, 3)), (sh_to, 3)], all_tw, 1, sems.at[3]),
        Part([(sh_down.at[4:8], slice(0, 4)), (sh_up.at[4:8], slice(4, 8))], all_tad, 1, sems.at[4]),
        Part([(sh_we, None)], all_we, 0, sems.at[5]),
    ]
    load_cot, load_x = row_loads(cot_hbm, cot, 8), row_loads(x_hbm, x, 4)
    for load in load_cot + load_x:
        load.start()
    y, core, z, across = place_of()
    greet(tok_peers(members) + [device_at(1 - y, core, z, across), device_at(y, 1 - core, z, across)])

    def stages(plan):
        for step in range(0, len(plan), 2):
            parts["ABCDEF".index(plan[step])].stage(int(plan[step + 1]))

    stages("A0B0C0")
    pads = slice(padded - 16, padded)
    for i in range(frames):
        stream[i * padded + padded - 16 : (i + 1) * padded] = jnp.zeros((16, width), BF16)
    for load in load_cot:
        load.wait()
    for b in range(clips):
        for i in range(frames):
            stream[i * padded : i * padded + places] = cot[i, b].astype(BF16)
        rows = nn(one_hot(to_send[...], half), stream[...])
        cots[b * share : (b + 1) * share] = rows.reshape(share, chunk, width).astype(BF16)
    stages("A1B1A2C1B2A3")
    for load in load_x:
        load.wait()
    for b in range(clips):
        for i in range(frames):
            base = b * half + i * padded
            zs[base + padded - 16 : base + padded] = jnp.zeros((16, width), BF16)
            zs[base : base + places] = norm_rows(
                x[i, b], gain[0:1], shift[0:1]
            ).astype(BF16)
    stages("C2B3C3D0E0A4B4C4")
    stages("D1E1A5B5C5A6B6C6")
    loads = [pltpu.make_async_copy(all_w, w, copy_sems.at[2]), pltpu.make_async_copy(all_ad, ad, copy_sems.at[3])]
    for load in loads:
        load.start()
    stages("D2E2F0")
    for load in loads:
        load.wait()

    keep = lax.broadcasted_iota(jnp.int32, (2 * padded, padded), 1) < places
    pairs = width // 128
    low = lax.broadcasted_iota(jnp.int32, (padded, 128), 1) < HEAD_DIM
    far = jnp.where(tok < share, 1, 0)
    for turn in range(clips):
        b = far if turn == 0 else 1 - far
        rows = pl.ds(pl.multiple_of(b * half, 16), half)
        mask = column_mask(idx[b])

        @pl.loop(0, 3)
        def _(n):
            hidden = (nn(zs[rows], ad[n]) * mask).astype(BF16)
            hid[n, rows] = hidden
            result = nn(zs[rows], w[n]) + nt(hidden, ad[4 + n])
            result = result * jnp.where(n == 0, HEAD_DIM**-0.5, 1.0)
            qkv[n, rows] = result.astype(BF16)

        stages("D3E3F1" if turn == 0 else "D5E5F4")

        attention_all(
            (b * half, frames, padded, pairs), b * frames, qkv, soft, mixed, keep, low, SPATIAL_UNROLL
        )
        if turn == 0:
            stages("D4E4F2")
        hidden = (nn(mixed[rows], ad[3]) * mask).astype(BF16)
        hid[3, rows] = hidden
        branch = nn(mixed[rows], w[3]) + nt(hidden, ad[7])
        for i in range(frames):
            stream[i * padded : i * padded + places] = (
                x[i, b] + branch[i * padded : i * padded + places]
            ).astype(BF16)
        made = nn(one_hot(to_send[...], half), stream[...]).reshape(share, chunk, width)
        slots[pl.ds(b * share, share)] = made.astype(BF16)
        send_blocks(slots, got, share, b * share, send_sems, recv_sems, copy_sems.at[0])
        if turn == 0:
            stages("F3")
    stores = [
        pltpu.make_async_copy(source, target, copy_sems.at[12 + n])
        for n, (source, target) in enumerate(
            ((qkv, qkv_hbm), (soft, soft_hbm), (mixed, mixed_hbm), (hid, hid_hbm), (zs, zs_hbm), (cots, cots_hbm))
        )
    ]
    for store in stores:
        store.start()
    stages("F5D6E6F6")
    wait_blocks(slots, got, members, send_sems, recv_sems, copy_sems.at[0])
    for store in stores:
        store.wait()


def attention_back(query, key, value, weights, grads, low):
    stacked = two_heads(grads, low)
    pulled = nt(stacked, value)
    wide = weights.astype(F32)
    inner = jnp.sum(wide * pulled, axis=-1, keepdims=True)
    score = (wide * (pulled - inner)).astype(BF16)
    query_grad = one_pair(nn(score, key), low) * HEAD_DIM**-0.5
    return query_grad, tn(score, two_heads(query, low)), tn(weights, stacked)


def spatial_backward(
    sizes, groups, members, step, idx, from_sent, gain, x_hbm, w_hbm, ad_hbm, qkv_hbm, soft_hbm, mixed_hbm, hid_hbm, zs_hbm,
    got_hbm, made_hbm, mid_pay,
    dx_hbm, out_hbm, down_out, up_out, ea, eb, ra, rb,
    w, ad, qkv, soft, mixed, hid, zs, got, made, x, out, mid, sp, pay, grad, gmix, gqkv, gpull, gdown, gup, copy_sems, send_sems, recv_sems
):
    frames, clips, places, width, padded = sizes
    half = frames * padded
    devices = groups * members

    def row_copies(view, rows, first, inward):
        copies = []
        for i in range(frames):
            for b in range(clips):
                ends = (view.at[i, :, b, :], rows.at[i, b])
                ends = ends if inward else ends[::-1]
                copies.append(pltpu.make_async_copy(*ends, copy_sems.at[first + i * clips + b]))
        return copies

    fills = [
        pltpu.make_async_copy(source, target, copy_sems.at[10 + n])
        for n, (source, target) in enumerate(
            (
                (got_hbm, got), (w_hbm.at[3], w.at[3]), (ad_hbm, ad), (mixed_hbm, mixed), (hid_hbm, hid),
                (soft_hbm, soft), (qkv_hbm, qkv), (w_hbm.at[0:3], w.at[0:3]), (zs_hbm, zs), (made_hbm, made),
            )
        )
    ]
    loads = row_copies(x_hbm, x, 0, True)
    for load in fills + loads:
        load.start()
    clip, tok = lax.axis_index("clip"), lax.axis_index("tok")
    me = clip * members + tok
    peers = all_peers(groups, members)
    greet(peers)

    def terms(source, target, kind):
        for n, peer in enumerate(peers):
            place = peer[0] * members + peer[1]
            remote(
                source.at[place], target.at[me], send_sems.at[kind, n], recv_sems.at[kind, n], peer
            ).start()
        pltpu.make_async_copy(source.at[me], target.at[me], copy_sems.at[8 + kind]).start()

    def await_terms(source, target, kind):
        for n, peer in enumerate(peers):
            remote(source.at[me], target.at[me], send_sems.at[kind, n], recv_sems.at[kind, n], peer).wait()
        pltpu.make_async_copy(source.at[me], target.at[me], copy_sems.at[8 + kind]).wait()

    terms(mid_pay, mid, 0)
    for fill in fills[0:5]:
        fill.wait()
    for b in range(clips):
        rows = slice(b * half, (b + 1) * half)
        mask = column_mask(idx[b])
        back = one_hot(from_sent[...], half)
        grad[rows] = nn(back, got[rows]).astype(BF16)
        hidden_grad = (nn(grad[rows], ad[7]) * mask).astype(BF16)
        gmix[rows] = (nt(grad[rows], w[3]) + nt(hidden_grad, ad[3])).astype(BF16)
        down, up = tn(hidden_grad, mixed[rows]), tn(hid[3, rows], grad[rows])
        if b == 0:
            gdown[3], gup[3] = down, up
        else:
            gdown[3] += down
            gup[3] += up

    pairs = width // 128
    low = lax.broadcasted_iota(jnp.int32, (padded, 128), 1) < HEAD_DIM

    for fill in fills[5:7]:
        fill.wait()
    attention_all_back((frames * clips, padded, pairs), qkv, soft, gmix, gqkv, low, SPATIAL_BACK_UNROLL)
    for fill in fills[7:10]:
        fill.wait()
    for b in range(clips):
        rows = slice(b * half, (b + 1) * half)
        mask = column_mask(idx[b])
        gpull[b] = jnp.zeros(gpull.shape[1:], F32)

        @pl.loop(0, 3)
        def _(n):
            own = gqkv[n, rows]
            hidden_grad = (nn(own, ad[4 + n]) * mask).astype(BF16)
            gpull[b] += nt(own, w[n]) + nt(hidden_grad, ad[n])
            down, up = tn(hidden_grad, zs[rows]), tn(hid[n, rows], own)
            if b == 0:
                gdown[n], gup[n] = down, up
            else:
                gdown[n] += down
                gup[n] += up

    repeat = jnp.where(idx[0] == idx[1], 0.0, 1.0)
    pieces = []
    for n in range(4):
        for source in (gdown, gup):
            pieces.append(set_rows(source[n], idx[0]))
            pieces.append(set_rows(source[n], idx[1]) * repeat)
    packed = jnp.transpose(jnp.concatenate(pieces, axis=0))
    pay[...] = packed.reshape(pay.shape).astype(BF16)
    terms(pay, sp, 1)
    for load in loads:
        load.wait()
    for b in range(clips):
        rows = slice(b * half, (b + 1) * half)
        final = nn(one_hot(from_sent[...], half), made[rows])
        for i in range(frames):
            base = i * padded
            out[i, b] = final[base : base + places]
            pulled = norm_back(x[i, b], gpull[b, base : base + places], gain[0:1])
            x[i, b] = grad[b * half + base : b * half + base + places].astype(F32) + pulled
    stores = row_copies(out_hbm, out, 4, False) + row_copies(dx_hbm, x, 0, False)
    for store in stores:
        store.start()
    await_terms(mid_pay, mid, 0)
    mids, mid_choice = combine_mid((groups, members, step, eb.shape[0] // step), mid, down_out, up_out, ea, eb, ra, rb)
    await_terms(pay, sp, 1)
    combine_spatial((groups, members, step), sp, mids, down_out, up_out)
    for store in stores:
        store.wait()


def middle(
    sizes, members, idx, to_place, to_frame, gain, shift, got_hbm, cots, tw_hbm, tad_hbm, we_hbm,
    sh_wr, sh_eup, sh_rdown, sh_edown, sh_rup,
    all_wr, all_tall, all_flat, cot_got, made, back, pay,
    got, cot, w, ad, we, wr, tall, flat, slots, gslots,
    x1, x2, zt, ze, qkv, soft, mixed, hid, hide, gy, acc, pull, ghe, gmix, gqkv, gdown, gup, wide,
    sems, copy_sems, send_sems, recv_sems
):
    rows_all, width, group, chunk, owners = sizes
    choice = idx[lax.axis_index("tok") // (members // 2)]
    mask = column_mask(choice)
    groups = rows_all // group
    loads = [
        pltpu.make_async_copy(source, target, copy_sems.at[n])
        for n, (source, target) in enumerate(((got_hbm, got), (tw_hbm, w), (tad_hbm, ad), (we_hbm, we)))
    ]
    for load in loads:
        load.start()
    parts = [
        Part([(sh_wr, None)], all_wr, 0, sems.at[0]),
        Part([(sh_eup, 0), (sh_rdown, 1)], all_tall, 1, sems.at[1]),
        Part([(sh_edown, 0), (sh_rup, 1)], all_flat, 1, sems.at[2]),
    ]
    y, core, z, across = place_of()
    greet(tok_peers(members) + [device_at(1 - y, core, z, across), device_at(y, 1 - core, z, across)])

    def stages(number):
        for part in parts:
            part.stage(number)

    def exchange_sems(n):
        return send_sems.at[n], recv_sems.at[n], copy_sems.at[8 + n]

    stages(0)
    loads[0].wait()

    @pl.loop(0, groups)
    def _(j):
        rows = pl.ds(pl.multiple_of(j * group, 16), group)
        own = nn(one_hot_rows(to_place[...], group, j * group), got[...])
        x1[rows] = own.astype(BF16)
        zt[rows] = norm_rows(own, gain[1:2], shift[1:2]).astype(BF16)

    stages(1)
    loads[1].wait()
    loads[2].wait()

    @pl.loop(0, 3)
    def _(n):
        hidden = (nn(zt[...], ad[n]) * mask).astype(BF16)
        hid[n] = hidden
        result = nn(zt[...], w[n]) + nt(hidden, ad[4 + n])
        result = result * jnp.where(n == 0, HEAD_DIM**-0.5, 1.0)
        qkv[n] = result.astype(BF16)

    stages(2)
    stages(3)
    send_blocks(cots, cot_got, members, 0, *exchange_sems(2))

    pairs = width // 128
    keep = (
        lax.rem(lax.broadcasted_iota(jnp.int32, (2 * group, group), 0), group) // FRAMES
        == lax.broadcasted_iota(jnp.int32, (2 * group, group), 1) // FRAMES
    )
    low = lax.broadcasted_iota(jnp.int32, (group, 128), 1) < HEAD_DIM

    attention_all((0, groups, group, pairs), 0, qkv, soft, mixed, keep, low, MIDDLE_UNROLL)
    stages(4)
    hidden = (nn(mixed[...], ad[3]) * mask).astype(BF16)
    hid[3] = hidden
    acc[...] = nn(mixed[...], w[3]) + nt(hidden, ad[7])

    @pl.loop(0, groups)
    def _(j):
        rows = pl.ds(pl.multiple_of(j * group, 16), group)
        own = x1[rows].astype(F32) + acc[rows]
        x2[rows] = own
        acc[rows] = own
        pull[rows] = jnp.zeros((group, width), F32)
        ze[rows] = norm_rows(own, gain[2:3], shift[2:3]).astype(BF16)

    stages(5)
    stages(6)
    fills = [
        pltpu.make_async_copy(source, target, copy_sems.at[5 + n])
        for n, (source, target) in enumerate(((all_wr, wr), (all_tall, tall), (all_flat, flat)))
    ]
    for fill in fills:
        fill.start()
    wait_blocks(cots, cot_got, members, *exchange_sems(2))
    fill = pltpu.make_async_copy(cot_got, cot, copy_sems.at[4])
    fill.start()
    fill.wait()

    @pl.loop(0, groups)
    def _(j):
        rows = pl.ds(pl.multiple_of(j * group, 16), group)
        gy[rows] = nn(one_hot_rows(to_place[...], group, j * group), cot[...]).astype(BF16)

    for fill in fills:
        fill.wait()
    loads[3].wait()
    hide[...] = (nn(ze[...], flat[0]) * mask).astype(BF16)
    ghr = (nn(gy[...], flat[1]) * mask).astype(BF16)
    hid[0 + 4] = ghr
    ghe[...] = jnp.zeros(ghe.shape, F32)

    @pl.loop(0, we.shape[1] // chunk)
    def _(c):
        part = pl.ds(pl.multiple_of(c * chunk, chunk), chunk)
        inner = nn(ze[...], we[:, part]) + nt(hide[...], tall[0, part])
        cube = 0.7978845608028654 * (inner + 0.044715 * inner * inner * inner)
        bend = jnp.tanh(cube)
        act = (0.5 * inner * (1.0 + bend)).astype(BF16)
        slope = 0.5 * (1.0 + bend) + 0.5 * inner * (1.0 - bend * bend) * (
            0.7978845608028654 * (1.0 + 3.0 * 0.044715 * inner * inner)
        )
        acc[...] += nn(act, wr[part])
        ghe[0] += nn(act, tall[1, part])
        wide[0, :, part] = tn(hid[4], act)
        gact = nt(gy[...], wr[part]) + nt(hid[4], tall[1, part])
        ginner = (gact * slope).astype(BF16)
        pull[...] += nt(ginner, we[:, part])
        ghe[1] += nn(ginner, tall[0, part])
        wide[1, :, part] = tn(hide[...], ginner)

    hidr = (ghe[0] * mask).astype(BF16)
    acc[...] += nt(hidr, flat[1])
    rows = nn(one_hot(to_frame[...], got.shape[0]), acc[...].astype(BF16))
    slots[...] = rows.reshape(slots.shape).astype(BF16)
    send_blocks(slots, made, members, 0, *exchange_sems(0))
    gdown[4] = tn(hidr, gy[...])
    gheb = (ghe[1] * mask).astype(BF16)
    gup[4] = tn(gheb, ze[...])
    pull[...] += nt(gheb, flat[0])

    @pl.loop(0, groups)
    def _(j):
        rows = pl.ds(pl.multiple_of(j * group, 16), group)
        own = gy[rows].astype(F32) + norm_back(x2[rows], pull[rows], gain[2:3])
        acc[rows] = own
        ze[rows] = own.astype(BF16)

    grad = ze
    hidden_grad = (nn(grad[...], ad[7]) * mask).astype(BF16)
    gmix[...] = (nt(grad[...], w[3]) + nt(hidden_grad, ad[3])).astype(BF16)
    gdown[3] = tn(hidden_grad, mixed[...])
    gup[3] = tn(hid[3], grad[...])

    attention_all_back((groups, group, pairs), qkv, soft, gmix, gqkv, low, MIDDLE_BACK_UNROLL)
    pull[...] = jnp.zeros(pull.shape, F32)

    @pl.loop(0, 3)
    def _(n):
        own = gqkv[n]
        hidden_grad = (nn(own, ad[4 + n]) * mask).astype(BF16)
        pull[...] += nt(own, w[n]) + nt(hidden_grad, ad[n])
        gdown[n] = tn(hidden_grad, zt[...])
        gup[n] = tn(hid[n], own)

    @pl.loop(0, groups)
    def _(j):
        rows = pl.ds(pl.multiple_of(j * group, 16), group)
        own = acc[rows] + norm_back(x1[rows].astype(F32), pull[rows], gain[1:2])
        ze[rows] = own.astype(BF16)

    rows = nn(one_hot(to_frame[...], got.shape[0]), ze[...])
    gslots[...] = rows.reshape(gslots.shape).astype(BF16)
    send_blocks(gslots, back, members, 0, *exchange_sems(1))

    pieces = []
    for n in range(4):
        pieces += [set_rows(gdown[n], choice), set_rows(gup[n], choice)]
    pay[:, 0:128] = jnp.transpose(jnp.concatenate(pieces, axis=0)).astype(BF16)
    line = lax.broadcasted_iota(jnp.int32, (128 - 2 * RANK, width), 0)
    blank = jnp.zeros((128 - 2 * RANK, width), F32)
    for k, number in enumerate((choice, idx[0], idx[1])):
        blank = jnp.where(line == k, number.astype(F32), blank)
    pay[:, 128:256] = jnp.transpose(
        jnp.concatenate([set_rows(gup[4], choice), set_rows(gdown[4], choice), blank], axis=0)
    ).astype(BF16)
    high = jnp.concatenate(
        [set_rows(wide[1], choice), set_rows(wide[0], choice), jnp.zeros((128 - 2 * RANK, we.shape[1]), F32)], axis=0
    )
    high = jnp.transpose(high)
    step = width // owners
    fold = we.shape[1] // width
    high = high.reshape(owners, fold, step, 128)
    total = high[:, 0].reshape(width, 128)
    for f in range(1, fold):
        total += pltpu.roll(high[:, f].reshape(width, 128), 2 * RANK * f, 1)
    pay[:, 256:384] = total.astype(BF16)
    wait_blocks(slots, made, members, *exchange_sems(0))
    wait_blocks(gslots, back, members, *exchange_sems(1))


def one_hot_rows(target_row, rows, first):
    row_ids = lax.broadcasted_iota(jnp.int32, (rows, target_row.shape[1]), 0) + first
    return (row_ids == target_row).astype(F32).astype(BF16)


def spread_sum(stack, columns, first, choice, count):
    lanes = lax.broadcasted_iota(jnp.int32, (columns, ADAPT), 1)
    lines = lax.broadcasted_iota(jnp.int32, (columns, ADAPT), 0)
    spread = (lines == first + lanes % RANK).astype(F32)
    wide = lax.dot_general(
        stack, spread, (((1,), (0,)), ((), ())),
        preferred_element_type=F32, precision=lax.Precision.HIGHEST,
    )
    sets = lax.broadcasted_iota(jnp.int32, (1, ADAPT), 1) // RANK
    kept = jnp.where(sets.astype(F32) == choice, wide, 0.0)
    step = stack.shape[0] // count
    total = kept[0:step]
    for k in range(1, count):
        total += kept[k * step : (k + 1) * step]
    return total


def combine_mid(sizes, got, down, up, ea, eb, ra, rb):
    groups, members, step, fold = sizes
    clips = 2
    share = members // clips
    mids = []
    for g in range(groups):
        for b in range(clips):
            part = jnp.zeros((step, 384), F32)
            for t in range(share):
                part += got[g * members + b * share + t].astype(F32)
            mids.append(part)
    mid = jnp.concatenate(mids, axis=0)
    choice = mid[:, 160:161] * (1.0 / share)
    count = groups * clips
    for n in range(4):
        for s, target in enumerate((down, up)):
            target[4 + n] = spread_sum(mid[:, 0:128], 128, (2 * n + s) * RANK, choice, count)
    ea[...] = spread_sum(mid[:, 128:256], 128, 0, choice, count)
    rb[...] = spread_sum(mid[:, 128:256], 128, RANK, choice, count)
    for f in range(fold):
        rows = slice(f * step, (f + 1) * step)
        eb[rows] = spread_sum(mid[:, 256:384], 128, 2 * RANK * f, choice, count)
        ra[rows] = spread_sum(mid[:, 256:384], 128, 2 * RANK * f + RANK, choice, count)
    choices = [
        jnp.concatenate([mids[g * clips][:, 161 + b : 162 + b] * (1.0 / share) for g in range(groups)], axis=0)
        for b in range(clips)
    ]
    return choices, choice


def combine_spatial(sizes, got, choices, down, up):
    groups, members, step = sizes
    clips = len(choices)
    sums = []
    for g in range(groups):
        total = jnp.zeros((step, 256), F32)
        for t in range(members):
            total += got[g * members + t].astype(F32)
        sums.append(total)
    stack = jnp.concatenate(sums, axis=0)
    for n in range(4):
        for s, target in enumerate((down, up)):
            total = jnp.zeros((step, ADAPT), F32)
            for b in range(clips):
                total += spread_sum(stack, 256, ((2 * n + s) * clips + b) * RANK, choices[b], groups)
            target[n] = total


def shape_of(*dims, kind=BF16):
    return jax.ShapeDtypeStruct(dims, kind)


def order_tables(frames, places, padded, blocks, part, chunk):
    half_rows, sent_rows = frames * padded, blocks * chunk
    assert half_rows == sent_rows
    to_send = [-1] * half_rows
    from_sent = [-1] * sent_rows
    for i in range(frames):
        for p in range(places):
            source, target = i * padded + p, (p // part) * chunk + i * part + p % part
            to_send[source] = target
            from_sent[target] = source
    senders = FRAMES // frames
    to_place = [-1] * (senders * chunk)
    to_frame = [-1] * (part * FRAMES)
    for p in range(part):
        for f in range(FRAMES):
            source, target = (f // frames) * chunk + (f % frames) * part + p, p * FRAMES + f
            to_place[source] = target
            to_frame[target] = source
    return [jnp.array([table], jnp.int32) for table in (to_send, from_sent, to_place, to_frame)]


def fits(mesh):
    return mesh.shape["tok"] == 8 and mesh.shape["clip"] == 4


MESH = pl.DeviceIdType.MESH


def place_of():
    clip, tok = lax.axis_index("clip"), lax.axis_index("tok")
    return clip // 2, lax.rem(clip, 2), tok // 2, lax.rem(tok, 2)


def device_at(y, core, z, x):
    return (y * 2 + core, z * 2 + x)


def greet(peers):
    barrier = pltpu.get_barrier_semaphore()
    for peer in peers:
        pl.semaphore_signal(barrier, inc=1, device_id=peer, device_id_type=MESH)
    pl.semaphore_wait(barrier, len(peers))


def remote(source, target, send_sem, recv_sem, peer):
    return pltpu.make_async_remote_copy(
        src_ref=source, dst_ref=target, send_sem=send_sem, recv_sem=recv_sem, device_id=peer, device_id_type=MESH
    )


class Part:
    def __init__(self, pieces, whole, dim, sems):
        self.pieces, self.whole, self.dim, self.sems = pieces, whole, dim, sems
        self.rows = whole.shape[dim] // (lax.axis_size("clip") * lax.axis_size("tok"))
        self.me = place_of()
        for piece, target in self.own():
            pltpu.make_async_copy(piece, target, sems.at[1]).start()

    def own(self):
        target = self.slot(*self.me)
        return [(piece, target if index is None else target.at[index]) for piece, index in self.pieces]

    def span(self, first, count, half=None):
        rows = pl.ds(pl.multiple_of(first * self.rows, 8), count * self.rows)
        if self.dim == 1:
            lead = max(self.whole.shape[0] * 3 // 4, 1)
            front = (slice(None), slice(0, lead), slice(lead, None))[0 if half is None else half + 1]
            return self.whole.at[front, rows]
        lanes = self.whole.shape[1] * 3 // 512 * 128
        return self.whole.at[rows, (slice(None), slice(0, lanes), slice(lanes, None))[0 if half is None else half + 1]]

    def slot(self, y, core, z, x, half=None):
        clip, tok = device_at(y, core, z, x)
        return self.span(clip * 8 + tok, 1, half)

    def send(self, source, target, sem, peer):
        remote(source, target, self.sems.at[0], self.sems.at[sem], device_at(*peer)).start()

    def arrive(self, target, sem):
        pltpu.make_async_copy(target, target, self.sems.at[sem]).wait()

    def pass_on(self, far, sources=None):
        y, core, z, x = self.me
        owner = (y, core, far, x)
        target = self.slot(*owner)
        for source, target in sources or [(target, target)]:
            self.send(source, target, 8 + far, (y, core, z, 1 - x))
            self.send(source, target, 12 + far, (1 - y, core, z, x))
            self.send(source, target, 2 + y, (y, 1 - core, z, x))

    def to_core(self, owner):
        y, core, z, x = self.me
        target = self.slot(*owner)
        self.send(target, target, 2 + owner[0], (y, 1 - core, z, x))

    def hop(self, far, up, sources=None):
        y, core, z, x = self.me
        target = self.slot(y, core, far, x)
        for source, target in sources or [(target, target)]:
            self.send(source, target, 4 + far, (y, core, z + up, x))

    def relay(self, distance, up):
        y, core, z, x = self.me
        far = z - distance * up
        here = z >= distance if up > 0 else z <= 3 - distance
        on = z < 3 if up > 0 else z > 0

        @pl.when(here)
        def _():
            self.arrive(self.slot(y, core, far, x), 4 + far)

            @pl.when(on)
            def _():
                self.hop(far, up)

            self.pass_on(far)

    def stage(self, number):
        y, core, z, x = self.me
        if number == 0:
            own = self.own()

            @pl.when(z < 3)
            def _():
                self.hop(z, 1, own)

            @pl.when(z > 0)
            def _():
                self.hop(z, -1, own)

            self.pass_on(z, own)
        elif number <= 3:
            self.relay(number, 1)
            self.relay(number, -1)
        elif number == 4:
            for d in range(4):
                far = lax.rem(z + 4 - d, 4)
                owner = (y, core, far, 1 - x)
                self.arrive(self.slot(*owner), 8 + far)
                self.send(self.slot(*owner, 0), self.slot(*owner, 0), 16 + far, (1 - y, core, z, x))
                self.to_core(owner)
                owner = (1 - y, core, far, x)
                self.arrive(self.slot(*owner), 12 + far)
                self.send(self.slot(*owner, 1), self.slot(*owner, 1), 20 + far, (y, core, z, 1 - x))
                self.to_core(owner)
        elif number == 5:
            for d in range(4):
                far = lax.rem(z + 4 - d, 4)
                owner = (1 - y, core, far, 1 - x)
                self.arrive(self.slot(*owner, 0), 16 + far)
                self.arrive(self.slot(*owner, 1), 20 + far)
                self.to_core(owner)
        else:
            self.arrive(self.slot(*self.me), 1)
            for far in range(2):
                self.arrive(self.span((far * 2 + 1 - core) * 8, 8), 2 + far)
            self.arrive(self.span(0, 28), 0)
            hops = jnp.where(z == 0, 1, 0) + jnp.where(z == 3, 1, 0)

            @pl.when(hops > 0)
            def _():
                self.arrive(self.span(0, 1), 0)

            @pl.when(hops == 0)
            def _():
                self.arrive(self.span(0, 5), 0)


PART_SEMS = 24


def tok_peers(count):
    clip, tok = lax.axis_index("clip"), lax.axis_index("tok")
    return [(clip, lax.rem(tok + d, count)) for d in range(1, count)]


def all_peers(groups, members):
    clip, tok = lax.axis_index("clip"), lax.axis_index("tok")
    return [
        (lax.rem(clip + c, groups), lax.rem(tok + t, members))
        for c in range(groups) for t in range(members) if c or t
    ]


def fast_device(
    tokens,
    adapter_index,
    norm_gain,
    norm_shift,
    spatial_weights,
    spatial_output,
    temporal_weights,
    temporal_output,
    expand_weight,
    reduce_weight,
    attention_down,
    attention_up,
    expand_down,
    expand_up,
    reduce_down,
    reduce_up,
    cotangent,
):
    frames, clips, places, width = tokens.shape[1:]
    members, groups = lax.axis_size("tok"), lax.axis_size("clip")
    blocks = members // clips
    part = places // blocks
    chunk = -(-frames * part // 8) * 8
    padded = -(-places // 16) * 16
    half, total = frames * padded, clips * frames * padded
    rows_all = FRAMES * part
    ff = expand_weight.shape[1]
    sizes = (frames, clips, places, width, padded)
    to_send, from_sent, to_place, to_frame = order_tables(frames, places, padded, blocks, part, chunk)
    devices = members * groups

    def placed_rows(rows):
        return rows[0].transpose(0, 2, 1, 3)

    def whole(shard, dim):
        dims = list(shard.shape)
        dims[dim] *= devices
        return jax.ShapeDtypeStruct(tuple(dims), shard.dtype)

    any_spec, vmem_spec = pl.BlockSpec(memory_space=pl.ANY), pl.BlockSpec(memory_space=pltpu.VMEM)
    smem_spec = pl.BlockSpec(memory_space=pltpu.SMEM)
    x_view, cot_view = placed_rows(tokens), placed_rows(cotangent)
    up_rows = jnp.swapaxes(attention_up, 1, 2)
    saved = [
        shape_of(3, total, width),
        shape_of(frames * clips * HEADS // 2, 2 * padded, padded),
        shape_of(total, width),
        shape_of(4, total, ADAPT),
        shape_of(total, width),
    ]
    weights = [shape_of(4, width, width), shape_of(2 * 4, width, ADAPT)]
    scratch = [pltpu.VMEM(value.shape, value.dtype) for value in saved + weights]
    sp_w, sp_adapt, tp_w, tp_adapt, we, got, cots, *kept = pl.pallas_call(
        functools.partial(spatial_kernel, sizes, members),
        out_shape=[
            *weights, *weights, whole(expand_weight, 0), shape_of(total, width), shape_of(members, chunk, width), *saved
        ],
        in_specs=[smem_spec, vmem_spec, any_spec, any_spec, vmem_spec, vmem_spec] + [any_spec] * 7,
        out_specs=[any_spec] * 12,
        scratch_shapes=[
            pltpu.VMEM((frames, clips, places, width), F32),
            pltpu.VMEM((frames, clips, places, width), F32),
            *scratch[5:7],
            pltpu.VMEM((members, chunk, width), BF16),
            pltpu.VMEM((members, chunk, width), BF16),
            pltpu.VMEM((half, width), BF16),
            *scratch[0:5],
            pltpu.SemaphoreType.DMA((6, PART_SEMS)),
            pltpu.SemaphoreType.DMA((18,)),
            pltpu.SemaphoreType.DMA((members,)),
            pltpu.SemaphoreType.DMA((members,)),
        ],
        compiler_params=pltpu.CompilerParams(collective_id=0, has_side_effects=True, vmem_limit_bytes=63 << 20),
        name="spatial",
    )(
        adapter_index, to_send, x_view, cot_view, norm_gain, norm_shift, spatial_weights, spatial_output,
        temporal_weights, temporal_output, attention_down, up_rows, expand_weight,
    )
    group = rows_all // 7
    last = [reduce_weight, expand_up.T, reduce_down, expand_down, reduce_up.T]
    outs = pl.pallas_call(
        functools.partial(middle, (rows_all, width, group, 512, devices), members),
        out_shape=[
            whole(reduce_weight, 0), shape_of(2, ff, ADAPT), shape_of(2, width, ADAPT),
            shape_of(total, width), shape_of(total, width), shape_of(total, width),
            shape_of(width, 384),
        ],
        in_specs=[smem_spec] + [vmem_spec] * 4 + [any_spec] * 10,
        out_specs=[any_spec] * 6 + [vmem_spec],
        scratch_shapes=[
            pltpu.VMEM((total, width), BF16),
            pltpu.VMEM((total, width), BF16),
            pltpu.VMEM((4, width, width), BF16),
            pltpu.VMEM((8, width, ADAPT), BF16),
            pltpu.VMEM((width, ff), BF16),
            pltpu.VMEM((ff, width), BF16),
            pltpu.VMEM((2, ff, ADAPT), BF16),
            pltpu.VMEM((2, width, ADAPT), BF16),
            pltpu.VMEM((members, chunk, width), BF16),
            pltpu.VMEM((members, chunk, width), BF16),
            pltpu.VMEM((rows_all, width), BF16),
            pltpu.VMEM((rows_all, width), F32),
            pltpu.VMEM((rows_all, width), BF16),
            pltpu.VMEM((rows_all, width), BF16),
            pltpu.VMEM((3, rows_all, width), BF16),
            pltpu.VMEM((rows_all // group * HEADS // 2, 2 * group, group), BF16),
            pltpu.VMEM((rows_all, width), BF16),
            pltpu.VMEM((5, rows_all, ADAPT), BF16),
            pltpu.VMEM((rows_all, ADAPT), BF16),
            pltpu.VMEM((rows_all, width), BF16),
            pltpu.VMEM((rows_all, width), F32),
            pltpu.VMEM((rows_all, width), F32),
            pltpu.VMEM((2, rows_all, ADAPT), F32),
            pltpu.VMEM((rows_all, width), BF16),
            pltpu.VMEM((3, rows_all, width), BF16),
            pltpu.VMEM((5, ADAPT, width), F32),
            pltpu.VMEM((5, ADAPT, width), F32),
            pltpu.VMEM((2, ADAPT, ff), F32),
            pltpu.SemaphoreType.DMA((3, PART_SEMS)),
            pltpu.SemaphoreType.DMA((11,)),
            pltpu.SemaphoreType.DMA((3, members)),
            pltpu.SemaphoreType.DMA((3, members)),
        ],
        compiler_params=pltpu.CompilerParams(collective_id=1, has_side_effects=True, vmem_limit_bytes=63 << 20),
        name="middle",
    )(adapter_index, to_place, to_frame, norm_gain, norm_shift, got, cots, tp_w, tp_adapt, we, *last)
    made, back, mid_pay = outs[4:7]
    step = width // devices
    fold = ff // width
    dx, out, down, up, gea, geb, gra, grb = pl.pallas_call(
        functools.partial(spatial_backward, sizes, groups, members, step),
        out_shape=[
            shape_of(*x_view.shape, kind=F32),
            shape_of(*x_view.shape, kind=F32),
            shape_of(8, step, ADAPT, kind=F32),
            shape_of(8, step, ADAPT, kind=F32),
            shape_of(step, ADAPT, kind=F32),
            shape_of(fold * step, ADAPT, kind=F32),
            shape_of(fold * step, ADAPT, kind=F32),
            shape_of(step, ADAPT, kind=F32),
        ],
        in_specs=[smem_spec, vmem_spec, vmem_spec] + [any_spec] * 11,
        out_specs=[any_spec] * 2 + [vmem_spec] * 6,
        scratch_shapes=[
            *scratch[5:7],
            *scratch[0:5],
            pltpu.VMEM((total, width), BF16),
            pltpu.VMEM((total, width), BF16),
            pltpu.VMEM((frames, clips, places, width), F32),
            pltpu.VMEM((frames, clips, places, width), F32),
            pltpu.VMEM((devices, step, 384), BF16),
            pltpu.VMEM((devices, step, 256), BF16),
            pltpu.VMEM((devices, step, 256), BF16),
            pltpu.VMEM((total, width), BF16),
            pltpu.VMEM((total, width), BF16),
            pltpu.VMEM((3, total, width), BF16),
            pltpu.VMEM((clips, half, width), F32),
            pltpu.VMEM((4, ADAPT, width), F32),
            pltpu.VMEM((4, ADAPT, width), F32),
            pltpu.SemaphoreType.DMA((20,)),
            pltpu.SemaphoreType.DMA((2, devices - 1)),
            pltpu.SemaphoreType.DMA((2, devices - 1)),
        ],
        compiler_params=pltpu.CompilerParams(collective_id=2, has_side_effects=True, vmem_limit_bytes=63 << 20),
        name="spatial_back",
    )(
        adapter_index, from_sent, norm_gain, x_view, sp_w, sp_adapt, *kept, back, made,
        mid_pay.reshape(devices, step, 384),
    )

    def whole_rows(rows):
        return rows.transpose(0, 2, 1, 3)[None]

    return (whole_rows(out), whole_rows(dx), down, jnp.swapaxes(up, 1, 2), gea, geb.T, gra, grb.T)


def solution(mesh):
    pick = fast_device if fits(mesh) else general_device

    placed = (
        P(("clip", "tok"), None, None, None, None),
        P("clip"),
        P(),
        P(),
        P(None, ("clip", "tok"), None),
        P(("clip", "tok"), None),
        P(None, ("clip", "tok"), None),
        P(("clip", "tok"), None),
        P(("clip", "tok"), None),
        P(("clip", "tok"), None),
        P(None, ("clip", "tok"), None),
        P(None, None, ("clip", "tok")),
        P(("clip", "tok"), None),
        P(None, ("clip", "tok")),
        P(("clip", "tok"), None),
        P(None, ("clip", "tok")),
        P(("clip", "tok"), None, None, None, None),
    )
    return jax.shard_map(
        pick,
        mesh=mesh,
        in_specs=placed,
        out_specs=(
            P(("clip", "tok"), None, None, None, None),
            P(("clip", "tok"), None, None, None, None),
            P(None, ("clip", "tok"), None),
            P(None, None, ("clip", "tok")),
            P(("clip", "tok"), None),
            P(None, ("clip", "tok")),
            P(("clip", "tok"), None),
            P(None, ("clip", "tok")),
        ),
        check_vma=False,
    )
```

```python
import functools

import jax
import jax.numpy as jnp
from jax import lax
from jax.experimental import pallas as pl
from jax.experimental.pallas import tpu as pltpu
from jax.sharding import PartitionSpec as P

HEADS = 12
HEAD_DIM = 64
FRAMES = 16
ADAPTERS = 8
RANK = 16


EPSILON = 1e-06


def layer_norm(stream, gain_row, shift_row):
    average = jnp.mean(stream, axis=-1, keepdims=True)
    centred = stream - average
    variance = jnp.mean(centred * centred, axis=-1, keepdims=True)
    return centred * lax.rsqrt(variance + EPSILON) * gain_row + shift_row


def adapter_mask(choice_rows):
    columns = jnp.arange(ADAPTERS * RANK, dtype=jnp.int32) // RANK
    return (columns[None, :] == choice_rows[:, None]).astype(jnp.float32)


def project_many(inputs, weight, down_rows, up_rows, mask):
    hidden = jnp.einsum("rd,ndc->nrc", inputs, down_rows, preferred_element_type=jnp.float32)
    hidden = (hidden * mask).astype(jnp.bfloat16)
    result = jnp.einsum("rd,nde->nre", inputs, weight, preferred_element_type=jnp.float32)
    result = result + jnp.einsum(
        "nrc,nce->nre", hidden, up_rows, preferred_element_type=jnp.float32
    )
    return (result, hidden)


def project_back(inputs, hidden, grad_rows, weight, down_rows, up_rows, mask):
    hidden_grad = jnp.einsum("nre,nce->nrc", grad_rows, up_rows, preferred_element_type=jnp.float32)
    hidden_grad = (hidden_grad * mask).astype(jnp.bfloat16)
    input_grad = jnp.einsum("nre,nde->rd", grad_rows, weight, preferred_element_type=jnp.float32)
    input_grad = input_grad + jnp.einsum(
        "nrc,ndc->rd", hidden_grad, down_rows, preferred_element_type=jnp.float32
    )
    down_grad = jnp.einsum("rd,nrc->ndc", inputs, hidden_grad, preferred_element_type=jnp.float32)
    up_grad = jnp.einsum("nrc,nre->nce", hidden, grad_rows, preferred_element_type=jnp.float32)
    return (input_grad, down_grad, up_grad)


def attend_forward(packed, layout):
    view_shape, score_eq, mix_eq, back_eq = layout
    queries = packed[0].reshape(view_shape)
    key_rows = packed[1].reshape(view_shape)
    values = packed[2].reshape(view_shape)
    scores = jnp.einsum(
        score_eq, queries, key_rows, preferred_element_type=jnp.float32
    ) * HEAD_DIM ** (-0.5)
    ceiling = jnp.max(scores, axis=-1, keepdims=True)
    expo_rows = jnp.exp(scores - ceiling)
    totals = jnp.sum(expo_rows, axis=-1, keepdims=True)
    weights_soft = (expo_rows / totals).astype(jnp.bfloat16)
    mixed_rows = jnp.einsum(mix_eq, weights_soft, values, preferred_element_type=jnp.float32)
    return (mixed_rows.reshape(packed.shape[1:]), ceiling + jnp.log(totals))


def attend_backward(packed, log_total, mixed_grad, layout):
    view_shape, score_eq, mix_eq, back_eq = layout
    scaling = HEAD_DIM ** (-0.5)
    queries = packed[0].reshape(view_shape)
    key_rows = packed[1].reshape(view_shape)
    values = packed[2].reshape(view_shape)
    scores = jnp.einsum(score_eq, queries, key_rows, preferred_element_type=jnp.float32) * scaling
    weights_soft = jnp.exp(scores - log_total)
    output_grad = mixed_grad.reshape(view_shape)
    soft_grad = jnp.einsum(score_eq, output_grad, values, preferred_element_type=jnp.float32)
    row_inner = jnp.sum(weights_soft * soft_grad, axis=-1, keepdims=True)
    score_grad = (weights_soft * (soft_grad - row_inner)).astype(jnp.bfloat16)
    query_grad = (
        jnp.einsum(mix_eq, score_grad, key_rows, preferred_element_type=jnp.float32) * scaling
    )
    key_grad = (
        jnp.einsum(back_eq, score_grad, queries, preferred_element_type=jnp.float32) * scaling
    )
    value_grad = jnp.einsum(
        back_eq, weights_soft.astype(jnp.bfloat16), output_grad, preferred_element_type=jnp.float32
    )
    stacked = jnp.stack([query_grad, key_grad, value_grad])
    return stacked.reshape(packed.shape).astype(jnp.bfloat16)


def attention_forward(stream, gain_row, shift_row, weight_set, mask, layout):
    inner_weights, outer_weight, down_rows, up_rows = weight_set
    normed = layer_norm(stream, gain_row, shift_row).astype(jnp.bfloat16)
    packed, packed_hidden = project_many(normed, inner_weights, down_rows[0:3], up_rows[0:3], mask)
    packed = packed.astype(jnp.bfloat16)
    mixed_rows, log_total = attend_forward(packed, layout)
    mixed_rows = mixed_rows.astype(jnp.bfloat16)
    branch, outer_hidden = project_many(
        mixed_rows, outer_weight[None], down_rows[3:4], up_rows[3:4], mask
    )
    return (
        stream + branch[0],
        (normed, packed, packed_hidden, mixed_rows, outer_hidden, log_total),
    )


def attention_backward(
    stream, stream_grad, gain_row, shift_row, weight_set, mask, layout, kept_values
):
    inner_weights, outer_weight, down_rows, up_rows = weight_set
    normed, packed, packed_hidden, mixed_rows, outer_hidden, log_total = kept_values
    branch_grad = stream_grad.astype(jnp.bfloat16)[None]
    mixed_grad, outer_down, outer_up = project_back(
        mixed_rows,
        outer_hidden,
        branch_grad,
        outer_weight[None],
        down_rows[3:4],
        up_rows[3:4],
        mask,
    )
    packed_grad = attend_backward(packed, log_total, mixed_grad.astype(jnp.bfloat16), layout)
    normed_grad, inner_down, inner_up = project_back(
        normed, packed_hidden, packed_grad, inner_weights, down_rows[0:3], up_rows[0:3], mask
    )
    unused, norm_pull = jax.vjp(lambda rows_in: layer_norm(rows_in, gain_row, shift_row), stream)
    before_grad = stream_grad + norm_pull(normed_grad)[0]
    return (
        before_grad,
        jnp.concatenate([inner_down, outer_down], axis=0),
        jnp.concatenate([inner_up, outer_up], axis=0),
    )


def expand_forward(stream, gain_row, shift_row, weight_set, mask):
    up_weight, down_weight, in_down, in_up, out_down, out_up = weight_set
    normed = layer_norm(stream, gain_row, shift_row).astype(jnp.bfloat16)
    inner_rows, inner_hidden = project_many(
        normed, up_weight[None], in_down[None], in_up[None], mask
    )
    inner_rows = inner_rows[0]
    active = jax.nn.gelu(inner_rows, approximate=True).astype(jnp.bfloat16)
    branch, outer_hidden = project_many(
        active, down_weight[None], out_down[None], out_up[None], mask
    )
    return (stream + branch[0], (normed, inner_rows, inner_hidden, active, outer_hidden))


def expand_backward(stream, stream_grad, gain_row, shift_row, weight_set, mask, kept_values):
    up_weight, down_weight, in_down, in_up, out_down, out_up = weight_set
    normed, inner_rows, inner_hidden, active, outer_hidden = kept_values
    branch_grad = stream_grad.astype(jnp.bfloat16)[None]
    active_grad, out_down_grad, out_up_grad = project_back(
        active, outer_hidden, branch_grad, down_weight[None], out_down[None], out_up[None], mask
    )
    unused, gelu_pull = jax.vjp(
        lambda values_in: jax.nn.gelu(values_in, approximate=True), inner_rows
    )
    inner_grad = gelu_pull(active_grad)[0].astype(jnp.bfloat16)[None]
    normed_grad, in_down_grad, in_up_grad = project_back(
        normed, inner_hidden, inner_grad, up_weight[None], in_down[None], in_up[None], mask
    )
    unused_norm, norm_pull = jax.vjp(
        lambda rows_in: layer_norm(rows_in, gain_row, shift_row), stream
    )
    before_grad = stream_grad + norm_pull(normed_grad)[0]
    return (before_grad, (in_down_grad[0], in_up_grad[0], out_down_grad[0], out_up_grad[0]))


def regroup_places(stream, layout_sizes, backward):
    frames_dev, clips_dev, places, model_width, clip_rows, place_blocks, place_part = layout_sizes
    padded = jnp.pad(
        stream.reshape(frames_dev, clips_dev, places, model_width),
        ((0, 0), (0, 0), (0, place_part * place_blocks - places), (0, 0)),
    )
    padded = padded.reshape(frames_dev, clips_dev * place_blocks, place_part, model_width)
    if backward:
        arrived = lax.all_to_all(
            padded.astype(jnp.bfloat16), "tok", split_axis=1, concat_axis=0, tiled=True
        ).astype(padded.dtype)
    else:
        arrived = lax.all_to_all(
            padded.astype(jnp.bfloat16), "tok", split_axis=1, concat_axis=0, tiled=True
        ).astype(padded.dtype)
    return arrived.reshape(clip_rows * FRAMES * place_part, model_width)


def regroup_frames(stream, layout_sizes, backward):
    frames_dev, clips_dev, places, model_width, clip_rows, place_blocks, place_part = layout_sizes
    shaped = stream.reshape(clip_rows * FRAMES, 1, place_part, model_width)
    if backward:
        arrived = lax.all_to_all(
            shaped.astype(jnp.bfloat16), "tok", split_axis=0, concat_axis=1, tiled=True
        ).astype(shaped.dtype)
    else:
        arrived = lax.all_to_all(
            shaped.astype(jnp.bfloat16), "tok", split_axis=0, concat_axis=1, tiled=True
        ).astype(shaped.dtype)
    arrived = arrived.reshape(frames_dev, clips_dev, place_part * place_blocks, model_width)
    return arrived[:, :, :places].reshape(frames_dev * clips_dev * places, model_width)


def general_device(
    tokens,
    adapter_index,
    norm_gain,
    norm_shift,
    spatial_weights,
    spatial_output,
    temporal_weights,
    temporal_output,
    expand_weight,
    reduce_weight,
    attention_down,
    attention_up,
    expand_down,
    expand_up,
    reduce_down,
    reduce_up,
    cotangent,
):
    frames_dev, clips_dev, places, model_width = tokens.shape[1:]
    tok_count = lax.axis_size("tok")
    frame_blocks = FRAMES // frames_dev
    clip_rows = tok_count // frame_blocks
    place_blocks = tok_count // clips_dev
    place_part = -(-places // place_blocks)
    layout_sizes = (frames_dev, clips_dev, places, model_width, clip_rows, place_blocks, place_part)
    adapt_cols = ADAPTERS * RANK
    position = lax.axis_index("tok")
    spatial_choice = lax.dynamic_slice_in_dim(
        adapter_index, position // frame_blocks * clips_dev, clips_dev
    )
    spatial_mask = jnp.broadcast_to(
        adapter_mask(spatial_choice)[None, :, None, :], (frames_dev, clips_dev, places, adapt_cols)
    ).reshape(-1, adapt_cols)
    temporal_choice = lax.dynamic_slice_in_dim(
        adapter_index.reshape(clip_rows, clips_dev), position // place_blocks, 1, 1
    )[:, 0]
    temporal_mask = jnp.broadcast_to(
        adapter_mask(temporal_choice)[:, None, None, :], (clip_rows, FRAMES, place_part, adapt_cols)
    ).reshape(-1, adapt_cols)
    spatial_layout = (
        (frames_dev * clips_dev, places, HEADS, HEAD_DIM),
        "gqhd,gkhd->ghqk",
        "ghqk,gkhd->gqhd",
        "ghqk,gqhd->gkhd",
    )
    temporal_layout = (
        (clip_rows, FRAMES, place_part, HEADS, HEAD_DIM),
        "aqphd,akphd->aphqk",
        "aphqk,akphd->aqphd",
        "aphqk,aqphd->akphd",
    )
    spatial_set = (
        lax.all_gather(spatial_weights, ("clip", "tok"), axis=1, tiled=True),
        lax.all_gather(spatial_output, ("clip", "tok"), axis=0, tiled=True),
        lax.all_gather(attention_down[0:4], ("clip", "tok"), axis=1, tiled=True),
        lax.all_gather(attention_up[0:4], ("clip", "tok"), axis=2, tiled=True),
    )
    stream0 = tokens.reshape(-1, model_width)
    stream1, spatial_kept = attention_forward(
        stream0, norm_gain[0], norm_shift[0], spatial_set, spatial_mask, spatial_layout
    )
    placed1 = regroup_places(stream1, layout_sizes, False)
    temporal_set = (
        lax.all_gather(temporal_weights, ("clip", "tok"), axis=1, tiled=True),
        lax.all_gather(temporal_output, ("clip", "tok"), axis=0, tiled=True),
        lax.all_gather(attention_down[4:8], ("clip", "tok"), axis=1, tiled=True),
        lax.all_gather(attention_up[4:8], ("clip", "tok"), axis=2, tiled=True),
    )
    placed2, temporal_kept = attention_forward(
        placed1, norm_gain[1], norm_shift[1], temporal_set, temporal_mask, temporal_layout
    )
    stream2 = regroup_frames(placed2, layout_sizes, False)
    expand_set = (
        lax.all_gather(expand_weight, ("clip", "tok"), axis=0, tiled=True),
        lax.all_gather(reduce_weight, ("clip", "tok"), axis=0, tiled=True),
        lax.all_gather(expand_down, ("clip", "tok"), axis=0, tiled=True),
        lax.all_gather(expand_up, ("clip", "tok"), axis=1, tiled=True),
        lax.all_gather(reduce_down, ("clip", "tok"), axis=0, tiled=True),
        lax.all_gather(reduce_up, ("clip", "tok"), axis=1, tiled=True),
    )
    stream3, expand_kept = expand_forward(
        stream2, norm_gain[2], norm_shift[2], expand_set, spatial_mask
    )
    expand_set = (
        lax.all_gather(expand_weight, ("clip", "tok"), axis=0, tiled=True),
        lax.all_gather(reduce_weight, ("clip", "tok"), axis=0, tiled=True),
        lax.all_gather(expand_down, ("clip", "tok"), axis=0, tiled=True),
        lax.all_gather(expand_up, ("clip", "tok"), axis=1, tiled=True),
        lax.all_gather(reduce_down, ("clip", "tok"), axis=0, tiled=True),
        lax.all_gather(reduce_up, ("clip", "tok"), axis=1, tiled=True),
    )
    grad2, expand_grads = expand_backward(
        stream2,
        cotangent.reshape(-1, model_width),
        norm_gain[2],
        norm_shift[2],
        expand_set,
        spatial_mask,
        expand_kept,
    )
    placed_grad2 = regroup_places(grad2, layout_sizes, True)
    temporal_set = (
        lax.all_gather(temporal_weights, ("clip", "tok"), axis=1, tiled=True),
        lax.all_gather(temporal_output, ("clip", "tok"), axis=0, tiled=True),
        lax.all_gather(attention_down[4:8], ("clip", "tok"), axis=1, tiled=True),
        lax.all_gather(attention_up[4:8], ("clip", "tok"), axis=2, tiled=True),
    )
    placed_grad1, temporal_down, temporal_up = attention_backward(
        placed1,
        placed_grad2,
        norm_gain[1],
        norm_shift[1],
        temporal_set,
        temporal_mask,
        temporal_layout,
        temporal_kept,
    )
    grad1 = regroup_frames(placed_grad1, layout_sizes, True)
    spatial_set = (
        lax.all_gather(spatial_weights, ("clip", "tok"), axis=1, tiled=True),
        lax.all_gather(spatial_output, ("clip", "tok"), axis=0, tiled=True),
        lax.all_gather(attention_down[0:4], ("clip", "tok"), axis=1, tiled=True),
        lax.all_gather(attention_up[0:4], ("clip", "tok"), axis=2, tiled=True),
    )
    grad0, spatial_down, spatial_up = attention_backward(
        stream0,
        grad1,
        norm_gain[0],
        norm_shift[0],
        spatial_set,
        spatial_mask,
        spatial_layout,
        spatial_kept,
    )
    owned = (
        lax.psum_scatter(
            jnp.concatenate([spatial_down, temporal_down], axis=0),
            ("clip", "tok"),
            scatter_dimension=1,
            tiled=True,
        ),
        lax.psum_scatter(
            jnp.concatenate([spatial_up, temporal_up], axis=0),
            ("clip", "tok"),
            scatter_dimension=2,
            tiled=True,
        ),
        lax.psum_scatter(expand_grads[0], ("clip", "tok"), scatter_dimension=0, tiled=True),
        lax.psum_scatter(expand_grads[1], ("clip", "tok"), scatter_dimension=1, tiled=True),
        lax.psum_scatter(expand_grads[2], ("clip", "tok"), scatter_dimension=0, tiled=True),
        lax.psum_scatter(expand_grads[3], ("clip", "tok"), scatter_dimension=1, tiled=True),
    )
    return (
        stream3.reshape(tokens.shape),
        grad0.reshape(tokens.shape),
        owned[0],
        owned[1],
        owned[2],
        owned[3],
        owned[4],
        owned[5],
    )


F32 = jnp.float32
BF16 = jnp.bfloat16
ADAPT = ADAPTERS * RANK
SPATIAL_UNROLL = 6
SPATIAL_BACK_UNROLL = 6
MIDDLE_UNROLL = 6
MIDDLE_BACK_UNROLL = 6


def nn(left, right):
    return lax.dot_general(left, right, (((1,), (0,)), ((), ())), preferred_element_type=F32)


def nt(left, right):
    return lax.dot_general(left, right, (((1,), (1,)), ((), ())), preferred_element_type=F32)


def tn(left, right):
    return lax.dot_general(left, right, (((0,), (0,)), ((), ())), preferred_element_type=F32)


def one_hot(target_row, rows):
    row_ids = lax.broadcasted_iota(jnp.int32, (rows, target_row.shape[1]), 0)
    return (row_ids == target_row).astype(F32).astype(BF16)


def column_mask(choice):
    return (lax.broadcasted_iota(jnp.int32, (1, ADAPT), 1) // RANK == choice).astype(F32)


def set_rows(rows, choice):
    total = jnp.zeros((RANK, rows.shape[1]), F32)
    for k in range(ADAPTERS):
        total = jnp.where(choice == k, rows[k * RANK : (k + 1) * RANK], total)
    return total


def norm_rows(rows, gain_row, shift_row):
    average = jnp.mean(rows, axis=-1, keepdims=True)
    centred = rows - average
    variance = jnp.mean(centred * centred, axis=-1, keepdims=True)
    return centred * lax.rsqrt(variance + EPSILON) * gain_row + shift_row


def norm_back(rows, pulled, gain_row):
    average = jnp.mean(rows, axis=-1, keepdims=True)
    centred = rows - average
    variance = jnp.mean(centred * centred, axis=-1, keepdims=True)
    scale = lax.rsqrt(variance + EPSILON)
    unit = centred * scale
    scaled = pulled * gain_row
    return scale * (
        scaled
        - jnp.mean(scaled, axis=-1, keepdims=True)
        - unit * jnp.mean(scaled * unit, axis=-1, keepdims=True)
    )


def soften(scores, keep):
    scores = jnp.where(keep, scores, -1e30)
    ceiling = jnp.max(scores, axis=-1, keepdims=True)
    expo = jnp.exp(scores - ceiling)
    return expo * (1.0 / jnp.sum(expo, axis=-1, keepdims=True))


def two_heads(rows, low):
    zero = jnp.zeros_like(rows)
    return jnp.concatenate([jnp.where(low, rows, zero), jnp.where(low, zero, rows)], axis=0)


def one_pair(both, low):
    count = both.shape[0] // 2
    return jnp.where(low, both[:count], both[count:])


def attention_pair(query, key, value, keep, low):
    weights = soften(nt(two_heads(query, low), key), keep).astype(BF16)
    return weights, one_pair(nn(weights, value), low).astype(BF16)


def attention_all(sizes, first, qkv, soft, mixed, keep, low, unroll):
    start, blocks, rows_each, pairs = sizes

    @pl.loop(0, blocks * pairs // unroll)
    def _(turn):
        block = turn // (pairs // unroll)
        lead = (turn - block * (pairs // unroll)) * unroll
        rows = pl.ds(pl.multiple_of(start + block * rows_each, 16), rows_each)
        for u in range(unroll):
            lanes = pl.ds(pl.multiple_of((lead + u) * 128, 128), 128)
            weights, made = attention_pair(
                qkv[0, rows, lanes], qkv[1, rows, lanes], qkv[2, rows, lanes], keep, low
            )
            soft[(first + block) * pairs + lead + u] = weights
            mixed[rows, lanes] = made


def attention_all_back(sizes, qkv, soft, gmix, gqkv, low, unroll, first=0):
    blocks, rows_each, pairs = sizes

    @pl.loop(0, blocks * pairs // unroll)
    def _(turn):
        block = turn // (pairs // unroll)
        lead = (turn - block * (pairs // unroll)) * unroll
        block = block + first
        rows = pl.ds(pl.multiple_of(block * rows_each, 16), rows_each)
        for u in range(unroll):
            lanes = pl.ds(pl.multiple_of((lead + u) * 128, 128), 128)
            made = attention_back(
                qkv[0, rows, lanes], qkv[1, rows, lanes], qkv[2, rows, lanes],
                soft[block * pairs + lead + u], gmix[rows, lanes], low,
            )
            for n in range(3):
                gqkv[n, rows, lanes] = made[n].astype(BF16)


def block_rows(ref, slots, number, offset=0):
    chunk = slots.shape[1]
    return ref.at[pl.ds(pl.multiple_of(offset + number * chunk, 8), chunk)]


def send_blocks(slots, got, count, first, send_sems, recv_sems, local_sem, offset=0):
    clip, tok = lax.axis_index("clip"), lax.axis_index("tok")
    target = block_rows(got, slots, tok, offset)
    for n in range(count):
        place = first + lax.rem(tok + n, count)

        @pl.when(place != tok)
        def _():
            remote(slots.at[place], target, send_sems.at[place], recv_sems.at[tok], (clip, place)).start()

        @pl.when(place == tok)
        def _():
            pltpu.make_async_copy(slots.at[place], target, local_sem).start()


def wait_blocks(slots, got, members, send_sems, recv_sems, local_sem, offset=0):
    tok = lax.axis_index("tok")
    for d in range(1, members):
        place = lax.rem(tok + d, members)
        target = block_rows(got, slots, place, offset)
        pltpu.make_async_copy(slots.at[place], slots.at[place], send_sems.at[place]).wait()
        pltpu.make_async_copy(target, target, recv_sems.at[place]).wait()
    pltpu.make_async_copy(slots.at[tok], block_rows(got, slots, tok, offset), local_sem).wait()


def attention_back(query, key, value, weights, grads, low):
    stacked = two_heads(grads, low)
    pulled = nt(stacked, value)
    wide = weights.astype(F32)
    inner = jnp.sum(wide * pulled, axis=-1, keepdims=True)
    score = (wide * (pulled - inner)).astype(BF16)
    query_grad = one_pair(nn(score, key), low) * HEAD_DIM**-0.5
    return query_grad, tn(score, two_heads(query, low)), tn(weights, stacked)


def spatial_backward(
    sizes, groups, members, step, regions, idx, from_sent, from_tails, gain, x_hbm, w_hbm, ad_hbm, qkv_hbm, soft_hbm, mixed_hbm, hid_hbm, zs_hbm,
    got_hbm, made_hbm, mid_pay,
    dx_hbm, out_hbm, down_out, up_out, ea, eb, ra, rb,
    w, ad, qkv, soft, mixed, hid, zs, got, made, x, out, mid, sp, pay, grad, gmix, gqkv, gpull, gdown, gup, copy_sems, send_sems, recv_sems
):
    frames, clips, places, width, padded = sizes
    half = frames * padded
    devices = groups * members

    def row_copies(view, rows, first, inward):
        copies = []
        for i in range(frames):
            for b in range(clips):
                ends = (view.at[i, :, b, :], rows.at[i, b])
                ends = ends if inward else ends[::-1]
                copies.append(pltpu.make_async_copy(*ends, copy_sems.at[first + i * clips + b]))
        return copies

    fills = [
        pltpu.make_async_copy(source, target, copy_sems.at[10 + n])
        for n, (source, target) in enumerate(
            (
                (got_hbm, got), (w_hbm.at[3], w.at[3]), (ad_hbm, ad), (mixed_hbm, mixed), (hid_hbm, hid),
                (soft_hbm, soft), (qkv_hbm, qkv), (w_hbm.at[0:3], w.at[0:3]), (zs_hbm, zs), (made_hbm, made),
            )
        )
    ]
    loads = row_copies(x_hbm, x, 0, True)
    for load in fills + loads:
        load.start()
    clip, tok = lax.axis_index("clip"), lax.axis_index("tok")
    me = clip * members + tok
    peers = all_peers(groups, members)
    greet(peers)

    def terms(source, target, kind):
        for n, peer in enumerate(peers):
            place = peer[0] * members + peer[1]
            remote(
                source.at[place], target.at[me], send_sems.at[kind, n], recv_sems.at[kind, n], peer
            ).start()
        pltpu.make_async_copy(source.at[me], target.at[me], copy_sems.at[8 + kind]).start()

    def await_terms(source, target, kind):
        for n, peer in enumerate(peers):
            remote(source.at[me], target.at[me], send_sems.at[kind, n], recv_sems.at[kind, n], peer).wait()
        pltpu.make_async_copy(source.at[me], target.at[me], copy_sems.at[8 + kind]).wait()

    terms(mid_pay, mid, 0)
    for fill in fills[0:5]:
        fill.wait()
    for b in range(clips):
        rows = slice(b * half, (b + 1) * half)
        mask = column_mask(idx[b])
        arrived = []
        for begin, size in regions:
            arrived.append(got[begin + b * size : begin + (b + 1) * size])
        grad[rows] = nn(one_hot(from_tails[...], half), jnp.concatenate(arrived, axis=0)).astype(BF16)
        hidden_grad = (nn(grad[rows], ad[7]) * mask).astype(BF16)
        gmix[rows] = (nt(grad[rows], w[3]) + nt(hidden_grad, ad[3])).astype(BF16)
        down, up = tn(hidden_grad, mixed[rows]), tn(hid[3, rows], grad[rows])
        if b == 0:
            gdown[3], gup[3] = down, up
        else:
            gdown[3] += down
            gup[3] += up

    pairs = width // 128
    low = lax.broadcasted_iota(jnp.int32, (padded, 128), 1) < HEAD_DIM

    for fill in fills[5:7]:
        fill.wait()
    attention_all_back((frames * clips, padded, pairs), qkv, soft, gmix, gqkv, low, SPATIAL_BACK_UNROLL)
    for fill in fills[7:10]:
        fill.wait()
    for b in range(clips):
        rows = slice(b * half, (b + 1) * half)
        mask = column_mask(idx[b])
        gpull[b] = jnp.zeros(gpull.shape[1:], F32)

        @pl.loop(0, 3)
        def _(n):
            own = gqkv[n, rows]
            hidden_grad = (nn(own, ad[4 + n]) * mask).astype(BF16)
            gpull[b] += nt(own, w[n]) + nt(hidden_grad, ad[n])
            down, up = tn(hidden_grad, zs[rows]), tn(hid[n, rows], own)
            if b == 0:
                gdown[n], gup[n] = down, up
            else:
                gdown[n] += down
                gup[n] += up

    repeat = jnp.where(idx[0] == idx[1], 0.0, 1.0)
    pieces = []
    for n in range(4):
        for source in (gdown, gup):
            pieces.append(set_rows(source[n], idx[0]))
            pieces.append(set_rows(source[n], idx[1]) * repeat)
    packed = jnp.transpose(jnp.concatenate(pieces, axis=0))
    pay[...] = packed.reshape(pay.shape).astype(BF16)
    terms(pay, sp, 1)
    for load in loads:
        load.wait()
    for b in range(clips):
        rows = slice(b * half, (b + 1) * half)
        final = nn(one_hot(from_sent[...], half), made[rows])
        for i in range(frames):
            base = i * padded
            out[i, b] = final[base : base + places]
            pulled = norm_back(x[i, b], gpull[b, base : base + places], gain[0:1])
            x[i, b] = grad[b * half + base : b * half + base + places].astype(F32) + pulled
    stores = row_copies(out_hbm, out, 4, False) + row_copies(dx_hbm, x, 0, False)
    for store in stores:
        store.start()
    await_terms(mid_pay, mid, 0)
    mids, mid_choice = combine_mid((groups, members, step, eb.shape[0] // step), mid, down_out, up_out, ea, eb, ra, rb)
    await_terms(pay, sp, 1)
    combine_spatial((groups, members, step), sp, mids, down_out, up_out)
    for store in stores:
        store.wait()


def front(
    sizes, shape, members, tail_parts, idx, to_send, to_place, to_frame, to_first, to_second, x_hbm, cot_hbm, gain, shift,
    sh_w, sh_o, sh_tw, sh_to, sh_down, sh_up, sh_we, sh_wr, sh_eup, sh_rdown, sh_edown, sh_rup,
    all_w, all_ad, all_tw, all_tad, all_we, all_wr, all_tall, all_flat, got_hbm, cot_got, made, back,
    qkv_hbm, soft_hbm, mixed_hbm, hid_hbm, zs_hbm, pay,
    w, ad, we, wr, tall, flat, slots, cots, tail_one, tail_two, sems, copy_sems, send_sems, recv_sems, *, scopes
):
    frames, clips, places, width, padded = sizes
    rows_all, group, ff_chunk, owners = shape
    chunk = slots.shape[1]
    tails, to_tails = (tail_one, tail_two), (to_first, to_second)
    half = frames * padded
    share = members // clips
    clip, tok = lax.axis_index("clip"), lax.axis_index("tok")
    parts = [
        Part([(sh_w.at[0:2], None)], all_w.at[0:2], 1, sems.at[0]),
        Part([(sh_w.at[2], 0), (sh_o, 1)], all_w.at[2:4], 1, sems.at[1]),
        Part([(sh_down.at[0:4], slice(0, 4)), (sh_up.at[0:4], slice(4, 8))], all_ad, 1, sems.at[2]),
        Part([(sh_tw, slice(0, 3)), (sh_to, 3)], all_tw, 1, sems.at[3]),
        Part([(sh_down.at[4:8], slice(0, 4)), (sh_up.at[4:8], slice(4, 8))], all_tad, 1, sems.at[4]),
        Part([(sh_we, None)], all_we, 0, sems.at[5]),
        Part([(sh_wr, None)], all_wr, 0, sems.at[6]),
        Part([(sh_eup, 0), (sh_rdown, 1)], all_tall, 1, sems.at[7]),
        Part([(sh_edown, 0), (sh_rup, 1)], all_flat, 1, sems.at[8]),
    ]
    y, core, z, across = place_of()
    greet(tok_peers(members) + [device_at(1 - y, core, z, across), device_at(y, 1 - core, z, across)])

    def stages(plan):
        for step in range(0, len(plan), 2):
            parts["ABCDEFGHI".index(plan[step])].stage(int(plan[step + 1]))

    def exchange_sems(n):
        return send_sems.at[n], recv_sems.at[n], copy_sems.at[25 + n]

    temporal_loads = [
        pltpu.make_async_copy(all_tw, w, copy_sems.at[2]), pltpu.make_async_copy(all_tad, ad, copy_sems.at[3])
    ]
    loads = [
        pltpu.make_async_copy(source, target, copy_sems.at[n])
        for n, (source, target) in zip((0, 1, 5, 6), ((all_wr, wr), (all_tall, tall), (all_flat, flat), (all_we, we)))
    ]
    stages("A0B0C0")

    def spatial_phase(x, cot, stream, qkv, soft, mixed, hid, zs):
        load_cot = row_loads(cot_hbm, cot, 21, frames, clips, copy_sems)
        load_x = row_loads(x_hbm, x, 17, frames, clips, copy_sems)
        for load in load_cot + load_x:
            load.start()
        pads = slice(padded - 16, padded)
        for i in range(frames):
            stream[i * padded + padded - 16 : (i + 1) * padded] = jnp.zeros((16, width), BF16)
        for load in load_cot:
            load.wait()
        for b in range(clips):
            for i in range(frames):
                stream[i * padded : i * padded + places] = cot[i, b].astype(BF16)
            rows = nn(one_hot(to_send[...], half), stream[...])
            cots[b * share : (b + 1) * share] = rows.reshape(share, chunk, width).astype(BF16)
        stages("A1B1A2C1B2A3")
        for load in load_x:
            load.wait()
        for b in range(clips):
            for i in range(frames):
                base = b * half + i * padded
                zs[base + padded - 16 : base + padded] = jnp.zeros((16, width), BF16)
                zs[base : base + places] = norm_rows(
                    x[i, b], gain[0:1], shift[0:1]
                ).astype(BF16)
        stages("C2B3C3D0E0A4B4C4")
        stages("D1E1A5B5C5A6B6C6")
        loads = [pltpu.make_async_copy(all_w, w, copy_sems.at[2]), pltpu.make_async_copy(all_ad, ad, copy_sems.at[3])]
        for load in loads:
            load.start()
        stages("D2E2F0G0H0I0")
        for load in loads:
            load.wait()

        keep = lax.broadcasted_iota(jnp.int32, (2 * padded, padded), 1) < places
        pairs = width // 128
        low = lax.broadcasted_iota(jnp.int32, (padded, 128), 1) < HEAD_DIM
        far = jnp.where(tok < share, 1, 0)
        for turn in range(clips):
            b = far if turn == 0 else 1 - far
            rows = pl.ds(pl.multiple_of(b * half, 16), half)
            mask = column_mask(idx[b])

            @pl.loop(0, 3)
            def _(n):
                hidden = (nn(zs[rows], ad[n]) * mask).astype(BF16)
                hid[n, rows] = hidden
                result = nn(zs[rows], w[n]) + nt(hidden, ad[4 + n])
                result = result * jnp.where(n == 0, HEAD_DIM**-0.5, 1.0)
                qkv[n, rows] = result.astype(BF16)

            stages("D3E3F1G1H1I1" if turn == 0 else "D5E5F4")

            attention_all(
                (b * half, frames, padded, pairs), b * frames, qkv, soft, mixed, keep, low, SPATIAL_UNROLL
            )
            if turn == 0:
                stages("D4E4F2G2H2I2")
            hidden = (nn(mixed[rows], ad[3]) * mask).astype(BF16)
            hid[3, rows] = hidden
            branch = nn(mixed[rows], w[3]) + nt(hidden, ad[7])
            for i in range(frames):
                stream[i * padded : i * padded + places] = (
                    x[i, b] + branch[i * padded : i * padded + places]
                ).astype(BF16)
            made = nn(one_hot(to_send[...], half), stream[...]).reshape(share, chunk, width)
            slots[pl.ds(b * share, share)] = made.astype(BF16)
            send_blocks(slots, got_hbm, share, b * share, *exchange_sems(0))
            if turn == 0:
                stages("F3G3H3I3")
        stores = [
            pltpu.make_async_copy(source, target, copy_sems.at[12 + n])
            for n, (source, target) in enumerate(
                ((qkv, qkv_hbm), (soft, soft_hbm), (mixed, mixed_hbm), (hid, hid_hbm), (zs, zs_hbm))
            )
        ]
        for store in stores:
            store.start()
        stages("D6E6")
        for load in temporal_loads:
            load.start()
        for store in stores:
            store.wait()

    def middle_phase(
        got, cot, x1, x2, zt, ze, qkv, soft, mixed, hid, hide, gy, acc, pull, ghe, gmix, gqkv, gdown, gup, wide
    ):
        choice = idx[tok // share]
        mask = column_mask(choice)
        groups = rows_all // group
        wait_blocks(slots, got_hbm, members, *exchange_sems(0))
        send_blocks(cots, cot_got, members, 0, *exchange_sems(1))
        load_got = pltpu.make_async_copy(got_hbm, got, copy_sems.at[4])
        load_got.start()
        load_got.wait()

        @pl.loop(0, groups)
        def _(j):
            rows = pl.ds(pl.multiple_of(j * group, 16), group)
            own = nn(one_hot_rows(to_place[...], group, j * group), got[...])
            x1[rows] = own.astype(BF16)
            zt[rows] = norm_rows(own, gain[1:2], shift[1:2]).astype(BF16)

        for load in temporal_loads:
            load.wait()

        @pl.loop(0, 3)
        def _(n):
            hidden = (nn(zt[...], ad[n]) * mask).astype(BF16)
            hid[n] = hidden
            result = nn(zt[...], w[n]) + nt(hidden, ad[4 + n])
            result = result * jnp.where(n == 0, HEAD_DIM**-0.5, 1.0)
            qkv[n] = result.astype(BF16)

        stages("F5G4H4I4")

        pairs = width // 128
        keep = (
            lax.rem(lax.broadcasted_iota(jnp.int32, (2 * group, group), 0), group) // FRAMES
            == lax.broadcasted_iota(jnp.int32, (2 * group, group), 1) // FRAMES
        )
        low = lax.broadcasted_iota(jnp.int32, (group, 128), 1) < HEAD_DIM

        attention_all((0, groups, group, pairs), 0, qkv, soft, mixed, keep, low, MIDDLE_UNROLL)
        stages("F6G5H5I5")
        loads[3].start()
        hidden = (nn(mixed[...], ad[3]) * mask).astype(BF16)
        hid[3] = hidden
        acc[...] = nn(mixed[...], w[3]) + nt(hidden, ad[7])

        @pl.loop(0, groups)
        def _(j):
            rows = pl.ds(pl.multiple_of(j * group, 16), group)
            own = x1[rows].astype(F32) + acc[rows]
            x2[rows] = own
            acc[rows] = own
            pull[rows] = jnp.zeros((group, width), F32)
            ze[rows] = norm_rows(own, gain[2:3], shift[2:3]).astype(BF16)

        stages("G6H6I6")
        for load in loads[0:3]:
            load.start()
        wait_blocks(cots, cot_got, members, *exchange_sems(1))
        load_cot = pltpu.make_async_copy(cot_got, cot, copy_sems.at[4])
        load_cot.start()
        load_cot.wait()

        @pl.loop(0, groups)
        def _(j):
            rows = pl.ds(pl.multiple_of(j * group, 16), group)
            gy[rows] = nn(one_hot_rows(to_place[...], group, j * group), cot[...]).astype(BF16)

        for load in loads:
            load.wait()
        hide[...] = (nn(ze[...], flat[0]) * mask).astype(BF16)
        ghr = (nn(gy[...], flat[1]) * mask).astype(BF16)
        hid[0 + 4] = ghr
        ghe[...] = jnp.zeros(ghe.shape, F32)

        @pl.loop(0, we.shape[1] // ff_chunk)
        def _(c):
            part = pl.ds(pl.multiple_of(c * ff_chunk, ff_chunk), ff_chunk)
            inner = nn(ze[...], we[:, part]) + nt(hide[...], tall[0, part])
            cube = 0.7978845608028654 * (inner + 0.044715 * inner * inner * inner)
            bend = jnp.tanh(cube)
            act = (0.5 * inner * (1.0 + bend)).astype(BF16)
            slope = 0.5 * (1.0 + bend) + 0.5 * inner * (1.0 - bend * bend) * (
                0.7978845608028654 * (1.0 + 3.0 * 0.044715 * inner * inner)
            )
            acc[...] += nn(act, wr[part])
            ghe[0] += nn(act, tall[1, part])
            wide[0, :, part] = tn(hid[4], act)
            gact = nt(gy[...], wr[part]) + nt(hid[4], tall[1, part])
            ginner = (gact * slope).astype(BF16)
            pull[...] += nt(ginner, we[:, part])
            ghe[1] += nn(ginner, tall[0, part])
            wide[1, :, part] = tn(hide[...], ginner)

        hidr = (ghe[0] * mask).astype(BF16)
        acc[...] += nt(hidr, flat[1])
        rows = nn(one_hot(to_frame[...], got.shape[0]), acc[...].astype(BF16))
        slots[...] = rows.reshape(slots.shape).astype(BF16)
        send_blocks(slots, made, members, 0, *exchange_sems(2))
        gdown[4] = tn(hidr, gy[...])
        gheb = (ghe[1] * mask).astype(BF16)
        gup[4] = tn(gheb, ze[...])
        pull[...] += nt(gheb, flat[0])

        @pl.loop(0, groups)
        def _(j):
            rows = pl.ds(pl.multiple_of(j * group, 16), group)
            own = gy[rows].astype(F32) + norm_back(x2[rows], pull[rows], gain[2:3])
            acc[rows] = own
            ze[rows] = own.astype(BF16)

        grad = ze
        hidden_grad = (nn(grad[...], ad[7]) * mask).astype(BF16)
        gmix[...] = (nt(grad[...], w[3]) + nt(hidden_grad, ad[3])).astype(BF16)
        gdown[3] = tn(hidden_grad, mixed[...])
        gup[3] = tn(hid[3], grad[...])

        offset = 0
        for turn, (first, count) in enumerate(tail_parts):
            lines = slice(first * group, (first + count) * group)
            attention_all_back(
                (count, group, pairs), qkv, soft, gmix, gqkv, low, MIDDLE_BACK_UNROLL, first
            )
            pull[lines] = jnp.zeros((count * group, width), F32)

            @pl.loop(0, 3)
            def _(n):
                own = gqkv[n, lines]
                hidden_grad = (nn(own, ad[4 + n]) * mask).astype(BF16)
                pull[lines] += nt(own, w[n]) + nt(hidden_grad, ad[n])
                down, up = tn(hidden_grad, zt[lines]), tn(hid[n, lines], own)
                if turn == 0:
                    gdown[n], gup[n] = down, up
                else:
                    gdown[n] += down
                    gup[n] += up

            @pl.loop(first, first + count)
            def _(j):
                rows = pl.ds(pl.multiple_of(j * group, 16), group)
                own = acc[rows] + norm_back(x1[rows].astype(F32), pull[rows], gain[1:2])
                ze[rows] = own.astype(BF16)

            tail = tails[turn]
            made_rows = nn(one_hot(to_tails[turn][...], members * tail.shape[1]), ze[lines])
            tail[...] = made_rows.reshape(tail.shape).astype(BF16)
            send_blocks(tail, back, members, 0, *exchange_sems(3 + turn), offset)
            offset += members * tail.shape[1]

        pieces = []
        for n in range(4):
            pieces += [set_rows(gdown[n], choice), set_rows(gup[n], choice)]
        pay[:, 0:128] = jnp.transpose(jnp.concatenate(pieces, axis=0)).astype(BF16)
        line = lax.broadcasted_iota(jnp.int32, (128 - 2 * RANK, width), 0)
        blank = jnp.zeros((128 - 2 * RANK, width), F32)
        for k, number in enumerate((choice, idx[0], idx[1])):
            blank = jnp.where(line == k, number.astype(F32), blank)
        pay[:, 128:256] = jnp.transpose(
            jnp.concatenate([set_rows(gup[4], choice), set_rows(gdown[4], choice), blank], axis=0)
        ).astype(BF16)
        high = jnp.concatenate(
            [set_rows(wide[1], choice), set_rows(wide[0], choice), jnp.zeros((128 - 2 * RANK, we.shape[1]), F32)], axis=0
        )
        high = jnp.transpose(high)
        step = width // owners
        fold = we.shape[1] // width
        high = high.reshape(owners, fold, step, 128)
        total = high[:, 0].reshape(width, 128)
        for f in range(1, fold):
            total += pltpu.roll(high[:, f].reshape(width, 128), 2 * RANK * f, 1)
        pay[:, 256:384] = total.astype(BF16)
        wait_blocks(slots, made, members, *exchange_sems(2))
        offset = 0
        for turn, tail in enumerate(tails):
            wait_blocks(tail, back, members, *exchange_sems(3 + turn), offset)
            offset += members * tail.shape[1]

    pl.run_scoped(spatial_phase, *scopes[0])
    pl.run_scoped(middle_phase, *scopes[1])


def deliver(count, *refs):
    sources, targets, held, sems = refs[:count], refs[count : 2 * count], refs[2 * count : 3 * count], refs[3 * count]
    loads = [pltpu.make_async_copy(sources[n], held[n], sems.at[n]) for n in range(count)]
    for load in loads:
        load.start()
    stores = [pltpu.make_async_copy(held[n], targets[n], sems.at[n + count]) for n in range(count)]
    for load, store in zip(loads, stores):
        load.wait()
        store.start()
    for store in stores:
        store.wait()


def row_loads(source, target, first, frames, clips, sems):
    return [
        pltpu.make_async_copy(source.at[i, :, b, :], target.at[i, b], sems.at[first + i * clips + b])
        for i in range(frames) for b in range(clips)
    ]


def one_hot_rows(target_row, rows, first):
    row_ids = lax.broadcasted_iota(jnp.int32, (rows, target_row.shape[1]), 0) + first
    return (row_ids == target_row).astype(F32).astype(BF16)


def spread_sum(stack, columns, first, choice, count):
    lanes = lax.broadcasted_iota(jnp.int32, (columns, ADAPT), 1)
    lines = lax.broadcasted_iota(jnp.int32, (columns, ADAPT), 0)
    spread = (lines == first + lanes % RANK).astype(F32)
    wide = lax.dot_general(
        stack, spread, (((1,), (0,)), ((), ())),
        preferred_element_type=F32, precision=lax.Precision.HIGHEST,
    )
    sets = lax.broadcasted_iota(jnp.int32, (1, ADAPT), 1) // RANK
    kept = jnp.where(sets.astype(F32) == choice, wide, 0.0)
    step = stack.shape[0] // count
    total = kept[0:step]
    for k in range(1, count):
        total += kept[k * step : (k + 1) * step]
    return total


def combine_mid(sizes, got, down, up, ea, eb, ra, rb):
    groups, members, step, fold = sizes
    clips = 2
    share = members // clips
    mids = []
    for g in range(groups):
        for b in range(clips):
            part = jnp.zeros((step, 384), F32)
            for t in range(share):
                part += got[g * members + b * share + t].astype(F32)
            mids.append(part)
    mid = jnp.concatenate(mids, axis=0)
    choice = mid[:, 160:161] * (1.0 / share)
    count = groups * clips
    for n in range(4):
        for s, target in enumerate((down, up)):
            target[4 + n] = spread_sum(mid[:, 0:128], 128, (2 * n + s) * RANK, choice, count)
    ea[...] = spread_sum(mid[:, 128:256], 128, 0, choice, count)
    rb[...] = spread_sum(mid[:, 128:256], 128, RANK, choice, count)
    for f in range(fold):
        rows = slice(f * step, (f + 1) * step)
        eb[rows] = spread_sum(mid[:, 256:384], 128, 2 * RANK * f, choice, count)
        ra[rows] = spread_sum(mid[:, 256:384], 128, 2 * RANK * f + RANK, choice, count)
    choices = [
        jnp.concatenate([mids[g * clips][:, 161 + b : 162 + b] * (1.0 / share) for g in range(groups)], axis=0)
        for b in range(clips)
    ]
    return choices, choice


def combine_spatial(sizes, got, choices, down, up):
    groups, members, step = sizes
    clips = len(choices)
    sums = []
    for g in range(groups):
        total = jnp.zeros((step, 256), F32)
        for t in range(members):
            total += got[g * members + t].astype(F32)
        sums.append(total)
    stack = jnp.concatenate(sums, axis=0)
    for n in range(4):
        for s, target in enumerate((down, up)):
            total = jnp.zeros((step, ADAPT), F32)
            for b in range(clips):
                total += spread_sum(stack, 256, ((2 * n + s) * clips + b) * RANK, choices[b], groups)
            target[n] = total


def shape_of(*dims, kind=BF16):
    return jax.ShapeDtypeStruct(dims, kind)


def order_tables(frames, places, padded, blocks, part, chunk):
    half_rows, sent_rows = frames * padded, blocks * chunk
    assert half_rows == sent_rows
    to_send = [-1] * half_rows
    from_sent = [-1] * sent_rows
    for i in range(frames):
        for p in range(places):
            source, target = i * padded + p, (p // part) * chunk + i * part + p % part
            to_send[source] = target
            from_sent[target] = source
    senders = FRAMES // frames
    to_place = [-1] * (senders * chunk)
    to_frame = [-1] * (part * FRAMES)
    for p in range(part):
        for f in range(FRAMES):
            source, target = (f // frames) * chunk + (f % frames) * part + p, p * FRAMES + f
            to_place[source] = target
            to_frame[target] = source
    return [jnp.array([table], jnp.int32) for table in (to_send, from_sent, to_place, to_frame)]


def tail_tables(parts, each, frames, places, padded, blocks, part):
    rows, to_parts, region = [], [], 0
    from_parts = []
    for first, count in parts:
        own = count * each
        size = -(-frames * own // 8) * 8
        rows.append(size)
        table = [-1] * (own * FRAMES)
        for p in range(own):
            for f in range(FRAMES):
                table[p * FRAMES + f] = (f // frames) * size + (f % frames) * own + p
        to_parts.append(jnp.array([table], jnp.int32))
        source = [-1] * (blocks * size)
        for block in range(blocks):
            for f in range(frames):
                for p in range(own):
                    source[block * size + f * own + p] = f * padded + block * part + first * each + p
        from_parts += source
    return rows, to_parts, jnp.array([from_parts], jnp.int32)


def fits(mesh):
    return mesh.shape["tok"] == 8 and mesh.shape["clip"] == 4


MESH = pl.DeviceIdType.MESH


def place_of():
    clip, tok = lax.axis_index("clip"), lax.axis_index("tok")
    return clip // 2, lax.rem(clip, 2), tok // 2, lax.rem(tok, 2)


def device_at(y, core, z, x):
    return (y * 2 + core, z * 2 + x)


def greet(peers):
    barrier = pltpu.get_barrier_semaphore()
    for peer in peers:
        pl.semaphore_signal(barrier, inc=1, device_id=peer, device_id_type=MESH)
    pl.semaphore_wait(barrier, len(peers))


def remote(source, target, send_sem, recv_sem, peer):
    return pltpu.make_async_remote_copy(
        src_ref=source, dst_ref=target, send_sem=send_sem, recv_sem=recv_sem, device_id=peer, device_id_type=MESH
    )


class Part:
    def __init__(self, pieces, whole, dim, sems):
        self.pieces, self.whole, self.dim, self.sems = pieces, whole, dim, sems
        self.rows = whole.shape[dim] // (lax.axis_size("clip") * lax.axis_size("tok"))
        self.me = place_of()
        for piece, target in self.own():
            pltpu.make_async_copy(piece, target, sems.at[1]).start()

    def own(self):
        target = self.slot(*self.me)
        return [(piece, target if index is None else target.at[index]) for piece, index in self.pieces]

    def span(self, first, count, half=None):
        rows = pl.ds(pl.multiple_of(first * self.rows, 8), count * self.rows)
        if self.dim == 1:
            lead = max(self.whole.shape[0] * 3 // 4, 1)
            front = (slice(None), slice(0, lead), slice(lead, None))[0 if half is None else half + 1]
            return self.whole.at[front, rows]
        lanes = self.whole.shape[1] * 3 // 512 * 128
        return self.whole.at[rows, (slice(None), slice(0, lanes), slice(lanes, None))[0 if half is None else half + 1]]

    def slot(self, y, core, z, x, half=None):
        clip, tok = device_at(y, core, z, x)
        return self.span(clip * 8 + tok, 1, half)

    def send(self, source, target, sem, peer):
        remote(source, target, self.sems.at[0], self.sems.at[sem], device_at(*peer)).start()

    def arrive(self, target, sem):
        pltpu.make_async_copy(target, target, self.sems.at[sem]).wait()

    def pass_on(self, far, sources=None):
        y, core, z, x = self.me
        owner = (y, core, far, x)
        target = self.slot(*owner)
        for source, target in sources or [(target, target)]:
            self.send(source, target, 8 + far, (y, core, z, 1 - x))
            self.send(source, target, 12 + far, (1 - y, core, z, x))
            self.send(source, target, 2 + y, (y, 1 - core, z, x))

    def to_core(self, owner):
        y, core, z, x = self.me
        target = self.slot(*owner)
        self.send(target, target, 2 + owner[0], (y, 1 - core, z, x))

    def hop(self, far, up, sources=None):
        y, core, z, x = self.me
        target = self.slot(y, core, far, x)
        for source, target in sources or [(target, target)]:
            self.send(source, target, 4 + far, (y, core, z + up, x))

    def relay(self, distance, up):
        y, core, z, x = self.me
        far = z - distance * up
        here = z >= distance if up > 0 else z <= 3 - distance
        on = z < 3 if up > 0 else z > 0

        @pl.when(here)
        def _():
            self.arrive(self.slot(y, core, far, x), 4 + far)

            @pl.when(on)
            def _():
                self.hop(far, up)

            self.pass_on(far)

    def stage(self, number):
        y, core, z, x = self.me
        if number == 0:
            own = self.own()

            @pl.when(z < 3)
            def _():
                self.hop(z, 1, own)

            @pl.when(z > 0)
            def _():
                self.hop(z, -1, own)

            self.pass_on(z, own)
        elif number <= 3:
            self.relay(number, 1)
            self.relay(number, -1)
        elif number == 4:
            for d in range(4):
                far = lax.rem(z + 4 - d, 4)
                owner = (y, core, far, 1 - x)
                self.arrive(self.slot(*owner), 8 + far)
                self.send(self.slot(*owner, 0), self.slot(*owner, 0), 16 + far, (1 - y, core, z, x))
                self.to_core(owner)
                owner = (1 - y, core, far, x)
                self.arrive(self.slot(*owner), 12 + far)
                self.send(self.slot(*owner, 1), self.slot(*owner, 1), 20 + far, (y, core, z, 1 - x))
                self.to_core(owner)
        elif number == 5:
            for d in range(4):
                far = lax.rem(z + 4 - d, 4)
                owner = (1 - y, core, far, 1 - x)
                self.arrive(self.slot(*owner, 0), 16 + far)
                self.arrive(self.slot(*owner, 1), 20 + far)
                self.to_core(owner)
        else:
            self.arrive(self.slot(*self.me), 1)
            for far in range(2):
                self.arrive(self.span((far * 2 + 1 - core) * 8, 8), 2 + far)
            self.arrive(self.span(0, 28), 0)
            hops = jnp.where(z == 0, 1, 0) + jnp.where(z == 3, 1, 0)

            @pl.when(hops > 0)
            def _():
                self.arrive(self.span(0, 1), 0)

            @pl.when(hops == 0)
            def _():
                self.arrive(self.span(0, 5), 0)


PART_SEMS = 24


def tok_peers(count):
    clip, tok = lax.axis_index("clip"), lax.axis_index("tok")
    return [(clip, lax.rem(tok + d, count)) for d in range(1, count)]


def all_peers(groups, members):
    clip, tok = lax.axis_index("clip"), lax.axis_index("tok")
    return [
        (lax.rem(clip + c, groups), lax.rem(tok + t, members))
        for c in range(groups) for t in range(members) if c or t
    ]


def fast_device(
    tokens,
    adapter_index,
    norm_gain,
    norm_shift,
    spatial_weights,
    spatial_output,
    temporal_weights,
    temporal_output,
    expand_weight,
    reduce_weight,
    attention_down,
    attention_up,
    expand_down,
    expand_up,
    reduce_down,
    reduce_up,
    cotangent,
):
    frames, clips, places, width = tokens.shape[1:]
    members, groups = lax.axis_size("tok"), lax.axis_size("clip")
    blocks = members // clips
    part = places // blocks
    chunk = -(-frames * part // 8) * 8
    padded = -(-places // 16) * 16
    half, total = frames * padded, clips * frames * padded
    rows_all = FRAMES * part
    ff = expand_weight.shape[1]
    sizes = (frames, clips, places, width, padded)
    to_send, from_sent, to_place, to_frame = order_tables(frames, places, padded, blocks, part, chunk)
    devices = members * groups

    def placed_rows(rows):
        return rows[0].transpose(0, 2, 1, 3)

    def whole(shard, dim):
        dims = list(shard.shape)
        dims[dim] *= devices
        return jax.ShapeDtypeStruct(tuple(dims), shard.dtype)

    any_spec, vmem_spec = pl.BlockSpec(memory_space=pl.ANY), pl.BlockSpec(memory_space=pltpu.VMEM)
    smem_spec = pl.BlockSpec(memory_space=pltpu.SMEM)
    x_view, cot_view = placed_rows(tokens), placed_rows(cotangent)
    up_rows = jnp.swapaxes(attention_up, 1, 2)
    saved = [
        shape_of(3, total, width),
        shape_of(frames * clips * HEADS // 2, 2 * padded, padded),
        shape_of(total, width),
        shape_of(4, total, ADAPT),
        shape_of(total, width),
    ]
    weights = [shape_of(4, width, width), shape_of(2 * 4, width, ADAPT)]
    scratch = [pltpu.VMEM(value.shape, value.dtype) for value in saved + weights]
    group = rows_all // 7
    tail_parts = ((0, 4), (4, 3))
    tail_rows, to_tails, from_tails = tail_tables(tail_parts, group // FRAMES, frames, places, padded, blocks, part)
    regions = []
    for rows_each in tail_rows:
        regions.append((sum(members * r for r in tail_rows[: len(regions)]), blocks * rows_each))
    blocks_shape = shape_of(total, width)
    outs = pl.pallas_call(
        functools.partial(
            front, sizes, (rows_all, group, 512, devices), members, tail_parts,
            scopes=(
                [
                    pltpu.VMEM((frames, clips, places, width), F32),
                    pltpu.VMEM((frames, clips, places, width), F32),
                    pltpu.VMEM((half, width), BF16),
                    *scratch[0:5],
                ],
                [
                    pltpu.VMEM((total, width), BF16),
                    pltpu.VMEM((total, width), BF16),
                    pltpu.VMEM((rows_all, width), BF16),
                    pltpu.VMEM((rows_all, width), F32),
                    pltpu.VMEM((rows_all, width), BF16),
                    pltpu.VMEM((rows_all, width), BF16),
                    pltpu.VMEM((3, rows_all, width), BF16),
                    pltpu.VMEM((rows_all // group * HEADS // 2, 2 * group, group), BF16),
                    pltpu.VMEM((rows_all, width), BF16),
                    pltpu.VMEM((5, rows_all, ADAPT), BF16),
                    pltpu.VMEM((rows_all, ADAPT), BF16),
                    pltpu.VMEM((rows_all, width), BF16),
                    pltpu.VMEM((rows_all, width), F32),
                    pltpu.VMEM((rows_all, width), F32),
                    pltpu.VMEM((2, rows_all, ADAPT), F32),
                    pltpu.VMEM((rows_all, width), BF16),
                    pltpu.VMEM((3, rows_all, width), BF16),
                    pltpu.VMEM((5, ADAPT, width), F32),
                    pltpu.VMEM((5, ADAPT, width), F32),
                    pltpu.VMEM((2, ADAPT, ff), F32),
                ],
            ),
        ),
        out_shape=[
            *weights, *weights, whole(expand_weight, 0), whole(reduce_weight, 0), shape_of(2, ff, ADAPT),
            shape_of(2, width, ADAPT), blocks_shape, blocks_shape, blocks_shape, blocks_shape, *saved,
            shape_of(width, 384),
        ],
        in_specs=[smem_spec] + [vmem_spec] * 5 + [any_spec] * 2 + [vmem_spec] * 2 + [any_spec] * 12,
        out_specs=[any_spec] * 17 + [vmem_spec],
        scratch_shapes=[
            *scratch[5:7],
            pltpu.VMEM((width, ff), BF16),
            pltpu.VMEM((ff, width), BF16),
            pltpu.VMEM((2, ff, ADAPT), BF16),
            pltpu.VMEM((2, width, ADAPT), BF16),
            pltpu.VMEM((members, chunk, width), BF16),
            pltpu.VMEM((members, chunk, width), BF16),
            *[pltpu.VMEM((members, rows_each, width), BF16) for rows_each in tail_rows],
            pltpu.SemaphoreType.DMA((9, PART_SEMS)),
            pltpu.SemaphoreType.DMA((30,)),
            pltpu.SemaphoreType.DMA((5, members)),
            pltpu.SemaphoreType.DMA((5, members)),
        ],
        compiler_params=pltpu.CompilerParams(collective_id=0, has_side_effects=True, vmem_limit_bytes=63 << 20),
        name="front",
    )(
        adapter_index, to_send, to_place, to_frame, *to_tails, x_view, cot_view, norm_gain, norm_shift,
        spatial_weights, spatial_output, temporal_weights, temporal_output, attention_down, up_rows,
        expand_weight, reduce_weight, expand_up.T, reduce_down, expand_down, reduce_up.T,
    )
    sp_w, sp_adapt = outs[0:2]
    made, back, *kept, mid_pay = outs[10:18]
    step = width // devices
    fold = ff // width
    results = pl.pallas_call(
        functools.partial(spatial_backward, sizes, groups, members, step, regions),
        out_shape=[
            shape_of(*x_view.shape, kind=F32),
            shape_of(*x_view.shape, kind=F32),
            shape_of(8, step, ADAPT, kind=F32),
            shape_of(8, step, ADAPT, kind=F32),
            shape_of(step, ADAPT, kind=F32),
            shape_of(fold * step, ADAPT, kind=F32),
            shape_of(fold * step, ADAPT, kind=F32),
            shape_of(step, ADAPT, kind=F32),
        ],
        in_specs=[smem_spec, vmem_spec, vmem_spec, vmem_spec] + [any_spec] * 11,
        out_specs=[any_spec] * 2 + [vmem_spec] * 6,
        scratch_shapes=[
            *scratch[5:7],
            *scratch[0:5],
            pltpu.VMEM((total, width), BF16),
            pltpu.VMEM((total, width), BF16),
            pltpu.VMEM((frames, clips, places, width), F32),
            pltpu.VMEM((frames, clips, places, width), F32),
            pltpu.VMEM((devices, step, 384), BF16),
            pltpu.VMEM((devices, step, 256), BF16),
            pltpu.VMEM((devices, step, 256), BF16),
            pltpu.VMEM((total, width), BF16),
            pltpu.VMEM((total, width), BF16),
            pltpu.VMEM((3, total, width), BF16),
            pltpu.VMEM((clips, half, width), F32),
            pltpu.VMEM((4, ADAPT, width), F32),
            pltpu.VMEM((4, ADAPT, width), F32),
            pltpu.SemaphoreType.DMA((20,)),
            pltpu.SemaphoreType.DMA((2, devices - 1)),
            pltpu.SemaphoreType.DMA((2, devices - 1)),
        ],
        compiler_params=pltpu.CompilerParams(collective_id=1, has_side_effects=True, vmem_limit_bytes=63 << 20),
        name="spatial_back",
    )(
        adapter_index, from_sent, from_tails, norm_gain, x_view, sp_w, sp_adapt, *kept, back, made,
        mid_pay.reshape(devices, step, 384),
    )
    dx, out, down, up, gea, geb, gra, grb = pl.pallas_call(
        functools.partial(deliver, len(results)),
        out_shape=[jax.ShapeDtypeStruct(value.shape, value.dtype) for value in results],
        in_specs=[any_spec] * len(results),
        out_specs=[any_spec] * len(results),
        scratch_shapes=[pltpu.VMEM(value.shape, value.dtype) for value in results]
        + [pltpu.SemaphoreType.DMA((2 * len(results),))],
        name="deliver",
    )(*results)

    def whole_rows(rows):
        return rows.transpose(0, 2, 1, 3)[None]

    return (whole_rows(out), whole_rows(dx), down, jnp.swapaxes(up, 1, 2), gea, geb.T, gra, grb.T)


def solution(mesh):
    pick = fast_device if fits(mesh) else general_device

    placed = (
        P(("clip", "tok"), None, None, None, None),
        P("clip"),
        P(),
        P(),
        P(None, ("clip", "tok"), None),
        P(("clip", "tok"), None),
        P(None, ("clip", "tok"), None),
        P(("clip", "tok"), None),
        P(("clip", "tok"), None),
        P(("clip", "tok"), None),
        P(None, ("clip", "tok"), None),
        P(None, None, ("clip", "tok")),
        P(("clip", "tok"), None),
        P(None, ("clip", "tok")),
        P(("clip", "tok"), None),
        P(None, ("clip", "tok")),
        P(("clip", "tok"), None, None, None, None),
    )
    return jax.shard_map(
        pick,
        mesh=mesh,
        in_specs=placed,
        out_specs=(
            P(("clip", "tok"), None, None, None, None),
            P(("clip", "tok"), None, None, None, None),
            P(None, ("clip", "tok"), None),
            P(None, None, ("clip", "tok")),
            P(("clip", "tok"), None),
            P(None, ("clip", "tok")),
            P(("clip", "tok"), None),
            P(None, ("clip", "tok")),
        ),
        check_vma=False,
    )
```

```python
import functools

import jax
import jax.numpy as jnp
from jax import lax
from jax.experimental import pallas as pl
from jax.experimental.pallas import tpu as pltpu
from jax.sharding import PartitionSpec as P

HEADS = 12
HEAD_DIM = 64
FRAMES = 16
ADAPTERS = 8
RANK = 16


EPSILON = 1e-06


def layer_norm(stream, gain_row, shift_row):
    average = jnp.mean(stream, axis=-1, keepdims=True)
    centred = stream - average
    variance = jnp.mean(centred * centred, axis=-1, keepdims=True)
    return centred * lax.rsqrt(variance + EPSILON) * gain_row + shift_row


def adapter_mask(choice_rows):
    columns = jnp.arange(ADAPTERS * RANK, dtype=jnp.int32) // RANK
    return (columns[None, :] == choice_rows[:, None]).astype(jnp.float32)


def project_many(inputs, weight, down_rows, up_rows, mask):
    hidden = jnp.einsum("rd,ndc->nrc", inputs, down_rows, preferred_element_type=jnp.float32)
    hidden = (hidden * mask).astype(jnp.bfloat16)
    result = jnp.einsum("rd,nde->nre", inputs, weight, preferred_element_type=jnp.float32)
    result = result + jnp.einsum(
        "nrc,nce->nre", hidden, up_rows, preferred_element_type=jnp.float32
    )
    return (result, hidden)


def project_back(inputs, hidden, grad_rows, weight, down_rows, up_rows, mask):
    hidden_grad = jnp.einsum("nre,nce->nrc", grad_rows, up_rows, preferred_element_type=jnp.float32)
    hidden_grad = (hidden_grad * mask).astype(jnp.bfloat16)
    input_grad = jnp.einsum("nre,nde->rd", grad_rows, weight, preferred_element_type=jnp.float32)
    input_grad = input_grad + jnp.einsum(
        "nrc,ndc->rd", hidden_grad, down_rows, preferred_element_type=jnp.float32
    )
    down_grad = jnp.einsum("rd,nrc->ndc", inputs, hidden_grad, preferred_element_type=jnp.float32)
    up_grad = jnp.einsum("nrc,nre->nce", hidden, grad_rows, preferred_element_type=jnp.float32)
    return (input_grad, down_grad, up_grad)


def attend_forward(packed, layout):
    view_shape, score_eq, mix_eq, back_eq = layout
    queries = packed[0].reshape(view_shape)
    key_rows = packed[1].reshape(view_shape)
    values = packed[2].reshape(view_shape)
    scores = jnp.einsum(
        score_eq, queries, key_rows, preferred_element_type=jnp.float32
    ) * HEAD_DIM ** (-0.5)
    ceiling = jnp.max(scores, axis=-1, keepdims=True)
    expo_rows = jnp.exp(scores - ceiling)
    totals = jnp.sum(expo_rows, axis=-1, keepdims=True)
    weights_soft = (expo_rows / totals).astype(jnp.bfloat16)
    mixed_rows = jnp.einsum(mix_eq, weights_soft, values, preferred_element_type=jnp.float32)
    return (mixed_rows.reshape(packed.shape[1:]), ceiling + jnp.log(totals))


def attend_backward(packed, log_total, mixed_grad, layout):
    view_shape, score_eq, mix_eq, back_eq = layout
    scaling = HEAD_DIM ** (-0.5)
    queries = packed[0].reshape(view_shape)
    key_rows = packed[1].reshape(view_shape)
    values = packed[2].reshape(view_shape)
    scores = jnp.einsum(score_eq, queries, key_rows, preferred_element_type=jnp.float32) * scaling
    weights_soft = jnp.exp(scores - log_total)
    output_grad = mixed_grad.reshape(view_shape)
    soft_grad = jnp.einsum(score_eq, output_grad, values, preferred_element_type=jnp.float32)
    row_inner = jnp.sum(weights_soft * soft_grad, axis=-1, keepdims=True)
    score_grad = (weights_soft * (soft_grad - row_inner)).astype(jnp.bfloat16)
    query_grad = (
        jnp.einsum(mix_eq, score_grad, key_rows, preferred_element_type=jnp.float32) * scaling
    )
    key_grad = (
        jnp.einsum(back_eq, score_grad, queries, preferred_element_type=jnp.float32) * scaling
    )
    value_grad = jnp.einsum(
        back_eq, weights_soft.astype(jnp.bfloat16), output_grad, preferred_element_type=jnp.float32
    )
    stacked = jnp.stack([query_grad, key_grad, value_grad])
    return stacked.reshape(packed.shape).astype(jnp.bfloat16)


def attention_forward(stream, gain_row, shift_row, weight_set, mask, layout):
    inner_weights, outer_weight, down_rows, up_rows = weight_set
    normed = layer_norm(stream, gain_row, shift_row).astype(jnp.bfloat16)
    packed, packed_hidden = project_many(normed, inner_weights, down_rows[0:3], up_rows[0:3], mask)
    packed = packed.astype(jnp.bfloat16)
    mixed_rows, log_total = attend_forward(packed, layout)
    mixed_rows = mixed_rows.astype(jnp.bfloat16)
    branch, outer_hidden = project_many(
        mixed_rows, outer_weight[None], down_rows[3:4], up_rows[3:4], mask
    )
    return (
        stream + branch[0],
        (normed, packed, packed_hidden, mixed_rows, outer_hidden, log_total),
    )


def attention_backward(
    stream, stream_grad, gain_row, shift_row, weight_set, mask, layout, kept_values
):
    inner_weights, outer_weight, down_rows, up_rows = weight_set
    normed, packed, packed_hidden, mixed_rows, outer_hidden, log_total = kept_values
    branch_grad = stream_grad.astype(jnp.bfloat16)[None]
    mixed_grad, outer_down, outer_up = project_back(
        mixed_rows,
        outer_hidden,
        branch_grad,
        outer_weight[None],
        down_rows[3:4],
        up_rows[3:4],
        mask,
    )
    packed_grad = attend_backward(packed, log_total, mixed_grad.astype(jnp.bfloat16), layout)
    normed_grad, inner_down, inner_up = project_back(
        normed, packed_hidden, packed_grad, inner_weights, down_rows[0:3], up_rows[0:3], mask
    )
    unused, norm_pull = jax.vjp(lambda rows_in: layer_norm(rows_in, gain_row, shift_row), stream)
    before_grad = stream_grad + norm_pull(normed_grad)[0]
    return (
        before_grad,
        jnp.concatenate([inner_down, outer_down], axis=0),
        jnp.concatenate([inner_up, outer_up], axis=0),
    )


def expand_forward(stream, gain_row, shift_row, weight_set, mask):
    up_weight, down_weight, in_down, in_up, out_down, out_up = weight_set
    normed = layer_norm(stream, gain_row, shift_row).astype(jnp.bfloat16)
    inner_rows, inner_hidden = project_many(
        normed, up_weight[None], in_down[None], in_up[None], mask
    )
    inner_rows = inner_rows[0]
    active = jax.nn.gelu(inner_rows, approximate=True).astype(jnp.bfloat16)
    branch, outer_hidden = project_many(
        active, down_weight[None], out_down[None], out_up[None], mask
    )
    return (stream + branch[0], (normed, inner_rows, inner_hidden, active, outer_hidden))


def expand_backward(stream, stream_grad, gain_row, shift_row, weight_set, mask, kept_values):
    up_weight, down_weight, in_down, in_up, out_down, out_up = weight_set
    normed, inner_rows, inner_hidden, active, outer_hidden = kept_values
    branch_grad = stream_grad.astype(jnp.bfloat16)[None]
    active_grad, out_down_grad, out_up_grad = project_back(
        active, outer_hidden, branch_grad, down_weight[None], out_down[None], out_up[None], mask
    )
    unused, gelu_pull = jax.vjp(
        lambda values_in: jax.nn.gelu(values_in, approximate=True), inner_rows
    )
    inner_grad = gelu_pull(active_grad)[0].astype(jnp.bfloat16)[None]
    normed_grad, in_down_grad, in_up_grad = project_back(
        normed, inner_hidden, inner_grad, up_weight[None], in_down[None], in_up[None], mask
    )
    unused_norm, norm_pull = jax.vjp(
        lambda rows_in: layer_norm(rows_in, gain_row, shift_row), stream
    )
    before_grad = stream_grad + norm_pull(normed_grad)[0]
    return (before_grad, (in_down_grad[0], in_up_grad[0], out_down_grad[0], out_up_grad[0]))


def regroup_places(stream, layout_sizes, backward):
    frames_dev, clips_dev, places, model_width, clip_rows, place_blocks, place_part = layout_sizes
    padded = jnp.pad(
        stream.reshape(frames_dev, clips_dev, places, model_width),
        ((0, 0), (0, 0), (0, place_part * place_blocks - places), (0, 0)),
    )
    padded = padded.reshape(frames_dev, clips_dev * place_blocks, place_part, model_width)
    if backward:
        arrived = lax.all_to_all(
            padded.astype(jnp.bfloat16), "tok", split_axis=1, concat_axis=0, tiled=True
        ).astype(padded.dtype)
    else:
        arrived = lax.all_to_all(
            padded.astype(jnp.bfloat16), "tok", split_axis=1, concat_axis=0, tiled=True
        ).astype(padded.dtype)
    return arrived.reshape(clip_rows * FRAMES * place_part, model_width)


def regroup_frames(stream, layout_sizes, backward):
    frames_dev, clips_dev, places, model_width, clip_rows, place_blocks, place_part = layout_sizes
    shaped = stream.reshape(clip_rows * FRAMES, 1, place_part, model_width)
    if backward:
        arrived = lax.all_to_all(
            shaped.astype(jnp.bfloat16), "tok", split_axis=0, concat_axis=1, tiled=True
        ).astype(shaped.dtype)
    else:
        arrived = lax.all_to_all(
            shaped.astype(jnp.bfloat16), "tok", split_axis=0, concat_axis=1, tiled=True
        ).astype(shaped.dtype)
    arrived = arrived.reshape(frames_dev, clips_dev, place_part * place_blocks, model_width)
    return arrived[:, :, :places].reshape(frames_dev * clips_dev * places, model_width)


def general_device(
    tokens,
    adapter_index,
    norm_gain,
    norm_shift,
    spatial_weights,
    spatial_output,
    temporal_weights,
    temporal_output,
    expand_weight,
    reduce_weight,
    attention_down,
    attention_up,
    expand_down,
    expand_up,
    reduce_down,
    reduce_up,
    cotangent,
):
    frames_dev, clips_dev, places, model_width = tokens.shape[1:]
    tok_count = lax.axis_size("tok")
    frame_blocks = FRAMES // frames_dev
    clip_rows = tok_count // frame_blocks
    place_blocks = tok_count // clips_dev
    place_part = -(-places // place_blocks)
    layout_sizes = (frames_dev, clips_dev, places, model_width, clip_rows, place_blocks, place_part)
    adapt_cols = ADAPTERS * RANK
    position = lax.axis_index("tok")
    spatial_choice = lax.dynamic_slice_in_dim(
        adapter_index, position // frame_blocks * clips_dev, clips_dev
    )
    spatial_mask = jnp.broadcast_to(
        adapter_mask(spatial_choice)[None, :, None, :], (frames_dev, clips_dev, places, adapt_cols)
    ).reshape(-1, adapt_cols)
    temporal_choice = lax.dynamic_slice_in_dim(
        adapter_index.reshape(clip_rows, clips_dev), position // place_blocks, 1, 1
    )[:, 0]
    temporal_mask = jnp.broadcast_to(
        adapter_mask(temporal_choice)[:, None, None, :], (clip_rows, FRAMES, place_part, adapt_cols)
    ).reshape(-1, adapt_cols)
    spatial_layout = (
        (frames_dev * clips_dev, places, HEADS, HEAD_DIM),
        "gqhd,gkhd->ghqk",
        "ghqk,gkhd->gqhd",
        "ghqk,gqhd->gkhd",
    )
    temporal_layout = (
        (clip_rows, FRAMES, place_part, HEADS, HEAD_DIM),
        "aqphd,akphd->aphqk",
        "aphqk,akphd->aqphd",
        "aphqk,aqphd->akphd",
    )
    spatial_set = (
        lax.all_gather(spatial_weights, ("clip", "tok"), axis=1, tiled=True),
        lax.all_gather(spatial_output, ("clip", "tok"), axis=0, tiled=True),
        lax.all_gather(attention_down[0:4], ("clip", "tok"), axis=1, tiled=True),
        lax.all_gather(attention_up[0:4], ("clip", "tok"), axis=2, tiled=True),
    )
    stream0 = tokens.reshape(-1, model_width)
    stream1, spatial_kept = attention_forward(
        stream0, norm_gain[0], norm_shift[0], spatial_set, spatial_mask, spatial_layout
    )
    placed1 = regroup_places(stream1, layout_sizes, False)
    temporal_set = (
        lax.all_gather(temporal_weights, ("clip", "tok"), axis=1, tiled=True),
        lax.all_gather(temporal_output, ("clip", "tok"), axis=0, tiled=True),
        lax.all_gather(attention_down[4:8], ("clip", "tok"), axis=1, tiled=True),
        lax.all_gather(attention_up[4:8], ("clip", "tok"), axis=2, tiled=True),
    )
    placed2, temporal_kept = attention_forward(
        placed1, norm_gain[1], norm_shift[1], temporal_set, temporal_mask, temporal_layout
    )
    stream2 = regroup_frames(placed2, layout_sizes, False)
    expand_set = (
        lax.all_gather(expand_weight, ("clip", "tok"), axis=0, tiled=True),
        lax.all_gather(reduce_weight, ("clip", "tok"), axis=0, tiled=True),
        lax.all_gather(expand_down, ("clip", "tok"), axis=0, tiled=True),
        lax.all_gather(expand_up, ("clip", "tok"), axis=1, tiled=True),
        lax.all_gather(reduce_down, ("clip", "tok"), axis=0, tiled=True),
        lax.all_gather(reduce_up, ("clip", "tok"), axis=1, tiled=True),
    )
    stream3, expand_kept = expand_forward(
        stream2, norm_gain[2], norm_shift[2], expand_set, spatial_mask
    )
    expand_set = (
        lax.all_gather(expand_weight, ("clip", "tok"), axis=0, tiled=True),
        lax.all_gather(reduce_weight, ("clip", "tok"), axis=0, tiled=True),
        lax.all_gather(expand_down, ("clip", "tok"), axis=0, tiled=True),
        lax.all_gather(expand_up, ("clip", "tok"), axis=1, tiled=True),
        lax.all_gather(reduce_down, ("clip", "tok"), axis=0, tiled=True),
        lax.all_gather(reduce_up, ("clip", "tok"), axis=1, tiled=True),
    )
    grad2, expand_grads = expand_backward(
        stream2,
        cotangent.reshape(-1, model_width),
        norm_gain[2],
        norm_shift[2],
        expand_set,
        spatial_mask,
        expand_kept,
    )
    placed_grad2 = regroup_places(grad2, layout_sizes, True)
    temporal_set = (
        lax.all_gather(temporal_weights, ("clip", "tok"), axis=1, tiled=True),
        lax.all_gather(temporal_output, ("clip", "tok"), axis=0, tiled=True),
        lax.all_gather(attention_down[4:8], ("clip", "tok"), axis=1, tiled=True),
        lax.all_gather(attention_up[4:8], ("clip", "tok"), axis=2, tiled=True),
    )
    placed_grad1, temporal_down, temporal_up = attention_backward(
        placed1,
        placed_grad2,
        norm_gain[1],
        norm_shift[1],
        temporal_set,
        temporal_mask,
        temporal_layout,
        temporal_kept,
    )
    grad1 = regroup_frames(placed_grad1, layout_sizes, True)
    spatial_set = (
        lax.all_gather(spatial_weights, ("clip", "tok"), axis=1, tiled=True),
        lax.all_gather(spatial_output, ("clip", "tok"), axis=0, tiled=True),
        lax.all_gather(attention_down[0:4], ("clip", "tok"), axis=1, tiled=True),
        lax.all_gather(attention_up[0:4], ("clip", "tok"), axis=2, tiled=True),
    )
    grad0, spatial_down, spatial_up = attention_backward(
        stream0,
        grad1,
        norm_gain[0],
        norm_shift[0],
        spatial_set,
        spatial_mask,
        spatial_layout,
        spatial_kept,
    )
    owned = (
        lax.psum_scatter(
            jnp.concatenate([spatial_down, temporal_down], axis=0),
            ("clip", "tok"),
            scatter_dimension=1,
            tiled=True,
        ),
        lax.psum_scatter(
            jnp.concatenate([spatial_up, temporal_up], axis=0),
            ("clip", "tok"),
            scatter_dimension=2,
            tiled=True,
        ),
        lax.psum_scatter(expand_grads[0], ("clip", "tok"), scatter_dimension=0, tiled=True),
        lax.psum_scatter(expand_grads[1], ("clip", "tok"), scatter_dimension=1, tiled=True),
        lax.psum_scatter(expand_grads[2], ("clip", "tok"), scatter_dimension=0, tiled=True),
        lax.psum_scatter(expand_grads[3], ("clip", "tok"), scatter_dimension=1, tiled=True),
    )
    return (
        stream3.reshape(tokens.shape),
        grad0.reshape(tokens.shape),
        owned[0],
        owned[1],
        owned[2],
        owned[3],
        owned[4],
        owned[5],
    )


F32 = jnp.float32
BF16 = jnp.bfloat16
ADAPT = ADAPTERS * RANK
SPATIAL_UNROLL = 6
SPATIAL_BACK_UNROLL = 6
MIDDLE_UNROLL = 6
MIDDLE_BACK_UNROLL = 6


def nn(left, right):
    return lax.dot_general(left, right, (((1,), (0,)), ((), ())), preferred_element_type=F32)


def nt(left, right):
    return lax.dot_general(left, right, (((1,), (1,)), ((), ())), preferred_element_type=F32)


def tn(left, right):
    return lax.dot_general(left, right, (((0,), (0,)), ((), ())), preferred_element_type=F32)


def one_hot(target_row, rows):
    row_ids = lax.broadcasted_iota(jnp.int32, (rows, target_row.shape[1]), 0)
    return (row_ids == target_row).astype(F32).astype(BF16)


def column_mask(choice):
    return (lax.broadcasted_iota(jnp.int32, (1, ADAPT), 1) // RANK == choice).astype(F32)


def set_rows(rows, choice):
    total = jnp.zeros((RANK, rows.shape[1]), F32)
    for k in range(ADAPTERS):
        total = jnp.where(choice == k, rows[k * RANK : (k + 1) * RANK], total)
    return total


def norm_rows(rows, gain_row, shift_row):
    average = jnp.mean(rows, axis=-1, keepdims=True)
    centred = rows - average
    variance = jnp.mean(centred * centred, axis=-1, keepdims=True)
    return centred * lax.rsqrt(variance + EPSILON) * gain_row + shift_row


def norm_back(rows, pulled, gain_row):
    average = jnp.mean(rows, axis=-1, keepdims=True)
    centred = rows - average
    variance = jnp.mean(centred * centred, axis=-1, keepdims=True)
    scale = lax.rsqrt(variance + EPSILON)
    unit = centred * scale
    scaled = pulled * gain_row
    return scale * (
        scaled
        - jnp.mean(scaled, axis=-1, keepdims=True)
        - unit * jnp.mean(scaled * unit, axis=-1, keepdims=True)
    )


def soften(scores, keep):
    scores = jnp.where(keep, scores, -1e30)
    ceiling = jnp.max(scores, axis=-1, keepdims=True)
    expo = jnp.exp(scores - ceiling)
    return expo * (1.0 / jnp.sum(expo, axis=-1, keepdims=True))


def two_heads(rows, low):
    zero = jnp.zeros_like(rows)
    return jnp.concatenate([jnp.where(low, rows, zero), jnp.where(low, zero, rows)], axis=0)


def one_pair(both, low):
    count = both.shape[0] // 2
    return jnp.where(low, both[:count], both[count:])


def attention_pair(query, key, value, keep, low):
    weights = soften(nt(two_heads(query, low), key), keep).astype(BF16)
    return weights, one_pair(nn(weights, value), low).astype(BF16)


def attention_all(sizes, first, qkv, soft, mixed, keep, low, unroll):
    start, blocks, rows_each, pairs = sizes

    @pl.loop(0, blocks * pairs // unroll)
    def _(turn):
        block = turn // (pairs // unroll)
        lead = (turn - block * (pairs // unroll)) * unroll
        rows = pl.ds(pl.multiple_of(start + block * rows_each, 16), rows_each)
        for u in range(unroll):
            lanes = pl.ds(pl.multiple_of((lead + u) * 128, 128), 128)
            weights, made = attention_pair(
                qkv[0, rows, lanes], qkv[1, rows, lanes], qkv[2, rows, lanes], keep, low
            )
            soft[(first + block) * pairs + lead + u] = weights
            mixed[rows, lanes] = made


def attention_all_back(sizes, qkv, soft, gmix, gqkv, low, unroll, first=0):
    blocks, rows_each, pairs = sizes

    @pl.loop(0, blocks * pairs // unroll)
    def _(turn):
        block = turn // (pairs // unroll)
        lead = (turn - block * (pairs // unroll)) * unroll
        block = block + first
        rows = pl.ds(pl.multiple_of(block * rows_each, 16), rows_each)
        spans = [pl.ds(pl.multiple_of((lead + u) * 128, 128), 128) for u in range(unroll)]
        made = attention_back(
            [[qkv[n, rows, lanes] for lanes in spans] for n in range(3)],
            [soft[block * pairs + lead + u] for u in range(unroll)],
            [gmix[rows, lanes] for lanes in spans],
            low,
        )
        for n in range(3):
            for lanes, value in zip(spans, made[n]):
                gqkv[n, rows, lanes] = value.astype(BF16)


def block_rows(ref, slots, number, offset=0):
    chunk = slots.shape[1]
    return ref.at[pl.ds(pl.multiple_of(offset + number * chunk, 8), chunk)]


def send_blocks(slots, got, count, first, send_sems, recv_sems, local_sem, offset=0):
    clip, tok = lax.axis_index("clip"), lax.axis_index("tok")
    target = block_rows(got, slots, tok, offset)
    for n in range(count):
        place = first + lax.rem(tok + n, count)

        @pl.when(place != tok)
        def _():
            remote(slots.at[place], target, send_sems.at[place], recv_sems.at[tok], (clip, place)).start()

        @pl.when(place == tok)
        def _():
            pltpu.make_async_copy(slots.at[place], target, local_sem).start()


def wait_blocks(slots, got, members, send_sems, recv_sems, local_sem, offset=0):
    tok = lax.axis_index("tok")
    for d in range(1, members):
        place = lax.rem(tok + d, members)
        target = block_rows(got, slots, place, offset)
        pltpu.make_async_copy(slots.at[place], slots.at[place], send_sems.at[place]).wait()
        pltpu.make_async_copy(target, target, recv_sems.at[place]).wait()
    pltpu.make_async_copy(slots.at[tok], block_rows(got, slots, tok, offset), local_sem).wait()


def attention_back(packed, weights, grads, low):
    queries, keys, values = packed
    stacked = [two_heads(grad, low) for grad in grads]
    pulled = [nt(grad, value) for grad, value in zip(stacked, values)]
    value_grads = [tn(soft, grad) for soft, grad in zip(weights, stacked)]
    scores = []
    for soft, pull in zip(weights, pulled):
        wide = soft.astype(F32)
        inner = jnp.sum(wide * pull, axis=-1, keepdims=True)
        scores.append((wide * (pull - inner)).astype(BF16))
    query_grads = [one_pair(nn(score, key), low) * HEAD_DIM**-0.5 for score, key in zip(scores, keys)]
    key_grads = [tn(score, two_heads(query, low)) for score, query in zip(scores, queries)]
    return query_grads, key_grads, value_grads


def spatial_backward(
    sizes, groups, members, step, regions, idx, from_sent, from_tails, gain, x_hbm, w_hbm, ad_hbm, qkv_hbm, soft_hbm, mixed_hbm, hid_hbm, zs_hbm,
    got_hbm, made_hbm, mid_pay,
    dx_hbm, out_hbm, down_out, up_out, ea, eb, ra, rb,
    w, ad, qkv, soft, mixed, hid, zs, got, made, x, out, mid, sp, pay, sp_late, pay_late, grad, gmix, gqkv, gpull, gdown, gup, copy_sems, send_sems, recv_sems
):
    frames, clips, places, width, padded = sizes
    half = frames * padded
    devices = groups * members

    def row_copies(view, rows, first, inward):
        copies = []
        for i in range(frames):
            for b in range(clips):
                ends = (view.at[i, :, b, :], rows.at[i, b])
                ends = ends if inward else ends[::-1]
                copies.append(pltpu.make_async_copy(*ends, copy_sems.at[first + i * clips + b]))
        return copies

    fills = [
        pltpu.make_async_copy(source, target, copy_sems.at[10 + n])
        for n, (source, target) in enumerate(
            (
                (got_hbm, got), (w_hbm.at[3], w.at[3]), (ad_hbm, ad), (mixed_hbm, mixed), (hid_hbm, hid),
                (soft_hbm, soft), (qkv_hbm, qkv), (w_hbm.at[0:3], w.at[0:3]), (zs_hbm, zs), (made_hbm, made),
            )
        )
    ]
    loads = row_copies(x_hbm, x, 0, True)
    for load in fills + loads:
        load.start()
    clip, tok = lax.axis_index("clip"), lax.axis_index("tok")
    me = clip * members + tok
    peers = all_peers(groups, members)
    greet(peers)

    def terms(source, target, kind):
        for n, peer in enumerate(peers):
            place = peer[0] * members + peer[1]
            remote(
                source.at[place], target.at[me], send_sems.at[kind, n], recv_sems.at[kind, n], peer
            ).start()
        pltpu.make_async_copy(source.at[me], target.at[me], copy_sems.at[(8, 9, 20)[kind]]).start()

    def await_terms(source, target, kind):
        for n, peer in enumerate(peers):
            remote(source.at[me], target.at[me], send_sems.at[kind, n], recv_sems.at[kind, n], peer).wait()
        pltpu.make_async_copy(source.at[me], target.at[me], copy_sems.at[(8, 9, 20)[kind]]).wait()

    terms(mid_pay, mid, 0)
    for fill in fills[0:5]:
        fill.wait()
    for b in range(clips):
        rows = slice(b * half, (b + 1) * half)
        mask = column_mask(idx[b])
        arrived = []
        for begin, size in regions:
            arrived.append(got[begin + b * size : begin + (b + 1) * size])
        grad[rows] = nn(one_hot(from_tails[...], half), jnp.concatenate(arrived, axis=0)).astype(BF16)
        hidden_grad = (nn(grad[rows], ad[7]) * mask).astype(BF16)
        gmix[rows] = (nt(grad[rows], w[3]) + nt(hidden_grad, ad[3])).astype(BF16)
        down, up = tn(hidden_grad, mixed[rows]), tn(hid[3, rows], grad[rows])
        if b == 0:
            gdown[3], gup[3] = down, up
        else:
            gdown[3] += down
            gup[3] += up

    pairs = width // 128
    low = lax.broadcasted_iota(jnp.int32, (padded, 128), 1) < HEAD_DIM

    for fill in fills[5:7]:
        fill.wait()
    attention_all_back((frames * clips, padded, pairs), qkv, soft, gmix, gqkv, low, SPATIAL_BACK_UNROLL)
    for fill in fills[7:10]:
        fill.wait()
    repeat = jnp.where(idx[0] == idx[1], 0.0, 1.0)

    def pull_back(n, b, fresh):
        rows = slice(b * half, (b + 1) * half)
        own = gqkv[n, rows]
        hidden_grad = (nn(own, ad[4 + n]) * column_mask(idx[b])).astype(BF16)
        pulled = nt(own, w[n]) + nt(hidden_grad, ad[n])
        gpull[b] = pulled if fresh else gpull[b] + pulled
        down, up = tn(hidden_grad, zs[rows]), tn(hid[n, rows], own)
        if b == 0:
            gdown[n], gup[n] = down, up
        else:
            gdown[n] += down
            gup[n] += up

    def send_pair(first, pay, sp, kind):
        pieces = []
        for n in (first, first + 1):
            for source in (gdown, gup):
                pieces.append(set_rows(source[n], idx[0]))
                pieces.append(set_rows(source[n], idx[1]) * repeat)
        packed = jnp.transpose(jnp.concatenate(pieces, axis=0))
        pay[...] = packed.reshape(pay.shape).astype(BF16)
        terms(pay, sp, kind)

    for b in range(clips):
        pull_back(2, b, True)
    send_pair(2, pay_late, sp_late, 1)
    for b in range(clips):

        @pl.loop(0, 2)
        def _(n):
            pull_back(n, b, False)

    send_pair(0, pay, sp, 2)
    for load in loads:
        load.wait()
    for b in range(clips):
        rows = slice(b * half, (b + 1) * half)
        final = nn(one_hot(from_sent[...], half), made[rows])
        for i in range(frames):
            base = i * padded
            out[i, b] = final[base : base + places]
            pulled = norm_back(x[i, b], gpull[b, base : base + places], gain[0:1])
            x[i, b] = grad[b * half + base : b * half + base + places].astype(F32) + pulled
    stores = row_copies(out_hbm, out, 4, False) + row_copies(dx_hbm, x, 0, False)
    for store in stores:
        store.start()
    await_terms(mid_pay, mid, 0)
    mids, mid_choice = combine_mid((groups, members, step, eb.shape[0] // step), mid, down_out, up_out, ea, eb, ra, rb)
    await_terms(pay_late, sp_late, 1)
    combine_spatial((groups, members, step), sp_late, mids, down_out, up_out, 2)
    await_terms(pay, sp, 2)
    combine_spatial((groups, members, step), sp, mids, down_out, up_out, 0)
    for store in stores:
        store.wait()


def front(
    sizes, shape, members, tail_parts, idx, to_send, to_place, to_frame, to_first, to_second, x_hbm, cot_hbm, gain, shift,
    sh_w, sh_o, sh_tw, sh_to, sh_down, sh_up, sh_we, sh_wr, sh_eup, sh_rdown, sh_edown, sh_rup,
    all_w, all_ad, all_tw, all_tad, all_we, all_wr, all_tall, all_flat, got_hbm, cot_got, made, back,
    qkv_hbm, soft_hbm, mixed_hbm, hid_hbm, zs_hbm, pay,
    w, ad, we, wr, tall, flat, slots, cots, tail_one, tail_two, sems, copy_sems, send_sems, recv_sems, *, scopes
):
    frames, clips, places, width, padded = sizes
    rows_all, group, ff_chunk, owners = shape
    chunk = slots.shape[1]
    tails, to_tails = (tail_one, tail_two), (to_first, to_second)
    half = frames * padded
    share = members // clips
    clip, tok = lax.axis_index("clip"), lax.axis_index("tok")
    parts = [
        Part([(sh_w.at[0:2], None)], all_w.at[0:2], 1, sems.at[0]),
        Part([(sh_w.at[2], 0), (sh_o, 1)], all_w.at[2:4], 1, sems.at[1]),
        Part([(sh_down.at[0:4], slice(0, 4)), (sh_up.at[0:4], slice(4, 8))], all_ad, 1, sems.at[2]),
        Part([(sh_tw, slice(0, 3)), (sh_to, 3)], all_tw, 1, sems.at[3]),
        Part([(sh_down.at[4:8], slice(0, 4)), (sh_up.at[4:8], slice(4, 8))], all_tad, 1, sems.at[4]),
        Part([(sh_we, None)], all_we, 0, sems.at[5]),
        Part([(sh_wr, None)], all_wr, 0, sems.at[6]),
        Part([(sh_eup, 0), (sh_rdown, 1)], all_tall, 1, sems.at[7]),
        Part([(sh_edown, 0), (sh_rup, 1)], all_flat, 1, sems.at[8]),
    ]
    y, core, z, across = place_of()
    greet(tok_peers(members) + [device_at(1 - y, core, z, across), device_at(y, 1 - core, z, across)])

    def stages(plan):
        for step in range(0, len(plan), 2):
            parts["ABCDEFGHI".index(plan[step])].stage(int(plan[step + 1]))

    def exchange_sems(n):
        return send_sems.at[n], recv_sems.at[n], copy_sems.at[25 + n]

    temporal_loads = [
        pltpu.make_async_copy(all_tw, w, copy_sems.at[2]), pltpu.make_async_copy(all_tad, ad, copy_sems.at[3])
    ]
    loads = [
        pltpu.make_async_copy(source, target, copy_sems.at[n])
        for n, (source, target) in zip((0, 1, 5, 6), ((all_wr, wr), (all_tall, tall), (all_flat, flat), (all_we, we)))
    ]
    stages("A0B0C0")

    def spatial_phase(x, cot, stream, qkv, soft, mixed, hid, zs):
        load_cot = row_loads(cot_hbm, cot, 21, frames, clips, copy_sems)
        load_x = row_loads(x_hbm, x, 17, frames, clips, copy_sems)
        for load in load_cot + load_x:
            load.start()
        pads = slice(padded - 16, padded)
        for i in range(frames):
            stream[i * padded + padded - 16 : (i + 1) * padded] = jnp.zeros((16, width), BF16)
        for load in load_cot:
            load.wait()
        for b in range(clips):
            for i in range(frames):
                stream[i * padded : i * padded + places] = cot[i, b].astype(BF16)
            rows = nn(one_hot(to_send[...], half), stream[...])
            cots[b * share : (b + 1) * share] = rows.reshape(share, chunk, width).astype(BF16)
        stages("A1B1A2C1B2A3")
        for load in load_x:
            load.wait()
        for b in range(clips):
            for i in range(frames):
                base = b * half + i * padded
                zs[base + padded - 16 : base + padded] = jnp.zeros((16, width), BF16)
                zs[base : base + places] = norm_rows(
                    x[i, b], gain[0:1], shift[0:1]
                ).astype(BF16)
        stages("C2B3C3D0E0A4B4C4")
        stages("D1E1A5B5C5A6B6C6")
        loads = [pltpu.make_async_copy(all_w, w, copy_sems.at[2]), pltpu.make_async_copy(all_ad, ad, copy_sems.at[3])]
        for load in loads:
            load.start()
        stages("D2E2F0G0H0I0")
        for load in loads:
            load.wait()

        keep = lax.broadcasted_iota(jnp.int32, (2 * padded, padded), 1) < places
        pairs = width // 128
        low = lax.broadcasted_iota(jnp.int32, (padded, 128), 1) < HEAD_DIM
        far = jnp.where(tok < share, 1, 0)
        for turn in range(clips):
            b = far if turn == 0 else 1 - far
            rows = pl.ds(pl.multiple_of(b * half, 16), half)
            mask = column_mask(idx[b])

            @pl.loop(0, 3)
            def _(n):
                hidden = (nn(zs[rows], ad[n]) * mask).astype(BF16)
                hid[n, rows] = hidden
                result = nn(zs[rows], w[n]) + nt(hidden, ad[4 + n])
                result = result * jnp.where(n == 0, HEAD_DIM**-0.5, 1.0)
                qkv[n, rows] = result.astype(BF16)

            stages("D3E3F1G1H1I1" if turn == 0 else "D5E5F4")

            attention_all(
                (b * half, frames, padded, pairs), b * frames, qkv, soft, mixed, keep, low, SPATIAL_UNROLL
            )
            if turn == 0:
                stages("D4E4F2G2H2I2")
            hidden = (nn(mixed[rows], ad[3]) * mask).astype(BF16)
            hid[3, rows] = hidden
            branch = nn(mixed[rows], w[3]) + nt(hidden, ad[7])
            for i in range(frames):
                stream[i * padded : i * padded + places] = (
                    x[i, b] + branch[i * padded : i * padded + places]
                ).astype(BF16)
            made = nn(one_hot(to_send[...], half), stream[...]).reshape(share, chunk, width)
            slots[pl.ds(b * share, share)] = made.astype(BF16)
            send_blocks(slots, got_hbm, share, b * share, *exchange_sems(0))
            if turn == 0:
                stages("F3G3H3I3")
        stores = [
            pltpu.make_async_copy(source, target, copy_sems.at[12 + n])
            for n, (source, target) in enumerate(
                ((qkv, qkv_hbm), (soft, soft_hbm), (mixed, mixed_hbm), (hid, hid_hbm), (zs, zs_hbm))
            )
        ]
        for store in stores:
            store.start()
        stages("D6E6")
        for load in temporal_loads:
            load.start()
        for store in stores:
            store.wait()

    def middle_phase(
        got, cot, x1, x2, zt, ze, qkv, soft, mixed, hid, hide, gy, acc, pull, ghe, gmix, gqkv, gdown, gup, wide
    ):
        choice = idx[tok // share]
        mask = column_mask(choice)
        groups = rows_all // group
        wait_blocks(slots, got_hbm, members, *exchange_sems(0))
        send_blocks(cots, cot_got, members, 0, *exchange_sems(1))
        load_got = pltpu.make_async_copy(got_hbm, got, copy_sems.at[4])
        load_got.start()
        load_got.wait()

        @pl.loop(0, groups)
        def _(j):
            rows = pl.ds(pl.multiple_of(j * group, 16), group)
            own = nn(one_hot_rows(to_place[...], group, j * group), got[...])
            x1[rows] = own.astype(BF16)
            zt[rows] = norm_rows(own, gain[1:2], shift[1:2]).astype(BF16)

        for load in temporal_loads:
            load.wait()

        @pl.loop(0, 3)
        def _(n):
            hidden = (nn(zt[...], ad[n]) * mask).astype(BF16)
            hid[n] = hidden
            result = nn(zt[...], w[n]) + nt(hidden, ad[4 + n])
            result = result * jnp.where(n == 0, HEAD_DIM**-0.5, 1.0)
            qkv[n] = result.astype(BF16)

        stages("F5G4H4I4")

        pairs = width // 128
        keep = (
            lax.rem(lax.broadcasted_iota(jnp.int32, (2 * group, group), 0), group) // FRAMES
            == lax.broadcasted_iota(jnp.int32, (2 * group, group), 1) // FRAMES
        )
        low = lax.broadcasted_iota(jnp.int32, (group, 128), 1) < HEAD_DIM

        attention_all((0, groups, group, pairs), 0, qkv, soft, mixed, keep, low, MIDDLE_UNROLL)
        stages("F6G5H5I5")
        loads[3].start()
        hidden = (nn(mixed[...], ad[3]) * mask).astype(BF16)
        hid[3] = hidden
        acc[...] = nn(mixed[...], w[3]) + nt(hidden, ad[7])

        @pl.loop(0, groups)
        def _(j):
            rows = pl.ds(pl.multiple_of(j * group, 16), group)
            own = x1[rows].astype(F32) + acc[rows]
            x2[rows] = own
            acc[rows] = own
            pull[rows] = jnp.zeros((group, width), F32)
            ze[rows] = norm_rows(own, gain[2:3], shift[2:3]).astype(BF16)

        stages("G6H6I6")
        for load in loads[0:3]:
            load.start()
        wait_blocks(cots, cot_got, members, *exchange_sems(1))
        load_cot = pltpu.make_async_copy(cot_got, cot, copy_sems.at[4])
        load_cot.start()
        load_cot.wait()

        @pl.loop(0, groups)
        def _(j):
            rows = pl.ds(pl.multiple_of(j * group, 16), group)
            gy[rows] = nn(one_hot_rows(to_place[...], group, j * group), cot[...]).astype(BF16)

        for load in loads:
            load.wait()
        hide[...] = (nn(ze[...], flat[0]) * mask).astype(BF16)
        ghr = (nn(gy[...], flat[1]) * mask).astype(BF16)
        hid[0 + 4] = ghr
        ghe[...] = jnp.zeros(ghe.shape, F32)

        @pl.loop(0, we.shape[1] // ff_chunk)
        def _(c):
            part = pl.ds(pl.multiple_of(c * ff_chunk, ff_chunk), ff_chunk)
            inner = nn(ze[...], we[:, part]) + nt(hide[...], tall[0, part])
            cube = 0.7978845608028654 * (inner + 0.044715 * inner * inner * inner)
            bend = jnp.tanh(cube)
            act = (0.5 * inner * (1.0 + bend)).astype(BF16)
            slope = 0.5 * (1.0 + bend) + 0.5 * inner * (1.0 - bend * bend) * (
                0.7978845608028654 * (1.0 + 3.0 * 0.044715 * inner * inner)
            )
            acc[...] += nn(act, wr[part])
            ghe[0] += nn(act, tall[1, part])
            wide[0, :, part] = tn(hid[4], act)
            gact = nt(gy[...], wr[part]) + nt(hid[4], tall[1, part])
            ginner = (gact * slope).astype(BF16)
            pull[...] += nt(ginner, we[:, part])
            ghe[1] += nn(ginner, tall[0, part])
            wide[1, :, part] = tn(hide[...], ginner)

        hidr = (ghe[0] * mask).astype(BF16)
        acc[...] += nt(hidr, flat[1])
        rows = nn(one_hot(to_frame[...], got.shape[0]), acc[...].astype(BF16))
        slots[...] = rows.reshape(slots.shape).astype(BF16)
        send_blocks(slots, made, members, 0, *exchange_sems(2))
        gdown[4] = tn(hidr, gy[...])
        gheb = (ghe[1] * mask).astype(BF16)
        gup[4] = tn(gheb, ze[...])
        pull[...] += nt(gheb, flat[0])

        @pl.loop(0, groups)
        def _(j):
            rows = pl.ds(pl.multiple_of(j * group, 16), group)
            own = gy[rows].astype(F32) + norm_back(x2[rows], pull[rows], gain[2:3])
            acc[rows] = own
            ze[rows] = own.astype(BF16)

        grad = ze
        hidden_grad = (nn(grad[...], ad[7]) * mask).astype(BF16)
        gmix[...] = (nt(grad[...], w[3]) + nt(hidden_grad, ad[3])).astype(BF16)
        gdown[3] = tn(hidden_grad, mixed[...])
        gup[3] = tn(hid[3], grad[...])

        offset = 0
        for turn, (first, count) in enumerate(tail_parts):
            lines = slice(first * group, (first + count) * group)
            attention_all_back(
                (count, group, pairs), qkv, soft, gmix, gqkv, low, MIDDLE_BACK_UNROLL, first
            )
            pull[lines] = jnp.zeros((count * group, width), F32)

            @pl.loop(0, 3)
            def _(n):
                own = gqkv[n, lines]
                hidden_grad = (nn(own, ad[4 + n]) * mask).astype(BF16)
                pull[lines] += nt(own, w[n]) + nt(hidden_grad, ad[n])
                down, up = tn(hidden_grad, zt[lines]), tn(hid[n, lines], own)
                if turn == 0:
                    gdown[n], gup[n] = down, up
                else:
                    gdown[n] += down
                    gup[n] += up

            @pl.loop(first, first + count)
            def _(j):
                rows = pl.ds(pl.multiple_of(j * group, 16), group)
                own = acc[rows] + norm_back(x1[rows].astype(F32), pull[rows], gain[1:2])
                ze[rows] = own.astype(BF16)

            tail = tails[turn]
            made_rows = nn(one_hot(to_tails[turn][...], members * tail.shape[1]), ze[lines])
            tail[...] = made_rows.reshape(tail.shape).astype(BF16)
            send_blocks(tail, back, members, 0, *exchange_sems(3 + turn), offset)
            offset += members * tail.shape[1]

        pieces = []
        for n in range(4):
            pieces += [set_rows(gdown[n], choice), set_rows(gup[n], choice)]
        pay[:, 0:128] = jnp.transpose(jnp.concatenate(pieces, axis=0)).astype(BF16)
        line = lax.broadcasted_iota(jnp.int32, (128 - 2 * RANK, width), 0)
        blank = jnp.zeros((128 - 2 * RANK, width), F32)
        for k, number in enumerate((choice, idx[0], idx[1])):
            blank = jnp.where(line == k, number.astype(F32), blank)
        pay[:, 128:256] = jnp.transpose(
            jnp.concatenate([set_rows(gup[4], choice), set_rows(gdown[4], choice), blank], axis=0)
        ).astype(BF16)
        high = jnp.concatenate(
            [set_rows(wide[1], choice), set_rows(wide[0], choice), jnp.zeros((128 - 2 * RANK, we.shape[1]), F32)], axis=0
        )
        high = jnp.transpose(high)
        step = width // owners
        fold = we.shape[1] // width
        high = high.reshape(owners, fold, step, 128)
        total = high[:, 0].reshape(width, 128)
        for f in range(1, fold):
            total += pltpu.roll(high[:, f].reshape(width, 128), 2 * RANK * f, 1)
        pay[:, 256:384] = total.astype(BF16)
        wait_blocks(slots, made, members, *exchange_sems(2))
        offset = 0
        for turn, tail in enumerate(tails):
            wait_blocks(tail, back, members, *exchange_sems(3 + turn), offset)
            offset += members * tail.shape[1]

    pl.run_scoped(spatial_phase, *scopes[0])
    pl.run_scoped(middle_phase, *scopes[1])


def deliver(count, *refs):
    sources, targets, held, sems = refs[:count], refs[count : 2 * count], refs[2 * count : 3 * count], refs[3 * count]
    loads = [pltpu.make_async_copy(sources[n], held[n], sems.at[n]) for n in range(count)]
    for load in loads:
        load.start()
    stores = [pltpu.make_async_copy(held[n], targets[n], sems.at[n + count]) for n in range(count)]
    for load, store in zip(loads, stores):
        load.wait()
        store.start()
    for store in stores:
        store.wait()


def row_loads(source, target, first, frames, clips, sems):
    return [
        pltpu.make_async_copy(source.at[i, :, b, :], target.at[i, b], sems.at[first + i * clips + b])
        for i in range(frames) for b in range(clips)
    ]


def one_hot_rows(target_row, rows, first):
    row_ids = lax.broadcasted_iota(jnp.int32, (rows, target_row.shape[1]), 0) + first
    return (row_ids == target_row).astype(F32).astype(BF16)


def spread_sum(stack, columns, first, choice, count):
    lanes = lax.broadcasted_iota(jnp.int32, (columns, ADAPT), 1)
    lines = lax.broadcasted_iota(jnp.int32, (columns, ADAPT), 0)
    spread = (lines == first + lanes % RANK).astype(F32)
    wide = lax.dot_general(
        stack, spread, (((1,), (0,)), ((), ())),
        preferred_element_type=F32, precision=lax.Precision.HIGHEST,
    )
    sets = lax.broadcasted_iota(jnp.int32, (1, ADAPT), 1) // RANK
    kept = jnp.where(sets.astype(F32) == choice, wide, 0.0)
    step = stack.shape[0] // count
    total = kept[0:step]
    for k in range(1, count):
        total += kept[k * step : (k + 1) * step]
    return total


def combine_mid(sizes, got, down, up, ea, eb, ra, rb):
    groups, members, step, fold = sizes
    clips = 2
    share = members // clips
    mids = []
    for g in range(groups):
        for b in range(clips):
            part = jnp.zeros((step, 384), F32)
            for t in range(share):
                part += got[g * members + b * share + t].astype(F32)
            mids.append(part)
    mid = jnp.concatenate(mids, axis=0)
    choice = mid[:, 160:161] * (1.0 / share)
    count = groups * clips
    for n in range(4):
        for s, target in enumerate((down, up)):
            target[4 + n] = spread_sum(mid[:, 0:128], 128, (2 * n + s) * RANK, choice, count)
    ea[...] = spread_sum(mid[:, 128:256], 128, 0, choice, count)
    rb[...] = spread_sum(mid[:, 128:256], 128, RANK, choice, count)
    for f in range(fold):
        rows = slice(f * step, (f + 1) * step)
        eb[rows] = spread_sum(mid[:, 256:384], 128, 2 * RANK * f, choice, count)
        ra[rows] = spread_sum(mid[:, 256:384], 128, 2 * RANK * f + RANK, choice, count)
    choices = [
        jnp.concatenate([mids[g * clips][:, 161 + b : 162 + b] * (1.0 / share) for g in range(groups)], axis=0)
        for b in range(clips)
    ]
    return choices, choice


def combine_spatial(sizes, got, choices, down, up, first):
    groups, members, step = sizes
    clips = len(choices)
    sums = []
    for g in range(groups):
        total = jnp.zeros((step, 128), F32)
        for t in range(members):
            total += got[g * members + t].astype(F32)
        sums.append(total)
    stack = jnp.concatenate(sums, axis=0)
    for n in range(2):
        for s, target in enumerate((down, up)):
            total = jnp.zeros((step, ADAPT), F32)
            for b in range(clips):
                total += spread_sum(stack, 128, ((2 * n + s) * clips + b) * RANK, choices[b], groups)
            target[first + n] = total


def shape_of(*dims, kind=BF16):
    return jax.ShapeDtypeStruct(dims, kind)


def order_tables(frames, places, padded, blocks, part, chunk):
    half_rows, sent_rows = frames * padded, blocks * chunk
    assert half_rows == sent_rows
    to_send = [-1] * half_rows
    from_sent = [-1] * sent_rows
    for i in range(frames):
        for p in range(places):
            source, target = i * padded + p, (p // part) * chunk + i * part + p % part
            to_send[source] = target
            from_sent[target] = source
    senders = FRAMES // frames
    to_place = [-1] * (senders * chunk)
    to_frame = [-1] * (part * FRAMES)
    for p in range(part):
        for f in range(FRAMES):
            source, target = (f // frames) * chunk + (f % frames) * part + p, p * FRAMES + f
            to_place[source] = target
            to_frame[target] = source
    return [jnp.array([table], jnp.int32) for table in (to_send, from_sent, to_place, to_frame)]


def tail_tables(parts, each, frames, places, padded, blocks, part):
    rows, to_parts, region = [], [], 0
    from_parts = []
    for first, count in parts:
        own = count * each
        size = -(-frames * own // 8) * 8
        rows.append(size)
        table = [-1] * (own * FRAMES)
        for p in range(own):
            for f in range(FRAMES):
                table[p * FRAMES + f] = (f // frames) * size + (f % frames) * own + p
        to_parts.append(jnp.array([table], jnp.int32))
        source = [-1] * (blocks * size)
        for block in range(blocks):
            for f in range(frames):
                for p in range(own):
                    source[block * size + f * own + p] = f * padded + block * part + first * each + p
        from_parts += source
    return rows, to_parts, jnp.array([from_parts], jnp.int32)


def fits(mesh):
    return mesh.shape["tok"] == 8 and mesh.shape["clip"] == 4


MESH = pl.DeviceIdType.MESH


def place_of():
    clip, tok = lax.axis_index("clip"), lax.axis_index("tok")
    return clip // 2, lax.rem(clip, 2), tok // 2, lax.rem(tok, 2)


def device_at(y, core, z, x):
    return (y * 2 + core, z * 2 + x)


def greet(peers):
    barrier = pltpu.get_barrier_semaphore()
    for peer in peers:
        pl.semaphore_signal(barrier, inc=1, device_id=peer, device_id_type=MESH)
    pl.semaphore_wait(barrier, len(peers))


def remote(source, target, send_sem, recv_sem, peer):
    return pltpu.make_async_remote_copy(
        src_ref=source, dst_ref=target, send_sem=send_sem, recv_sem=recv_sem, device_id=peer, device_id_type=MESH
    )


class Part:
    def __init__(self, pieces, whole, dim, sems):
        self.pieces, self.whole, self.dim, self.sems = pieces, whole, dim, sems
        self.rows = whole.shape[dim] // (lax.axis_size("clip") * lax.axis_size("tok"))
        self.me = place_of()
        for piece, target in self.own():
            pltpu.make_async_copy(piece, target, sems.at[1]).start()

    def own(self):
        target = self.slot(*self.me)
        return [(piece, target if index is None else target.at[index]) for piece, index in self.pieces]

    def span(self, first, count, half=None):
        rows = pl.ds(pl.multiple_of(first * self.rows, 8), count * self.rows)
        if self.dim == 1:
            lead = max(self.whole.shape[0] * 3 // 4, 1)
            front = (slice(None), slice(0, lead), slice(lead, None))[0 if half is None else half + 1]
            return self.whole.at[front, rows]
        lanes = self.whole.shape[1] * 3 // 512 * 128
        return self.whole.at[rows, (slice(None), slice(0, lanes), slice(lanes, None))[0 if half is None else half + 1]]

    def slot(self, y, core, z, x, half=None):
        clip, tok = device_at(y, core, z, x)
        return self.span(clip * 8 + tok, 1, half)

    def send(self, source, target, sem, peer):
        remote(source, target, self.sems.at[0], self.sems.at[sem], device_at(*peer)).start()

    def arrive(self, target, sem):
        pltpu.make_async_copy(target, target, self.sems.at[sem]).wait()

    def pass_on(self, far, sources=None):
        y, core, z, x = self.me
        owner = (y, core, far, x)
        target = self.slot(*owner)
        for source, target in sources or [(target, target)]:
            self.send(source, target, 8 + far, (y, core, z, 1 - x))
            self.send(source, target, 12 + far, (1 - y, core, z, x))
            self.send(source, target, 2 + y, (y, 1 - core, z, x))

    def to_core(self, owner):
        y, core, z, x = self.me
        target = self.slot(*owner)
        self.send(target, target, 2 + owner[0], (y, 1 - core, z, x))

    def hop(self, far, up, sources=None):
        y, core, z, x = self.me
        target = self.slot(y, core, far, x)
        for source, target in sources or [(target, target)]:
            self.send(source, target, 4 + far, (y, core, z + up, x))

    def relay(self, distance, up):
        y, core, z, x = self.me
        far = z - distance * up
        here = z >= distance if up > 0 else z <= 3 - distance
        on = z < 3 if up > 0 else z > 0

        @pl.when(here)
        def _():
            self.arrive(self.slot(y, core, far, x), 4 + far)

            @pl.when(on)
            def _():
                self.hop(far, up)

            self.pass_on(far)

    def stage(self, number):
        y, core, z, x = self.me
        if number == 0:
            own = self.own()

            @pl.when(z < 3)
            def _():
                self.hop(z, 1, own)

            @pl.when(z > 0)
            def _():
                self.hop(z, -1, own)

            self.pass_on(z, own)
        elif number <= 3:
            self.relay(number, 1)
            self.relay(number, -1)
        elif number == 4:
            for d in range(4):
                far = lax.rem(z + 4 - d, 4)
                owner = (y, core, far, 1 - x)
                self.arrive(self.slot(*owner), 8 + far)
                self.send(self.slot(*owner, 0), self.slot(*owner, 0), 16 + far, (1 - y, core, z, x))
                self.to_core(owner)
                owner = (1 - y, core, far, x)
                self.arrive(self.slot(*owner), 12 + far)
                self.send(self.slot(*owner, 1), self.slot(*owner, 1), 20 + far, (y, core, z, 1 - x))
                self.to_core(owner)
        elif number == 5:
            for d in range(4):
                far = lax.rem(z + 4 - d, 4)
                owner = (1 - y, core, far, 1 - x)
                self.arrive(self.slot(*owner, 0), 16 + far)
                self.arrive(self.slot(*owner, 1), 20 + far)
                self.to_core(owner)
        else:
            self.arrive(self.slot(*self.me), 1)
            for far in range(2):
                self.arrive(self.span((far * 2 + 1 - core) * 8, 8), 2 + far)
            self.arrive(self.span(0, 28), 0)
            hops = jnp.where(z == 0, 1, 0) + jnp.where(z == 3, 1, 0)

            @pl.when(hops > 0)
            def _():
                self.arrive(self.span(0, 1), 0)

            @pl.when(hops == 0)
            def _():
                self.arrive(self.span(0, 5), 0)


PART_SEMS = 24


def tok_peers(count):
    clip, tok = lax.axis_index("clip"), lax.axis_index("tok")
    return [(clip, lax.rem(tok + d, count)) for d in range(1, count)]


def all_peers(groups, members):
    clip, tok = lax.axis_index("clip"), lax.axis_index("tok")
    return [
        (lax.rem(clip + c, groups), lax.rem(tok + t, members))
        for c in range(groups) for t in range(members) if c or t
    ]


def fast_device(
    tokens,
    adapter_index,
    norm_gain,
    norm_shift,
    spatial_weights,
    spatial_output,
    temporal_weights,
    temporal_output,
    expand_weight,
    reduce_weight,
    attention_down,
    attention_up,
    expand_down,
    expand_up,
    reduce_down,
    reduce_up,
    cotangent,
):
    frames, clips, places, width = tokens.shape[1:]
    members, groups = lax.axis_size("tok"), lax.axis_size("clip")
    blocks = members // clips
    part = places // blocks
    chunk = -(-frames * part // 8) * 8
    padded = -(-places // 16) * 16
    half, total = frames * padded, clips * frames * padded
    rows_all = FRAMES * part
    ff = expand_weight.shape[1]
    sizes = (frames, clips, places, width, padded)
    to_send, from_sent, to_place, to_frame = order_tables(frames, places, padded, blocks, part, chunk)
    devices = members * groups

    def placed_rows(rows):
        return rows[0].transpose(0, 2, 1, 3)

    def whole(shard, dim):
        dims = list(shard.shape)
        dims[dim] *= devices
        return jax.ShapeDtypeStruct(tuple(dims), shard.dtype)

    any_spec, vmem_spec = pl.BlockSpec(memory_space=pl.ANY), pl.BlockSpec(memory_space=pltpu.VMEM)
    smem_spec = pl.BlockSpec(memory_space=pltpu.SMEM)
    x_view, cot_view = placed_rows(tokens), placed_rows(cotangent)
    up_rows = jnp.swapaxes(attention_up, 1, 2)
    saved = [
        shape_of(3, total, width),
        shape_of(frames * clips * HEADS // 2, 2 * padded, padded),
        shape_of(total, width),
        shape_of(4, total, ADAPT),
        shape_of(total, width),
    ]
    weights = [shape_of(4, width, width), shape_of(2 * 4, width, ADAPT)]
    scratch = [pltpu.VMEM(value.shape, value.dtype) for value in saved + weights]
    group = rows_all // 7
    tail_parts = ((0, 4), (4, 3))
    tail_rows, to_tails, from_tails = tail_tables(tail_parts, group // FRAMES, frames, places, padded, blocks, part)
    regions = []
    for rows_each in tail_rows:
        regions.append((sum(members * r for r in tail_rows[: len(regions)]), blocks * rows_each))
    blocks_shape = shape_of(total, width)
    outs = pl.pallas_call(
        functools.partial(
            front, sizes, (rows_all, group, 512, devices), members, tail_parts,
            scopes=(
                [
                    pltpu.VMEM((frames, clips, places, width), F32),
                    pltpu.VMEM((frames, clips, places, width), F32),
                    pltpu.VMEM((half, width), BF16),
                    *scratch[0:5],
                ],
                [
                    pltpu.VMEM((total, width), BF16),
                    pltpu.VMEM((total, width), BF16),
                    pltpu.VMEM((rows_all, width), BF16),
                    pltpu.VMEM((rows_all, width), F32),
                    pltpu.VMEM((rows_all, width), BF16),
                    pltpu.VMEM((rows_all, width), BF16),
                    pltpu.VMEM((3, rows_all, width), BF16),
                    pltpu.VMEM((rows_all // group * HEADS // 2, 2 * group, group), BF16),
                    pltpu.VMEM((rows_all, width), BF16),
                    pltpu.VMEM((5, rows_all, ADAPT), BF16),
                    pltpu.VMEM((rows_all, ADAPT), BF16),
                    pltpu.VMEM((rows_all, width), BF16),
                    pltpu.VMEM((rows_all, width), F32),
                    pltpu.VMEM((rows_all, width), F32),
                    pltpu.VMEM((2, rows_all, ADAPT), F32),
                    pltpu.VMEM((rows_all, width), BF16),
                    pltpu.VMEM((3, rows_all, width), BF16),
                    pltpu.VMEM((5, ADAPT, width), F32),
                    pltpu.VMEM((5, ADAPT, width), F32),
                    pltpu.VMEM((2, ADAPT, ff), F32),
                ],
            ),
        ),
        out_shape=[
            *weights, *weights, whole(expand_weight, 0), whole(reduce_weight, 0), shape_of(2, ff, ADAPT),
            shape_of(2, width, ADAPT), blocks_shape, blocks_shape, blocks_shape, blocks_shape, *saved,
            shape_of(width, 384),
        ],
        in_specs=[smem_spec] + [vmem_spec] * 5 + [any_spec] * 2 + [vmem_spec] * 2 + [any_spec] * 12,
        out_specs=[any_spec] * 17 + [vmem_spec],
        scratch_shapes=[
            *scratch[5:7],
            pltpu.VMEM((width, ff), BF16),
            pltpu.VMEM((ff, width), BF16),
            pltpu.VMEM((2, ff, ADAPT), BF16),
            pltpu.VMEM((2, width, ADAPT), BF16),
            pltpu.VMEM((members, chunk, width), BF16),
            pltpu.VMEM((members, chunk, width), BF16),
            *[pltpu.VMEM((members, rows_each, width), BF16) for rows_each in tail_rows],
            pltpu.SemaphoreType.DMA((9, PART_SEMS)),
            pltpu.SemaphoreType.DMA((30,)),
            pltpu.SemaphoreType.DMA((5, members)),
            pltpu.SemaphoreType.DMA((5, members)),
        ],
        compiler_params=pltpu.CompilerParams(collective_id=0, has_side_effects=True, vmem_limit_bytes=63 << 20),
        name="front",
    )(
        adapter_index, to_send, to_place, to_frame, *to_tails, x_view, cot_view, norm_gain, norm_shift,
        spatial_weights, spatial_output, temporal_weights, temporal_output, attention_down, up_rows,
        expand_weight, reduce_weight, expand_up.T, reduce_down, expand_down, reduce_up.T,
    )
    sp_w, sp_adapt = outs[0:2]
    made, back, *kept, mid_pay = outs[10:18]
    step = width // devices
    fold = ff // width
    results = pl.pallas_call(
        functools.partial(spatial_backward, sizes, groups, members, step, regions),
        out_shape=[
            shape_of(*x_view.shape, kind=F32),
            shape_of(*x_view.shape, kind=F32),
            shape_of(8, step, ADAPT, kind=F32),
            shape_of(8, step, ADAPT, kind=F32),
            shape_of(step, ADAPT, kind=F32),
            shape_of(fold * step, ADAPT, kind=F32),
            shape_of(fold * step, ADAPT, kind=F32),
            shape_of(step, ADAPT, kind=F32),
        ],
        in_specs=[smem_spec, vmem_spec, vmem_spec, vmem_spec] + [any_spec] * 11,
        out_specs=[any_spec] * 2 + [vmem_spec] * 6,
        scratch_shapes=[
            *scratch[5:7],
            *scratch[0:5],
            pltpu.VMEM((total, width), BF16),
            pltpu.VMEM((total, width), BF16),
            pltpu.VMEM((frames, clips, places, width), F32),
            pltpu.VMEM((frames, clips, places, width), F32),
            pltpu.VMEM((devices, step, 384), BF16),
            *[pltpu.VMEM((devices, step, 128), BF16)] * 4,
            pltpu.VMEM((total, width), BF16),
            pltpu.VMEM((total, width), BF16),
            pltpu.VMEM((3, total, width), BF16),
            pltpu.VMEM((clips, half, width), F32),
            pltpu.VMEM((4, ADAPT, width), F32),
            pltpu.VMEM((4, ADAPT, width), F32),
            pltpu.SemaphoreType.DMA((21,)),
            pltpu.SemaphoreType.DMA((3, devices - 1)),
            pltpu.SemaphoreType.DMA((3, devices - 1)),
        ],
        compiler_params=pltpu.CompilerParams(collective_id=1, has_side_effects=True, vmem_limit_bytes=63 << 20),
        name="spatial_back",
    )(
        adapter_index, from_sent, from_tails, norm_gain, x_view, sp_w, sp_adapt, *kept, back, made,
        mid_pay.reshape(devices, step, 384),
    )
    dx, out, down, up, gea, geb, gra, grb = pl.pallas_call(
        functools.partial(deliver, len(results)),
        out_shape=[jax.ShapeDtypeStruct(value.shape, value.dtype) for value in results],
        in_specs=[any_spec] * len(results),
        out_specs=[any_spec] * len(results),
        scratch_shapes=[pltpu.VMEM(value.shape, value.dtype) for value in results]
        + [pltpu.SemaphoreType.DMA((2 * len(results),))],
        name="deliver",
    )(*results)

    def whole_rows(rows):
        return rows.transpose(0, 2, 1, 3)[None]

    return (whole_rows(out), whole_rows(dx), down, jnp.swapaxes(up, 1, 2), gea, geb.T, gra, grb.T)


def solution(mesh):
    pick = fast_device if fits(mesh) else general_device

    placed = (
        P(("clip", "tok"), None, None, None, None),
        P("clip"),
        P(),
        P(),
        P(None, ("clip", "tok"), None),
        P(("clip", "tok"), None),
        P(None, ("clip", "tok"), None),
        P(("clip", "tok"), None),
        P(("clip", "tok"), None),
        P(("clip", "tok"), None),
        P(None, ("clip", "tok"), None),
        P(None, None, ("clip", "tok")),
        P(("clip", "tok"), None),
        P(None, ("clip", "tok")),
        P(("clip", "tok"), None),
        P(None, ("clip", "tok")),
        P(("clip", "tok"), None, None, None, None),
    )
    return jax.shard_map(
        pick,
        mesh=mesh,
        in_specs=placed,
        out_specs=(
            P(("clip", "tok"), None, None, None, None),
            P(("clip", "tok"), None, None, None, None),
            P(None, ("clip", "tok"), None),
            P(None, None, ("clip", "tok")),
            P(("clip", "tok"), None),
            P(None, ("clip", "tok")),
            P(("clip", "tok"), None),
            P(None, ("clip", "tok")),
        ),
        check_vma=False,
    )
```

```python
import functools

import jax
import jax.numpy as jnp
from jax import lax
from jax.experimental import pallas as pl
from jax.experimental.pallas import tpu as pltpu
from jax.sharding import PartitionSpec as P

HEADS = 12
HEAD_DIM = 64
FRAMES = 16
ADAPTERS = 8
RANK = 16


EPSILON = 1e-06


def layer_norm(stream, gain_row, shift_row):
    average = jnp.mean(stream, axis=-1, keepdims=True)
    centred = stream - average
    variance = jnp.mean(centred * centred, axis=-1, keepdims=True)
    return centred * lax.rsqrt(variance + EPSILON) * gain_row + shift_row


def adapter_mask(choice_rows):
    columns = jnp.arange(ADAPTERS * RANK, dtype=jnp.int32) // RANK
    return (columns[None, :] == choice_rows[:, None]).astype(jnp.float32)


def project_many(inputs, weight, down_rows, up_rows, mask):
    hidden = jnp.einsum("rd,ndc->nrc", inputs, down_rows, preferred_element_type=jnp.float32)
    hidden = (hidden * mask).astype(jnp.bfloat16)
    result = jnp.einsum("rd,nde->nre", inputs, weight, preferred_element_type=jnp.float32)
    result = result + jnp.einsum(
        "nrc,nce->nre", hidden, up_rows, preferred_element_type=jnp.float32
    )
    return (result, hidden)


def project_back(inputs, hidden, grad_rows, weight, down_rows, up_rows, mask):
    hidden_grad = jnp.einsum("nre,nce->nrc", grad_rows, up_rows, preferred_element_type=jnp.float32)
    hidden_grad = (hidden_grad * mask).astype(jnp.bfloat16)
    input_grad = jnp.einsum("nre,nde->rd", grad_rows, weight, preferred_element_type=jnp.float32)
    input_grad = input_grad + jnp.einsum(
        "nrc,ndc->rd", hidden_grad, down_rows, preferred_element_type=jnp.float32
    )
    down_grad = jnp.einsum("rd,nrc->ndc", inputs, hidden_grad, preferred_element_type=jnp.float32)
    up_grad = jnp.einsum("nrc,nre->nce", hidden, grad_rows, preferred_element_type=jnp.float32)
    return (input_grad, down_grad, up_grad)


def attend_forward(packed, layout):
    view_shape, score_eq, mix_eq, back_eq = layout
    queries = packed[0].reshape(view_shape)
    key_rows = packed[1].reshape(view_shape)
    values = packed[2].reshape(view_shape)
    scores = jnp.einsum(
        score_eq, queries, key_rows, preferred_element_type=jnp.float32
    ) * HEAD_DIM ** (-0.5)
    ceiling = jnp.max(scores, axis=-1, keepdims=True)
    expo_rows = jnp.exp(scores - ceiling)
    totals = jnp.sum(expo_rows, axis=-1, keepdims=True)
    weights_soft = (expo_rows / totals).astype(jnp.bfloat16)
    mixed_rows = jnp.einsum(mix_eq, weights_soft, values, preferred_element_type=jnp.float32)
    return (mixed_rows.reshape(packed.shape[1:]), ceiling + jnp.log(totals))


def attend_backward(packed, log_total, mixed_grad, layout):
    view_shape, score_eq, mix_eq, back_eq = layout
    scaling = HEAD_DIM ** (-0.5)
    queries = packed[0].reshape(view_shape)
    key_rows = packed[1].reshape(view_shape)
    values = packed[2].reshape(view_shape)
    scores = jnp.einsum(score_eq, queries, key_rows, preferred_element_type=jnp.float32) * scaling
    weights_soft = jnp.exp(scores - log_total)
    output_grad = mixed_grad.reshape(view_shape)
    soft_grad = jnp.einsum(score_eq, output_grad, values, preferred_element_type=jnp.float32)
    row_inner = jnp.sum(weights_soft * soft_grad, axis=-1, keepdims=True)
    score_grad = (weights_soft * (soft_grad - row_inner)).astype(jnp.bfloat16)
    query_grad = (
        jnp.einsum(mix_eq, score_grad, key_rows, preferred_element_type=jnp.float32) * scaling
    )
    key_grad = (
        jnp.einsum(back_eq, score_grad, queries, preferred_element_type=jnp.float32) * scaling
    )
    value_grad = jnp.einsum(
        back_eq, weights_soft.astype(jnp.bfloat16), output_grad, preferred_element_type=jnp.float32
    )
    stacked = jnp.stack([query_grad, key_grad, value_grad])
    return stacked.reshape(packed.shape).astype(jnp.bfloat16)


def attention_forward(stream, gain_row, shift_row, weight_set, mask, layout):
    inner_weights, outer_weight, down_rows, up_rows = weight_set
    normed = layer_norm(stream, gain_row, shift_row).astype(jnp.bfloat16)
    packed, packed_hidden = project_many(normed, inner_weights, down_rows[0:3], up_rows[0:3], mask)
    packed = packed.astype(jnp.bfloat16)
    mixed_rows, log_total = attend_forward(packed, layout)
    mixed_rows = mixed_rows.astype(jnp.bfloat16)
    branch, outer_hidden = project_many(
        mixed_rows, outer_weight[None], down_rows[3:4], up_rows[3:4], mask
    )
    return (
        stream + branch[0],
        (normed, packed, packed_hidden, mixed_rows, outer_hidden, log_total),
    )


def attention_backward(
    stream, stream_grad, gain_row, shift_row, weight_set, mask, layout, kept_values
):
    inner_weights, outer_weight, down_rows, up_rows = weight_set
    normed, packed, packed_hidden, mixed_rows, outer_hidden, log_total = kept_values
    branch_grad = stream_grad.astype(jnp.bfloat16)[None]
    mixed_grad, outer_down, outer_up = project_back(
        mixed_rows,
        outer_hidden,
        branch_grad,
        outer_weight[None],
        down_rows[3:4],
        up_rows[3:4],
        mask,
    )
    packed_grad = attend_backward(packed, log_total, mixed_grad.astype(jnp.bfloat16), layout)
    normed_grad, inner_down, inner_up = project_back(
        normed, packed_hidden, packed_grad, inner_weights, down_rows[0:3], up_rows[0:3], mask
    )
    unused, norm_pull = jax.vjp(lambda rows_in: layer_norm(rows_in, gain_row, shift_row), stream)
    before_grad = stream_grad + norm_pull(normed_grad)[0]
    return (
        before_grad,
        jnp.concatenate([inner_down, outer_down], axis=0),
        jnp.concatenate([inner_up, outer_up], axis=0),
    )


def expand_forward(stream, gain_row, shift_row, weight_set, mask):
    up_weight, down_weight, in_down, in_up, out_down, out_up = weight_set
    normed = layer_norm(stream, gain_row, shift_row).astype(jnp.bfloat16)
    inner_rows, inner_hidden = project_many(
        normed, up_weight[None], in_down[None], in_up[None], mask
    )
    inner_rows = inner_rows[0]
    active = jax.nn.gelu(inner_rows, approximate=True).astype(jnp.bfloat16)
    branch, outer_hidden = project_many(
        active, down_weight[None], out_down[None], out_up[None], mask
    )
    return (stream + branch[0], (normed, inner_rows, inner_hidden, active, outer_hidden))


def expand_backward(stream, stream_grad, gain_row, shift_row, weight_set, mask, kept_values):
    up_weight, down_weight, in_down, in_up, out_down, out_up = weight_set
    normed, inner_rows, inner_hidden, active, outer_hidden = kept_values
    branch_grad = stream_grad.astype(jnp.bfloat16)[None]
    active_grad, out_down_grad, out_up_grad = project_back(
        active, outer_hidden, branch_grad, down_weight[None], out_down[None], out_up[None], mask
    )
    unused, gelu_pull = jax.vjp(
        lambda values_in: jax.nn.gelu(values_in, approximate=True), inner_rows
    )
    inner_grad = gelu_pull(active_grad)[0].astype(jnp.bfloat16)[None]
    normed_grad, in_down_grad, in_up_grad = project_back(
        normed, inner_hidden, inner_grad, up_weight[None], in_down[None], in_up[None], mask
    )
    unused_norm, norm_pull = jax.vjp(
        lambda rows_in: layer_norm(rows_in, gain_row, shift_row), stream
    )
    before_grad = stream_grad + norm_pull(normed_grad)[0]
    return (before_grad, (in_down_grad[0], in_up_grad[0], out_down_grad[0], out_up_grad[0]))


def regroup_places(stream, layout_sizes, backward):
    frames_dev, clips_dev, places, model_width, clip_rows, place_blocks, place_part = layout_sizes
    padded = jnp.pad(
        stream.reshape(frames_dev, clips_dev, places, model_width),
        ((0, 0), (0, 0), (0, place_part * place_blocks - places), (0, 0)),
    )
    padded = padded.reshape(frames_dev, clips_dev * place_blocks, place_part, model_width)
    if backward:
        arrived = lax.all_to_all(
            padded.astype(jnp.bfloat16), "tok", split_axis=1, concat_axis=0, tiled=True
        ).astype(padded.dtype)
    else:
        arrived = lax.all_to_all(
            padded.astype(jnp.bfloat16), "tok", split_axis=1, concat_axis=0, tiled=True
        ).astype(padded.dtype)
    return arrived.reshape(clip_rows * FRAMES * place_part, model_width)


def regroup_frames(stream, layout_sizes, backward):
    frames_dev, clips_dev, places, model_width, clip_rows, place_blocks, place_part = layout_sizes
    shaped = stream.reshape(clip_rows * FRAMES, 1, place_part, model_width)
    if backward:
        arrived = lax.all_to_all(
            shaped.astype(jnp.bfloat16), "tok", split_axis=0, concat_axis=1, tiled=True
        ).astype(shaped.dtype)
    else:
        arrived = lax.all_to_all(
            shaped.astype(jnp.bfloat16), "tok", split_axis=0, concat_axis=1, tiled=True
        ).astype(shaped.dtype)
    arrived = arrived.reshape(frames_dev, clips_dev, place_part * place_blocks, model_width)
    return arrived[:, :, :places].reshape(frames_dev * clips_dev * places, model_width)


def general_device(
    tokens,
    adapter_index,
    norm_gain,
    norm_shift,
    spatial_weights,
    spatial_output,
    temporal_weights,
    temporal_output,
    expand_weight,
    reduce_weight,
    attention_down,
    attention_up,
    expand_down,
    expand_up,
    reduce_down,
    reduce_up,
    cotangent,
):
    frames_dev, clips_dev, places, model_width = tokens.shape[1:]
    tok_count = lax.axis_size("tok")
    frame_blocks = FRAMES // frames_dev
    clip_rows = tok_count // frame_blocks
    place_blocks = tok_count // clips_dev
    place_part = -(-places // place_blocks)
    layout_sizes = (frames_dev, clips_dev, places, model_width, clip_rows, place_blocks, place_part)
    adapt_cols = ADAPTERS * RANK
    position = lax.axis_index("tok")
    spatial_choice = lax.dynamic_slice_in_dim(
        adapter_index, position // frame_blocks * clips_dev, clips_dev
    )
    spatial_mask = jnp.broadcast_to(
        adapter_mask(spatial_choice)[None, :, None, :], (frames_dev, clips_dev, places, adapt_cols)
    ).reshape(-1, adapt_cols)
    temporal_choice = lax.dynamic_slice_in_dim(
        adapter_index.reshape(clip_rows, clips_dev), position // place_blocks, 1, 1
    )[:, 0]
    temporal_mask = jnp.broadcast_to(
        adapter_mask(temporal_choice)[:, None, None, :], (clip_rows, FRAMES, place_part, adapt_cols)
    ).reshape(-1, adapt_cols)
    spatial_layout = (
        (frames_dev * clips_dev, places, HEADS, HEAD_DIM),
        "gqhd,gkhd->ghqk",
        "ghqk,gkhd->gqhd",
        "ghqk,gqhd->gkhd",
    )
    temporal_layout = (
        (clip_rows, FRAMES, place_part, HEADS, HEAD_DIM),
        "aqphd,akphd->aphqk",
        "aphqk,akphd->aqphd",
        "aphqk,aqphd->akphd",
    )
    spatial_set = (
        lax.all_gather(spatial_weights, ("clip", "tok"), axis=1, tiled=True),
        lax.all_gather(spatial_output, ("clip", "tok"), axis=0, tiled=True),
        lax.all_gather(attention_down[0:4], ("clip", "tok"), axis=1, tiled=True),
        lax.all_gather(attention_up[0:4], ("clip", "tok"), axis=2, tiled=True),
    )
    stream0 = tokens.reshape(-1, model_width)
    stream1, spatial_kept = attention_forward(
        stream0, norm_gain[0], norm_shift[0], spatial_set, spatial_mask, spatial_layout
    )
    placed1 = regroup_places(stream1, layout_sizes, False)
    temporal_set = (
        lax.all_gather(temporal_weights, ("clip", "tok"), axis=1, tiled=True),
        lax.all_gather(temporal_output, ("clip", "tok"), axis=0, tiled=True),
        lax.all_gather(attention_down[4:8], ("clip", "tok"), axis=1, tiled=True),
        lax.all_gather(attention_up[4:8], ("clip", "tok"), axis=2, tiled=True),
    )
    placed2, temporal_kept = attention_forward(
        placed1, norm_gain[1], norm_shift[1], temporal_set, temporal_mask, temporal_layout
    )
    stream2 = regroup_frames(placed2, layout_sizes, False)
    expand_set = (
        lax.all_gather(expand_weight, ("clip", "tok"), axis=0, tiled=True),
        lax.all_gather(reduce_weight, ("clip", "tok"), axis=0, tiled=True),
        lax.all_gather(expand_down, ("clip", "tok"), axis=0, tiled=True),
        lax.all_gather(expand_up, ("clip", "tok"), axis=1, tiled=True),
        lax.all_gather(reduce_down, ("clip", "tok"), axis=0, tiled=True),
        lax.all_gather(reduce_up, ("clip", "tok"), axis=1, tiled=True),
    )
    stream3, expand_kept = expand_forward(
        stream2, norm_gain[2], norm_shift[2], expand_set, spatial_mask
    )
    expand_set = (
        lax.all_gather(expand_weight, ("clip", "tok"), axis=0, tiled=True),
        lax.all_gather(reduce_weight, ("clip", "tok"), axis=0, tiled=True),
        lax.all_gather(expand_down, ("clip", "tok"), axis=0, tiled=True),
        lax.all_gather(expand_up, ("clip", "tok"), axis=1, tiled=True),
        lax.all_gather(reduce_down, ("clip", "tok"), axis=0, tiled=True),
        lax.all_gather(reduce_up, ("clip", "tok"), axis=1, tiled=True),
    )
    grad2, expand_grads = expand_backward(
        stream2,
        cotangent.reshape(-1, model_width),
        norm_gain[2],
        norm_shift[2],
        expand_set,
        spatial_mask,
        expand_kept,
    )
    placed_grad2 = regroup_places(grad2, layout_sizes, True)
    temporal_set = (
        lax.all_gather(temporal_weights, ("clip", "tok"), axis=1, tiled=True),
        lax.all_gather(temporal_output, ("clip", "tok"), axis=0, tiled=True),
        lax.all_gather(attention_down[4:8], ("clip", "tok"), axis=1, tiled=True),
        lax.all_gather(attention_up[4:8], ("clip", "tok"), axis=2, tiled=True),
    )
    placed_grad1, temporal_down, temporal_up = attention_backward(
        placed1,
        placed_grad2,
        norm_gain[1],
        norm_shift[1],
        temporal_set,
        temporal_mask,
        temporal_layout,
        temporal_kept,
    )
    grad1 = regroup_frames(placed_grad1, layout_sizes, True)
    spatial_set = (
        lax.all_gather(spatial_weights, ("clip", "tok"), axis=1, tiled=True),
        lax.all_gather(spatial_output, ("clip", "tok"), axis=0, tiled=True),
        lax.all_gather(attention_down[0:4], ("clip", "tok"), axis=1, tiled=True),
        lax.all_gather(attention_up[0:4], ("clip", "tok"), axis=2, tiled=True),
    )
    grad0, spatial_down, spatial_up = attention_backward(
        stream0,
        grad1,
        norm_gain[0],
        norm_shift[0],
        spatial_set,
        spatial_mask,
        spatial_layout,
        spatial_kept,
    )
    owned = (
        lax.psum_scatter(
            jnp.concatenate([spatial_down, temporal_down], axis=0),
            ("clip", "tok"),
            scatter_dimension=1,
            tiled=True,
        ),
        lax.psum_scatter(
            jnp.concatenate([spatial_up, temporal_up], axis=0),
            ("clip", "tok"),
            scatter_dimension=2,
            tiled=True,
        ),
        lax.psum_scatter(expand_grads[0], ("clip", "tok"), scatter_dimension=0, tiled=True),
        lax.psum_scatter(expand_grads[1], ("clip", "tok"), scatter_dimension=1, tiled=True),
        lax.psum_scatter(expand_grads[2], ("clip", "tok"), scatter_dimension=0, tiled=True),
        lax.psum_scatter(expand_grads[3], ("clip", "tok"), scatter_dimension=1, tiled=True),
    )
    return (
        stream3.reshape(tokens.shape),
        grad0.reshape(tokens.shape),
        owned[0],
        owned[1],
        owned[2],
        owned[3],
        owned[4],
        owned[5],
    )


F32 = jnp.float32
BF16 = jnp.bfloat16
ADAPT = ADAPTERS * RANK
SPATIAL_UNROLL = 6
SPATIAL_BACK_UNROLL = 6
MIDDLE_UNROLL = 6
MIDDLE_BACK_UNROLL = 6


def nn(left, right):
    return lax.dot_general(left, right, (((1,), (0,)), ((), ())), preferred_element_type=F32)


def nt(left, right):
    return lax.dot_general(left, right, (((1,), (1,)), ((), ())), preferred_element_type=F32)


def tn(left, right):
    return lax.dot_general(left, right, (((0,), (0,)), ((), ())), preferred_element_type=F32)


def one_hot(target_row, rows):
    row_ids = lax.broadcasted_iota(jnp.int32, (rows, target_row.shape[1]), 0)
    return (row_ids == target_row).astype(F32).astype(BF16)


def column_mask(choice):
    return (lax.broadcasted_iota(jnp.int32, (1, ADAPT), 1) // RANK == choice).astype(F32)


def set_rows(rows, choice):
    total = jnp.zeros((RANK, rows.shape[1]), F32)
    for k in range(ADAPTERS):
        total = jnp.where(choice == k, rows[k * RANK : (k + 1) * RANK], total)
    return total


def norm_rows(rows, gain_row, shift_row):
    average = jnp.mean(rows, axis=-1, keepdims=True)
    centred = rows - average
    variance = jnp.mean(centred * centred, axis=-1, keepdims=True)
    return centred * lax.rsqrt(variance + EPSILON) * gain_row + shift_row


def norm_back(rows, pulled, gain_row):
    average = jnp.mean(rows, axis=-1, keepdims=True)
    centred = rows - average
    variance = jnp.mean(centred * centred, axis=-1, keepdims=True)
    scale = lax.rsqrt(variance + EPSILON)
    unit = centred * scale
    scaled = pulled * gain_row
    return scale * (
        scaled
        - jnp.mean(scaled, axis=-1, keepdims=True)
        - unit * jnp.mean(scaled * unit, axis=-1, keepdims=True)
    )


def soften(scores, keep):
    scores = jnp.where(keep, scores, -1e30)
    ceiling = jnp.max(scores, axis=-1, keepdims=True)
    expo = jnp.exp(scores - ceiling)
    return expo * (1.0 / jnp.sum(expo, axis=-1, keepdims=True))


def two_heads(rows, low):
    zero = jnp.zeros_like(rows)
    return jnp.concatenate([jnp.where(low, rows, zero), jnp.where(low, zero, rows)], axis=0)


def one_pair(both, low):
    count = both.shape[0] // 2
    return jnp.where(low, both[:count], both[count:])


def attention_pair(query, key, value, keep, low):
    weights = soften(nt(two_heads(query, low), key), keep).astype(BF16)
    return weights, one_pair(nn(weights, value), low).astype(BF16)


def attention_all(sizes, first, qkv, soft, mixed, keep, low, unroll):
    start, blocks, rows_each, pairs = sizes

    @pl.loop(0, blocks * pairs // unroll)
    def _(turn):
        block = turn // (pairs // unroll)
        lead = (turn - block * (pairs // unroll)) * unroll
        rows = pl.ds(pl.multiple_of(start + block * rows_each, 16), rows_each)
        for u in range(unroll):
            lanes = pl.ds(pl.multiple_of((lead + u) * 128, 128), 128)
            weights, made = attention_pair(
                qkv[0, rows, lanes], qkv[1, rows, lanes], qkv[2, rows, lanes], keep, low
            )
            soft[(first + block) * pairs + lead + u] = weights
            mixed[rows, lanes] = made


def attention_all_back(sizes, qkv, soft, gmix, gqkv, low, unroll, first=0):
    blocks, rows_each, pairs = sizes

    @pl.loop(0, blocks * pairs // unroll)
    def _(turn):
        block = turn // (pairs // unroll)
        lead = (turn - block * (pairs // unroll)) * unroll
        block = block + first
        rows = pl.ds(pl.multiple_of(block * rows_each, 16), rows_each)
        spans = [pl.ds(pl.multiple_of((lead + u) * 128, 128), 128) for u in range(unroll)]
        made = attention_back(
            [[qkv[n, rows, lanes] for lanes in spans] for n in range(3)],
            [soft[block * pairs + lead + u] for u in range(unroll)],
            [gmix[rows, lanes] for lanes in spans],
            low,
        )
        for n in range(3):
            for lanes, value in zip(spans, made[n]):
                gqkv[n, rows, lanes] = value.astype(BF16)


def block_rows(ref, slots, number, offset=0):
    chunk = slots.shape[1]
    return ref.at[pl.ds(pl.multiple_of(offset + number * chunk, 8), chunk)]


def send_blocks(slots, got, count, first, send_sems, recv_sems, local_sem, offset=0):
    clip, tok = lax.axis_index("clip"), lax.axis_index("tok")
    target = block_rows(got, slots, tok, offset)
    for n in range(count):
        place = first + lax.rem(tok + n, count)

        @pl.when(place != tok)
        def _():
            remote(slots.at[place], target, send_sems.at[place], recv_sems.at[tok], (clip, place)).start()

        @pl.when(place == tok)
        def _():
            pltpu.make_async_copy(slots.at[place], target, local_sem).start()


def wait_blocks(slots, got, members, send_sems, recv_sems, local_sem, offset=0):
    tok = lax.axis_index("tok")
    for d in range(1, members):
        place = lax.rem(tok + d, members)
        target = block_rows(got, slots, place, offset)
        pltpu.make_async_copy(slots.at[place], slots.at[place], send_sems.at[place]).wait()
        pltpu.make_async_copy(target, target, recv_sems.at[place]).wait()
    pltpu.make_async_copy(slots.at[tok], block_rows(got, slots, tok, offset), local_sem).wait()


def attention_back(packed, weights, grads, low):
    queries, keys, values = packed
    stacked = [two_heads(grad, low) for grad in grads]
    pulled = [nt(grad, value) for grad, value in zip(stacked, values)]
    value_grads = [tn(soft, grad) for soft, grad in zip(weights, stacked)]
    scores = []
    for soft, pull in zip(weights, pulled):
        wide = soft.astype(F32)
        inner = jnp.sum(wide * pull, axis=-1, keepdims=True)
        scores.append((wide * (pull - inner)).astype(BF16))
    query_grads = [one_pair(nn(score, key), low) * HEAD_DIM**-0.5 for score, key in zip(scores, keys)]
    key_grads = [tn(score, two_heads(query, low)) for score, query in zip(scores, queries)]
    return query_grads, key_grads, value_grads


def spatial_backward(
    sizes, groups, members, step, regions, idx, from_sent, from_tails, gain, x_hbm, w_hbm, ad_hbm, qkv_hbm, soft_hbm, mixed_hbm, hid_hbm, zs_hbm,
    got_hbm, made_hbm, mid_pay,
    dx_hbm, out_hbm, down_out, up_out, ea, eb, ra, rb,
    w, ad, qkv, soft, mixed, hid, zs, got, made, x, out, mid, sp, pay, sp_late, pay_late, grad, gmix, gqkv, gpull, gdown, gup, copy_sems, send_sems, recv_sems
):
    frames, clips, places, width, padded = sizes
    half = frames * padded
    devices = groups * members

    def row_copies(view, rows, first, inward):
        copies = []
        for i in range(frames):
            for b in range(clips):
                ends = (view.at[i, :, b, :], rows.at[i, b])
                ends = ends if inward else ends[::-1]
                copies.append(pltpu.make_async_copy(*ends, copy_sems.at[first + i * clips + b]))
        return copies

    fills = [
        pltpu.make_async_copy(source, target, copy_sems.at[10 + n])
        for n, (source, target) in enumerate(
            (
                (got_hbm, got), (w_hbm.at[3], w.at[3]), (ad_hbm, ad), (mixed_hbm, mixed), (hid_hbm, hid),
                (soft_hbm, soft), (qkv_hbm, qkv), (w_hbm.at[0:3], w.at[0:3]), (zs_hbm, zs), (made_hbm, made),
            )
        )
    ]
    loads = row_copies(x_hbm, x, 0, True)
    for load in fills + loads:
        load.start()
    clip, tok = lax.axis_index("clip"), lax.axis_index("tok")
    me = clip * members + tok
    peers = all_peers(groups, members)
    greet(peers)

    def terms(source, target, kind):
        for n, peer in enumerate(peers):
            place = peer[0] * members + peer[1]
            remote(
                source.at[place], target.at[me], send_sems.at[kind, n], recv_sems.at[kind, n], peer
            ).start()
        pltpu.make_async_copy(source.at[me], target.at[me], copy_sems.at[(8, 9, 20)[kind]]).start()

    def await_terms(source, target, kind):
        for n, peer in enumerate(peers):
            remote(source.at[me], target.at[me], send_sems.at[kind, n], recv_sems.at[kind, n], peer).wait()
        pltpu.make_async_copy(source.at[me], target.at[me], copy_sems.at[(8, 9, 20)[kind]]).wait()

    terms(mid_pay, mid, 0)
    for fill in fills[0:5]:
        fill.wait()
    for b in range(clips):
        rows = slice(b * half, (b + 1) * half)
        mask = column_mask(idx[b])
        arrived = []
        for begin, size in regions:
            arrived.append(got[begin + b * size : begin + (b + 1) * size])
        grad[rows] = nn(one_hot(from_tails[...], half), jnp.concatenate(arrived, axis=0)).astype(BF16)
        hidden_grad = (nn(grad[rows], ad[7]) * mask).astype(BF16)
        gmix[rows] = (nt(grad[rows], w[3]) + nt(hidden_grad, ad[3])).astype(BF16)
        down, up = tn(hidden_grad, mixed[rows]), tn(hid[3, rows], grad[rows])
        if b == 0:
            gdown[3], gup[3] = down, up
        else:
            gdown[3] += down
            gup[3] += up

    pairs = width // 128
    low = lax.broadcasted_iota(jnp.int32, (padded, 128), 1) < HEAD_DIM

    for fill in fills[5:7]:
        fill.wait()
    attention_all_back((frames * clips, padded, pairs), qkv, soft, gmix, gqkv, low, SPATIAL_BACK_UNROLL)
    for fill in fills[7:10]:
        fill.wait()
    repeat = jnp.where(idx[0] == idx[1], 0.0, 1.0)

    def pull_back(n, b, fresh):
        rows = slice(b * half, (b + 1) * half)
        own = gqkv[n, rows]
        hidden_grad = (nn(own, ad[4 + n]) * column_mask(idx[b])).astype(BF16)
        pulled = nt(own, w[n]) + nt(hidden_grad, ad[n])
        gpull[b] = pulled if fresh else gpull[b] + pulled
        down, up = tn(hidden_grad, zs[rows]), tn(hid[n, rows], own)
        if b == 0:
            gdown[n], gup[n] = down, up
        else:
            gdown[n] += down
            gup[n] += up

    def send_pair(first, pay, sp, kind):
        pieces = []
        for n in (first, first + 1):
            for source in (gdown, gup):
                pieces.append(set_rows(source[n], idx[0]))
                pieces.append(set_rows(source[n], idx[1]) * repeat)
        packed = jnp.transpose(jnp.concatenate(pieces, axis=0))
        pay[...] = packed.reshape(pay.shape).astype(BF16)
        terms(pay, sp, kind)

    for b in range(clips):
        pull_back(2, b, True)
    send_pair(2, pay_late, sp_late, 1)
    for b in range(clips):

        @pl.loop(0, 2)
        def _(n):
            pull_back(n, b, False)

    send_pair(0, pay, sp, 2)
    for load in loads:
        load.wait()
    for b in range(clips):
        rows = slice(b * half, (b + 1) * half)
        final = nn(one_hot(from_sent[...], half), made[rows])
        for i in range(frames):
            base = i * padded
            out[i, b] = final[base : base + places]
            pulled = norm_back(x[i, b], gpull[b, base : base + places], gain[0:1])
            x[i, b] = grad[b * half + base : b * half + base + places].astype(F32) + pulled
    stores = row_copies(out_hbm, out, 4, False) + row_copies(dx_hbm, x, 0, False)
    for store in stores:
        store.start()
    await_terms(mid_pay, mid, 0)
    mids, mid_choice = combine_mid((groups, members, step, eb.shape[0] // step), mid, down_out, up_out, ea, eb, ra, rb)
    await_terms(pay_late, sp_late, 1)
    combine_spatial((groups, members, step), sp_late, mids, down_out, up_out, 2)
    await_terms(pay, sp, 2)
    combine_spatial((groups, members, step), sp, mids, down_out, up_out, 0)
    for store in stores:
        store.wait()


def front(
    sizes, shape, members, tail_parts, idx, to_send, to_place, to_frame, to_first, to_second, x_hbm, cot_hbm, gain, shift,
    sh_w, sh_o, sh_tw, sh_to, sh_down, sh_up, sh_we, sh_wr, sh_eup, sh_rdown, sh_edown, sh_rup,
    all_w, all_ad, all_tw, all_tad, all_we, all_wr, all_tall, all_flat, got_hbm, cot_got, made, back,
    qkv_hbm, soft_hbm, mixed_hbm, hid_hbm, zs_hbm, pay,
    w, ad, we, wr, tall, flat, slots, cots, tail_one, tail_two, sems, copy_sems, send_sems, recv_sems, *, scopes
):
    frames, clips, places, width, padded = sizes
    rows_all, group, ff_chunk, owners = shape
    chunk = slots.shape[1]
    tails, to_tails = (tail_one, tail_two), (to_first, to_second)
    half = frames * padded
    share = members // clips
    clip, tok = lax.axis_index("clip"), lax.axis_index("tok")
    parts = [
        Part([(sh_w.at[0:2], None)], all_w.at[0:2], 1, sems.at[0]),
        Part([(sh_w.at[2], 0), (sh_o, 1)], all_w.at[2:4], 1, sems.at[1]),
        Part([(sh_down.at[0:4], slice(0, 4)), (sh_up.at[0:4], slice(4, 8))], all_ad, 1, sems.at[2]),
        Part([(sh_tw, slice(0, 3)), (sh_to, 3)], all_tw, 1, sems.at[3]),
        Part([(sh_down.at[4:8], slice(0, 4)), (sh_up.at[4:8], slice(4, 8))], all_tad, 1, sems.at[4]),
        Part([(sh_we, None)], all_we, 0, sems.at[5]),
        Part([(sh_wr, None)], all_wr, 0, sems.at[6]),
        Part([(sh_eup, 0), (sh_rdown, 1)], all_tall, 1, sems.at[7]),
        Part([(sh_edown, 0), (sh_rup, 1)], all_flat, 1, sems.at[8]),
    ]
    y, core, z, across = place_of()
    greet(tok_peers(members) + [device_at(1 - y, core, z, across), device_at(y, 1 - core, z, across)])

    def stages(plan):
        for step in range(0, len(plan), 2):
            parts["ABCDEFGHI".index(plan[step])].stage(int(plan[step + 1]))

    def exchange_sems(n):
        return send_sems.at[n], recv_sems.at[n], copy_sems.at[25 + n]

    temporal_loads = [
        pltpu.make_async_copy(all_tw, w, copy_sems.at[2]), pltpu.make_async_copy(all_tad, ad, copy_sems.at[3])
    ]
    loads = [
        pltpu.make_async_copy(source, target, copy_sems.at[n])
        for n, (source, target) in zip((0, 1, 5, 6), ((all_wr, wr), (all_tall, tall), (all_flat, flat), (all_we, we)))
    ]
    stages("A0B0C0")

    def spatial_phase(x, cot, stream, qkv, soft, mixed, hid, zs):
        load_cot = row_loads(cot_hbm, cot, 21, frames, clips, copy_sems)
        load_x = row_loads(x_hbm, x, 17, frames, clips, copy_sems)
        for load in load_cot + load_x:
            load.start()
        pads = slice(padded - 16, padded)
        for i in range(frames):
            stream[i * padded + padded - 16 : (i + 1) * padded] = jnp.zeros((16, width), BF16)
        for load in load_cot:
            load.wait()
        for b in range(clips):
            for i in range(frames):
                stream[i * padded : i * padded + places] = cot[i, b].astype(BF16)
            rows = nn(one_hot(to_send[...], half), stream[...])
            cots[b * share : (b + 1) * share] = rows.reshape(share, chunk, width).astype(BF16)
        stages("A1B1A2C1B2A3")
        for load in load_x:
            load.wait()
        for b in range(clips):
            for i in range(frames):
                base = b * half + i * padded
                zs[base + padded - 16 : base + padded] = jnp.zeros((16, width), BF16)
                zs[base : base + places] = norm_rows(
                    x[i, b], gain[0:1], shift[0:1]
                ).astype(BF16)
        stages("C2B3C3D0E0A4B4C4")
        stages("D1E1A5B5C5A6B6C6")
        loads = [pltpu.make_async_copy(all_w, w, copy_sems.at[2]), pltpu.make_async_copy(all_ad, ad, copy_sems.at[3])]
        for load in loads:
            load.start()
        stages("D2E2F0G0H0I0")
        for load in loads:
            load.wait()

        keep = lax.broadcasted_iota(jnp.int32, (2 * padded, padded), 1) < places
        pairs = width // 128
        low = lax.broadcasted_iota(jnp.int32, (padded, 128), 1) < HEAD_DIM
        far = jnp.where(tok < share, 1, 0)
        for turn in range(clips):
            b = far if turn == 0 else 1 - far
            rows = pl.ds(pl.multiple_of(b * half, 16), half)
            mask = column_mask(idx[b])

            @pl.loop(0, 3)
            def _(n):
                hidden = (nn(zs[rows], ad[n]) * mask).astype(BF16)
                hid[n, rows] = hidden
                result = nn(zs[rows], w[n]) + nt(hidden, ad[4 + n])
                result = result * jnp.where(n == 0, HEAD_DIM**-0.5, 1.0)
                qkv[n, rows] = result.astype(BF16)

            stages("D3E3" if turn == 0 else "F3G3H3I3")

            attention_all(
                (b * half, frames, padded, pairs), b * frames, qkv, soft, mixed, keep, low, SPATIAL_UNROLL
            )
            if turn == 0:
                stages("F1G1H1I1")
            hidden = (nn(mixed[rows], ad[3]) * mask).astype(BF16)
            hid[3, rows] = hidden
            branch = nn(mixed[rows], w[3]) + nt(hidden, ad[7])
            for i in range(frames):
                stream[i * padded : i * padded + places] = (
                    x[i, b] + branch[i * padded : i * padded + places]
                ).astype(BF16)
            made = nn(one_hot(to_send[...], half), stream[...]).reshape(share, chunk, width)
            slots[pl.ds(b * share, share)] = made.astype(BF16)
            send_blocks(slots, got_hbm, share, b * share, *exchange_sems(0))
            if turn == 0:
                stages("F2G2H2I2D4E4")
        stores = [
            pltpu.make_async_copy(source, target, copy_sems.at[12 + n])
            for n, (source, target) in enumerate(
                ((qkv, qkv_hbm), (soft, soft_hbm), (mixed, mixed_hbm), (hid, hid_hbm), (zs, zs_hbm))
            )
        ]
        for store in stores:
            store.start()
        stages("D5E5F4G4H4I4D6E6")
        for load in temporal_loads:
            load.start()
        for store in stores:
            store.wait()

    def middle_phase(
        got, cot, x1, x2, zt, ze, qkv, soft, mixed, hid, hide, gy, acc, pull, ghe, gmix, gqkv, gdown, gup, wide
    ):
        choice = idx[tok // share]
        mask = column_mask(choice)
        groups = rows_all // group
        wait_blocks(slots, got_hbm, members, *exchange_sems(0))
        send_blocks(cots, cot_got, members, 0, *exchange_sems(1))
        load_got = pltpu.make_async_copy(got_hbm, got, copy_sems.at[4])
        load_got.start()
        load_got.wait()

        @pl.loop(0, groups)
        def _(j):
            rows = pl.ds(pl.multiple_of(j * group, 16), group)
            own = nn(one_hot_rows(to_place[...], group, j * group), got[...])
            x1[rows] = own.astype(BF16)
            zt[rows] = norm_rows(own, gain[1:2], shift[1:2]).astype(BF16)

        for load in temporal_loads:
            load.wait()

        @pl.loop(0, 3)
        def _(n):
            hidden = (nn(zt[...], ad[n]) * mask).astype(BF16)
            hid[n] = hidden
            result = nn(zt[...], w[n]) + nt(hidden, ad[4 + n])
            result = result * jnp.where(n == 0, HEAD_DIM**-0.5, 1.0)
            qkv[n] = result.astype(BF16)

        stages("F5G5")

        pairs = width // 128
        keep = (
            lax.rem(lax.broadcasted_iota(jnp.int32, (2 * group, group), 0), group) // FRAMES
            == lax.broadcasted_iota(jnp.int32, (2 * group, group), 1) // FRAMES
        )
        low = lax.broadcasted_iota(jnp.int32, (group, 128), 1) < HEAD_DIM

        attention_all((0, groups, group, pairs), 0, qkv, soft, mixed, keep, low, MIDDLE_UNROLL)
        stages("H5I5F6G6")
        loads[3].start()
        hidden = (nn(mixed[...], ad[3]) * mask).astype(BF16)
        hid[3] = hidden
        acc[...] = nn(mixed[...], w[3]) + nt(hidden, ad[7])

        @pl.loop(0, groups)
        def _(j):
            rows = pl.ds(pl.multiple_of(j * group, 16), group)
            own = x1[rows].astype(F32) + acc[rows]
            x2[rows] = own
            acc[rows] = own
            pull[rows] = jnp.zeros((group, width), F32)
            ze[rows] = norm_rows(own, gain[2:3], shift[2:3]).astype(BF16)

        stages("H6I6")
        for load in loads[0:3]:
            load.start()
        wait_blocks(cots, cot_got, members, *exchange_sems(1))
        load_cot = pltpu.make_async_copy(cot_got, cot, copy_sems.at[4])
        load_cot.start()
        load_cot.wait()

        @pl.loop(0, groups)
        def _(j):
            rows = pl.ds(pl.multiple_of(j * group, 16), group)
            gy[rows] = nn(one_hot_rows(to_place[...], group, j * group), cot[...]).astype(BF16)

        for load in loads:
            load.wait()
        hide[...] = (nn(ze[...], flat[0]) * mask).astype(BF16)
        ghr = (nn(gy[...], flat[1]) * mask).astype(BF16)
        hid[0 + 4] = ghr
        ghe[...] = jnp.zeros(ghe.shape, F32)

        @pl.loop(0, we.shape[1] // ff_chunk)
        def _(c):
            part = pl.ds(pl.multiple_of(c * ff_chunk, ff_chunk), ff_chunk)
            inner = nn(ze[...], we[:, part]) + nt(hide[...], tall[0, part])
            cube = 0.7978845608028654 * (inner + 0.044715 * inner * inner * inner)
            bend = jnp.tanh(cube)
            act = (0.5 * inner * (1.0 + bend)).astype(BF16)
            slope = 0.5 * (1.0 + bend) + 0.5 * inner * (1.0 - bend * bend) * (
                0.7978845608028654 * (1.0 + 3.0 * 0.044715 * inner * inner)
            )
            acc[...] += nn(act, wr[part])
            ghe[0] += nn(act, tall[1, part])
            wide[0, :, part] = tn(hid[4], act)
            gact = nt(gy[...], wr[part]) + nt(hid[4], tall[1, part])
            ginner = (gact * slope).astype(BF16)
            pull[...] += nt(ginner, we[:, part])
            ghe[1] += nn(ginner, tall[0, part])
            wide[1, :, part] = tn(hide[...], ginner)

        hidr = (ghe[0] * mask).astype(BF16)
        acc[...] += nt(hidr, flat[1])
        rows = nn(one_hot(to_frame[...], got.shape[0]), acc[...].astype(BF16))
        slots[...] = rows.reshape(slots.shape).astype(BF16)
        send_blocks(slots, made, members, 0, *exchange_sems(2))
        gdown[4] = tn(hidr, gy[...])
        gheb = (ghe[1] * mask).astype(BF16)
        gup[4] = tn(gheb, ze[...])
        pull[...] += nt(gheb, flat[0])

        @pl.loop(0, groups)
        def _(j):
            rows = pl.ds(pl.multiple_of(j * group, 16), group)
            own = gy[rows].astype(F32) + norm_back(x2[rows], pull[rows], gain[2:3])
            acc[rows] = own
            ze[rows] = own.astype(BF16)

        grad = ze
        hidden_grad = (nn(grad[...], ad[7]) * mask).astype(BF16)
        gmix[...] = (nt(grad[...], w[3]) + nt(hidden_grad, ad[3])).astype(BF16)
        gdown[3] = tn(hidden_grad, mixed[...])
        gup[3] = tn(hid[3], grad[...])

        offset = 0
        for turn, (first, count) in enumerate(tail_parts):
            lines = slice(first * group, (first + count) * group)
            attention_all_back(
                (count, group, pairs), qkv, soft, gmix, gqkv, low, MIDDLE_BACK_UNROLL, first
            )
            pull[lines] = jnp.zeros((count * group, width), F32)

            @pl.loop(0, 3)
            def _(n):
                own = gqkv[n, lines]
                hidden_grad = (nn(own, ad[4 + n]) * mask).astype(BF16)
                pull[lines] += nt(own, w[n]) + nt(hidden_grad, ad[n])
                down, up = tn(hidden_grad, zt[lines]), tn(hid[n, lines], own)
                if turn == 0:
                    gdown[n], gup[n] = down, up
                else:
                    gdown[n] += down
                    gup[n] += up

            @pl.loop(first, first + count)
            def _(j):
                rows = pl.ds(pl.multiple_of(j * group, 16), group)
                own = acc[rows] + norm_back(x1[rows].astype(F32), pull[rows], gain[1:2])
                ze[rows] = own.astype(BF16)

            tail = tails[turn]
            made_rows = nn(one_hot(to_tails[turn][...], members * tail.shape[1]), ze[lines])
            tail[...] = made_rows.reshape(tail.shape).astype(BF16)
            send_blocks(tail, back, members, 0, *exchange_sems(3 + turn), offset)
            offset += members * tail.shape[1]

        pieces = []
        for n in range(4):
            pieces += [set_rows(gdown[n], choice), set_rows(gup[n], choice)]
        pay[:, 0:128] = jnp.transpose(jnp.concatenate(pieces, axis=0)).astype(BF16)
        line = lax.broadcasted_iota(jnp.int32, (128 - 2 * RANK, width), 0)
        blank = jnp.zeros((128 - 2 * RANK, width), F32)
        for k, number in enumerate((choice, idx[0], idx[1])):
            blank = jnp.where(line == k, number.astype(F32), blank)
        pay[:, 128:256] = jnp.transpose(
            jnp.concatenate([set_rows(gup[4], choice), set_rows(gdown[4], choice), blank], axis=0)
        ).astype(BF16)
        high = jnp.concatenate(
            [set_rows(wide[1], choice), set_rows(wide[0], choice), jnp.zeros((128 - 2 * RANK, we.shape[1]), F32)], axis=0
        )
        high = jnp.transpose(high)
        step = width // owners
        fold = we.shape[1] // width
        high = high.reshape(owners, fold, step, 128)
        total = high[:, 0].reshape(width, 128)
        for f in range(1, fold):
            total += pltpu.roll(high[:, f].reshape(width, 128), 2 * RANK * f, 1)
        pay[:, 256:384] = total.astype(BF16)
        wait_blocks(slots, made, members, *exchange_sems(2))
        offset = 0
        for turn, tail in enumerate(tails):
            wait_blocks(tail, back, members, *exchange_sems(3 + turn), offset)
            offset += members * tail.shape[1]

    pl.run_scoped(spatial_phase, *scopes[0])
    pl.run_scoped(middle_phase, *scopes[1])


def deliver(count, *refs):
    sources, targets, held, sems = refs[:count], refs[count : 2 * count], refs[2 * count : 3 * count], refs[3 * count]
    loads = [pltpu.make_async_copy(sources[n], held[n], sems.at[n]) for n in range(count)]
    for load in loads:
        load.start()
    stores = [pltpu.make_async_copy(held[n], targets[n], sems.at[n + count]) for n in range(count)]
    for load, store in zip(loads, stores):
        load.wait()
        store.start()
    for store in stores:
        store.wait()


def row_loads(source, target, first, frames, clips, sems):
    return [
        pltpu.make_async_copy(source.at[i, :, b, :], target.at[i, b], sems.at[first + i * clips + b])
        for i in range(frames) for b in range(clips)
    ]


def one_hot_rows(target_row, rows, first):
    row_ids = lax.broadcasted_iota(jnp.int32, (rows, target_row.shape[1]), 0) + first
    return (row_ids == target_row).astype(F32).astype(BF16)


def spread_sum(stack, columns, first, choice, count):
    lanes = lax.broadcasted_iota(jnp.int32, (columns, ADAPT), 1)
    lines = lax.broadcasted_iota(jnp.int32, (columns, ADAPT), 0)
    spread = (lines == first + lanes % RANK).astype(F32)
    wide = lax.dot_general(
        stack, spread, (((1,), (0,)), ((), ())),
        preferred_element_type=F32, precision=lax.Precision.HIGHEST,
    )
    sets = lax.broadcasted_iota(jnp.int32, (1, ADAPT), 1) // RANK
    kept = jnp.where(sets.astype(F32) == choice, wide, 0.0)
    step = stack.shape[0] // count
    total = kept[0:step]
    for k in range(1, count):
        total += kept[k * step : (k + 1) * step]
    return total


def combine_mid(sizes, got, down, up, ea, eb, ra, rb):
    groups, members, step, fold = sizes
    clips = 2
    share = members // clips
    mids = []
    for g in range(groups):
        for b in range(clips):
            part = jnp.zeros((step, 384), F32)
            for t in range(share):
                part += got[g * members + b * share + t].astype(F32)
            mids.append(part)
    mid = jnp.concatenate(mids, axis=0)
    choice = mid[:, 160:161] * (1.0 / share)
    count = groups * clips
    for n in range(4):
        for s, target in enumerate((down, up)):
            target[4 + n] = spread_sum(mid[:, 0:128], 128, (2 * n + s) * RANK, choice, count)
    ea[...] = spread_sum(mid[:, 128:256], 128, 0, choice, count)
    rb[...] = spread_sum(mid[:, 128:256], 128, RANK, choice, count)
    for f in range(fold):
        rows = slice(f * step, (f + 1) * step)
        eb[rows] = spread_sum(mid[:, 256:384], 128, 2 * RANK * f, choice, count)
        ra[rows] = spread_sum(mid[:, 256:384], 128, 2 * RANK * f + RANK, choice, count)
    choices = [
        jnp.concatenate([mids[g * clips][:, 161 + b : 162 + b] * (1.0 / share) for g in range(groups)], axis=0)
        for b in range(clips)
    ]
    return choices, choice


def combine_spatial(sizes, got, choices, down, up, first):
    groups, members, step = sizes
    clips = len(choices)
    sums = []
    for g in range(groups):
        total = jnp.zeros((step, 128), F32)
        for t in range(members):
            total += got[g * members + t].astype(F32)
        sums.append(total)
    stack = jnp.concatenate(sums, axis=0)
    for n in range(2):
        for s, target in enumerate((down, up)):
            total = jnp.zeros((step, ADAPT), F32)
            for b in range(clips):
                total += spread_sum(stack, 128, ((2 * n + s) * clips + b) * RANK, choices[b], groups)
            target[first + n] = total


def shape_of(*dims, kind=BF16):
    return jax.ShapeDtypeStruct(dims, kind)


def order_tables(frames, places, padded, blocks, part, chunk):
    half_rows, sent_rows = frames * padded, blocks * chunk
    assert half_rows == sent_rows
    to_send = [-1] * half_rows
    from_sent = [-1] * sent_rows
    for i in range(frames):
        for p in range(places):
            source, target = i * padded + p, (p // part) * chunk + i * part + p % part
            to_send[source] = target
            from_sent[target] = source
    senders = FRAMES // frames
    to_place = [-1] * (senders * chunk)
    to_frame = [-1] * (part * FRAMES)
    for p in range(part):
        for f in range(FRAMES):
            source, target = (f // frames) * chunk + (f % frames) * part + p, p * FRAMES + f
            to_place[source] = target
            to_frame[target] = source
    return [jnp.array([table], jnp.int32) for table in (to_send, from_sent, to_place, to_frame)]


def tail_tables(parts, each, frames, places, padded, blocks, part):
    rows, to_parts, region = [], [], 0
    from_parts = []
    for first, count in parts:
        own = count * each
        size = -(-frames * own // 8) * 8
        rows.append(size)
        table = [-1] * (own * FRAMES)
        for p in range(own):
            for f in range(FRAMES):
                table[p * FRAMES + f] = (f // frames) * size + (f % frames) * own + p
        to_parts.append(jnp.array([table], jnp.int32))
        source = [-1] * (blocks * size)
        for block in range(blocks):
            for f in range(frames):
                for p in range(own):
                    source[block * size + f * own + p] = f * padded + block * part + first * each + p
        from_parts += source
    return rows, to_parts, jnp.array([from_parts], jnp.int32)


def fits(mesh):
    return mesh.shape["tok"] == 8 and mesh.shape["clip"] == 4


MESH = pl.DeviceIdType.MESH


def place_of():
    clip, tok = lax.axis_index("clip"), lax.axis_index("tok")
    return clip // 2, lax.rem(clip, 2), tok // 2, lax.rem(tok, 2)


def device_at(y, core, z, x):
    return (y * 2 + core, z * 2 + x)


def greet(peers):
    barrier = pltpu.get_barrier_semaphore()
    for peer in peers:
        pl.semaphore_signal(barrier, inc=1, device_id=peer, device_id_type=MESH)
    pl.semaphore_wait(barrier, len(peers))


def remote(source, target, send_sem, recv_sem, peer):
    return pltpu.make_async_remote_copy(
        src_ref=source, dst_ref=target, send_sem=send_sem, recv_sem=recv_sem, device_id=peer, device_id_type=MESH
    )


class Part:
    def __init__(self, pieces, whole, dim, sems):
        self.pieces, self.whole, self.dim, self.sems = pieces, whole, dim, sems
        self.rows = whole.shape[dim] // (lax.axis_size("clip") * lax.axis_size("tok"))
        self.me = place_of()
        for piece, target in self.own():
            pltpu.make_async_copy(piece, target, sems.at[1]).start()

    def own(self):
        target = self.slot(*self.me)
        return [(piece, target if index is None else target.at[index]) for piece, index in self.pieces]

    def span(self, first, count, half=None):
        rows = pl.ds(pl.multiple_of(first * self.rows, 8), count * self.rows)
        if self.dim == 1:
            lead = max(self.whole.shape[0] * 3 // 4, 1)
            front = (slice(None), slice(0, lead), slice(lead, None))[0 if half is None else half + 1]
            return self.whole.at[front, rows]
        lanes = self.whole.shape[1] * 3 // 512 * 128
        return self.whole.at[rows, (slice(None), slice(0, lanes), slice(lanes, None))[0 if half is None else half + 1]]

    def slot(self, y, core, z, x, half=None):
        clip, tok = device_at(y, core, z, x)
        return self.span(clip * 8 + tok, 1, half)

    def send(self, source, target, sem, peer):
        remote(source, target, self.sems.at[0], self.sems.at[sem], device_at(*peer)).start()

    def arrive(self, target, sem):
        pltpu.make_async_copy(target, target, self.sems.at[sem]).wait()

    def pass_on(self, far, sources=None):
        y, core, z, x = self.me
        owner = (y, core, far, x)
        target = self.slot(*owner)
        for source, target in sources or [(target, target)]:
            self.send(source, target, 8 + far, (y, core, z, 1 - x))
            self.send(source, target, 12 + far, (1 - y, core, z, x))
            self.send(source, target, 2 + y, (y, 1 - core, z, x))

    def to_core(self, owner):
        y, core, z, x = self.me
        target = self.slot(*owner)
        self.send(target, target, 2 + owner[0], (y, 1 - core, z, x))

    def hop(self, far, up, sources=None):
        y, core, z, x = self.me
        target = self.slot(y, core, far, x)
        for source, target in sources or [(target, target)]:
            self.send(source, target, 4 + far, (y, core, z + up, x))

    def relay(self, distance, up):
        y, core, z, x = self.me
        far = z - distance * up
        here = z >= distance if up > 0 else z <= 3 - distance
        on = z < 3 if up > 0 else z > 0

        @pl.when(here)
        def _():
            self.arrive(self.slot(y, core, far, x), 4 + far)

            @pl.when(on)
            def _():
                self.hop(far, up)

            self.pass_on(far)

    def stage(self, number):
        y, core, z, x = self.me
        if number == 0:
            own = self.own()

            @pl.when(z < 3)
            def _():
                self.hop(z, 1, own)

            @pl.when(z > 0)
            def _():
                self.hop(z, -1, own)

            self.pass_on(z, own)
        elif number <= 3:
            self.relay(number, 1)
            self.relay(number, -1)
        elif number == 4:
            for d in range(4):
                far = lax.rem(z + 4 - d, 4)
                owner = (y, core, far, 1 - x)
                self.arrive(self.slot(*owner), 8 + far)
                self.send(self.slot(*owner, 0), self.slot(*owner, 0), 16 + far, (1 - y, core, z, x))
                self.to_core(owner)
                owner = (1 - y, core, far, x)
                self.arrive(self.slot(*owner), 12 + far)
                self.send(self.slot(*owner, 1), self.slot(*owner, 1), 20 + far, (y, core, z, 1 - x))
                self.to_core(owner)
        elif number == 5:
            for d in range(4):
                far = lax.rem(z + 4 - d, 4)
                owner = (1 - y, core, far, 1 - x)
                self.arrive(self.slot(*owner, 0), 16 + far)
                self.arrive(self.slot(*owner, 1), 20 + far)
                self.to_core(owner)
        else:
            self.arrive(self.slot(*self.me), 1)
            for far in range(2):
                self.arrive(self.span((far * 2 + 1 - core) * 8, 8), 2 + far)
            self.arrive(self.span(0, 28), 0)
            hops = jnp.where(z == 0, 1, 0) + jnp.where(z == 3, 1, 0)

            @pl.when(hops > 0)
            def _():
                self.arrive(self.span(0, 1), 0)

            @pl.when(hops == 0)
            def _():
                self.arrive(self.span(0, 5), 0)


PART_SEMS = 24


def tok_peers(count):
    clip, tok = lax.axis_index("clip"), lax.axis_index("tok")
    return [(clip, lax.rem(tok + d, count)) for d in range(1, count)]


def all_peers(groups, members):
    clip, tok = lax.axis_index("clip"), lax.axis_index("tok")
    return [
        (lax.rem(clip + c, groups), lax.rem(tok + t, members))
        for c in range(groups) for t in range(members) if c or t
    ]


def fast_device(
    tokens,
    adapter_index,
    norm_gain,
    norm_shift,
    spatial_weights,
    spatial_output,
    temporal_weights,
    temporal_output,
    expand_weight,
    reduce_weight,
    attention_down,
    attention_up,
    expand_down,
    expand_up,
    reduce_down,
    reduce_up,
    cotangent,
):
    frames, clips, places, width = tokens.shape[1:]
    members, groups = lax.axis_size("tok"), lax.axis_size("clip")
    blocks = members // clips
    part = places // blocks
    chunk = -(-frames * part // 8) * 8
    padded = -(-places // 16) * 16
    half, total = frames * padded, clips * frames * padded
    rows_all = FRAMES * part
    ff = expand_weight.shape[1]
    sizes = (frames, clips, places, width, padded)
    to_send, from_sent, to_place, to_frame = order_tables(frames, places, padded, blocks, part, chunk)
    devices = members * groups

    def placed_rows(rows):
        return rows[0].transpose(0, 2, 1, 3)

    def whole(shard, dim):
        dims = list(shard.shape)
        dims[dim] *= devices
        return jax.ShapeDtypeStruct(tuple(dims), shard.dtype)

    any_spec, vmem_spec = pl.BlockSpec(memory_space=pl.ANY), pl.BlockSpec(memory_space=pltpu.VMEM)
    smem_spec = pl.BlockSpec(memory_space=pltpu.SMEM)
    x_view, cot_view = placed_rows(tokens), placed_rows(cotangent)
    up_rows = jnp.swapaxes(attention_up, 1, 2)
    saved = [
        shape_of(3, total, width),
        shape_of(frames * clips * HEADS // 2, 2 * padded, padded),
        shape_of(total, width),
        shape_of(4, total, ADAPT),
        shape_of(total, width),
    ]
    weights = [shape_of(4, width, width), shape_of(2 * 4, width, ADAPT)]
    scratch = [pltpu.VMEM(value.shape, value.dtype) for value in saved + weights]
    group = rows_all // 7
    tail_parts = ((0, 4), (4, 3))
    tail_rows, to_tails, from_tails = tail_tables(tail_parts, group // FRAMES, frames, places, padded, blocks, part)
    regions = []
    for rows_each in tail_rows:
        regions.append((sum(members * r for r in tail_rows[: len(regions)]), blocks * rows_each))
    blocks_shape = shape_of(total, width)
    outs = pl.pallas_call(
        functools.partial(
            front, sizes, (rows_all, group, 512, devices), members, tail_parts,
            scopes=(
                [
                    pltpu.VMEM((frames, clips, places, width), F32),
                    pltpu.VMEM((frames, clips, places, width), F32),
                    pltpu.VMEM((half, width), BF16),
                    *scratch[0:5],
                ],
                [
                    pltpu.VMEM((total, width), BF16),
                    pltpu.VMEM((total, width), BF16),
                    pltpu.VMEM((rows_all, width), BF16),
                    pltpu.VMEM((rows_all, width), F32),
                    pltpu.VMEM((rows_all, width), BF16),
                    pltpu.VMEM((rows_all, width), BF16),
                    pltpu.VMEM((3, rows_all, width), BF16),
                    pltpu.VMEM((rows_all // group * HEADS // 2, 2 * group, group), BF16),
                    pltpu.VMEM((rows_all, width), BF16),
                    pltpu.VMEM((5, rows_all, ADAPT), BF16),
                    pltpu.VMEM((rows_all, ADAPT), BF16),
                    pltpu.VMEM((rows_all, width), BF16),
                    pltpu.VMEM((rows_all, width), F32),
                    pltpu.VMEM((rows_all, width), F32),
                    pltpu.VMEM((2, rows_all, ADAPT), F32),
                    pltpu.VMEM((rows_all, width), BF16),
                    pltpu.VMEM((3, rows_all, width), BF16),
                    pltpu.VMEM((5, ADAPT, width), F32),
                    pltpu.VMEM((5, ADAPT, width), F32),
                    pltpu.VMEM((2, ADAPT, ff), F32),
                ],
            ),
        ),
        out_shape=[
            *weights, *weights, whole(expand_weight, 0), whole(reduce_weight, 0), shape_of(2, ff, ADAPT),
            shape_of(2, width, ADAPT), blocks_shape, blocks_shape, blocks_shape, blocks_shape, *saved,
            shape_of(width, 384),
        ],
        in_specs=[smem_spec] + [vmem_spec] * 5 + [any_spec] * 2 + [vmem_spec] * 2 + [any_spec] * 12,
        out_specs=[any_spec] * 17 + [vmem_spec],
        scratch_shapes=[
            *scratch[5:7],
            pltpu.VMEM((width, ff), BF16),
            pltpu.VMEM((ff, width), BF16),
            pltpu.VMEM((2, ff, ADAPT), BF16),
            pltpu.VMEM((2, width, ADAPT), BF16),
            pltpu.VMEM((members, chunk, width), BF16),
            pltpu.VMEM((members, chunk, width), BF16),
            *[pltpu.VMEM((members, rows_each, width), BF16) for rows_each in tail_rows],
            pltpu.SemaphoreType.DMA((9, PART_SEMS)),
            pltpu.SemaphoreType.DMA((30,)),
            pltpu.SemaphoreType.DMA((5, members)),
            pltpu.SemaphoreType.DMA((5, members)),
        ],
        compiler_params=pltpu.CompilerParams(collective_id=0, has_side_effects=True, vmem_limit_bytes=63 << 20),
        name="front",
    )(
        adapter_index, to_send, to_place, to_frame, *to_tails, x_view, cot_view, norm_gain, norm_shift,
        spatial_weights, spatial_output, temporal_weights, temporal_output, attention_down, up_rows,
        expand_weight, reduce_weight, expand_up.T, reduce_down, expand_down, reduce_up.T,
    )
    sp_w, sp_adapt = outs[0:2]
    made, back, *kept, mid_pay = outs[10:18]
    step = width // devices
    fold = ff // width
    results = pl.pallas_call(
        functools.partial(spatial_backward, sizes, groups, members, step, regions),
        out_shape=[
            shape_of(*x_view.shape, kind=F32),
            shape_of(*x_view.shape, kind=F32),
            shape_of(8, step, ADAPT, kind=F32),
            shape_of(8, step, ADAPT, kind=F32),
            shape_of(step, ADAPT, kind=F32),
            shape_of(fold * step, ADAPT, kind=F32),
            shape_of(fold * step, ADAPT, kind=F32),
            shape_of(step, ADAPT, kind=F32),
        ],
        in_specs=[smem_spec, vmem_spec, vmem_spec, vmem_spec] + [any_spec] * 11,
        out_specs=[any_spec] * 2 + [vmem_spec] * 6,
        scratch_shapes=[
            *scratch[5:7],
            *scratch[0:5],
            pltpu.VMEM((total, width), BF16),
            pltpu.VMEM((total, width), BF16),
            pltpu.VMEM((frames, clips, places, width), F32),
            pltpu.VMEM((frames, clips, places, width), F32),
            pltpu.VMEM((devices, step, 384), BF16),
            *[pltpu.VMEM((devices, step, 128), BF16)] * 4,
            pltpu.VMEM((total, width), BF16),
            pltpu.VMEM((total, width), BF16),
            pltpu.VMEM((3, total, width), BF16),
            pltpu.VMEM((clips, half, width), F32),
            pltpu.VMEM((4, ADAPT, width), F32),
            pltpu.VMEM((4, ADAPT, width), F32),
            pltpu.SemaphoreType.DMA((21,)),
            pltpu.SemaphoreType.DMA((3, devices - 1)),
            pltpu.SemaphoreType.DMA((3, devices - 1)),
        ],
        compiler_params=pltpu.CompilerParams(collective_id=1, has_side_effects=True, vmem_limit_bytes=63 << 20),
        name="spatial_back",
    )(
        adapter_index, from_sent, from_tails, norm_gain, x_view, sp_w, sp_adapt, *kept, back, made,
        mid_pay.reshape(devices, step, 384),
    )
    dx, out, down, up, gea, geb, gra, grb = pl.pallas_call(
        functools.partial(deliver, len(results)),
        out_shape=[jax.ShapeDtypeStruct(value.shape, value.dtype) for value in results],
        in_specs=[any_spec] * len(results),
        out_specs=[any_spec] * len(results),
        scratch_shapes=[pltpu.VMEM(value.shape, value.dtype) for value in results]
        + [pltpu.SemaphoreType.DMA((2 * len(results),))],
        name="deliver",
    )(*results)

    def whole_rows(rows):
        return rows.transpose(0, 2, 1, 3)[None]

    return (whole_rows(out), whole_rows(dx), down, jnp.swapaxes(up, 1, 2), gea, geb.T, gra, grb.T)


def solution(mesh):
    pick = fast_device if fits(mesh) else general_device

    placed = (
        P(("clip", "tok"), None, None, None, None),
        P("clip"),
        P(),
        P(),
        P(None, ("clip", "tok"), None),
        P(("clip", "tok"), None),
        P(None, ("clip", "tok"), None),
        P(("clip", "tok"), None),
        P(("clip", "tok"), None),
        P(("clip", "tok"), None),
        P(None, ("clip", "tok"), None),
        P(None, None, ("clip", "tok")),
        P(("clip", "tok"), None),
        P(None, ("clip", "tok")),
        P(("clip", "tok"), None),
        P(None, ("clip", "tok")),
        P(("clip", "tok"), None, None, None, None),
    )
    return jax.shard_map(
        pick,
        mesh=mesh,
        in_specs=placed,
        out_specs=(
            P(("clip", "tok"), None, None, None, None),
            P(("clip", "tok"), None, None, None, None),
            P(None, ("clip", "tok"), None),
            P(None, None, ("clip", "tok")),
            P(("clip", "tok"), None),
            P(None, ("clip", "tok")),
            P(("clip", "tok"), None),
            P(None, ("clip", "tok")),
        ),
        check_vma=False,
    )
```

```python
import functools

import jax
import jax.numpy as jnp
from jax import lax
from jax.experimental import pallas as pl
from jax.experimental.pallas import tpu as pltpu
from jax.sharding import PartitionSpec as P

HEADS = 12
HEAD_DIM = 64
FRAMES = 16
ADAPTERS = 8
RANK = 16


EPSILON = 1e-06


def layer_norm(stream, gain_row, shift_row):
    average = jnp.mean(stream, axis=-1, keepdims=True)
    centred = stream - average
    variance = jnp.mean(centred * centred, axis=-1, keepdims=True)
    return centred * lax.rsqrt(variance + EPSILON) * gain_row + shift_row


def adapter_mask(choice_rows):
    columns = jnp.arange(ADAPTERS * RANK, dtype=jnp.int32) // RANK
    return (columns[None, :] == choice_rows[:, None]).astype(jnp.float32)


def project_many(inputs, weight, down_rows, up_rows, mask):
    hidden = jnp.einsum("rd,ndc->nrc", inputs, down_rows, preferred_element_type=jnp.float32)
    hidden = (hidden * mask).astype(jnp.bfloat16)
    result = jnp.einsum("rd,nde->nre", inputs, weight, preferred_element_type=jnp.float32)
    result = result + jnp.einsum(
        "nrc,nce->nre", hidden, up_rows, preferred_element_type=jnp.float32
    )
    return (result, hidden)


def project_back(inputs, hidden, grad_rows, weight, down_rows, up_rows, mask):
    hidden_grad = jnp.einsum("nre,nce->nrc", grad_rows, up_rows, preferred_element_type=jnp.float32)
    hidden_grad = (hidden_grad * mask).astype(jnp.bfloat16)
    input_grad = jnp.einsum("nre,nde->rd", grad_rows, weight, preferred_element_type=jnp.float32)
    input_grad = input_grad + jnp.einsum(
        "nrc,ndc->rd", hidden_grad, down_rows, preferred_element_type=jnp.float32
    )
    down_grad = jnp.einsum("rd,nrc->ndc", inputs, hidden_grad, preferred_element_type=jnp.float32)
    up_grad = jnp.einsum("nrc,nre->nce", hidden, grad_rows, preferred_element_type=jnp.float32)
    return (input_grad, down_grad, up_grad)


def attend_forward(packed, layout):
    view_shape, score_eq, mix_eq, back_eq = layout
    queries = packed[0].reshape(view_shape)
    key_rows = packed[1].reshape(view_shape)
    values = packed[2].reshape(view_shape)
    scores = jnp.einsum(
        score_eq, queries, key_rows, preferred_element_type=jnp.float32
    ) * HEAD_DIM ** (-0.5)
    ceiling = jnp.max(scores, axis=-1, keepdims=True)
    expo_rows = jnp.exp(scores - ceiling)
    totals = jnp.sum(expo_rows, axis=-1, keepdims=True)
    weights_soft = (expo_rows / totals).astype(jnp.bfloat16)
    mixed_rows = jnp.einsum(mix_eq, weights_soft, values, preferred_element_type=jnp.float32)
    return (mixed_rows.reshape(packed.shape[1:]), ceiling + jnp.log(totals))


def attend_backward(packed, log_total, mixed_grad, layout):
    view_shape, score_eq, mix_eq, back_eq = layout
    scaling = HEAD_DIM ** (-0.5)
    queries = packed[0].reshape(view_shape)
    key_rows = packed[1].reshape(view_shape)
    values = packed[2].reshape(view_shape)
    scores = jnp.einsum(score_eq, queries, key_rows, preferred_element_type=jnp.float32) * scaling
    weights_soft = jnp.exp(scores - log_total)
    output_grad = mixed_grad.reshape(view_shape)
    soft_grad = jnp.einsum(score_eq, output_grad, values, preferred_element_type=jnp.float32)
    row_inner = jnp.sum(weights_soft * soft_grad, axis=-1, keepdims=True)
    score_grad = (weights_soft * (soft_grad - row_inner)).astype(jnp.bfloat16)
    query_grad = (
        jnp.einsum(mix_eq, score_grad, key_rows, preferred_element_type=jnp.float32) * scaling
    )
    key_grad = (
        jnp.einsum(back_eq, score_grad, queries, preferred_element_type=jnp.float32) * scaling
    )
    value_grad = jnp.einsum(
        back_eq, weights_soft.astype(jnp.bfloat16), output_grad, preferred_element_type=jnp.float32
    )
    stacked = jnp.stack([query_grad, key_grad, value_grad])
    return stacked.reshape(packed.shape).astype(jnp.bfloat16)


def attention_forward(stream, gain_row, shift_row, weight_set, mask, layout):
    inner_weights, outer_weight, down_rows, up_rows = weight_set
    normed = layer_norm(stream, gain_row, shift_row).astype(jnp.bfloat16)
    packed, packed_hidden = project_many(normed, inner_weights, down_rows[0:3], up_rows[0:3], mask)
    packed = packed.astype(jnp.bfloat16)
    mixed_rows, log_total = attend_forward(packed, layout)
    mixed_rows = mixed_rows.astype(jnp.bfloat16)
    branch, outer_hidden = project_many(
        mixed_rows, outer_weight[None], down_rows[3:4], up_rows[3:4], mask
    )
    return (
        stream + branch[0],
        (normed, packed, packed_hidden, mixed_rows, outer_hidden, log_total),
    )


def attention_backward(
    stream, stream_grad, gain_row, shift_row, weight_set, mask, layout, kept_values
):
    inner_weights, outer_weight, down_rows, up_rows = weight_set
    normed, packed, packed_hidden, mixed_rows, outer_hidden, log_total = kept_values
    branch_grad = stream_grad.astype(jnp.bfloat16)[None]
    mixed_grad, outer_down, outer_up = project_back(
        mixed_rows,
        outer_hidden,
        branch_grad,
        outer_weight[None],
        down_rows[3:4],
        up_rows[3:4],
        mask,
    )
    packed_grad = attend_backward(packed, log_total, mixed_grad.astype(jnp.bfloat16), layout)
    normed_grad, inner_down, inner_up = project_back(
        normed, packed_hidden, packed_grad, inner_weights, down_rows[0:3], up_rows[0:3], mask
    )
    unused, norm_pull = jax.vjp(lambda rows_in: layer_norm(rows_in, gain_row, shift_row), stream)
    before_grad = stream_grad + norm_pull(normed_grad)[0]
    return (
        before_grad,
        jnp.concatenate([inner_down, outer_down], axis=0),
        jnp.concatenate([inner_up, outer_up], axis=0),
    )


def expand_forward(stream, gain_row, shift_row, weight_set, mask):
    up_weight, down_weight, in_down, in_up, out_down, out_up = weight_set
    normed = layer_norm(stream, gain_row, shift_row).astype(jnp.bfloat16)
    inner_rows, inner_hidden = project_many(
        normed, up_weight[None], in_down[None], in_up[None], mask
    )
    inner_rows = inner_rows[0]
    active = jax.nn.gelu(inner_rows, approximate=True).astype(jnp.bfloat16)
    branch, outer_hidden = project_many(
        active, down_weight[None], out_down[None], out_up[None], mask
    )
    return (stream + branch[0], (normed, inner_rows, inner_hidden, active, outer_hidden))


def expand_backward(stream, stream_grad, gain_row, shift_row, weight_set, mask, kept_values):
    up_weight, down_weight, in_down, in_up, out_down, out_up = weight_set
    normed, inner_rows, inner_hidden, active, outer_hidden = kept_values
    branch_grad = stream_grad.astype(jnp.bfloat16)[None]
    active_grad, out_down_grad, out_up_grad = project_back(
        active, outer_hidden, branch_grad, down_weight[None], out_down[None], out_up[None], mask
    )
    unused, gelu_pull = jax.vjp(
        lambda values_in: jax.nn.gelu(values_in, approximate=True), inner_rows
    )
    inner_grad = gelu_pull(active_grad)[0].astype(jnp.bfloat16)[None]
    normed_grad, in_down_grad, in_up_grad = project_back(
        normed, inner_hidden, inner_grad, up_weight[None], in_down[None], in_up[None], mask
    )
    unused_norm, norm_pull = jax.vjp(
        lambda rows_in: layer_norm(rows_in, gain_row, shift_row), stream
    )
    before_grad = stream_grad + norm_pull(normed_grad)[0]
    return (before_grad, (in_down_grad[0], in_up_grad[0], out_down_grad[0], out_up_grad[0]))


def regroup_places(stream, layout_sizes, backward):
    frames_dev, clips_dev, places, model_width, clip_rows, place_blocks, place_part = layout_sizes
    padded = jnp.pad(
        stream.reshape(frames_dev, clips_dev, places, model_width),
        ((0, 0), (0, 0), (0, place_part * place_blocks - places), (0, 0)),
    )
    padded = padded.reshape(frames_dev, clips_dev * place_blocks, place_part, model_width)
    if backward:
        arrived = lax.all_to_all(
            padded.astype(jnp.bfloat16), "tok", split_axis=1, concat_axis=0, tiled=True
        ).astype(padded.dtype)
    else:
        arrived = lax.all_to_all(
            padded.astype(jnp.bfloat16), "tok", split_axis=1, concat_axis=0, tiled=True
        ).astype(padded.dtype)
    return arrived.reshape(clip_rows * FRAMES * place_part, model_width)


def regroup_frames(stream, layout_sizes, backward):
    frames_dev, clips_dev, places, model_width, clip_rows, place_blocks, place_part = layout_sizes
    shaped = stream.reshape(clip_rows * FRAMES, 1, place_part, model_width)
    if backward:
        arrived = lax.all_to_all(
            shaped.astype(jnp.bfloat16), "tok", split_axis=0, concat_axis=1, tiled=True
        ).astype(shaped.dtype)
    else:
        arrived = lax.all_to_all(
            shaped.astype(jnp.bfloat16), "tok", split_axis=0, concat_axis=1, tiled=True
        ).astype(shaped.dtype)
    arrived = arrived.reshape(frames_dev, clips_dev, place_part * place_blocks, model_width)
    return arrived[:, :, :places].reshape(frames_dev * clips_dev * places, model_width)


def general_device(
    tokens,
    adapter_index,
    norm_gain,
    norm_shift,
    spatial_weights,
    spatial_output,
    temporal_weights,
    temporal_output,
    expand_weight,
    reduce_weight,
    attention_down,
    attention_up,
    expand_down,
    expand_up,
    reduce_down,
    reduce_up,
    cotangent,
):
    frames_dev, clips_dev, places, model_width = tokens.shape[1:]
    tok_count = lax.axis_size("tok")
    frame_blocks = FRAMES // frames_dev
    clip_rows = tok_count // frame_blocks
    place_blocks = tok_count // clips_dev
    place_part = -(-places // place_blocks)
    layout_sizes = (frames_dev, clips_dev, places, model_width, clip_rows, place_blocks, place_part)
    adapt_cols = ADAPTERS * RANK
    position = lax.axis_index("tok")
    spatial_choice = lax.dynamic_slice_in_dim(
        adapter_index, position // frame_blocks * clips_dev, clips_dev
    )
    spatial_mask = jnp.broadcast_to(
        adapter_mask(spatial_choice)[None, :, None, :], (frames_dev, clips_dev, places, adapt_cols)
    ).reshape(-1, adapt_cols)
    temporal_choice = lax.dynamic_slice_in_dim(
        adapter_index.reshape(clip_rows, clips_dev), position // place_blocks, 1, 1
    )[:, 0]
    temporal_mask = jnp.broadcast_to(
        adapter_mask(temporal_choice)[:, None, None, :], (clip_rows, FRAMES, place_part, adapt_cols)
    ).reshape(-1, adapt_cols)
    spatial_layout = (
        (frames_dev * clips_dev, places, HEADS, HEAD_DIM),
        "gqhd,gkhd->ghqk",
        "ghqk,gkhd->gqhd",
        "ghqk,gqhd->gkhd",
    )
    temporal_layout = (
        (clip_rows, FRAMES, place_part, HEADS, HEAD_DIM),
        "aqphd,akphd->aphqk",
        "aphqk,akphd->aqphd",
        "aphqk,aqphd->akphd",
    )
    spatial_set = (
        lax.all_gather(spatial_weights, ("clip", "tok"), axis=1, tiled=True),
        lax.all_gather(spatial_output, ("clip", "tok"), axis=0, tiled=True),
        lax.all_gather(attention_down[0:4], ("clip", "tok"), axis=1, tiled=True),
        lax.all_gather(attention_up[0:4], ("clip", "tok"), axis=2, tiled=True),
    )
    stream0 = tokens.reshape(-1, model_width)
    stream1, spatial_kept = attention_forward(
        stream0, norm_gain[0], norm_shift[0], spatial_set, spatial_mask, spatial_layout
    )
    placed1 = regroup_places(stream1, layout_sizes, False)
    temporal_set = (
        lax.all_gather(temporal_weights, ("clip", "tok"), axis=1, tiled=True),
        lax.all_gather(temporal_output, ("clip", "tok"), axis=0, tiled=True),
        lax.all_gather(attention_down[4:8], ("clip", "tok"), axis=1, tiled=True),
        lax.all_gather(attention_up[4:8], ("clip", "tok"), axis=2, tiled=True),
    )
    placed2, temporal_kept = attention_forward(
        placed1, norm_gain[1], norm_shift[1], temporal_set, temporal_mask, temporal_layout
    )
    stream2 = regroup_frames(placed2, layout_sizes, False)
    expand_set = (
        lax.all_gather(expand_weight, ("clip", "tok"), axis=0, tiled=True),
        lax.all_gather(reduce_weight, ("clip", "tok"), axis=0, tiled=True),
        lax.all_gather(expand_down, ("clip", "tok"), axis=0, tiled=True),
        lax.all_gather(expand_up, ("clip", "tok"), axis=1, tiled=True),
        lax.all_gather(reduce_down, ("clip", "tok"), axis=0, tiled=True),
        lax.all_gather(reduce_up, ("clip", "tok"), axis=1, tiled=True),
    )
    stream3, expand_kept = expand_forward(
        stream2, norm_gain[2], norm_shift[2], expand_set, spatial_mask
    )
    expand_set = (
        lax.all_gather(expand_weight, ("clip", "tok"), axis=0, tiled=True),
        lax.all_gather(reduce_weight, ("clip", "tok"), axis=0, tiled=True),
        lax.all_gather(expand_down, ("clip", "tok"), axis=0, tiled=True),
        lax.all_gather(expand_up, ("clip", "tok"), axis=1, tiled=True),
        lax.all_gather(reduce_down, ("clip", "tok"), axis=0, tiled=True),
        lax.all_gather(reduce_up, ("clip", "tok"), axis=1, tiled=True),
    )
    grad2, expand_grads = expand_backward(
        stream2,
        cotangent.reshape(-1, model_width),
        norm_gain[2],
        norm_shift[2],
        expand_set,
        spatial_mask,
        expand_kept,
    )
    placed_grad2 = regroup_places(grad2, layout_sizes, True)
    temporal_set = (
        lax.all_gather(temporal_weights, ("clip", "tok"), axis=1, tiled=True),
        lax.all_gather(temporal_output, ("clip", "tok"), axis=0, tiled=True),
        lax.all_gather(attention_down[4:8], ("clip", "tok"), axis=1, tiled=True),
        lax.all_gather(attention_up[4:8], ("clip", "tok"), axis=2, tiled=True),
    )
    placed_grad1, temporal_down, temporal_up = attention_backward(
        placed1,
        placed_grad2,
        norm_gain[1],
        norm_shift[1],
        temporal_set,
        temporal_mask,
        temporal_layout,
        temporal_kept,
    )
    grad1 = regroup_frames(placed_grad1, layout_sizes, True)
    spatial_set = (
        lax.all_gather(spatial_weights, ("clip", "tok"), axis=1, tiled=True),
        lax.all_gather(spatial_output, ("clip", "tok"), axis=0, tiled=True),
        lax.all_gather(attention_down[0:4], ("clip", "tok"), axis=1, tiled=True),
        lax.all_gather(attention_up[0:4], ("clip", "tok"), axis=2, tiled=True),
    )
    grad0, spatial_down, spatial_up = attention_backward(
        stream0,
        grad1,
        norm_gain[0],
        norm_shift[0],
        spatial_set,
        spatial_mask,
        spatial_layout,
        spatial_kept,
    )
    owned = (
        lax.psum_scatter(
            jnp.concatenate([spatial_down, temporal_down], axis=0),
            ("clip", "tok"),
            scatter_dimension=1,
            tiled=True,
        ),
        lax.psum_scatter(
            jnp.concatenate([spatial_up, temporal_up], axis=0),
            ("clip", "tok"),
            scatter_dimension=2,
            tiled=True,
        ),
        lax.psum_scatter(expand_grads[0], ("clip", "tok"), scatter_dimension=0, tiled=True),
        lax.psum_scatter(expand_grads[1], ("clip", "tok"), scatter_dimension=1, tiled=True),
        lax.psum_scatter(expand_grads[2], ("clip", "tok"), scatter_dimension=0, tiled=True),
        lax.psum_scatter(expand_grads[3], ("clip", "tok"), scatter_dimension=1, tiled=True),
    )
    return (
        stream3.reshape(tokens.shape),
        grad0.reshape(tokens.shape),
        owned[0],
        owned[1],
        owned[2],
        owned[3],
        owned[4],
        owned[5],
    )


F32 = jnp.float32
BF16 = jnp.bfloat16
ADAPT = ADAPTERS * RANK
SPATIAL_UNROLL = 6
SPATIAL_BACK_UNROLL = 3
MIDDLE_UNROLL = 6
MIDDLE_BACK_UNROLL = 6


def nn(left, right):
    return lax.dot_general(left, right, (((1,), (0,)), ((), ())), preferred_element_type=F32)


def nt(left, right):
    return lax.dot_general(left, right, (((1,), (1,)), ((), ())), preferred_element_type=F32)


def tn(left, right):
    return lax.dot_general(left, right, (((0,), (0,)), ((), ())), preferred_element_type=F32)


def one_hot(target_row, rows):
    row_ids = lax.broadcasted_iota(jnp.int32, (rows, target_row.shape[1]), 0)
    return (row_ids == target_row).astype(F32).astype(BF16)


def column_mask(choice):
    return (lax.broadcasted_iota(jnp.int32, (1, ADAPT), 1) // RANK == choice).astype(F32)


def set_rows(rows, choice):
    total = jnp.zeros((RANK, rows.shape[1]), F32)
    for k in range(ADAPTERS):
        total = jnp.where(choice == k, rows[k * RANK : (k + 1) * RANK], total)
    return total


def norm_rows(rows, gain_row, shift_row):
    average = jnp.mean(rows, axis=-1, keepdims=True)
    centred = rows - average
    variance = jnp.mean(centred * centred, axis=-1, keepdims=True)
    return centred * lax.rsqrt(variance + EPSILON) * gain_row + shift_row


def norm_back(rows, pulled, gain_row):
    average = jnp.mean(rows, axis=-1, keepdims=True)
    centred = rows - average
    variance = jnp.mean(centred * centred, axis=-1, keepdims=True)
    scale = lax.rsqrt(variance + EPSILON)
    unit = centred * scale
    scaled = pulled * gain_row
    return scale * (
        scaled
        - jnp.mean(scaled, axis=-1, keepdims=True)
        - unit * jnp.mean(scaled * unit, axis=-1, keepdims=True)
    )


def soften(scores, keep):
    scores = jnp.where(keep, scores, -1e30)
    ceiling = jnp.max(scores, axis=-1, keepdims=True)
    expo = jnp.exp(scores - ceiling)
    return expo * (1.0 / jnp.sum(expo, axis=-1, keepdims=True))


def two_heads(rows, low):
    zero = jnp.zeros_like(rows)
    return jnp.concatenate([jnp.where(low, rows, zero), jnp.where(low, zero, rows)], axis=0)


def one_pair(both, low):
    count = both.shape[0] // 2
    return jnp.where(low, both[:count], both[count:])


def attention_pair(query, key, value, keep, low):
    weights = soften(nt(two_heads(query, low), key), keep).astype(BF16)
    return weights, one_pair(nn(weights, value), low).astype(BF16)


def attention_all(sizes, first, qkv, soft, mixed, keep, low, unroll):
    start, blocks, rows_each, pairs = sizes

    @pl.loop(0, blocks * pairs // unroll)
    def _(turn):
        block = turn // (pairs // unroll)
        lead = (turn - block * (pairs // unroll)) * unroll
        rows = pl.ds(pl.multiple_of(start + block * rows_each, 16), rows_each)
        for u in range(unroll):
            lanes = pl.ds(pl.multiple_of((lead + u) * 128, 128), 128)
            weights, made = attention_pair(
                qkv[0, rows, lanes], qkv[1, rows, lanes], qkv[2, rows, lanes], keep, low
            )
            soft[(first + block) * pairs + lead + u] = weights
            mixed[rows, lanes] = made


def attention_all_back(sizes, qkv, soft, gmix, gqkv, low, unroll, first=0):
    blocks, rows_each, pairs = sizes

    @pl.loop(0, blocks * pairs // unroll)
    def _(turn):
        block = turn // (pairs // unroll)
        lead = (turn - block * (pairs // unroll)) * unroll
        block = block + first
        rows = pl.ds(pl.multiple_of(block * rows_each, 16), rows_each)
        spans = [pl.ds(pl.multiple_of((lead + u) * 128, 128), 128) for u in range(unroll)]
        made = attention_back(
            [[qkv[n, rows, lanes] for lanes in spans] for n in range(3)],
            [soft[block * pairs + lead + u] for u in range(unroll)],
            [gmix[rows, lanes] for lanes in spans],
            low,
        )
        for n in range(3):
            for lanes, value in zip(spans, made[n]):
                gqkv[n, rows, lanes] = value.astype(BF16)


def block_rows(ref, slots, number, offset=0):
    chunk = slots.shape[1]
    return ref.at[pl.ds(pl.multiple_of(offset + number * chunk, 8), chunk)]


def send_blocks(slots, got, count, first, send_sems, recv_sems, local_sem, offset=0):
    clip, tok = lax.axis_index("clip"), lax.axis_index("tok")
    target = block_rows(got, slots, tok, offset)
    for n in range(count):
        place = first + lax.rem(tok + n, count)

        @pl.when(place != tok)
        def _():
            remote(slots.at[place], target, send_sems.at[place], recv_sems.at[tok], (clip, place)).start()

        @pl.when(place == tok)
        def _():
            pltpu.make_async_copy(slots.at[place], target, local_sem).start()


def wait_blocks(slots, got, members, send_sems, recv_sems, local_sem, offset=0):
    tok = lax.axis_index("tok")
    for d in range(1, members):
        place = lax.rem(tok + d, members)
        target = block_rows(got, slots, place, offset)
        pltpu.make_async_copy(slots.at[place], slots.at[place], send_sems.at[place]).wait()
        pltpu.make_async_copy(target, target, recv_sems.at[place]).wait()
    pltpu.make_async_copy(slots.at[tok], block_rows(got, slots, tok, offset), local_sem).wait()


def attention_back(packed, weights, grads, low):
    queries, keys, values = packed
    stacked = [two_heads(grad, low) for grad in grads]
    pulled = [nt(grad, value) for grad, value in zip(stacked, values)]
    value_grads = [tn(soft, grad) for soft, grad in zip(weights, stacked)]
    scores = []
    for soft, pull in zip(weights, pulled):
        wide = soft.astype(F32)
        inner = jnp.sum(wide * pull, axis=-1, keepdims=True)
        scores.append((wide * (pull - inner)).astype(BF16))
    query_grads = [one_pair(nn(score, key), low) * HEAD_DIM**-0.5 for score, key in zip(scores, keys)]
    key_grads = [tn(score, two_heads(query, low)) for score, query in zip(scores, queries)]
    return query_grads, key_grads, value_grads


def spatial_backward(
    sizes, groups, members, step, regions, idx, from_sent, from_tails, gain, x_hbm, w_hbm, ad_hbm, qkv_hbm, soft_hbm, mixed_hbm, hid_hbm, zs_hbm,
    got_hbm, made_hbm, mid_pay,
    dx_hbm, out_hbm, down_out, up_out, ea, eb, ra, rb,
    w, ad, qkv, soft, mixed, hid, zs, got, made, x, out, mid, sp, pay, sp_late, pay_late, grad, gmix, gqkv, gpull, gdown, gup, copy_sems, send_sems, recv_sems
):
    frames, clips, places, width, padded = sizes
    half = frames * padded
    devices = groups * members

    def row_copies(view, rows, first, inward):
        copies = []
        for i in range(frames):
            for b in range(clips):
                ends = (view.at[i, :, b, :], rows.at[i, b])
                ends = ends if inward else ends[::-1]
                copies.append(pltpu.make_async_copy(*ends, copy_sems.at[first + i * clips + b]))
        return copies

    fills = [
        pltpu.make_async_copy(source, target, copy_sems.at[10 + n])
        for n, (source, target) in enumerate(
            (
                (got_hbm, got), (w_hbm.at[3], w.at[3]), (ad_hbm, ad), (mixed_hbm, mixed), (hid_hbm, hid),
                (soft_hbm, soft), (qkv_hbm, qkv), (w_hbm.at[0:3], w.at[0:3]), (zs_hbm, zs), (made_hbm, made),
            )
        )
    ]
    loads = row_copies(x_hbm, x, 0, True)
    for load in fills + loads:
        load.start()
    clip, tok = lax.axis_index("clip"), lax.axis_index("tok")
    me = clip * members + tok
    peers = all_peers(groups, members)
    greet(peers)

    def terms(source, target, kind):
        for n, peer in enumerate(peers):
            place = peer[0] * members + peer[1]
            remote(
                source.at[place], target.at[me], send_sems.at[kind, n], recv_sems.at[kind, n], peer
            ).start()
        pltpu.make_async_copy(source.at[me], target.at[me], copy_sems.at[(8, 9, 20)[kind]]).start()

    def await_terms(source, target, kind):
        for n, peer in enumerate(peers):
            remote(source.at[me], target.at[me], send_sems.at[kind, n], recv_sems.at[kind, n], peer).wait()
        pltpu.make_async_copy(source.at[me], target.at[me], copy_sems.at[(8, 9, 20)[kind]]).wait()

    terms(mid_pay, mid, 0)
    for fill in fills[0:5]:
        fill.wait()
    for b in range(clips):
        rows = slice(b * half, (b + 1) * half)
        mask = column_mask(idx[b])
        arrived = []
        for begin, size in regions:
            arrived.append(got[begin + b * size : begin + (b + 1) * size])
        grad[rows] = nn(one_hot(from_tails[...], half), jnp.concatenate(arrived, axis=0)).astype(BF16)
        hidden_grad = (nn(grad[rows], ad[7]) * mask).astype(BF16)
        gmix[rows] = (nt(grad[rows], w[3]) + nt(hidden_grad, ad[3])).astype(BF16)
        down, up = tn(hidden_grad, mixed[rows]), tn(hid[3, rows], grad[rows])
        if b == 0:
            gdown[3], gup[3] = down, up
        else:
            gdown[3] += down
            gup[3] += up

    pairs = width // 128
    low = lax.broadcasted_iota(jnp.int32, (padded, 128), 1) < HEAD_DIM

    for fill in fills[5:7]:
        fill.wait()
    attention_all_back((frames * clips, padded, pairs), qkv, soft, gmix, gqkv, low, SPATIAL_BACK_UNROLL)
    for fill in fills[7:10]:
        fill.wait()
    repeat = jnp.where(idx[0] == idx[1], 0.0, 1.0)

    def pull_back(n, b, fresh):
        rows = slice(b * half, (b + 1) * half)
        own = gqkv[n, rows]
        hidden_grad = (nn(own, ad[4 + n]) * column_mask(idx[b])).astype(BF16)
        pulled = nt(own, w[n]) + nt(hidden_grad, ad[n])
        gpull[b] = pulled if fresh else gpull[b] + pulled
        down, up = tn(hidden_grad, zs[rows]), tn(hid[n, rows], own)
        if b == 0:
            gdown[n], gup[n] = down, up
        else:
            gdown[n] += down
            gup[n] += up

    def send_pair(first, pay, sp, kind):
        pieces = []
        for n in (first, first + 1):
            for source in (gdown, gup):
                pieces.append(set_rows(source[n], idx[0]))
                pieces.append(set_rows(source[n], idx[1]) * repeat)
        packed = jnp.transpose(jnp.concatenate(pieces, axis=0))
        pay[...] = packed.reshape(pay.shape).astype(BF16)
        terms(pay, sp, kind)

    for b in range(clips):
        pull_back(2, b, True)
    send_pair(2, pay_late, sp_late, 1)
    for b in range(clips):

        @pl.loop(0, 2)
        def _(n):
            pull_back(n, b, False)

    send_pair(0, pay, sp, 2)
    for load in loads:
        load.wait()
    for b in range(clips):
        rows = slice(b * half, (b + 1) * half)
        final = nn(one_hot(from_sent[...], half), made[rows])
        for i in range(frames):
            base = i * padded
            out[i, b] = final[base : base + places]
            pulled = norm_back(x[i, b], gpull[b, base : base + places], gain[0:1])
            x[i, b] = grad[b * half + base : b * half + base + places].astype(F32) + pulled
    stores = row_copies(out_hbm, out, 4, False) + row_copies(dx_hbm, x, 0, False)
    for store in stores:
        store.start()
    await_terms(mid_pay, mid, 0)
    mids, mid_choice = combine_mid((groups, members, step, eb.shape[0] // step), mid, down_out, up_out, ea, eb, ra, rb)
    await_terms(pay_late, sp_late, 1)
    combine_spatial((groups, members, step), sp_late, mids, down_out, up_out, 2)
    await_terms(pay, sp, 2)
    combine_spatial((groups, members, step), sp, mids, down_out, up_out, 0)
    for store in stores:
        store.wait()


def front(
    sizes, shape, members, tail_parts, idx, to_send, to_place, to_frame, to_first, to_second, x_hbm, cot_hbm, gain, shift,
    sh_w, sh_o, sh_tw, sh_to, sh_down, sh_up, sh_we, sh_wr, sh_eup, sh_rdown, sh_edown, sh_rup,
    all_w, all_ad, all_tw, all_tad, all_we, all_wr, all_tall, all_flat, got_hbm, cot_got, made, back,
    qkv_hbm, soft_hbm, mixed_hbm, hid_hbm, zs_hbm, pay,
    w, ad, we, wr, tall, flat, slots, cots, tail_one, tail_two, sems, copy_sems, send_sems, recv_sems, *, scopes
):
    frames, clips, places, width, padded = sizes
    rows_all, group, ff_chunk, owners = shape
    chunk = slots.shape[1]
    tails, to_tails = (tail_one, tail_two), (to_first, to_second)
    half = frames * padded
    share = members // clips
    clip, tok = lax.axis_index("clip"), lax.axis_index("tok")
    parts = [
        Part([(sh_w.at[0:2], None)], all_w.at[0:2], 1, sems.at[0]),
        Part([(sh_w.at[2], 0), (sh_o, 1)], all_w.at[2:4], 1, sems.at[1]),
        Part([(sh_down.at[0:4], slice(0, 4)), (sh_up.at[0:4], slice(4, 8))], all_ad, 1, sems.at[2]),
        Part([(sh_tw, slice(0, 3)), (sh_to, 3)], all_tw, 1, sems.at[3]),
        Part([(sh_down.at[4:8], slice(0, 4)), (sh_up.at[4:8], slice(4, 8))], all_tad, 1, sems.at[4]),
        Part([(sh_we, None)], all_we, 0, sems.at[5]),
        Part([(sh_wr, None)], all_wr, 0, sems.at[6]),
        Part([(sh_eup, 0), (sh_rdown, 1)], all_tall, 1, sems.at[7]),
        Part([(sh_edown, 0), (sh_rup, 1)], all_flat, 1, sems.at[8]),
    ]
    y, core, z, across = place_of()
    greet(tok_peers(members) + [device_at(1 - y, core, z, across), device_at(y, 1 - core, z, across)])

    def stages(plan):
        for step in range(0, len(plan), 2):
            parts["ABCDEFGHI".index(plan[step])].stage(int(plan[step + 1]))

    def exchange_sems(n):
        return send_sems.at[n], recv_sems.at[n], copy_sems.at[25 + n]

    temporal_loads = [
        pltpu.make_async_copy(all_tw, w, copy_sems.at[2]), pltpu.make_async_copy(all_tad, ad, copy_sems.at[3])
    ]
    loads = [
        pltpu.make_async_copy(source, target, copy_sems.at[n])
        for n, (source, target) in zip((0, 1, 5, 6), ((all_wr, wr), (all_tall, tall), (all_flat, flat), (all_we, we)))
    ]
    stages("A0B0C0")

    def spatial_phase(x, cot, stream, qkv, soft, mixed, hid, zs):
        load_cot = row_loads(cot_hbm, cot, 21, frames, clips, copy_sems)
        load_x = row_loads(x_hbm, x, 17, frames, clips, copy_sems)
        for load in load_cot + load_x:
            load.start()
        pads = slice(padded - 16, padded)
        for i in range(frames):
            stream[i * padded + padded - 16 : (i + 1) * padded] = jnp.zeros((16, width), BF16)
        for load in load_cot:
            load.wait()
        for b in range(clips):
            for i in range(frames):
                stream[i * padded : i * padded + places] = cot[i, b].astype(BF16)
            rows = nn(one_hot(to_send[...], half), stream[...])
            cots[b * share : (b + 1) * share] = rows.reshape(share, chunk, width).astype(BF16)
        stages("A1B1A2C1B2A3")
        for load in load_x:
            load.wait()
        for b in range(clips):
            for i in range(frames):
                base = b * half + i * padded
                zs[base + padded - 16 : base + padded] = jnp.zeros((16, width), BF16)
                zs[base : base + places] = norm_rows(
                    x[i, b], gain[0:1], shift[0:1]
                ).astype(BF16)
        stages("C2B3C3A4B4C4D0E0")
        stages("A5B5C5D1E1A6B6C6")
        loads = [pltpu.make_async_copy(all_w, w, copy_sems.at[2]), pltpu.make_async_copy(all_ad, ad, copy_sems.at[3])]
        for load in loads:
            load.start()
        stages("D2E2F0G0H0I0")
        for load in loads:
            load.wait()

        keep = lax.broadcasted_iota(jnp.int32, (2 * padded, padded), 1) < places
        pairs = width // 128
        low = lax.broadcasted_iota(jnp.int32, (padded, 128), 1) < HEAD_DIM
        far = jnp.where(tok < share, 1, 0)
        for turn in range(clips):
            b = far if turn == 0 else 1 - far
            rows = pl.ds(pl.multiple_of(b * half, 16), half)
            mask = column_mask(idx[b])

            @pl.loop(0, 3)
            def _(n):
                hidden = (nn(zs[rows], ad[n]) * mask).astype(BF16)
                hid[n, rows] = hidden
                result = nn(zs[rows], w[n]) + nt(hidden, ad[4 + n])
                result = result * jnp.where(n == 0, HEAD_DIM**-0.5, 1.0)
                qkv[n, rows] = result.astype(BF16)

            stages("D3E3" if turn == 0 else "F3G3H3I3")

            attention_all(
                (b * half, frames, padded, pairs), b * frames, qkv, soft, mixed, keep, low, SPATIAL_UNROLL
            )
            if turn == 0:
                stages("F1G1H1I1")
            hidden = (nn(mixed[rows], ad[3]) * mask).astype(BF16)
            hid[3, rows] = hidden
            branch = nn(mixed[rows], w[3]) + nt(hidden, ad[7])
            for i in range(frames):
                stream[i * padded : i * padded + places] = (
                    x[i, b] + branch[i * padded : i * padded + places]
                ).astype(BF16)
            made = nn(one_hot(to_send[...], half), stream[...]).reshape(share, chunk, width)
            slots[pl.ds(b * share, share)] = made.astype(BF16)
            send_blocks(slots, got_hbm, share, b * share, *exchange_sems(0))
            if turn == 0:
                stages("F2G2H2I2D4E4")
        stores = [
            pltpu.make_async_copy(source, target, copy_sems.at[12 + n])
            for n, (source, target) in enumerate(
                ((qkv, qkv_hbm), (soft, soft_hbm), (mixed, mixed_hbm), (hid, hid_hbm), (zs, zs_hbm))
            )
        ]
        for store in stores:
            store.start()
        stages("D5E5F4G4H4I4D6E6")
        for load in temporal_loads:
            load.start()
        for store in stores:
            store.wait()

    def middle_phase(
        got, cot, x1, x2, zt, ze, qkv, soft, mixed, hid, hide, gy, acc, pull, ghe, gmix, gqkv, gdown, gup, wide
    ):
        choice = idx[tok // share]
        mask = column_mask(choice)
        groups = rows_all // group
        wait_blocks(slots, got_hbm, members, *exchange_sems(0))
        send_blocks(cots, cot_got, members, 0, *exchange_sems(1))
        load_got = pltpu.make_async_copy(got_hbm, got, copy_sems.at[4])
        load_got.start()
        load_got.wait()

        @pl.loop(0, groups)
        def _(j):
            rows = pl.ds(pl.multiple_of(j * group, 16), group)
            own = nn(one_hot_rows(to_place[...], group, j * group), got[...])
            x1[rows] = own.astype(BF16)
            zt[rows] = norm_rows(own, gain[1:2], shift[1:2]).astype(BF16)

        for load in temporal_loads:
            load.wait()

        @pl.loop(0, 3)
        def _(n):
            hidden = (nn(zt[...], ad[n]) * mask).astype(BF16)
            hid[n] = hidden
            result = nn(zt[...], w[n]) + nt(hidden, ad[4 + n])
            result = result * jnp.where(n == 0, HEAD_DIM**-0.5, 1.0)
            qkv[n] = result.astype(BF16)

        stages("F5G5")

        pairs = width // 128
        keep = (
            lax.rem(lax.broadcasted_iota(jnp.int32, (2 * group, group), 0), group) // FRAMES
            == lax.broadcasted_iota(jnp.int32, (2 * group, group), 1) // FRAMES
        )
        low = lax.broadcasted_iota(jnp.int32, (group, 128), 1) < HEAD_DIM

        attention_all((0, groups, group, pairs), 0, qkv, soft, mixed, keep, low, MIDDLE_UNROLL)
        stages("H5I5F6G6")
        loads[3].start()
        hidden = (nn(mixed[...], ad[3]) * mask).astype(BF16)
        hid[3] = hidden
        acc[...] = nn(mixed[...], w[3]) + nt(hidden, ad[7])

        @pl.loop(0, groups)
        def _(j):
            rows = pl.ds(pl.multiple_of(j * group, 16), group)
            own = x1[rows].astype(F32) + acc[rows]
            x2[rows] = own
            acc[rows] = own
            pull[rows] = jnp.zeros((group, width), F32)
            ze[rows] = norm_rows(own, gain[2:3], shift[2:3]).astype(BF16)

        stages("H6I6")
        for load in loads[0:3]:
            load.start()
        wait_blocks(cots, cot_got, members, *exchange_sems(1))
        load_cot = pltpu.make_async_copy(cot_got, cot, copy_sems.at[4])
        load_cot.start()
        load_cot.wait()

        @pl.loop(0, groups)
        def _(j):
            rows = pl.ds(pl.multiple_of(j * group, 16), group)
            gy[rows] = nn(one_hot_rows(to_place[...], group, j * group), cot[...]).astype(BF16)

        for load in loads:
            load.wait()
        hide[...] = (nn(ze[...], flat[0]) * mask).astype(BF16)
        ghr = (nn(gy[...], flat[1]) * mask).astype(BF16)
        hid[0 + 4] = ghr
        ghe[...] = jnp.zeros(ghe.shape, F32)

        @pl.loop(0, we.shape[1] // ff_chunk)
        def _(c):
            part = pl.ds(pl.multiple_of(c * ff_chunk, ff_chunk), ff_chunk)
            inner = nn(ze[...], we[:, part]) + nt(hide[...], tall[0, part])
            cube = 0.7978845608028654 * (inner + 0.044715 * inner * inner * inner)
            bend = jnp.tanh(cube)
            act = (0.5 * inner * (1.0 + bend)).astype(BF16)
            slope = 0.5 * (1.0 + bend) + 0.5 * inner * (1.0 - bend * bend) * (
                0.7978845608028654 * (1.0 + 3.0 * 0.044715 * inner * inner)
            )
            acc[...] += nn(act, wr[part])
            ghe[0] += nn(act, tall[1, part])
            wide[0, :, part] = tn(hid[4], act)
            gact = nt(gy[...], wr[part]) + nt(hid[4], tall[1, part])
            ginner = (gact * slope).astype(BF16)
            pull[...] += nt(ginner, we[:, part])
            ghe[1] += nn(ginner, tall[0, part])
            wide[1, :, part] = tn(hide[...], ginner)

        hidr = (ghe[0] * mask).astype(BF16)
        acc[...] += nt(hidr, flat[1])
        rows = nn(one_hot(to_frame[...], got.shape[0]), acc[...].astype(BF16))
        slots[...] = rows.reshape(slots.shape).astype(BF16)
        send_blocks(slots, made, members, 0, *exchange_sems(2))
        gdown[4] = tn(hidr, gy[...])
        gheb = (ghe[1] * mask).astype(BF16)
        gup[4] = tn(gheb, ze[...])
        pull[...] += nt(gheb, flat[0])

        @pl.loop(0, groups)
        def _(j):
            rows = pl.ds(pl.multiple_of(j * group, 16), group)
            own = gy[rows].astype(F32) + norm_back(x2[rows], pull[rows], gain[2:3])
            acc[rows] = own
            ze[rows] = own.astype(BF16)

        grad = ze
        hidden_grad = (nn(grad[...], ad[7]) * mask).astype(BF16)
        gmix[...] = (nt(grad[...], w[3]) + nt(hidden_grad, ad[3])).astype(BF16)
        gdown[3] = tn(hidden_grad, mixed[...])
        gup[3] = tn(hid[3], grad[...])

        offset = 0
        for turn, (first, count) in enumerate(tail_parts):
            lines = slice(first * group, (first + count) * group)
            attention_all_back(
                (count, group, pairs), qkv, soft, gmix, gqkv, low, MIDDLE_BACK_UNROLL, first
            )
            pull[lines] = jnp.zeros((count * group, width), F32)

            @pl.loop(0, 3)
            def _(n):
                own = gqkv[n, lines]
                hidden_grad = (nn(own, ad[4 + n]) * mask).astype(BF16)
                pull[lines] += nt(own, w[n]) + nt(hidden_grad, ad[n])
                down, up = tn(hidden_grad, zt[lines]), tn(hid[n, lines], own)
                if turn == 0:
                    gdown[n], gup[n] = down, up
                else:
                    gdown[n] += down
                    gup[n] += up

            @pl.loop(first, first + count)
            def _(j):
                rows = pl.ds(pl.multiple_of(j * group, 16), group)
                own = acc[rows] + norm_back(x1[rows].astype(F32), pull[rows], gain[1:2])
                ze[rows] = own.astype(BF16)

            tail = tails[turn]
            made_rows = nn(one_hot(to_tails[turn][...], members * tail.shape[1]), ze[lines])
            tail[...] = made_rows.reshape(tail.shape).astype(BF16)
            send_blocks(tail, back, members, 0, *exchange_sems(3 + turn), offset)
            offset += members * tail.shape[1]

        pieces = []
        for n in range(4):
            pieces += [set_rows(gdown[n], choice), set_rows(gup[n], choice)]
        pay[:, 0:128] = jnp.transpose(jnp.concatenate(pieces, axis=0)).astype(BF16)
        line = lax.broadcasted_iota(jnp.int32, (128 - 2 * RANK, width), 0)
        blank = jnp.zeros((128 - 2 * RANK, width), F32)
        for k, number in enumerate((choice, idx[0], idx[1])):
            blank = jnp.where(line == k, number.astype(F32), blank)
        pay[:, 128:256] = jnp.transpose(
            jnp.concatenate([set_rows(gup[4], choice), set_rows(gdown[4], choice), blank], axis=0)
        ).astype(BF16)
        high = jnp.concatenate(
            [set_rows(wide[1], choice), set_rows(wide[0], choice), jnp.zeros((128 - 2 * RANK, we.shape[1]), F32)], axis=0
        )
        high = jnp.transpose(high)
        step = width // owners
        fold = we.shape[1] // width
        high = high.reshape(owners, fold, step, 128)
        total = high[:, 0].reshape(width, 128)
        for f in range(1, fold):
            total += pltpu.roll(high[:, f].reshape(width, 128), 2 * RANK * f, 1)
        pay[:, 256:384] = total.astype(BF16)
        wait_blocks(slots, made, members, *exchange_sems(2))
        offset = 0
        for turn, tail in enumerate(tails):
            wait_blocks(tail, back, members, *exchange_sems(3 + turn), offset)
            offset += members * tail.shape[1]

    pl.run_scoped(spatial_phase, *scopes[0])
    pl.run_scoped(middle_phase, *scopes[1])


def deliver(count, *refs):
    sources, targets, held, sems = refs[:count], refs[count : 2 * count], refs[2 * count : 3 * count], refs[3 * count]
    loads = [pltpu.make_async_copy(sources[n], held[n], sems.at[n]) for n in range(count)]
    for load in loads:
        load.start()
    stores = [pltpu.make_async_copy(held[n], targets[n], sems.at[n + count]) for n in range(count)]
    for load, store in zip(loads, stores):
        load.wait()
        store.start()
    for store in stores:
        store.wait()


def row_loads(source, target, first, frames, clips, sems):
    return [
        pltpu.make_async_copy(source.at[i, :, b, :], target.at[i, b], sems.at[first + i * clips + b])
        for i in range(frames) for b in range(clips)
    ]


def one_hot_rows(target_row, rows, first):
    row_ids = lax.broadcasted_iota(jnp.int32, (rows, target_row.shape[1]), 0) + first
    return (row_ids == target_row).astype(F32).astype(BF16)


def spread_sum(stack, columns, first, choice, count):
    lanes = lax.broadcasted_iota(jnp.int32, (columns, ADAPT), 1)
    lines = lax.broadcasted_iota(jnp.int32, (columns, ADAPT), 0)
    spread = (lines == first + lanes % RANK).astype(F32)
    wide = lax.dot_general(
        stack, spread, (((1,), (0,)), ((), ())),
        preferred_element_type=F32, precision=lax.Precision.HIGHEST,
    )
    sets = lax.broadcasted_iota(jnp.int32, (1, ADAPT), 1) // RANK
    kept = jnp.where(sets.astype(F32) == choice, wide, 0.0)
    step = stack.shape[0] // count
    total = kept[0:step]
    for k in range(1, count):
        total += kept[k * step : (k + 1) * step]
    return total


def combine_mid(sizes, got, down, up, ea, eb, ra, rb):
    groups, members, step, fold = sizes
    clips = 2
    share = members // clips
    mids = []
    for g in range(groups):
        for b in range(clips):
            part = jnp.zeros((step, 384), F32)
            for t in range(share):
                part += got[g * members + b * share + t].astype(F32)
            mids.append(part)
    mid = jnp.concatenate(mids, axis=0)
    choice = mid[:, 160:161] * (1.0 / share)
    count = groups * clips
    for n in range(4):
        for s, target in enumerate((down, up)):
            target[4 + n] = spread_sum(mid[:, 0:128], 128, (2 * n + s) * RANK, choice, count)
    ea[...] = spread_sum(mid[:, 128:256], 128, 0, choice, count)
    rb[...] = spread_sum(mid[:, 128:256], 128, RANK, choice, count)
    for f in range(fold):
        rows = slice(f * step, (f + 1) * step)
        eb[rows] = spread_sum(mid[:, 256:384], 128, 2 * RANK * f, choice, count)
        ra[rows] = spread_sum(mid[:, 256:384], 128, 2 * RANK * f + RANK, choice, count)
    choices = [
        jnp.concatenate([mids[g * clips][:, 161 + b : 162 + b] * (1.0 / share) for g in range(groups)], axis=0)
        for b in range(clips)
    ]
    return choices, choice


def combine_spatial(sizes, got, choices, down, up, first):
    groups, members, step = sizes
    clips = len(choices)
    sums = []
    for g in range(groups):
        total = jnp.zeros((step, 128), F32)
        for t in range(members):
            total += got[g * members + t].astype(F32)
        sums.append(total)
    stack = jnp.concatenate(sums, axis=0)
    for n in range(2):
        for s, target in enumerate((down, up)):
            total = jnp.zeros((step, ADAPT), F32)
            for b in range(clips):
                total += spread_sum(stack, 128, ((2 * n + s) * clips + b) * RANK, choices[b], groups)
            target[first + n] = total


def shape_of(*dims, kind=BF16):
    return jax.ShapeDtypeStruct(dims, kind)


def order_tables(frames, places, padded, blocks, part, chunk):
    half_rows, sent_rows = frames * padded, blocks * chunk
    assert half_rows == sent_rows
    to_send = [-1] * half_rows
    from_sent = [-1] * sent_rows
    for i in range(frames):
        for p in range(places):
            source, target = i * padded + p, (p // part) * chunk + i * part + p % part
            to_send[source] = target
            from_sent[target] = source
    senders = FRAMES // frames
    to_place = [-1] * (senders * chunk)
    to_frame = [-1] * (part * FRAMES)
    for p in range(part):
        for f in range(FRAMES):
            source, target = (f // frames) * chunk + (f % frames) * part + p, p * FRAMES + f
            to_place[source] = target
            to_frame[target] = source
    return [jnp.array([table], jnp.int32) for table in (to_send, from_sent, to_place, to_frame)]


def tail_tables(parts, each, frames, places, padded, blocks, part):
    rows, to_parts, region = [], [], 0
    from_parts = []
    for first, count in parts:
        own = count * each
        size = -(-frames * own // 8) * 8
        rows.append(size)
        table = [-1] * (own * FRAMES)
        for p in range(own):
            for f in range(FRAMES):
                table[p * FRAMES + f] = (f // frames) * size + (f % frames) * own + p
        to_parts.append(jnp.array([table], jnp.int32))
        source = [-1] * (blocks * size)
        for block in range(blocks):
            for f in range(frames):
                for p in range(own):
                    source[block * size + f * own + p] = f * padded + block * part + first * each + p
        from_parts += source
    return rows, to_parts, jnp.array([from_parts], jnp.int32)


def fits(mesh):
    return mesh.shape["tok"] == 8 and mesh.shape["clip"] == 4


MESH = pl.DeviceIdType.MESH


def place_of():
    clip, tok = lax.axis_index("clip"), lax.axis_index("tok")
    return clip // 2, lax.rem(clip, 2), tok // 2, lax.rem(tok, 2)


def device_at(y, core, z, x):
    return (y * 2 + core, z * 2 + x)


def greet(peers):
    barrier = pltpu.get_barrier_semaphore()
    for peer in peers:
        pl.semaphore_signal(barrier, inc=1, device_id=peer, device_id_type=MESH)
    pl.semaphore_wait(barrier, len(peers))


def remote(source, target, send_sem, recv_sem, peer):
    return pltpu.make_async_remote_copy(
        src_ref=source, dst_ref=target, send_sem=send_sem, recv_sem=recv_sem, device_id=peer, device_id_type=MESH
    )


class Part:
    def __init__(self, pieces, whole, dim, sems):
        self.pieces, self.whole, self.dim, self.sems = pieces, whole, dim, sems
        self.rows = whole.shape[dim] // (lax.axis_size("clip") * lax.axis_size("tok"))
        self.me = place_of()
        for piece, target in self.own():
            pltpu.make_async_copy(piece, target, sems.at[1]).start()

    def own(self):
        target = self.slot(*self.me)
        return [(piece, target if index is None else target.at[index]) for piece, index in self.pieces]

    def span(self, first, count, half=None):
        rows = pl.ds(pl.multiple_of(first * self.rows, 8), count * self.rows)
        if self.dim == 1:
            lead = max(self.whole.shape[0] * 3 // 4, 1)
            front = (slice(None), slice(0, lead), slice(lead, None))[0 if half is None else half + 1]
            return self.whole.at[front, rows]
        lanes = self.whole.shape[1] * 3 // 512 * 128
        return self.whole.at[rows, (slice(None), slice(0, lanes), slice(lanes, None))[0 if half is None else half + 1]]

    def slot(self, y, core, z, x, half=None):
        clip, tok = device_at(y, core, z, x)
        return self.span(clip * 8 + tok, 1, half)

    def send(self, source, target, sem, peer):
        remote(source, target, self.sems.at[0], self.sems.at[sem], device_at(*peer)).start()

    def arrive(self, target, sem):
        pltpu.make_async_copy(target, target, self.sems.at[sem]).wait()

    def pass_on(self, far, sources=None):
        y, core, z, x = self.me
        owner = (y, core, far, x)
        target = self.slot(*owner)
        for source, target in sources or [(target, target)]:
            self.send(source, target, 8 + far, (y, core, z, 1 - x))
            self.send(source, target, 12 + far, (1 - y, core, z, x))
            self.send(source, target, 2 + y, (y, 1 - core, z, x))

    def to_core(self, owner):
        y, core, z, x = self.me
        target = self.slot(*owner)
        self.send(target, target, 2 + owner[0], (y, 1 - core, z, x))

    def hop(self, far, up, sources=None):
        y, core, z, x = self.me
        target = self.slot(y, core, far, x)
        for source, target in sources or [(target, target)]:
            self.send(source, target, 4 + far, (y, core, z + up, x))

    def relay(self, distance, up):
        y, core, z, x = self.me
        far = z - distance * up
        here = z >= distance if up > 0 else z <= 3 - distance
        on = z < 3 if up > 0 else z > 0

        @pl.when(here)
        def _():
            self.arrive(self.slot(y, core, far, x), 4 + far)

            @pl.when(on)
            def _():
                self.hop(far, up)

            self.pass_on(far)

    def stage(self, number):
        y, core, z, x = self.me
        if number == 0:
            own = self.own()

            @pl.when(z < 3)
            def _():
                self.hop(z, 1, own)

            @pl.when(z > 0)
            def _():
                self.hop(z, -1, own)

            self.pass_on(z, own)
        elif number <= 3:
            self.relay(number, 1)
            self.relay(number, -1)
        elif number == 4:
            for d in range(4):
                far = lax.rem(z + 4 - d, 4)
                owner = (y, core, far, 1 - x)
                self.arrive(self.slot(*owner), 8 + far)
                self.send(self.slot(*owner, 0), self.slot(*owner, 0), 16 + far, (1 - y, core, z, x))
                self.to_core(owner)
                owner = (1 - y, core, far, x)
                self.arrive(self.slot(*owner), 12 + far)
                self.send(self.slot(*owner, 1), self.slot(*owner, 1), 20 + far, (y, core, z, 1 - x))
                self.to_core(owner)
        elif number == 5:
            for d in range(4):
                far = lax.rem(z + 4 - d, 4)
                owner = (1 - y, core, far, 1 - x)
                self.arrive(self.slot(*owner, 0), 16 + far)
                self.arrive(self.slot(*owner, 1), 20 + far)
                self.to_core(owner)
        else:
            self.arrive(self.slot(*self.me), 1)
            for far in range(2):
                self.arrive(self.span((far * 2 + 1 - core) * 8, 8), 2 + far)
            self.arrive(self.span(0, 28), 0)
            hops = jnp.where(z == 0, 1, 0) + jnp.where(z == 3, 1, 0)

            @pl.when(hops > 0)
            def _():
                self.arrive(self.span(0, 1), 0)

            @pl.when(hops == 0)
            def _():
                self.arrive(self.span(0, 5), 0)


PART_SEMS = 24


def tok_peers(count):
    clip, tok = lax.axis_index("clip"), lax.axis_index("tok")
    return [(clip, lax.rem(tok + d, count)) for d in range(1, count)]


def all_peers(groups, members):
    clip, tok = lax.axis_index("clip"), lax.axis_index("tok")
    return [
        (lax.rem(clip + c, groups), lax.rem(tok + t, members))
        for c in range(groups) for t in range(members) if c or t
    ]


def fast_device(
    tokens,
    adapter_index,
    norm_gain,
    norm_shift,
    spatial_weights,
    spatial_output,
    temporal_weights,
    temporal_output,
    expand_weight,
    reduce_weight,
    attention_down,
    attention_up,
    expand_down,
    expand_up,
    reduce_down,
    reduce_up,
    cotangent,
):
    frames, clips, places, width = tokens.shape[1:]
    members, groups = lax.axis_size("tok"), lax.axis_size("clip")
    blocks = members // clips
    part = places // blocks
    chunk = -(-frames * part // 8) * 8
    padded = -(-places // 16) * 16
    half, total = frames * padded, clips * frames * padded
    rows_all = FRAMES * part
    ff = expand_weight.shape[1]
    sizes = (frames, clips, places, width, padded)
    to_send, from_sent, to_place, to_frame = order_tables(frames, places, padded, blocks, part, chunk)
    devices = members * groups

    def placed_rows(rows):
        return rows[0].transpose(0, 2, 1, 3)

    def whole(shard, dim):
        dims = list(shard.shape)
        dims[dim] *= devices
        return jax.ShapeDtypeStruct(tuple(dims), shard.dtype)

    any_spec, vmem_spec = pl.BlockSpec(memory_space=pl.ANY), pl.BlockSpec(memory_space=pltpu.VMEM)
    smem_spec = pl.BlockSpec(memory_space=pltpu.SMEM)
    x_view, cot_view = placed_rows(tokens), placed_rows(cotangent)
    up_rows = jnp.swapaxes(attention_up, 1, 2)
    saved = [
        shape_of(3, total, width),
        shape_of(frames * clips * HEADS // 2, 2 * padded, padded),
        shape_of(total, width),
        shape_of(4, total, ADAPT),
        shape_of(total, width),
    ]
    weights = [shape_of(4, width, width), shape_of(2 * 4, width, ADAPT)]
    scratch = [pltpu.VMEM(value.shape, value.dtype) for value in saved + weights]
    group = rows_all // 7
    tail_parts = ((0, 4), (4, 3))
    tail_rows, to_tails, from_tails = tail_tables(tail_parts, group // FRAMES, frames, places, padded, blocks, part)
    regions = []
    for rows_each in tail_rows:
        regions.append((sum(members * r for r in tail_rows[: len(regions)]), blocks * rows_each))
    blocks_shape = shape_of(total, width)
    outs = pl.pallas_call(
        functools.partial(
            front, sizes, (rows_all, group, 512, devices), members, tail_parts,
            scopes=(
                [
                    pltpu.VMEM((frames, clips, places, width), F32),
                    pltpu.VMEM((frames, clips, places, width), F32),
                    pltpu.VMEM((half, width), BF16),
                    *scratch[0:5],
                ],
                [
                    pltpu.VMEM((total, width), BF16),
                    pltpu.VMEM((total, width), BF16),
                    pltpu.VMEM((rows_all, width), BF16),
                    pltpu.VMEM((rows_all, width), F32),
                    pltpu.VMEM((rows_all, width), BF16),
                    pltpu.VMEM((rows_all, width), BF16),
                    pltpu.VMEM((3, rows_all, width), BF16),
                    pltpu.VMEM((rows_all // group * HEADS // 2, 2 * group, group), BF16),
                    pltpu.VMEM((rows_all, width), BF16),
                    pltpu.VMEM((5, rows_all, ADAPT), BF16),
                    pltpu.VMEM((rows_all, ADAPT), BF16),
                    pltpu.VMEM((rows_all, width), BF16),
                    pltpu.VMEM((rows_all, width), F32),
                    pltpu.VMEM((rows_all, width), F32),
                    pltpu.VMEM((2, rows_all, ADAPT), F32),
                    pltpu.VMEM((rows_all, width), BF16),
                    pltpu.VMEM((3, rows_all, width), BF16),
                    pltpu.VMEM((5, ADAPT, width), F32),
                    pltpu.VMEM((5, ADAPT, width), F32),
                    pltpu.VMEM((2, ADAPT, ff), F32),
                ],
            ),
        ),
        out_shape=[
            *weights, *weights, whole(expand_weight, 0), whole(reduce_weight, 0), shape_of(2, ff, ADAPT),
            shape_of(2, width, ADAPT), blocks_shape, blocks_shape, blocks_shape, blocks_shape, *saved,
            shape_of(width, 384),
        ],
        in_specs=[smem_spec] + [vmem_spec] * 5 + [any_spec] * 2 + [vmem_spec] * 2 + [any_spec] * 12,
        out_specs=[any_spec] * 17 + [vmem_spec],
        scratch_shapes=[
            *scratch[5:7],
            pltpu.VMEM((width, ff), BF16),
            pltpu.VMEM((ff, width), BF16),
            pltpu.VMEM((2, ff, ADAPT), BF16),
            pltpu.VMEM((2, width, ADAPT), BF16),
            pltpu.VMEM((members, chunk, width), BF16),
            pltpu.VMEM((members, chunk, width), BF16),
            *[pltpu.VMEM((members, rows_each, width), BF16) for rows_each in tail_rows],
            pltpu.SemaphoreType.DMA((9, PART_SEMS)),
            pltpu.SemaphoreType.DMA((30,)),
            pltpu.SemaphoreType.DMA((5, members)),
            pltpu.SemaphoreType.DMA((5, members)),
        ],
        compiler_params=pltpu.CompilerParams(collective_id=0, has_side_effects=True, vmem_limit_bytes=63 << 20),
        name="front",
    )(
        adapter_index, to_send, to_place, to_frame, *to_tails, x_view, cot_view, norm_gain, norm_shift,
        spatial_weights, spatial_output, temporal_weights, temporal_output, attention_down, up_rows,
        expand_weight, reduce_weight, expand_up.T, reduce_down, expand_down, reduce_up.T,
    )
    sp_w, sp_adapt = outs[0:2]
    made, back, *kept, mid_pay = outs[10:18]
    step = width // devices
    fold = ff // width
    results = pl.pallas_call(
        functools.partial(spatial_backward, sizes, groups, members, step, regions),
        out_shape=[
            shape_of(*x_view.shape, kind=F32),
            shape_of(*x_view.shape, kind=F32),
            shape_of(8, step, ADAPT, kind=F32),
            shape_of(8, step, ADAPT, kind=F32),
            shape_of(step, ADAPT, kind=F32),
            shape_of(fold * step, ADAPT, kind=F32),
            shape_of(fold * step, ADAPT, kind=F32),
            shape_of(step, ADAPT, kind=F32),
        ],
        in_specs=[smem_spec, vmem_spec, vmem_spec, vmem_spec] + [any_spec] * 11,
        out_specs=[any_spec] * 2 + [vmem_spec] * 6,
        scratch_shapes=[
            *scratch[5:7],
            *scratch[0:5],
            pltpu.VMEM((total, width), BF16),
            pltpu.VMEM((total, width), BF16),
            pltpu.VMEM((frames, clips, places, width), F32),
            pltpu.VMEM((frames, clips, places, width), F32),
            pltpu.VMEM((devices, step, 384), BF16),
            *[pltpu.VMEM((devices, step, 128), BF16)] * 4,
            pltpu.VMEM((total, width), BF16),
            pltpu.VMEM((total, width), BF16),
            pltpu.VMEM((3, total, width), BF16),
            pltpu.VMEM((clips, half, width), F32),
            pltpu.VMEM((4, ADAPT, width), F32),
            pltpu.VMEM((4, ADAPT, width), F32),
            pltpu.SemaphoreType.DMA((21,)),
            pltpu.SemaphoreType.DMA((3, devices - 1)),
            pltpu.SemaphoreType.DMA((3, devices - 1)),
        ],
        compiler_params=pltpu.CompilerParams(collective_id=1, has_side_effects=True, vmem_limit_bytes=63 << 20),
        name="spatial_back",
    )(
        adapter_index, from_sent, from_tails, norm_gain, x_view, sp_w, sp_adapt, *kept, back, made,
        mid_pay.reshape(devices, step, 384),
    )
    dx, out, down, up, gea, geb, gra, grb = pl.pallas_call(
        functools.partial(deliver, len(results)),
        out_shape=[jax.ShapeDtypeStruct(value.shape, value.dtype) for value in results],
        in_specs=[any_spec] * len(results),
        out_specs=[any_spec] * len(results),
        scratch_shapes=[pltpu.VMEM(value.shape, value.dtype) for value in results]
        + [pltpu.SemaphoreType.DMA((2 * len(results),))],
        name="deliver",
    )(*results)

    def whole_rows(rows):
        return rows.transpose(0, 2, 1, 3)[None]

    return (whole_rows(out), whole_rows(dx), down, jnp.swapaxes(up, 1, 2), gea, geb.T, gra, grb.T)


def solution(mesh):
    pick = fast_device if fits(mesh) else general_device

    placed = (
        P(("clip", "tok"), None, None, None, None),
        P("clip"),
        P(),
        P(),
        P(None, ("clip", "tok"), None),
        P(("clip", "tok"), None),
        P(None, ("clip", "tok"), None),
        P(("clip", "tok"), None),
        P(("clip", "tok"), None),
        P(("clip", "tok"), None),
        P(None, ("clip", "tok"), None),
        P(None, None, ("clip", "tok")),
        P(("clip", "tok"), None),
        P(None, ("clip", "tok")),
        P(("clip", "tok"), None),
        P(None, ("clip", "tok")),
        P(("clip", "tok"), None, None, None, None),
    )
    return jax.shard_map(
        pick,
        mesh=mesh,
        in_specs=placed,
        out_specs=(
            P(("clip", "tok"), None, None, None, None),
            P(("clip", "tok"), None, None, None, None),
            P(None, ("clip", "tok"), None),
            P(None, None, ("clip", "tok")),
            P(("clip", "tok"), None),
            P(None, ("clip", "tok")),
            P(("clip", "tok"), None),
            P(None, ("clip", "tok")),
        ),
        check_vma=False,
    )
```
